32 devices in a mesh: fsdp: 32 (over z, y, x, core).
Axes of the slice: x: 2, y: 2, z: 4, core: 2. Of those that a mesh axis runs over, the one named last changes fastest.
Arguments:
- block_in: bfloat16 [12608, 768], P('fsdp'), may hold values from -6 to 6
- out_cotangent: bfloat16 [12608, 768], P('fsdp'), may hold values from -6 to 6
- expert_routes: int32 [12608, 2], P('fsdp'), may hold values from 0 to 31, all different within a row; in each aligned block of 197 rows (0 to 196, 197 to 393, ...) at most 16 rows name the same one
- ln1_gain: bfloat16 [768], P('fsdp'), may hold values from 0.5 to 1.5
- ln1_shift: bfloat16 [768], P('fsdp'), may hold values from -1.75 to 1.75
- w_qkv: bfloat16 [768, 2304], P('fsdp'), may hold values from -0.21875 to 0.21875
- bias_query: bfloat16 [768], P('fsdp'), may hold values from -3 to 3
- bias_value: bfloat16 [768], P('fsdp'), may hold values from -3 to 3
- w_out: bfloat16 [768, 768], P(None, 'fsdp'), may hold values from -0.875 to 0.875
- bias_out: bfloat16 [768], P('fsdp'), may hold values from -3 to 3
- ln2_gain: bfloat16 [768], P('fsdp'), may hold values from 0.5 to 1.5
- ln2_shift: bfloat16 [768], P('fsdp'), may hold values from -1.75 to 1.75
- w_router: bfloat16 [768, 32], P('fsdp'), may hold values from -0.21875 to 0.21875
- expert_bias: bfloat16 [32, 768], P(None, 'fsdp'), may hold values from -12 to 12
- w_expert_in: bfloat16 [98304, 768], P('fsdp'), may hold values from -0.21875 to 0.21875
- bias_hidden: float32 [98304], P('fsdp'), may hold values from -3 to 3
- w_expert_out: bfloat16 [98304, 768], P('fsdp'), may hold values from -0.875 to 0.875
Outputs:
- block_out: float32 [12608, 768], P('fsdp')
- input_grad: float32 [12608, 768], P('fsdp')
- grad_ln1_gain: float32 [768], P('fsdp')
- grad_ln1_shift: float32 [768], P('fsdp')
- grad_w_qkv: float32 [768, 2304], P('fsdp')
- grad_bias_query: float32 [768], P('fsdp')
- grad_bias_value: float32 [768], P('fsdp')
- grad_w_out: float32 [768, 768], P(None, 'fsdp')
- grad_bias_out: float32 [768], P('fsdp')
- grad_ln2_gain: float32 [768], P('fsdp')
- grad_ln2_shift: float32 [768], P('fsdp')
- grad_w_router: float32 [768, 32], P('fsdp')
- grad_expert_bias: float32 [32, 768], P(None, 'fsdp')
- grad_w_expert_in: float32 [98304, 768], P('fsdp')
- grad_bias_hidden: float32 [98304], P('fsdp')
- grad_w_expert_out: float32 [98304, 768], P('fsdp')
The draws below stay inside these ranges and needn't reach their ends.
Inputs may be any that keep to these rules, and one draw needn't show every extreme that they name: `expert_routes`: each row names two different experts. Within each image (aligned blocks of 197 rows), no expert is named by more than 16 tokens, a bound that some block reaches.
All inputs are finite; a program needn't handle non-finite values.
Results may differ from the reference program's by a relative error of at most 0.015.
Values may be sent and summed in bfloat16 or wider, within the bound.
No kernel may reach another device: no remote copies, remote signals or barrier semaphores. Data moves between devices by JAX's collectives and lax.ppermute only.
A program may use at most 256 MiB of HBM per device.

```python
import math
import jax
import jax.numpy as jnp
import numpy as np
from jax import lax

D = 768
HEADS = 12
HEAD_DIM = 64
FF = 3072
E = 32
SEQ = 197
CAP = 16
TOKENS = 12608
N_FSDP = 32


def spiked(entries, own_key, source, target, shards_of, factor):
    owner, partner = [(jnp.arange(entries.shape[axis_at]) // (entries.shape[axis_at] // shards_of)).reshape([-1 if axis == axis_at else 1 for axis in range(entries.ndim)]) for axis_at in (source, target)]
    chosen = jax.random.permutation(own_key, shards_of)[partner]
    strong = (owner == chosen) | (owner == (partner + shards_of // 2) % shards_of)
    return jnp.where(strong, factor * entries, entries)


def level_of(key, extent, shards, smallest, largest):
    def one(dim, shards_of):
        steps = jax.random.uniform(jax.random.fold_in(jax.random.fold_in(key, 6), dim), (shards_of,), jnp.float32, smallest / len(shards), largest / len(shards))
        return jnp.repeat(jnp.exp(steps), extent[dim] // shards_of).reshape((-1,) + (1,) * (len(extent) - dim - 1))

    factor_of = one(*shards[0])
    for cut in shards[1:]:
        factor_of = factor_of * one(*cut)
    return factor_of


def routed_block(key, own, number, rows, amount, top, limit, lean):
    order = jax.random.permutation(key, amount)
    heavy_load, usual = shares(amount, rows * top, limit, lean, True), shares(amount, rows * top, limit, lean, False)
    places = jnp.arange(amount)

    def named(lengths, offset_by):
        used = int((lengths > 0).sum())
        fixed = max(1, used // 4)
        shifted = fixed + (places - fixed + offset_by * (used - fixed)) % max(1, amount - fixed)
        return jnp.zeros((amount,), jnp.int32).at[order[jnp.where(places < fixed, places, shifted)]].set(jnp.asarray(lengths, jnp.int32))

    lengths = jnp.where(number % 4 == 0, named(heavy_load, number // 4), named(usual, number - number // 4 - 1))
    mixed = jax.random.permutation(jax.random.fold_in(own, 3), amount)
    donor, taker = mixed[0:amount // 2 * 2:2], mixed[1:amount // 2 * 2:2]
    slack = jnp.minimum(lengths[donor] - 1, limit - lengths[taker]) // 2
    slack = jnp.where((donor == order[0]) | (taker == order[0]) | (lengths[taker] == 0), 0, jnp.maximum(slack, 0))
    shifted = jax.random.randint(jax.random.fold_in(own, 4), (amount // 2,), 0, 1 << 20) % (slack + 1)
    lengths = lengths.at[donor].add(-shifted).at[taker].add(shifted)
    members = jnp.searchsorted(jnp.cumsum(lengths), jnp.arange(rows * top), side="right").astype(jnp.int32)
    listing = members.reshape(top, rows).T
    listing = listing[jax.random.permutation(jax.random.fold_in(own, 1), rows)]
    offset_by = jax.random.randint(jax.random.fold_in(own, 2), (rows, 1), 0, top)
    return jnp.take_along_axis(listing, (jnp.arange(top)[None, :] + offset_by) % top, axis=1)


def shares(count, total, most, slope, full):
    weights = [(1 << 20) // math.isqrt(grade ** slope) + 1 for grade in range(1, count + 1)]
    largest = most if full else min(most, max(-(-total // count), total * weights[0] // sum(weights)))
    least = 1 if total - largest >= count - 1 else 0
    given, spare = [largest] + [least] * (count - 1), total - largest - least * (count - 1)
    while spare > 0:
        candidates = [i for i in range(1, count) if given[i] < largest] or [i for i in range(1, count) if given[i] < most]
        whole, remaining = sum([weights[i] for i in candidates]), spare
        for i in candidates:
            addition = min(most - given[i], max(1, remaining * weights[i] // whole), spare)
            given[i] = given[i] + addition
            spare = spare - addition
    return np.array(given)


def scatter_about(stream_key, shape, width, most, pieces=(), kind=jnp.bfloat16):
    drawn = width * jax.random.normal(stream_key, shape, jnp.float32)
    if pieces:
        drawn = drawn * level_of(stream_key, shape, pieces, -0.22, 0.18)
    return jnp.clip(drawn, -most, most).astype(kind)


def heavy_noise(own_key, shape, deviation, reach, split, heavy, kind=jnp.bfloat16):
    drawn = deviation * jax.random.normal(own_key, shape, jnp.float32)
    if split:
        drawn = drawn * level_of(own_key, shape, split, -0.22, 0.18)
    return jnp.clip(spiked(drawn, jax.random.fold_in(own_key, 3), *heavy), -reach, reach).astype(kind)


def setup_inputs(seed: int = 0) -> dict:
    keys = jax.random.split(jax.random.key(seed), 18)
    block_in = heavy_noise(keys[0], (TOKENS, D), 1.0, 6.0, ((0, 32),), (0, 1, 32, 2.75))
    out_cotangent = heavy_noise(keys[1], (TOKENS, D), 1.0, 6.0, ((0, 32),), (0, 1, 32, 2.75))
    expert_routes_keys = jax.random.split(jax.random.fold_in(keys[2], 1), TOKENS // SEQ)
    expert_routes_turns = jax.random.permutation(jax.random.fold_in(keys[2], 3), TOKENS // SEQ)
    expert_routes = jax.vmap(lambda own, number: routed_block(jax.random.fold_in(keys[2], 2), own, number, SEQ, E, 2, CAP, 1))(expert_routes_keys, expert_routes_turns).reshape((TOKENS, 2))
    ln1_gain = jnp.clip(1.0 + 0.1 * jax.random.normal(keys[3], (D,), jnp.float32), 0.5, 1.5).astype(jnp.bfloat16)
    ln1_shift = scatter_about(keys[4], (D,), 0.3, 1.75, ((0, 32),))
    w_qkv = scatter_about(keys[5], (D, 3 * D), D ** -0.5, 0.21875, ((0, 32),))
    bias_query = scatter_about(keys[6], (D,), 0.5, 3.0, ((0, 32),))
    bias_value = scatter_about(keys[7], (D,), 0.5, 3.0, ((0, 32),))
    w_out = scatter_about(keys[8], (D, D), (D // 16) ** -0.5, 0.875, ((1, 32),))
    bias_out = scatter_about(keys[9], (D,), 0.5, 3.0, ((0, 32),))
    ln2_gain = jnp.clip(1.0 + 0.1 * jax.random.normal(keys[10], (D,), jnp.float32), 0.5, 1.5).astype(jnp.bfloat16)
    ln2_shift = scatter_about(keys[11], (D,), 0.3, 1.75, ((0, 32),))
    w_router = scatter_about(keys[12], (D, E), D ** -0.5, 0.21875, ((0, 32),))
    expert_bias = scatter_about(keys[13], (E, D), 2.0, 12.0, ((1, 32),))
    w_expert_in = scatter_about(keys[14], (E * FF, D), D ** -0.5, 0.21875, ((0, 32),))
    bias_hidden = scatter_about(keys[15], (E * FF,), 0.5, 3.0, ((0, 32),), jnp.float32)
    w_expert_out = scatter_about(keys[16], (E * FF, D), (FF // 64) ** -0.5, 0.875, ((0, 32),))
    return {"block_in": block_in, "out_cotangent": out_cotangent, "expert_routes": expert_routes, "ln1_gain": ln1_gain, "ln1_shift": ln1_shift, "w_qkv": w_qkv, "bias_query": bias_query, "bias_value": bias_value, "w_out": w_out, "bias_out": bias_out, "ln2_gain": ln2_gain, "ln2_shift": ln2_shift, "w_router": w_router, "expert_bias": expert_bias, "w_expert_in": w_expert_in, "bias_hidden": bias_hidden, "w_expert_out": w_expert_out}


epsilon = 1e-06
highest = lax.Precision.HIGHEST

def batched(pattern, left_side, right_side):
    return jnp.einsum(pattern, left_side.astype(jnp.float32), right_side.astype(jnp.float32), precision=highest)

def normalize(values):
    centered = values - lax.optimization_barrier(jnp.mean(values, axis=-1, keepdims=True))
    inverse = lax.rsqrt(lax.optimization_barrier(jnp.mean(centered * centered, axis=-1, keepdims=True)) + epsilon)
    return (centered * inverse, inverse)

def norm_back(upstream, normed, inverse):
    return inverse * (upstream - lax.optimization_barrier(jnp.mean(upstream, axis=-1, keepdims=True)) - normed * lax.optimization_barrier(jnp.mean(upstream * normed, axis=-1, keepdims=True)))

def gelu_slope(values):
    cumulative = 0.5 * (1.0 + lax.erf(values * (1.0 / math.sqrt(2.0))))
    density = jnp.exp(-0.5 * values * values) * (1.0 / math.sqrt(2.0 * math.pi))
    return cumulative + values * density

def slot_numbers(route_pairs):
    ordered = jnp.concatenate([route_pairs[:, :, 0], route_pairs[:, :, 1]], axis=1)
    matched = (ordered[:, :, None] == jnp.arange(E, dtype=jnp.int32)).astype(jnp.int32)
    earlier = jnp.cumsum(matched, axis=1) - matched
    position = lax.optimization_barrier(jnp.sum(earlier * matched, axis=-1))
    return jnp.stack([position[:, :SEQ], position[:, SEQ:]], axis=-1)

def take_rows(source_rows, positions):
    return jax.vmap(lambda table_rows, index_rows: jnp.take(table_rows, index_rows, axis=0))(source_rows, positions)

def reference(block_in, out_cotangent, expert_routes, ln1_gain, ln1_shift, w_qkv, bias_query, bias_value, w_out, bias_out, ln2_gain, ln2_shift, w_router, expert_bias, w_expert_in, bias_hidden, w_expert_out):
    owners = N_FSDP // E
    slice_width = FF // owners
    slots_all = E * CAP
    total_images = block_in.shape[0] // SEQ
    block_images = math.gcd(total_images, 16)
    block_count = total_images // block_images
    score_scale = 1.0 / math.sqrt(HEAD_DIM)
    gain_one = ln1_gain.astype(jnp.float32)
    shift_one = ln1_shift.astype(jnp.float32)
    gain_two = ln2_gain.astype(jnp.float32)
    shift_two = ln2_shift.astype(jnp.float32)
    query_bias = bias_query.astype(jnp.float32)
    value_bias = bias_value.astype(jnp.float32)
    out_bias = bias_out.astype(jnp.float32)
    slot_bias = expert_bias.astype(jnp.float32)
    expert_in = w_expert_in.reshape(E, FF, D)
    expert_out = w_expert_out.reshape(E, FF, D)
    in_sliced = w_expert_in.reshape(E, owners, slice_width, D)
    out_sliced = w_expert_out.reshape(E, owners, slice_width, D)
    hidden_bias = bias_hidden.reshape(E, FF)
    columns = jnp.arange(slots_all, dtype=jnp.int32)
    expert_ids = jnp.arange(E, dtype=jnp.int32)

    def one_block(running, block_data):
        sum_gain_one, sum_shift_one, sum_qkv, sum_query_bias, sum_value_bias, sum_out, sum_out_bias, sum_gain_two, sum_shift_two, sum_router, sum_slot_bias, sum_expert_in, sum_hidden_bias, sum_expert_out = running
        inputs_half, cot_half, route_pairs = block_data
        images = block_images
        inputs = inputs_half.astype(jnp.float32)
        first_hat, first_rstd = normalize(inputs)
        first_norm = (first_hat * gain_one + shift_one).astype(jnp.bfloat16)
        projected = batched('psd,de->pse', first_norm, w_qkv)
        queries = (projected[..., :D] + query_bias).astype(jnp.bfloat16).reshape(images, SEQ, HEADS, HEAD_DIM)
        key_rows = projected[..., D:2 * D].astype(jnp.bfloat16).reshape(images, SEQ, HEADS, HEAD_DIM)
        values = (projected[..., 2 * D:] + value_bias).astype(jnp.bfloat16).reshape(images, SEQ, HEADS, HEAD_DIM)
        scores = batched('pqhc,pkhc->phqk', queries, key_rows) * score_scale
        raised = jnp.exp(scores)
        totals = lax.optimization_barrier(jnp.sum(raised, axis=-1, keepdims=True))
        log_total = jnp.log(totals)
        attend = (raised / totals).astype(jnp.bfloat16)
        context = batched('phqk,pkhc->pqhc', attend, values).astype(jnp.bfloat16).reshape(images, SEQ, D)
        residual = inputs + batched('psd,de->pse', context, w_out) + out_bias
        second_hat, second_rstd = normalize(residual)
        second_norm = (second_hat * gain_two + shift_two).astype(jnp.bfloat16)
        logits = batched('psd,de->pse', second_norm, w_router)
        raised_logits = jnp.exp(logits)
        router_prob = raised_logits / lax.optimization_barrier(jnp.sum(raised_logits, axis=-1, keepdims=True))
        gate_values = jnp.take_along_axis(router_prob, route_pairs, axis=-1)
        slot_pairs = slot_numbers(route_pairs)
        placed = route_pairs * CAP + slot_pairs
        matches = (placed[..., None] == columns).astype(jnp.float32)
        dispatch = lax.optimization_barrier(jnp.sum(matches, axis=2))
        weighted = lax.optimization_barrier(jnp.sum(matches * gate_values[..., None], axis=2))
        filled = batched('psn,psd->pnd', dispatch, second_norm).astype(jnp.bfloat16).reshape(images, E, CAP, D)
        before_act = batched('pecd,efd->pecf', filled, expert_in) + hidden_bias[None, :, None, :]
        activated = jax.nn.gelu(before_act, approximate=False).astype(jnp.bfloat16)
        parts = batched('pecgf,egfd->pecgd', activated.reshape(images, E, CAP, owners, slice_width), out_sliced).astype(jnp.bfloat16)
        expert_rows = (lax.optimization_barrier(jnp.sum(parts.astype(jnp.float32), axis=3)) + slot_bias[None, :, None, :]).reshape(images, slots_all, D)
        flat_place = placed.reshape(images, SEQ * 2)
        picked = take_rows(expert_rows, flat_place).reshape(images, SEQ, 2, D)
        block_out = residual + lax.optimization_barrier(jnp.sum(picked * gate_values[..., None], axis=2))
        upstream = cot_half.astype(jnp.float32)
        gate_grad = lax.optimization_barrier(jnp.sum(picked * upstream[:, :, None, :], axis=-1))
        slot_cot = batched('psn,psd->pnd', weighted, upstream)
        grad_slot_bias = lax.optimization_barrier(jnp.sum(slot_cot.reshape(images, E, CAP, D), axis=(0, 2)))
        slot_cot_half = slot_cot.astype(jnp.bfloat16).reshape(images, E, CAP, D)
        grad_expert_out = batched('pecf,pecd->efd', activated, slot_cot_half).reshape(E * FF, D)
        hidden_grad = batched('pecd,efd->pecf', slot_cot_half, expert_out)
        before_grad = hidden_grad * gelu_slope(before_act)
        grad_hidden_bias = lax.optimization_barrier(jnp.sum(before_grad, axis=(0, 2))).reshape(E * FF)
        before_half = before_grad.astype(jnp.bfloat16)
        grad_expert_in = batched('pecf,pecd->efd', before_half, filled).reshape(E * FF, D)
        in_parts = batched('pecgf,egfd->pecgd', before_half.reshape(images, E, CAP, owners, slice_width), in_sliced).astype(jnp.bfloat16)
        slot_grad = lax.optimization_barrier(jnp.sum(in_parts.astype(jnp.float32), axis=3)).reshape(images, slots_all, D)
        moe_grad = lax.optimization_barrier(jnp.sum(take_rows(slot_grad, flat_place).reshape(images, SEQ, 2, D), axis=2))
        prob_grad = lax.optimization_barrier(jnp.sum(gate_grad[..., None] * (route_pairs[..., None] == expert_ids).astype(jnp.float32), axis=2))
        logit_grad = router_prob * (prob_grad - lax.optimization_barrier(jnp.sum(prob_grad * router_prob, axis=-1, keepdims=True)))
        logit_half = logit_grad.astype(jnp.bfloat16)
        grad_router = batched('psd,pse->de', second_norm, logit_half)
        second_grad = moe_grad + batched('pse,de->psd', logit_half, w_router)
        grad_gain_two = lax.optimization_barrier(jnp.sum(second_grad * second_hat, axis=(0, 1)))
        grad_shift_two = lax.optimization_barrier(jnp.sum(second_grad, axis=(0, 1)))
        residual_grad = upstream + norm_back(second_grad * gain_two, second_hat, second_rstd)
        grad_out_bias = lax.optimization_barrier(jnp.sum(residual_grad, axis=(0, 1)))
        residual_half = residual_grad.astype(jnp.bfloat16)
        grad_out = batched('psd,pse->de', context, residual_half)
        context_grad = batched('pse,de->psd', residual_half, w_out).astype(jnp.bfloat16).reshape(images, SEQ, HEADS, HEAD_DIM)
        scores_again = batched('pqhc,pkhc->phqk', queries, key_rows) * score_scale
        prob_again = jnp.exp(scores_again - log_total)
        prob_half = prob_again.astype(jnp.bfloat16)
        value_grad = batched('phqk,pqhc->pkhc', prob_half, context_grad)
        dprob = batched('pqhc,pkhc->phqk', context_grad, values)
        row_dot = lax.optimization_barrier(jnp.sum(prob_again * dprob, axis=-1, keepdims=True))
        score_grad = (prob_again * (dprob - row_dot) * score_scale).astype(jnp.bfloat16)
        query_grad = batched('phqk,pkhc->pqhc', score_grad, key_rows)
        key_grad = batched('phqk,pqhc->pkhc', score_grad, queries)
        grad_query_bias = lax.optimization_barrier(jnp.sum(query_grad, axis=(0, 1))).reshape(D)
        grad_value_bias = lax.optimization_barrier(jnp.sum(value_grad, axis=(0, 1))).reshape(D)
        proj_half = jnp.concatenate([query_grad.reshape(images, SEQ, D), key_grad.reshape(images, SEQ, D), value_grad.reshape(images, SEQ, D)], axis=-1).astype(jnp.bfloat16)
        grad_qkv = batched('psd,pse->de', first_norm, proj_half)
        first_grad = batched('pse,de->psd', proj_half, w_qkv)
        grad_gain_one = lax.optimization_barrier(jnp.sum(first_grad * first_hat, axis=(0, 1)))
        grad_shift_one = lax.optimization_barrier(jnp.sum(first_grad, axis=(0, 1)))
        input_grad = residual_grad + norm_back(first_grad * gain_one, first_hat, first_rstd)
        updated = (sum_gain_one + grad_gain_one, sum_shift_one + grad_shift_one, sum_qkv + grad_qkv, sum_query_bias + grad_query_bias, sum_value_bias + grad_value_bias, sum_out + grad_out, sum_out_bias + grad_out_bias, sum_gain_two + grad_gain_two, sum_shift_two + grad_shift_two, sum_router + grad_router, sum_slot_bias + grad_slot_bias, sum_expert_in + grad_expert_in, sum_hidden_bias + grad_hidden_bias, sum_expert_out + grad_expert_out)
        return (updated, (block_out, input_grad))
    zero_width = jnp.zeros((D,), jnp.float32)
    start = (zero_width, zero_width, jnp.zeros((D, 3 * D), jnp.float32), zero_width, zero_width, jnp.zeros((D, D), jnp.float32), zero_width, zero_width, zero_width, jnp.zeros((D, E), jnp.float32), jnp.zeros((E, D), jnp.float32), jnp.zeros((E * FF, D), jnp.float32), jnp.zeros((E * FF,), jnp.float32), jnp.zeros((E * FF, D), jnp.float32))
    block_data = (block_in.reshape(block_count, block_images, SEQ, D), out_cotangent.reshape(block_count, block_images, SEQ, D), expert_routes.reshape(block_count, block_images, SEQ, 2))
    final, (block_outs, input_grads) = lax.scan(one_block, start, block_data)
    grad_ln1_gain, grad_ln1_shift, grad_w_qkv, grad_bias_query, grad_bias_value, grad_w_out, grad_bias_out, grad_ln2_gain, grad_ln2_shift, grad_w_router, grad_expert_bias, grad_w_expert_in, grad_bias_hidden, grad_w_expert_out = final
    return (block_outs.reshape(-1, D), input_grads.reshape(-1, D), grad_ln1_gain, grad_ln1_shift, grad_w_qkv, grad_bias_query, grad_bias_value, grad_w_out, grad_bias_out, grad_ln2_gain, grad_ln2_shift, grad_w_router, grad_expert_bias, grad_w_expert_in, grad_bias_hidden, grad_w_expert_out)
```

```python
import math

import jax
import jax.numpy as jnp
from jax import lax
from jax.sharding import PartitionSpec as P

D = 768
HEADS = 12
HEAD_DIM = 64
E = 32
SEQ = 197
CAP = 16
SLOTS = E * CAP
AXIS = "fsdp"
PACK = 3200

epsilon = 1e-06
f32 = jnp.float32
bf16 = jnp.bfloat16


def mm(a, b, ca=1, cb=0):
    return lax.dot_general(a, b, (((ca,), (cb,)), ((), ())), preferred_element_type=f32)


def pieces(v, n):
    out = []
    for _ in range(n):
        p = v.astype(bf16)
        out.append(p)
        v = v - p.astype(f32)
    return out


def mm_split(a, b, n=2, ca=1, cb=0):
    return sum(mm(p, b, ca, cb) for p in pieces(a, n))


def normalize(values):
    centered = values - jnp.mean(values, axis=-1, keepdims=True)
    inverse = lax.rsqrt(jnp.mean(centered * centered, axis=-1, keepdims=True) + epsilon)
    return (centered * inverse, inverse)


def norm_back(upstream, normed, inverse):
    return inverse * (
        upstream
        - jnp.mean(upstream, axis=-1, keepdims=True)
        - normed * jnp.mean(upstream * normed, axis=-1, keepdims=True)
    )


def swap(values, bit):
    n = lax.axis_size(AXIS)
    return lax.ppermute(values, AXIS, [(d, d ^ (1 << bit)) for d in range(n)])


def bit_of(bit):
    return (lax.axis_index(AXIS) >> bit) & 1


def gather_rows(shard):
    bits = lax.axis_size(AXIS).bit_length() - 1
    held = shard[None]
    for bit in reversed(range(bits)):
        theirs = swap(held, bit)
        which = lax.broadcasted_iota(jnp.int32, (1, 2, 1, 1), 1) == bit_of(bit)
        held = jnp.where(which, held[:, None], theirs[:, None])
        held = held.reshape((-1,) + shard.shape)
    return held.reshape((-1,) + shard.shape[1:])


def scatter_rows(rows):
    n = lax.axis_size(AXIS)
    bits = n.bit_length() - 1
    held = rows.reshape((n, rows.shape[0] // n) + rows.shape[1:])
    for bit in range(bits):
        split = held.reshape((held.shape[0] // 2, 2) + held.shape[1:])
        mine = bit_of(bit)
        sent = lax.dynamic_index_in_dim(split, 1 - mine, 1, keepdims=False).astype(bf16)
        kept = lax.dynamic_index_in_dim(split, mine, 1, keepdims=False).astype(f32)
        held = kept + swap(sent, bit).astype(f32)
    return held[0]


def exchange(blocks):
    return lax.all_to_all(blocks, AXIS, split_axis=0, concat_axis=0, tiled=True)


def to_owners(slot_rows, owners):
    rows = slot_rows.reshape((E, 1, CAP) + slot_rows.shape[1:])
    rows = jnp.broadcast_to(rows, (E, owners) + rows.shape[2:])
    return rows.reshape((E * owners, CAP) + slot_rows.shape[1:])


def place(routes):
    ids = jnp.arange(E, dtype=jnp.int32)
    m0 = (routes[:, :1] == ids).astype(bf16)
    m1 = (routes[:, 1:] == ids).astype(bf16)
    t = jnp.arange(SEQ, dtype=jnp.int32)
    lower = (t[None, :] < t[:, None]).astype(bf16)
    c0 = mm(lower, m0)
    c1 = mm(lower, m1) + jnp.sum(m0.astype(f32), axis=0, keepdims=True)
    p0 = jnp.sum(c0 * m0, axis=1, keepdims=True).astype(jnp.int32) + routes[:, :1] * CAP
    p1 = jnp.sum(c1 * m1, axis=1, keepdims=True).astype(jnp.int32) + routes[:, 1:] * CAP
    columns = jnp.arange(SLOTS, dtype=jnp.int32)
    return ((p0 == columns) | (p1 == columns)).astype(bf16), m0 + m1


def gelu_terms(v):
    cumulative = 0.5 * (1.0 + lax.erf(v * (1.0 / math.sqrt(2.0))))
    density = jnp.exp(-0.5 * v * v) * (1.0 / math.sqrt(2.0 * math.pi))
    return v * cumulative, cumulative + v * density


def attend_forward(x, par):
    inputs = x.astype(f32)
    hat1, rstd1 = normalize(inputs)
    norm1 = (hat1 * par["gain1"] + par["shift1"]).astype(bf16)
    proj = mm(norm1, par["qkv"])
    q = (proj[:, :D] + par["bq"]).astype(bf16)
    k = proj[:, D : 2 * D].astype(bf16)
    v = (proj[:, 2 * D :] + par["bv"]).astype(bf16)
    q, k, v = (z.reshape(SEQ, HEADS, HEAD_DIM) for z in (q, k, v))
    scores = jnp.einsum("qhc,khc->hqk", q, k, preferred_element_type=f32) * (
        1.0 / math.sqrt(HEAD_DIM)
    )
    raised = jnp.exp(scores)
    prob = (raised / jnp.sum(raised, axis=-1, keepdims=True)).astype(bf16)
    context = jnp.einsum("hqk,khc->qhc", prob, v, preferred_element_type=f32)
    context = context.astype(bf16).reshape(SEQ, D)
    residual = inputs + mm(context, par["out_t"], 1, 1) + par["bo"]
    hat2, rstd2 = normalize(residual)
    norm2 = (hat2 * par["gain2"] + par["shift2"]).astype(bf16)
    raised2 = jnp.exp(mm(norm2, par["router"]))
    router = raised2 / jnp.sum(raised2, axis=-1, keepdims=True)
    return dict(
        hat1=hat1, rstd1=rstd1, norm1=norm1, q=q, k=k, v=v, prob=prob, context=context,
        residual=residual, hat2=hat2, rstd2=rstd2, norm2=norm2, router=router,
    )


def expert_main(x_rows, c_rows, w_in, w_out, bias_hidden, router_w, expert):
    raised = jnp.exp(mm(x_rows, router_w))
    prob = raised / jnp.sum(raised, axis=-1, keepdims=True)
    picked = jnp.arange(E, dtype=jnp.int32)[None] == expert
    gate = jnp.sum(jnp.where(picked, prob, 0.0), axis=-1, keepdims=True)
    act, slope = gelu_terms(mm(x_rows, w_in, 1, 1) + bias_hidden)
    act = act.astype(bf16)
    hidden = mm(c_rows, w_out, 1, 1)
    gg = jnp.sum(act.astype(f32) * hidden, axis=-1)
    before = hidden * slope * gate
    grad_bias = jnp.sum(before, axis=0)
    before = before.astype(bf16)
    d_rows = mm(before, w_in).astype(bf16)
    gated = (c_rows.astype(f32) * gate).astype(bf16)
    return act, before, gg, grad_bias, d_rows, gated


def token_backward(s, hot, dispatch, slot_grads, gg, cot, par):
    upstream = cot.astype(f32)
    spread = jnp.repeat(jnp.eye(E, dtype=f32), CAP, axis=0) * gg[:, None]
    prob_grad = sum(mm(dispatch, p) for p in pieces(spread, 3))
    prob_grad = prob_grad + mm(cot, par["ebias_t"]) * hot.astype(f32)
    moe_grad = sum(mm(dispatch, rows) for rows in slot_grads)
    router = s["router"]
    logit = router * (prob_grad - jnp.sum(prob_grad * router, axis=-1, keepdims=True))
    logit = logit.astype(bf16)
    g = {}
    g["router"] = mm(s["norm2"], logit, 0, 0)
    second = moe_grad + mm(logit, par["router"], 1, 1)
    g["gain2"] = jnp.sum(second * s["hat2"], axis=0)
    g["shift2"] = jnp.sum(second, axis=0)
    res_grad = upstream + norm_back(second * par["gain2"], s["hat2"], s["rstd2"])
    g["bo"] = jnp.sum(res_grad, axis=0)
    res_half = res_grad.astype(bf16)
    g["out_t"] = mm(res_half, s["context"], 0, 0)
    cg = mm(res_half, par["out_t"]).astype(bf16).reshape(SEQ, HEADS, HEAD_DIM)
    prob = s["prob"]
    vg = jnp.einsum("hqk,qhc->khc", prob, cg, preferred_element_type=f32).reshape(SEQ, D)
    dprob = jnp.einsum("qhc,khc->hqk", cg, s["v"], preferred_element_type=f32)
    pf = prob.astype(f32)
    row_dot = jnp.sum(pf * dprob, axis=-1, keepdims=True)
    sg = (pf * (dprob - row_dot) * (1.0 / math.sqrt(HEAD_DIM))).astype(bf16)
    qg = jnp.einsum("hqk,khc->qhc", sg, s["k"], preferred_element_type=f32).reshape(SEQ, D)
    kg = jnp.einsum("hqk,qhc->khc", sg, s["q"], preferred_element_type=f32).reshape(SEQ, D)
    g["bq"] = jnp.sum(qg, axis=0)
    g["bv"] = jnp.sum(vg, axis=0)
    ph = jnp.concatenate([qg, kg, vg], axis=-1).astype(bf16)
    g["qkv"] = mm(s["norm1"], ph, 0, 0)
    first = mm(ph, par["qkv"], 1, 1)
    g["gain1"] = jnp.sum(first * s["hat1"], axis=0)
    g["shift1"] = jnp.sum(first, axis=0)
    input_grad = res_grad + norm_back(first * par["gain1"], s["hat1"], s["rstd1"])
    weighted = router * hot.astype(f32)
    g["ebias_t"] = sum(mm(cot, p, 0, 0) for p in pieces(weighted, 2))
    return input_grad, g


VECTORS = ("gain1", "shift1", "bq", "bv", "bo", "gain2", "shift2")


def on_device(
    block_in, out_cotangent, expert_routes, ln1_gain, ln1_shift, w_qkv, bias_query, bias_value,
    w_out, bias_out, ln2_gain, ln2_shift, w_router, expert_bias, w_expert_in, bias_hidden,
    w_expert_out,
):
    images = block_in.shape[0] // SEQ
    n = lax.axis_size(AXIS)
    owners = n // E
    expert = lax.axis_index(AXIS) // owners
    own = ln1_gain.shape[0]
    vectors = jnp.stack(
        [ln1_gain, ln1_shift, bias_query, bias_value, bias_out, ln2_gain, ln2_shift], axis=1
    )
    pad = jnp.zeros((own, 128 - 2 * E - len(VECTORS)), bf16)
    shard = jnp.concatenate([w_qkv, w_out.T, w_router, expert_bias.T, vectors, pad], axis=1)
    full = gather_rows(shard)
    small = full[:, 4 * D :]
    rows = small[:, 2 * E : 2 * E + len(VECTORS)].T.astype(f32)
    par = {name: rows[i : i + 1] for i, name in enumerate(VECTORS)}
    par["qkv"] = full[:, : 3 * D]
    par["out_t"] = full[:, 3 * D : 4 * D]
    par["router"] = small[:, :E]
    par["ebias_t"] = small[:, E : 2 * E]

    xs, cots, hots, disp, states, arrived, cot_arrived = [], [], [], [], [], [], []
    for i in range(images):
        xs.append(block_in[i * SEQ : (i + 1) * SEQ])
        cots.append(out_cotangent[i * SEQ : (i + 1) * SEQ])
        d, hot = place(expert_routes[i * SEQ : (i + 1) * SEQ])
        disp.append(d)
        hots.append(hot)
        slots = mm(d, cots[i], 0, 0).astype(bf16)
        cot_arrived.append(exchange(to_owners(slots, owners)).reshape(-1, D))
    for i in range(images):
        states.append(attend_forward(xs[i], par))
        slots = mm(disp[i], states[i]["norm2"], 0, 0).astype(bf16)
        arrived.append(exchange(to_owners(slots, owners)).reshape(-1, D))
    acts, befores, gates, slot_grads, ggs = [], [], [], [], []
    grad_hidden = 0.0
    for i in range(images):
        act, before, gg, gb, d_rows, gated = expert_main(
            arrived[i], cot_arrived[i], w_expert_in, w_expert_out, bias_hidden, par["router"], expert
        )
        acts.append(act)
        befores.append(before)
        gates.append(gated)
        grad_hidden = grad_hidden + gb
        back = exchange(d_rows.reshape(n, CAP, D)).reshape(E, owners, CAP, D)
        slot_grads.append([back[:, o].reshape(SLOTS, D) for o in range(owners)])
        gg_back = exchange(gg.reshape(n, CAP)).reshape(E, owners, CAP)
        ggs.append(jnp.sum(gg_back, axis=1).reshape(SLOTS))
    parts = []
    for i in range(images):
        p = mm(acts[i], w_expert_out).astype(bf16)
        back = exchange(p.reshape(n, CAP, D)).reshape(E, owners, CAP, D)
        parts.append([back[:, o].reshape(SLOTS, D) for o in range(owners)])
    grad_expert_out = sum(mm(acts[i], gates[i], 0, 0) for i in range(images))
    grad_expert_in = sum(mm(befores[i], arrived[i], 0, 0) for i in range(images))

    outs, input_grads, grads = [], [], None
    for i in range(images):
        s = states[i]
        ig, g = token_backward(s, hots[i], disp[i], slot_grads[i], ggs[i], cots[i], par)
        input_grads.append(ig)
        grads = g if grads is None else {k: grads[k] + g[k] for k in g}
    for i in range(images):
        s = states[i]
        gate_hot = s["router"] * hots[i].astype(f32)
        weighted = jnp.repeat(gate_hot, CAP, axis=1) * disp[i].astype(f32)
        moe = mm_split(gate_hot, par["ebias_t"], 2, 1, 1)
        for p in parts[i]:
            moe = moe + mm_split(weighted, p, 2)
        outs.append(s["residual"] + moe)

    vec = jnp.stack([grads[name] for name in VECTORS], axis=1)
    pad = jnp.zeros((D, 128 - 2 * E - len(VECTORS)), f32)
    packed = jnp.concatenate(
        [grads["qkv"], grads["out_t"], grads["router"], grads["ebias_t"], vec, pad], axis=1
    )
    mine = scatter_rows(packed)
    small = mine[:, 4 * D :]
    vec = [small[:, 2 * E + i] for i in range(len(VECTORS))]
    return (
        jnp.concatenate(outs, axis=0),
        jnp.concatenate(input_grads, axis=0),
        vec[0], vec[1], mine[:, : 3 * D], vec[2], vec[3],
        mine[:, 3 * D : 4 * D].T, vec[4], vec[5], vec[6],
        small[:, :E], small[:, E : 2 * E].T,
        grad_expert_in, grad_hidden, grad_expert_out,
    )


def solution(mesh):
    rows, line, cols = P(AXIS, None), P(AXIS), P(None, AXIS)
    in_specs = (
        rows, rows, rows, line, line, rows, line, line, cols, line, line, line, rows, cols,
        rows, line, rows,
    )
    out_specs = (
        rows, rows, line, line, rows, line, line, cols, line, line, line, rows, cols, rows,
        line, rows,
    )
    return jax.shard_map(
        on_device, mesh=mesh, in_specs=in_specs, out_specs=out_specs, check_vma=False
    )
```

```python
import math

import jax
import jax.numpy as jnp
from jax import lax
from jax.experimental import pallas as pl
from jax.experimental.pallas import tpu as pltpu
from jax.sharding import PartitionSpec as P

D = 768
HEADS = 12
HEAD_DIM = 64
E = 32
SEQ = 197
CAP = 16
SLOTS = E * CAP
AXIS = "fsdp"
PACK = 3200

epsilon = 1e-06
f32 = jnp.float32
bf16 = jnp.bfloat16


def mm(a, b, ca=1, cb=0):
    return lax.dot_general(a, b, (((ca,), (cb,)), ((), ())), preferred_element_type=f32)


def pieces(v, n):
    out = []
    for _ in range(n):
        p = v.astype(bf16)
        out.append(p)
        v = v - p.astype(f32)
    return out


def mm_split(a, b, n=2, ca=1, cb=0):
    return sum(mm(p, b, ca, cb) for p in pieces(a, n))


def normalize(values):
    centered = values - jnp.mean(values, axis=-1, keepdims=True)
    inverse = lax.rsqrt(jnp.mean(centered * centered, axis=-1, keepdims=True) + epsilon)
    return (centered * inverse, inverse)


def norm_back(upstream, normed, inverse):
    return inverse * (
        upstream
        - jnp.mean(upstream, axis=-1, keepdims=True)
        - normed * jnp.mean(upstream * normed, axis=-1, keepdims=True)
    )


def swap(values, bit):
    n = lax.axis_size(AXIS)
    return lax.ppermute(values, AXIS, [(d, d ^ (1 << bit)) for d in range(n)])


def bit_of(bit):
    return (lax.axis_index(AXIS) >> bit) & 1


def gather_rows(shard):
    bits = lax.axis_size(AXIS).bit_length() - 1
    held = shard[None]
    for bit in reversed(range(bits)):
        theirs = swap(held, bit)
        which = lax.broadcasted_iota(jnp.int32, (1, 2, 1, 1), 1) == bit_of(bit)
        held = jnp.where(which, held[:, None], theirs[:, None])
        held = held.reshape((-1,) + shard.shape)
    return held.reshape((-1,) + shard.shape[1:])


def scatter_rows(rows):
    n = lax.axis_size(AXIS)
    bits = n.bit_length() - 1
    held = rows.reshape((n, rows.shape[0] // n) + rows.shape[1:])
    for bit in range(bits):
        split = held.reshape((held.shape[0] // 2, 2) + held.shape[1:])
        mine = bit_of(bit)
        sent = lax.dynamic_index_in_dim(split, 1 - mine, 1, keepdims=False).astype(bf16)
        kept = lax.dynamic_index_in_dim(split, mine, 1, keepdims=False).astype(f32)
        held = kept + swap(sent, bit).astype(f32)
    return held[0]


def exchange(blocks):
    return lax.all_to_all(blocks, AXIS, split_axis=0, concat_axis=0, tiled=True)


def to_owners(slot_rows, owners):
    rows = slot_rows.reshape((E, 1, CAP) + slot_rows.shape[1:])
    rows = jnp.broadcast_to(rows, (E, owners) + rows.shape[2:])
    return rows.reshape((E * owners, CAP) + slot_rows.shape[1:])


def place(routes):
    ids = jnp.arange(E, dtype=jnp.int32)
    m0 = (routes[:, :1] == ids).astype(bf16)
    m1 = (routes[:, 1:] == ids).astype(bf16)
    t = jnp.arange(SEQ, dtype=jnp.int32)
    lower = (t[None, :] < t[:, None]).astype(bf16)
    c0 = mm(lower, m0)
    c1 = mm(lower, m1) + jnp.sum(m0.astype(f32), axis=0, keepdims=True)
    p0 = jnp.sum(c0 * m0, axis=1, keepdims=True).astype(jnp.int32) + routes[:, :1] * CAP
    p1 = jnp.sum(c1 * m1, axis=1, keepdims=True).astype(jnp.int32) + routes[:, 1:] * CAP
    columns = jnp.arange(SLOTS, dtype=jnp.int32)
    return ((p0 == columns) | (p1 == columns)).astype(bf16), m0 + m1


def gelu_terms(v):
    cumulative = 0.5 * (1.0 + lax.erf(v * (1.0 / math.sqrt(2.0))))
    density = jnp.exp(-0.5 * v * v) * (1.0 / math.sqrt(2.0 * math.pi))
    return v * cumulative, cumulative + v * density


def attend_forward(x, par):
    inputs = x.astype(f32)
    hat1, rstd1 = normalize(inputs)
    norm1 = (hat1 * par["gain1"] + par["shift1"]).astype(bf16)
    proj = mm(norm1, par["qkv"])
    q = (proj[:, :D] + par["bq"]).astype(bf16)
    k = proj[:, D : 2 * D].astype(bf16)
    v = (proj[:, 2 * D :] + par["bv"]).astype(bf16)
    q, k, v = (z.reshape(SEQ, HEADS, HEAD_DIM) for z in (q, k, v))
    scores = jnp.einsum("qhc,khc->hqk", q, k, preferred_element_type=f32) * (
        1.0 / math.sqrt(HEAD_DIM)
    )
    raised = jnp.exp(scores)
    prob = (raised / jnp.sum(raised, axis=-1, keepdims=True)).astype(bf16)
    context = jnp.einsum("hqk,khc->qhc", prob, v, preferred_element_type=f32)
    context = context.astype(bf16).reshape(SEQ, D)
    residual = inputs + mm(context, par["out_t"], 1, 1) + par["bo"]
    hat2, rstd2 = normalize(residual)
    norm2 = (hat2 * par["gain2"] + par["shift2"]).astype(bf16)
    raised2 = jnp.exp(mm(norm2, par["router"]))
    router = raised2 / jnp.sum(raised2, axis=-1, keepdims=True)
    return dict(
        hat1=hat1, rstd1=rstd1, norm1=norm1, q=q, k=k, v=v, prob=prob, context=context,
        residual=residual, hat2=hat2, rstd2=rstd2, norm2=norm2, router=router,
    )


def expert_kernel(
    idx, x, c, w_in, hidden, bias, router, act, back, d_rows, gated, grad_bias, acc, gg, gate
):
    r, f = pl.program_id(0), pl.program_id(1)
    rows, width = act.shape

    @pl.when(f == 0)
    def _():
        raised = jnp.exp(mm(x[...], router[...]))
        picked = lax.broadcasted_iota(jnp.int32, raised.shape, 1) == idx[0]
        g = jnp.sum(jnp.where(picked, raised, 0.0), axis=1, keepdims=True)
        g = g / jnp.sum(raised, axis=1, keepdims=True)
        gate[...] = jnp.broadcast_to(g, gate.shape)
        gated[...] = (c[...].astype(f32) * g).astype(bf16)
        gg[...] = jnp.zeros_like(gg)
        acc[...] = jnp.zeros_like(acc)

    value, slope = gelu_terms(mm(x[...], w_in[...], 1, 1) + bias[...])
    hid = hidden[...].astype(f32)
    act[...] = value.astype(bf16)
    both = value * hid
    part = both[:, :128]
    for j in range(1, width // 128):
        part = part + both[:, j * 128 : (j + 1) * 128]
    gg[...] += part
    before = hid * slope * gate[:, :1]
    total = jnp.sum(before, axis=0, keepdims=True)
    half = before.astype(bf16)
    back[...] = half
    acc[...] += mm(half, w_in[...])
    cols = pl.ds(pl.multiple_of(f * width, width), width)

    @pl.when(r == 0)
    def _():
        grad_bias[:, cols] = total

    @pl.when(r > 0)
    def _():
        grad_bias[:, cols] += total

    @pl.when(f == pl.num_programs(1) - 1)
    def _():
        d_rows[:, :D] = acc[...].astype(bf16)
        g = jnp.sum(gg[...], axis=1, keepdims=True)
        high = g.astype(bf16)
        low = (g - high.astype(f32)).astype(bf16)
        lane = lax.broadcasted_iota(jnp.int32, (rows, 128), 1)
        d_rows[:, D:] = jnp.where(
            lane == 0,
            jnp.broadcast_to(high, lane.shape),
            jnp.where(lane == 1, jnp.broadcast_to(low, lane.shape), jnp.zeros(lane.shape, bf16)),
        )


def expert_main(x, c, w_in, hidden, bias, router, expert):
    total, width = x.shape[0], w_in.shape[0]
    rb, fb = min(512, total), min(768, width)
    row = lambda r, f, *_: (r, 0)
    tile = lambda r, f, *_: (r, f)
    fixed = lambda r, f, *_: (0, 0)
    return pl.pallas_call(
        expert_kernel,
        grid_spec=pltpu.PrefetchScalarGridSpec(
            num_scalar_prefetch=1,
            grid=(total // rb, width // fb),
            in_specs=[
                pl.BlockSpec((rb, D), row),
                pl.BlockSpec((rb, D), row),
                pl.BlockSpec((fb, D), lambda r, f, *_: (f, 0)),
                pl.BlockSpec((rb, fb), tile),
                pl.BlockSpec((1, fb), lambda r, f, *_: (0, f)),
                pl.BlockSpec((D, E), fixed),
            ],
            out_specs=[
                pl.BlockSpec((rb, fb), tile),
                pl.BlockSpec((rb, fb), tile),
                pl.BlockSpec((rb, D + 128), row),
                pl.BlockSpec((rb, D), row),
                pl.BlockSpec((1, width), fixed),
            ],
            scratch_shapes=[
                pltpu.VMEM((rb, D), f32),
                pltpu.VMEM((rb, 128), f32),
                pltpu.VMEM((rb, 128), f32),
            ],
        ),
        out_shape=[
            jax.ShapeDtypeStruct((total, width), bf16),
            jax.ShapeDtypeStruct((total, width), bf16),
            jax.ShapeDtypeStruct((total, D + 128), bf16),
            jax.ShapeDtypeStruct((total, D), bf16),
            jax.ShapeDtypeStruct((1, width), f32),
        ],
        compiler_params=pltpu.CompilerParams(
            dimension_semantics=("arbitrary", "arbitrary"), vmem_limit_bytes=30 << 20
        ),
        name="expert_main",
    )(expert.reshape(1), x, c, w_in, hidden, bias.reshape(1, width), router)


def token_backward(s, hot, dispatch, slot_grads, gg, cot, par):
    upstream = cot.astype(f32)
    spread = jnp.repeat(jnp.eye(E, dtype=f32), CAP, axis=0) * gg[:, None]
    prob_grad = sum(mm(dispatch, p) for p in pieces(spread, 3))
    prob_grad = prob_grad + mm(cot, par["ebias_t"]) * hot.astype(f32)
    moe_grad = sum(mm(dispatch, rows) for rows in slot_grads)
    router = s["router"]
    logit = router * (prob_grad - jnp.sum(prob_grad * router, axis=-1, keepdims=True))
    logit = logit.astype(bf16)
    g = {}
    g["router"] = mm(s["norm2"], logit, 0, 0)
    second = moe_grad + mm(logit, par["router"], 1, 1)
    g["gain2"] = jnp.sum(second * s["hat2"], axis=0)
    g["shift2"] = jnp.sum(second, axis=0)
    res_grad = upstream + norm_back(second * par["gain2"], s["hat2"], s["rstd2"])
    g["bo"] = jnp.sum(res_grad, axis=0)
    res_half = res_grad.astype(bf16)
    g["out_t"] = mm(res_half, s["context"], 0, 0)
    cg = mm(res_half, par["out_t"]).astype(bf16).reshape(SEQ, HEADS, HEAD_DIM)
    prob = s["prob"]
    vg = jnp.einsum("hqk,qhc->khc", prob, cg, preferred_element_type=f32).reshape(SEQ, D)
    dprob = jnp.einsum("qhc,khc->hqk", cg, s["v"], preferred_element_type=f32)
    pf = prob.astype(f32)
    row_dot = jnp.sum(pf * dprob, axis=-1, keepdims=True)
    sg = (pf * (dprob - row_dot) * (1.0 / math.sqrt(HEAD_DIM))).astype(bf16)
    qg = jnp.einsum("hqk,khc->qhc", sg, s["k"], preferred_element_type=f32).reshape(SEQ, D)
    kg = jnp.einsum("hqk,qhc->khc", sg, s["q"], preferred_element_type=f32).reshape(SEQ, D)
    g["bq"] = jnp.sum(qg, axis=0)
    g["bv"] = jnp.sum(vg, axis=0)
    ph = jnp.concatenate([qg, kg, vg], axis=-1).astype(bf16)
    g["qkv"] = mm(s["norm1"], ph, 0, 0)
    first = mm(ph, par["qkv"], 1, 1)
    g["gain1"] = jnp.sum(first * s["hat1"], axis=0)
    g["shift1"] = jnp.sum(first, axis=0)
    input_grad = res_grad + norm_back(first * par["gain1"], s["hat1"], s["rstd1"])
    weighted = router * hot.astype(f32)
    g["ebias_t"] = sum(mm(cot, p, 0, 0) for p in pieces(weighted, 2))
    return input_grad, g


VECTORS = ("gain1", "shift1", "bq", "bv", "bo", "gain2", "shift2")


def on_device(
    block_in, out_cotangent, expert_routes, ln1_gain, ln1_shift, w_qkv, bias_query, bias_value,
    w_out, bias_out, ln2_gain, ln2_shift, w_router, expert_bias, w_expert_in, bias_hidden,
    w_expert_out,
):
    images = block_in.shape[0] // SEQ
    n = lax.axis_size(AXIS)
    owners = n // E
    expert = lax.axis_index(AXIS) // owners
    own = ln1_gain.shape[0]
    vectors = jnp.stack(
        [ln1_gain, ln1_shift, bias_query, bias_value, bias_out, ln2_gain, ln2_shift], axis=1
    )
    pad = jnp.zeros((own, 128 - 2 * E - len(VECTORS)), bf16)
    shard = jnp.concatenate([w_qkv, w_out.T, w_router, expert_bias.T, vectors, pad], axis=1)
    full = gather_rows(shard)
    small = full[:, 4 * D :]
    rows = small[:, 2 * E : 2 * E + len(VECTORS)].T.astype(f32)
    par = {name: rows[i : i + 1] for i, name in enumerate(VECTORS)}
    par["qkv"] = full[:, : 3 * D]
    par["out_t"] = full[:, 3 * D : 4 * D]
    par["router"] = small[:, :E]
    par["ebias_t"] = small[:, E : 2 * E]

    xs, cots, hots, disp, states, arrived, outgoing = [], [], [], [], [], [], []
    for i in range(images):
        xs.append(block_in[i * SEQ : (i + 1) * SEQ])
        cots.append(out_cotangent[i * SEQ : (i + 1) * SEQ])
        d, hot = place(expert_routes[i * SEQ : (i + 1) * SEQ])
        disp.append(d)
        hots.append(hot)
        outgoing.append(to_owners(mm(d, cots[i], 0, 0).astype(bf16), owners))
    cot_in = exchange(jnp.stack(outgoing, axis=1))
    cot_rows = [cot_in[:, i].reshape(-1, D) for i in range(images)]
    hidden = [mm(c, w_expert_out, 1, 1).astype(bf16) for c in cot_rows]
    for i in range(images):
        states.append(attend_forward(xs[i], par))
        slots = mm(disp[i], states[i]["norm2"], 0, 0).astype(bf16)
        arrived.append(exchange(to_owners(slots, owners)).reshape(-1, D))
    acts, befores, gates, slot_grads, ggs = [], [], [], [], []
    grad_hidden = 0.0
    for i in range(images):
        act, before, d_rows, gated, gb = expert_main(
            arrived[i], cot_rows[i], w_expert_in, hidden[i], bias_hidden, par["router"], expert
        )
        acts.append(act)
        befores.append(before)
        gates.append(gated)
        grad_hidden = grad_hidden + gb[0]
        back = exchange(d_rows.reshape(n, CAP, D + 128)).reshape(E, owners, CAP, D + 128)
        slot_grads.append([back[:, o, :, :D].reshape(SLOTS, D) for o in range(owners)])
        gg = jnp.sum(back[:, :, :, D : D + 2].astype(f32), axis=(1, 3))
        ggs.append(gg.reshape(SLOTS))
    sent = [mm(a, w_expert_out).astype(bf16).reshape(n, CAP, D) for a in acts]
    back = exchange(jnp.stack(sent, axis=1)).reshape(E, owners, images, CAP, D)
    parts = [
        [back[:, o, i].reshape(SLOTS, D) for o in range(owners)] for i in range(images)
    ]
    grad_expert_out = sum(mm(acts[i], gates[i], 0, 0) for i in range(images))
    grad_expert_in = sum(mm(befores[i], arrived[i], 0, 0) for i in range(images))

    outs, input_grads, grads = [], [], None
    for i in range(images):
        s = states[i]
        ig, g = token_backward(s, hots[i], disp[i], slot_grads[i], ggs[i], cots[i], par)
        input_grads.append(ig)
        grads = g if grads is None else {k: grads[k] + g[k] for k in g}
    for i in range(images):
        s = states[i]
        gate_hot = s["router"] * hots[i].astype(f32)
        weighted = jnp.repeat(gate_hot, CAP, axis=1) * disp[i].astype(f32)
        moe = mm_split(gate_hot, par["ebias_t"], 2, 1, 1)
        for p in parts[i]:
            moe = moe + mm_split(weighted, p, 2)
        outs.append(s["residual"] + moe)

    vec = jnp.stack([grads[name] for name in VECTORS], axis=1)
    pad = jnp.zeros((D, 128 - 2 * E - len(VECTORS)), f32)
    packed = jnp.concatenate(
        [grads["qkv"], grads["out_t"], grads["router"], grads["ebias_t"], vec, pad], axis=1
    )
    mine = scatter_rows(packed)
    small = mine[:, 4 * D :]
    vec = [small[:, 2 * E + i] for i in range(len(VECTORS))]
    return (
        jnp.concatenate(outs, axis=0),
        jnp.concatenate(input_grads, axis=0),
        vec[0], vec[1], mine[:, : 3 * D], vec[2], vec[3],
        mine[:, 3 * D : 4 * D].T, vec[4], vec[5], vec[6],
        small[:, :E], small[:, E : 2 * E].T,
        grad_expert_in, grad_hidden, grad_expert_out,
    )


def solution(mesh):
    rows, line, cols = P(AXIS, None), P(AXIS), P(None, AXIS)
    in_specs = (
        rows, rows, rows, line, line, rows, line, line, cols, line, line, line, rows, cols,
        rows, line, rows,
    )
    out_specs = (
        rows, rows, line, line, rows, line, line, cols, line, line, line, rows, cols, rows,
        line, rows,
    )
    return jax.shard_map(
        on_device, mesh=mesh, in_specs=in_specs, out_specs=out_specs, check_vma=False
    )
```

```python
import functools
import math

import jax
import jax.numpy as jnp
from jax import lax
from jax.experimental import pallas as pl
from jax.experimental.pallas import tpu as pltpu
from jax.sharding import PartitionSpec as P

D = 768
HEADS = 12
HEAD_DIM = 64
PAIRS = HEADS // 2
E = 32
SEQ = 197
ROWS = 208
CAP = 16
SLOTS = E * CAP
AXIS = "fsdp"
PACK = 3200
CUT = 1664
GAIN1, SHIFT1, BQ, BV, BO, GAIN2, SHIFT2, VECTORS = range(8)
SCALE = 1.0 / math.sqrt(HEAD_DIM)

epsilon = 1e-06
f32 = jnp.float32
bf16 = jnp.bfloat16
i32 = jnp.int32


def mm(a, b, ca=1, cb=0):
    return lax.dot_general(a, b, (((ca,), (cb,)), ((), ())), preferred_element_type=f32)


def pieces(v, n):
    out = []
    for _ in range(n):
        p = v.astype(bf16)
        out.append(p)
        v = v - p.astype(f32)
    return out


def normalize(values):
    centered = values - jnp.mean(values, axis=-1, keepdims=True)
    inverse = lax.rsqrt(jnp.mean(centered * centered, axis=-1, keepdims=True) + epsilon)
    return (centered * inverse, inverse)


def norm_back(upstream, normed, inverse):
    return inverse * (
        upstream
        - jnp.mean(upstream, axis=-1, keepdims=True)
        - normed * jnp.mean(upstream * normed, axis=-1, keepdims=True)
    )


def swap(values, bit):
    n = lax.axis_size(AXIS)
    return lax.ppermute(values, AXIS, [(d, d ^ (1 << bit)) for d in range(n)])


def bit_of(bit):
    return (lax.axis_index(AXIS) >> bit) & 1


def bit_orders():
    bits = lax.axis_size(AXIS).bit_length() - 1
    inner = (bits - 1) // 3 if bits != 5 else 1
    x = list(range(1, 1 + inner))
    y = list(range(1 + inner, 1 + 2 * inner))
    z = list(range(1 + 2 * inner, bits))
    return [0] + x + y + z, [0] + y + x + z


def gather_rows(shards):
    orders = bit_orders()
    held = [(shard[None], []) for shard in shards]
    for step in range(len(orders[0])):
        moved = []
        for (values, done), order in zip(held, orders):
            bit = order[-1 - step]
            theirs = swap(values, bit)
            at = sum(1 for b in done if b > bit)
            lead = values.shape[0]
            high = 1 << at
            mine = values.reshape((high, lead // high) + values.shape[1:])
            theirs = theirs.reshape(mine.shape)
            which = lax.broadcasted_iota(i32, (1, 2, 1, 1, 1), 1) == bit_of(bit)
            both = jnp.where(which, mine[:, None], theirs[:, None])
            moved.append((both.reshape((2 * lead,) + values.shape[1:]), done + [bit]))
        held = moved
    return [values.reshape((-1, values.shape[-1])) for values, _ in held]


def owner_order(order):
    n = lax.axis_size(AXIS)
    own = D // n
    position = jnp.arange(D, dtype=i32)
    chunk = position // own
    owner = jnp.zeros_like(chunk)
    for step, bit in enumerate(order):
        owner = owner | (((chunk >> (len(order) - 1 - step)) & 1) << bit)
    return (owner ^ lax.axis_index(AXIS)) * own + position % own


def permutation(order):
    return (jnp.arange(D, dtype=i32)[:, None] == owner_order(order)[None]).astype(bf16)


def scatter_rows(sent, kept, order):
    for step, bit in enumerate(order):
        held = kept.astype(f32) + swap(sent, bit).astype(f32)
        if step + 1 < len(order):
            half = held.shape[0] // 2
            kept, sent = held[:half], held[half:].astype(bf16)
    return held


def exchange(blocks):
    return lax.all_to_all(blocks, AXIS, split_axis=0, concat_axis=0, tiled=True)


def to_owners(slot_rows, owners):
    rows = slot_rows.reshape((E, 1, CAP) + slot_rows.shape[1:])
    rows = jnp.broadcast_to(rows, (E, owners) + rows.shape[2:])
    return rows.reshape((E * owners, CAP) + slot_rows.shape[1:])


def place(routes):
    choice = jnp.pad(routes.T, ((0, 0), (0, ROWS - SEQ)), constant_values=-1)
    ids = jnp.arange(E, dtype=i32)[:, None]
    first = (choice[:1] == ids).astype(bf16)
    second = (choice[1:] == ids).astype(bf16)
    t = jnp.arange(ROWS, dtype=i32)
    earlier = (t[:, None] < t[None, :]).astype(bf16)
    before = mm(jnp.concatenate([first, second], axis=0), earlier)
    rank0 = jnp.sum(before[:E] * first, axis=0)
    seen = before[E:] + jnp.sum(first.astype(f32), axis=1, keepdims=True)
    rank1 = jnp.sum(seen * second, axis=0)
    return choice * CAP + jnp.stack([rank0, rank1]).astype(i32)


def gelu_terms(v):
    cumulative = 0.5 * (1.0 + lax.erf(v * (1.0 / math.sqrt(2.0))))
    density = jnp.exp(-0.5 * v * v) * (1.0 / math.sqrt(2.0 * math.pi))
    return v * cumulative, cumulative + v * density


def dispatch_of(placed):
    slot = lax.broadcasted_iota(i32, (SLOTS, ROWS), 0)
    hit = (slot == placed[0:1, :]) | (slot == placed[1:2, :])
    return hit.astype(f32).astype(bf16)

def half_of(pair, second):
    lane = lax.broadcasted_iota(i32, pair.shape, 1)
    keep = (lane >= HEAD_DIM) if second else (lane < HEAD_DIM)
    return jnp.where(keep, pair, jnp.zeros_like(pair))

def join(first, second):
    lane = lax.broadcasted_iota(i32, first.shape, 1)
    return jnp.where(lane < HEAD_DIM, first, second)

def forward_kernel(x, placed, qkv_a, qkv_b, out_t, small, vec, slots, residual, prob, acts, norm1_o, norm2_o, context_o, router_o):
    inputs = x[...].astype(f32)
    hat1, _ = normalize(inputs)
    norm1 = (hat1 * vec[GAIN1:GAIN1+1, :] + vec[SHIFT1:SHIFT1+1, :]).astype(bf16)
    norm1_o[...] = norm1
    proj = jnp.concatenate([mm(norm1, qkv_a[...]), mm(norm1, qkv_b[...])], axis=1)
    acts[:, :D] = (proj[:, :D] + vec[BQ:BQ+1, :]).astype(bf16)
    acts[:, D:2*D] = proj[:, D:2*D].astype(bf16)
    acts[:, 2*D:] = (proj[:, 2*D:] + vec[BV:BV+1, :]).astype(bf16)
    token = lax.broadcasted_iota(i32, (ROWS, ROWS), 0) < SEQ
    for j in range(PAIRS):
        q = acts[:, j*128:(j+1)*128] * jnp.asarray(SCALE, bf16)
        k = acts[:, D + j*128:D + (j+1)*128]
        v = acts[:, 2*D + j*128:2*D + (j+1)*128]
        outs = []
        for h in range(2):
            raised = jnp.exp(mm(half_of(k, h), q, 1, 1))
            raised = jnp.where(token, raised, 0.0)
            p = (raised * (1.0 / jnp.sum(raised, axis=0, keepdims=True))).astype(bf16)
            prob[2*j+h, :, :] = p
            outs.append(mm(p, v, 0, 0))
        context_o[:, j*128:(j+1)*128] = join(outs[0], outs[1]).astype(bf16)
    res = inputs + mm(context_o[...], out_t[...], 1, 1) + vec[BO:BO+1, :]
    residual[...] = res
    hat2, _ = normalize(res)
    norm2 = (hat2 * vec[GAIN2:GAIN2+1, :] + vec[SHIFT2:SHIFT2+1, :]).astype(bf16)
    norm2_o[...] = norm2
    slots[...] = mm(dispatch_of(placed[...]), norm2).astype(bf16)
    lane = lax.broadcasted_iota(i32, (ROWS, 128), 1)
    raised = jnp.where(lane < E, jnp.exp(jnp.where(lane < E, mm(norm2, small[...]), 0.0)), 0.0)
    router_o[...] = raised / jnp.sum(raised, axis=1, keepdims=True)

def call(kernel, ins, outs, name, scratch=(), limit=40):
    return pl.pallas_call(kernel, out_shape=[jax.ShapeDtypeStruct(s, d) for s, d in outs], scratch_shapes=list(scratch),
        compiler_params=pltpu.CompilerParams(vmem_limit_bytes=limit << 20), name=name)(*ins)

def attend_forward(x, placed, par):
    names = ("slots", "residual", "prob", "acts", "norm1", "norm2", "context", "router")
    outs = call(
        forward_kernel,
        (x, placed, par["qkv_a"], par["qkv_b"], par["out_t"], par["small"], par["vec"]),
        [
            ((SLOTS, D), bf16), ((ROWS, D), f32), ((HEADS, ROWS, ROWS), bf16),
            ((ROWS, 3 * D), bf16), ((ROWS, D), bf16), ((ROWS, D), bf16), ((ROWS, D), bf16),
            ((ROWS, 128), f32),
        ],
        "attend_forward",
    )
    return dict(zip(names, outs))

def backward_kernel(rec, x, cot, placed, residual, prob, acts, router, qkv_a, qkv_b, out_t, small, vec,
                    input_grad, ph, res_half_o, logit_o, gate_o, sums):
    upstream = cot[...].astype(f32)
    disp = dispatch_of(placed[...])
    lane = lax.broadcasted_iota(i32, (SLOTS, 128), 1)
    slot_expert = lax.broadcasted_iota(i32, (SLOTS, 128), 0) // CAP
    moe = 0.0; pg = 0.0
    for o in range(rec.shape[0]):
        moe = moe + mm(disp, rec[o, :, :D], 0, 0)
        gg = jnp.where((lane & 63) == slot_expert, rec[o, :, D:], jnp.zeros((SLOTS, 128), bf16))
        pg = pg + mm(disp, gg, 0, 0)
    pg = pg + pltpu.roll(pg, 64, 1)
    hot = mm(disp, (lane == slot_expert).astype(f32).astype(bf16), 0, 0)
    pg = (pg + pltpu.roll(mm(cot[...], small[...]), 128 - E, 1)) * hot
    prob_r = router[...]
    gate_o[...] = prob_r * hot
    logit = (prob_r * (pg - jnp.sum(pg * prob_r, axis=1, keepdims=True)))
    row = lax.broadcasted_iota(i32, (ROWS, 1), 0) < SEQ
    logit = jnp.where(row, logit, 0.0).astype(bf16)
    logit_o[...] = logit
    second = moe + mm(logit, small[...], 1, 1)
    hat2, rstd2 = normalize(residual[...])
    sums[GAIN2:GAIN2+1, :] = jnp.sum(second * hat2, axis=0, keepdims=True)
    sums[SHIFT2:SHIFT2+1, :] = jnp.sum(second, axis=0, keepdims=True)
    res_grad = upstream + norm_back(second * vec[GAIN2:GAIN2+1, :], hat2, rstd2)
    input_grad[...] = res_grad
    sums[BO:BO+1, :] = jnp.sum(res_grad, axis=0, keepdims=True)
    res_half = res_grad.astype(bf16)
    res_half_o[...] = res_half
    cg = mm(res_half, out_t[...]).astype(bf16)
    for j in range(PAIRS):
        q = acts[:, j*128:(j+1)*128]
        k = acts[:, D + j*128:D + (j+1)*128]
        v = acts[:, 2*D + j*128:2*D + (j+1)*128]
        c = cg[:, j*128:(j+1)*128]
        qs, ks, vs = [], [], []
        for h in range(2):
            p = prob[2*j+h, :, :]
            pf = p.astype(f32)
            dp = mm(half_of(v, h), c, 1, 1)
            t = pf * dp
            sg = ((t - pf * jnp.sum(t, axis=0, keepdims=True)) * SCALE).astype(bf16)
            vs.append(mm(p, c))
            qs.append(mm(sg, k, 0, 0))
            ks.append(mm(sg, q))
        qg, kg, vg = join(*qs), join(*ks), join(*vs)
        cols = slice(j*128, (j+1)*128)
        sums[BQ:BQ+1, cols] = jnp.sum(qg, axis=0, keepdims=True)
        sums[BV:BV+1, cols] = jnp.sum(vg, axis=0, keepdims=True)
        ph[:, j*128:(j+1)*128] = qg.astype(bf16)
        ph[:, D + j*128:D + (j+1)*128] = kg.astype(bf16)
        ph[:, 2*D + j*128:2*D + (j+1)*128] = vg.astype(bf16)
    first = mm(ph[:, :CUT], qkv_a[...], 1, 1) + mm(ph[:, CUT:], qkv_b[...], 1, 1)
    hat1, rstd1 = normalize(x[...].astype(f32))
    sums[GAIN1:GAIN1+1, :] = jnp.sum(first * hat1, axis=0, keepdims=True)
    sums[SHIFT1:SHIFT1+1, :] = jnp.sum(first, axis=0, keepdims=True)
    sums[7:8, :] = jnp.zeros((1, D), f32)
    input_grad[...] += norm_back(first * vec[GAIN1:GAIN1+1, :], hat1, rstd1)

def token_backward(rec, x, cot, placed, s, par):
    return call(backward_kernel, (rec, x, cot, placed, s["residual"], s["prob"], s["acts"], s["router"], par["qkv_a"], par["qkv_b"], par["out_t"], par["small"], par["vec"]),
        [((ROWS, D), f32), ((ROWS, 3*D), bf16), ((ROWS, D), bf16), ((ROWS, 128), bf16), ((ROWS, 128), f32), ((8, D), f32)], "token_backward")


def expert_kernel(
    idx, x, c, w_in, hidden, bias, router, act, back, d_rows, gated, gate, grad_bias, acc, gg
):
    r, f = pl.program_id(0), pl.program_id(1)
    rows, width = act.shape

    @pl.when(f == 0)
    def _():
        logits = mm(x[...], router[...])
        lane = lax.broadcasted_iota(i32, logits.shape, 1)
        raised = jnp.where(lane < E, jnp.exp(jnp.where(lane < E, logits, 0.0)), 0.0)
        picked = lane == idx[0]
        g = jnp.sum(jnp.where(picked, raised, 0.0), axis=1, keepdims=True)
        g = g / jnp.sum(raised, axis=1, keepdims=True)
        gate[...] = jnp.broadcast_to(g, gate.shape)
        gated[...] = (c[...].astype(f32) * g).astype(bf16)
        gg[...] = jnp.zeros_like(gg)
        acc[...] = jnp.zeros_like(acc)

    value, slope = gelu_terms(mm(x[...], w_in[...], 1, 1) + bias[...])
    hid = hidden[...].astype(f32)
    act[...] = value.astype(bf16)
    both = value * hid
    part = both[:, :128]
    for j in range(1, width // 128):
        part = part + both[:, j * 128 : (j + 1) * 128]
    gg[...] += part
    before = hid * slope * gate[:, :1]
    total = jnp.sum(before, axis=0, keepdims=True)
    half = before.astype(bf16)
    back[...] = half
    acc[...] += mm(half, w_in[...])
    cols = pl.ds(pl.multiple_of(f * width, width), width)

    @pl.when(r == 0)
    def _():
        grad_bias[:, cols] = total

    @pl.when(r > 0)
    def _():
        grad_bias[:, cols] += total

    @pl.when(f == pl.num_programs(1) - 1)
    def _():
        d_rows[:, :D] = acc[...].astype(bf16)
        g = jnp.sum(gg[...], axis=1, keepdims=True)
        high = g.astype(bf16)
        low = (g - high.astype(f32)).astype(bf16)
        lane = lax.broadcasted_iota(i32, (rows, 128), 1)
        d_rows[:, D:] = jnp.where(
            lane < 64, jnp.broadcast_to(high, lane.shape), jnp.broadcast_to(low, lane.shape)
        )


def expert_main(x, c, w_in, hidden, bias, router, expert):
    total, width = x.shape[0], w_in.shape[0]
    rb, fb = min(512, total), min(768, width)
    row = lambda r, f, *_: (r, 0)
    tile = lambda r, f, *_: (r, f)
    fixed = lambda r, f, *_: (0, 0)
    return pl.pallas_call(
        expert_kernel,
        grid_spec=pltpu.PrefetchScalarGridSpec(
            num_scalar_prefetch=1,
            grid=(total // rb, width // fb),
            in_specs=[
                pl.BlockSpec((rb, D), row),
                pl.BlockSpec((rb, D), row),
                pl.BlockSpec((fb, D), lambda r, f, *_: (f, 0)),
                pl.BlockSpec((rb, fb), tile),
                pl.BlockSpec((1, fb), lambda r, f, *_: (0, f)),
                pl.BlockSpec((D, 128), fixed),
            ],
            out_specs=[
                pl.BlockSpec((rb, fb), tile),
                pl.BlockSpec((rb, fb), tile),
                pl.BlockSpec((rb, D + 128), row),
                pl.BlockSpec((rb, D), row),
                pl.BlockSpec((rb, 128), row),
                pl.BlockSpec((1, width), fixed),
            ],
            scratch_shapes=[
                pltpu.VMEM((rb, D), f32),
                pltpu.VMEM((rb, 128), f32),
            ],
        ),
        out_shape=[
            jax.ShapeDtypeStruct((total, width), bf16),
            jax.ShapeDtypeStruct((total, width), bf16),
            jax.ShapeDtypeStruct((total, D + 128), bf16),
            jax.ShapeDtypeStruct((total, D), bf16),
            jax.ShapeDtypeStruct((total, 128), f32),
            jax.ShapeDtypeStruct((1, width), f32),
        ],
        compiler_params=pltpu.CompilerParams(
            dimension_semantics=("arbitrary", "arbitrary"), vmem_limit_bytes=30 << 20
        ),
        name="expert_main",
    )(expert.reshape(1), x, c, w_in, hidden, bias.reshape(1, width), router)


def grads_kernel(
    norm1a, norm1b, norm2b, cotb, ph0, ph1, rh0, rh1, ctx0, ctx1, lg0, lg1, gt0, gt1, sm0, sm1,
    perm, sent_a, kept_a, sent_b, kept_b,
):
    half = D // 2

    def lay(value, sent, kept, start):
        kept[:, start : start + value.shape[1]] = value[:half]
        sent[:, start : start + value.shape[1]] = value[half:].astype(bf16)

    ph = (ph0, ph1)
    lay(sum(mm(norm1a[i], ph[i][:, :CUT], 0, 0) for i in range(2)), sent_a, kept_a, 0)
    lay(sum(mm(norm1b[i], ph[i][:, CUT:], 0, 0) for i in range(2)), sent_b, kept_b, 0)
    start = 3 * D - CUT
    out = 0.0
    for rh, ctx in ((rh0, ctx0), (rh1, ctx1)):
        out = out + mm(mm(rh[...], perm[...]).astype(bf16), ctx[...], 0, 0)
    lay(out, sent_b, kept_b, start)
    sums = sm0[...] + sm1[...]
    moved = sum(mm(p, perm[...]) for p in pieces(sums, 3))
    zeros = jnp.zeros((56, D), f32)
    tail = jnp.concatenate([jnp.zeros((2 * E, D), f32), moved, zeros], axis=0).T
    for i, (lg, gt) in enumerate(((lg0, gt0), (lg1, gt1))):
        tail = tail + mm(norm2b[i], lg[...], 0, 0)
        for p in pieces(pltpu.roll(gt[...], E, 1), 2):
            tail = tail + mm(cotb[i], p, 0, 0)
    lay(tail, sent_b, kept_b, start + D)


def output_kernel(owners, *refs):
    ins, (block_out, input_grad) = refs[:-2], refs[-2:]
    small = ins[-1]
    for i in range(2):
        rows, placed, residual, gate, grad = ins[5 * i : 5 * i + 5]
        disp = dispatch_of(placed[...])
        out = residual[...]
        for o in range(owners):
            out = out + mm(disp, rows[o], 0, 0)
        for p in pieces(pltpu.roll(gate[...], E, 1), 2):
            out = out + mm(p, small[...], 1, 1)
        block_out[i * SEQ : (i + 1) * SEQ, :] = out[:SEQ]
        input_grad[i * SEQ : (i + 1) * SEQ, :] = grad[:SEQ, :]


def weights_kernel(act0, act1, back0, back1, g0, g1, x0, x1, out_w, in_w):
    out_w[...] = mm(act0[...], g0[...], 0, 0) + mm(act1[...], g1[...], 0, 0)
    in_w[...] = mm(back0[...], x0[...], 0, 0) + mm(back1[...], x1[...], 0, 0)


def expert_weights(acts, backs, gated, xs):
    total, width = acts[0].shape
    fb = min(512, width)
    cols = pl.BlockSpec((total, fb), lambda f: (0, f))
    full = pl.BlockSpec((total, D), lambda f: (0, 0))
    rows = pl.BlockSpec((fb, D), lambda f: (f, 0))
    return pl.pallas_call(
        weights_kernel,
        grid=(width // fb,),
        in_specs=[cols] * 4 + [full] * 4,
        out_specs=[rows, rows],
        out_shape=[jax.ShapeDtypeStruct((width, D), f32)] * 2,
        compiler_params=pltpu.CompilerParams(
            dimension_semantics=("arbitrary",), vmem_limit_bytes=40 << 20
        ),
        name="expert_weights",
    )(*acts, *backs, *gated, *xs)


def on_device(
    block_in, out_cotangent, expert_routes, ln1_gain, ln1_shift, w_qkv, bias_query, bias_value,
    w_out, bias_out, ln2_gain, ln2_shift, w_router, expert_bias, w_expert_in, bias_hidden,
    w_expert_out,
):
    images = block_in.shape[0] // SEQ
    n = lax.axis_size(AXIS)
    owners = n // E
    expert = lax.axis_index(AXIS) // owners
    order_a, order_b = bit_orders()
    vectors = jnp.stack(
        [ln1_gain, ln1_shift, bias_query, bias_value, bias_out, ln2_gain, ln2_shift], axis=1
    )
    pad = jnp.zeros((vectors.shape[0], 128 - 2 * E - VECTORS), bf16)
    part_a = w_qkv[:, :CUT]
    part_b = jnp.concatenate(
        [w_qkv[:, CUT:], w_out.T, w_router, expert_bias.T, vectors, pad], axis=1
    )
    full_a, full_b = gather_rows([part_a, part_b])
    start = 3 * D - CUT
    small = full_b[:, start + D :]
    par = {
        "qkv_a": full_a,
        "qkv_b": full_b[:, :start],
        "out_t": full_b[:, start : start + D],
        "small": small,
        "vec": small[:, 2 * E : 2 * E + 8].T.astype(f32),
    }

    pad_rows = ((0, ROWS - SEQ), (0, 0))
    xs, cots, placed, states, arrived, outgoing = [], [], [], [], [], []
    for i in range(images):
        xs.append(jnp.pad(block_in[i * SEQ : (i + 1) * SEQ], pad_rows))
        cots.append(jnp.pad(out_cotangent[i * SEQ : (i + 1) * SEQ], pad_rows))
        placed.append(place(expert_routes[i * SEQ : (i + 1) * SEQ]))
        slots = mm(dispatch_of(placed[i]), cots[i]).astype(bf16)
        outgoing.append(to_owners(slots, owners))
    cot_in = exchange(jnp.stack(outgoing, axis=1))
    cot_rows = [cot_in[:, i].reshape(-1, D) for i in range(images)]
    hidden = [mm(c, w_expert_out, 1, 1).astype(bf16) for c in cot_rows]
    for i in range(images):
        states.append(attend_forward(xs[i], placed[i], par))
        arrived.append(exchange(to_owners(states[i]["slots"], owners)).reshape(-1, D))
    done = []
    grad_hidden = 0.0
    received = []
    for i in range(images):
        act, back, d_rows, gated, gate, gb = expert_main(
            arrived[i], cot_rows[i], w_expert_in, hidden[i], bias_hidden, small, expert
        )
        done.append((act, back, gated, gate))
        grad_hidden = grad_hidden + gb[0]
        rows = exchange(d_rows.reshape(n, CAP, D + 128)).reshape(E, owners, CAP, D + 128)
        received.append(rows.transpose(1, 0, 2, 3).reshape(owners, SLOTS, D + 128))
    sent = [(mm(act, w_expert_out) * gate[:, :1]).astype(bf16) for act, _, _, gate in done]
    sent = jnp.stack([p.reshape(n, CAP, D) for p in sent], axis=1)
    parts = exchange(sent).reshape(E, owners, images, CAP, D).transpose(2, 1, 0, 3, 4)
    parts = parts.reshape(images, owners, SLOTS, D)
    grad_expert_out, grad_expert_in = expert_weights(
        [d[0] for d in done], [d[1] for d in done], [d[2] for d in done], arrived
    )

    perm_a, perm_b = permutation(order_a), permutation(order_b)
    moved = lambda values, perm: jnp.stack([mm(v, perm).astype(bf16) for v in values])
    norm1a = moved([s["norm1"] for s in states], perm_a)
    norm1b = moved([s["norm1"] for s in states], perm_b)
    norm2b = moved([s["norm2"] for s in states], perm_b)
    cotb = moved(cots, perm_b)
    back = [
        token_backward(received[i], xs[i], cots[i], placed[i], states[i], par)
        for i in range(images)
    ]
    pair = lambda index: tuple(b[index] for b in back)
    sent_a, kept_a, sent_b, kept_b = call(
        grads_kernel,
        (norm1a, norm1b, norm2b, cotb) + pair(1) + pair(2)
        + tuple(s["context"] for s in states) + pair(3) + pair(4) + pair(5) + (perm_b,),
        [
            ((D // 2, CUT), bf16), ((D // 2, CUT), f32),
            ((D // 2, PACK - CUT), bf16), ((D // 2, PACK - CUT), f32),
        ],
        "pack_grads",
    )
    mine_a = scatter_rows(sent_a, kept_a, order_a)
    mine_b = scatter_rows(sent_b, kept_b, order_b)
    ins = []
    for i in range(images):
        ins += [parts[i], placed[i], states[i]["residual"], back[i][4], back[i][0]]
    block_out, input_grad = call(
        functools.partial(output_kernel, owners),
        tuple(ins) + (small,),
        [((images * SEQ, D), f32)] * 2,
        "outputs",
    )
    tail = mine_b[:, start + D :]
    vec = [tail[:, 2 * E + i] for i in range(VECTORS)]
    return (
        block_out, input_grad, vec[GAIN1], vec[SHIFT1],
        jnp.concatenate([mine_a, mine_b[:, :start]], axis=1), vec[BQ], vec[BV],
        mine_b[:, start : start + D].T, vec[BO], vec[GAIN2], vec[SHIFT2],
        tail[:, :E], tail[:, E : 2 * E].T, grad_expert_in, grad_hidden, grad_expert_out,
    )


def solution(mesh):
    rows, line, cols = P(AXIS, None), P(AXIS), P(None, AXIS)
    in_specs = (
        rows, rows, rows, line, line, rows, line, line, cols, line, line, line, rows, cols,
        rows, line, rows,
    )
    out_specs = (
        rows, rows, line, line, rows, line, line, cols, line, line, line, rows, cols, rows,
        line, rows,
    )
    return jax.shard_map(
        on_device, mesh=mesh, in_specs=in_specs, out_specs=out_specs, check_vma=False
    )
```

```python
import functools
import math

import jax
import jax.numpy as jnp
from jax import lax
from jax.experimental import pallas as pl
from jax.experimental.pallas import tpu as pltpu
from jax.sharding import PartitionSpec as P

D = 768
HEADS = 12
HEAD_DIM = 64
PAIRS = HEADS // 2
E = 32
SEQ = 197
ROWS = 208
CAP = 16
SLOTS = E * CAP
AXIS = "fsdp"
PACK = 3200
CUT = 1664
GAIN1, SHIFT1, BQ, BV, BO, GAIN2, SHIFT2, VECTORS = range(8)
SCALE = 1.0 / math.sqrt(HEAD_DIM)

epsilon = 1e-06
f32 = jnp.float32
bf16 = jnp.bfloat16
i32 = jnp.int32


def mm(a, b, ca=1, cb=0):
    return lax.dot_general(a, b, (((ca,), (cb,)), ((), ())), preferred_element_type=f32)


def pieces(v, n):
    out = []
    for _ in range(n):
        p = v.astype(bf16)
        out.append(p)
        v = v - p.astype(f32)
    return out


def normalize(values):
    centered = values - jnp.mean(values, axis=-1, keepdims=True)
    inverse = lax.rsqrt(jnp.mean(centered * centered, axis=-1, keepdims=True) + epsilon)
    return (centered * inverse, inverse)


def norm_back(upstream, normed, inverse):
    return inverse * (
        upstream
        - jnp.mean(upstream, axis=-1, keepdims=True)
        - normed * jnp.mean(upstream * normed, axis=-1, keepdims=True)
    )


def swap(values, bit):
    n = lax.axis_size(AXIS)
    return lax.ppermute(values, AXIS, [(d, d ^ (1 << bit)) for d in range(n)])


def bit_of(bit):
    return (lax.axis_index(AXIS) >> bit) & 1


def bit_orders():
    bits = lax.axis_size(AXIS).bit_length() - 1
    inner = (bits - 1) // 3 if bits != 5 else 1
    x = list(range(1, 1 + inner))
    y = list(range(1 + inner, 1 + 2 * inner))
    z = list(range(1 + 2 * inner, bits))
    return [0] + x + y + z, [0] + y + x + z


def gather_rows(shards, early, wait_for):
    orders = bit_orders()
    held = [(shard[None], []) for shard in shards]
    for step in range(len(orders[0])):
        moved = []
        for (values, done), order in zip(held, orders):
            bit = order[-1 - step]
            theirs = swap(values, bit)
            at = sum(1 for b in done if b > bit)
            lead = values.shape[0]
            high = 1 << at
            mine = values.reshape((high, lead // high) + values.shape[1:])
            theirs = theirs.reshape(mine.shape)
            which = lax.broadcasted_iota(i32, (1, 2, 1, 1, 1), 1) == bit_of(bit)
            both = jnp.where(which, mine[:, None], theirs[:, None])
            moved.append((both.reshape((2 * lead,) + values.shape[1:]), done + [bit]))
        held = moved
        if step + 1 == early:
            tied = lax.optimization_barrier([values for values, _ in held] + [wait_for])
            held = [(t, done) for t, (_, done) in zip(tied, held)]
            wait_for = tied[-1]
    return [values.reshape((-1, values.shape[-1])) for values, _ in held], wait_for


def owner_order(order):
    n = lax.axis_size(AXIS)
    own = D // n
    position = jnp.arange(D, dtype=i32)
    chunk = position // own
    owner = jnp.zeros_like(chunk)
    for step, bit in enumerate(order):
        owner = owner | (((chunk >> (len(order) - 1 - step)) & 1) << bit)
    return (owner ^ lax.axis_index(AXIS)) * own + position % own


def permutation(order):
    return (jnp.arange(D, dtype=i32)[:, None] == owner_order(order)[None]).astype(bf16)


def scatter_rows(sent, kept, order):
    for step, bit in enumerate(order):
        held = kept.astype(f32) + swap(sent, bit).astype(f32)
        if step + 1 < len(order):
            half = held.shape[0] // 2
            kept, sent = held[:half], held[half:].astype(bf16)
    return held


def exchange(blocks):
    return lax.all_to_all(blocks, AXIS, split_axis=0, concat_axis=0, tiled=True)


def to_owners(slot_rows, owners):
    rows = slot_rows.reshape((E, 1, CAP) + slot_rows.shape[1:])
    rows = jnp.broadcast_to(rows, (E, owners) + rows.shape[2:])
    return rows.reshape((E * owners, CAP) + slot_rows.shape[1:])


def place(routes):
    choice = jnp.pad(routes.T, ((0, 0), (0, ROWS - SEQ)), constant_values=-1)
    ids = jnp.arange(E, dtype=i32)[:, None]
    first = (choice[:1] == ids).astype(bf16)
    second = (choice[1:] == ids).astype(bf16)
    t = jnp.arange(ROWS, dtype=i32)
    earlier = (t[:, None] < t[None, :]).astype(bf16)
    before = mm(jnp.concatenate([first, second], axis=0), earlier)
    rank0 = jnp.sum(before[:E] * first, axis=0)
    seen = before[E:] + jnp.sum(first.astype(f32), axis=1, keepdims=True)
    rank1 = jnp.sum(seen * second, axis=0)
    return choice * CAP + jnp.stack([rank0, rank1]).astype(i32)


def gelu_terms(v):
    cumulative = 0.5 * (1.0 + lax.erf(v * (1.0 / math.sqrt(2.0))))
    density = jnp.exp(-0.5 * v * v) * (1.0 / math.sqrt(2.0 * math.pi))
    return v * cumulative, cumulative + v * density


def dispatch_of(placed):
    slot = lax.broadcasted_iota(i32, (SLOTS, ROWS), 0)
    hit = (slot == placed[0:1, :]) | (slot == placed[1:2, :])
    return hit.astype(f32).astype(bf16)

def half_of(pair, second):
    lane = lax.broadcasted_iota(i32, pair.shape, 1)
    keep = (lane >= HEAD_DIM) if second else (lane < HEAD_DIM)
    return jnp.where(keep, pair, jnp.zeros_like(pair))

def join(first, second):
    lane = lax.broadcasted_iota(i32, first.shape, 1)
    return jnp.where(lane < HEAD_DIM, first, second)

def forward_kernel(get, outs, flush):
    slots, residual, prob, acts, norm1_o, norm2_o, context_o, router_o = outs
    inputs = get(0)[...].astype(f32)
    hat1, _ = normalize(inputs)
    vec = get(1)
    row = lambda k: vec[k : k + 1, :]
    norm1 = (hat1 * row(GAIN1) + row(SHIFT1)).astype(bf16)
    norm1_o[...] = norm1
    flush(4)
    proj = jnp.concatenate([mm(norm1, get(2)[...]), mm(norm1, get(3)[...])], axis=1)
    acts[:, :D] = (proj[:, :D] + row(BQ)).astype(bf16)
    acts[:, D : 2 * D] = proj[:, D : 2 * D].astype(bf16)
    acts[:, 2 * D :] = (proj[:, 2 * D :] + row(BV)).astype(bf16)
    flush(3)
    token = lax.broadcasted_iota(i32, (ROWS, ROWS), 0) < SEQ
    for j in range(PAIRS):
        q = acts[:, j * 128 : (j + 1) * 128] * jnp.asarray(SCALE, bf16)
        k = acts[:, D + j * 128 : D + (j + 1) * 128]
        v = acts[:, 2 * D + j * 128 : 2 * D + (j + 1) * 128]
        both = []
        for h in range(2):
            raised = jnp.exp(mm(half_of(k, h), q, 1, 1))
            raised = jnp.where(token, raised, 0.0)
            p = (raised * (1.0 / jnp.sum(raised, axis=0, keepdims=True))).astype(bf16)
            prob[2 * j + h, :, :] = p
            both.append(mm(p, v, 0, 0))
        context_o[:, j * 128 : (j + 1) * 128] = join(both[0], both[1]).astype(bf16)
    flush(2)
    flush(6)
    res = inputs + mm(context_o[...], get(4)[...], 1, 1) + row(BO)
    residual[...] = res
    flush(1)
    hat2, _ = normalize(res)
    norm2 = (hat2 * row(GAIN2) + row(SHIFT2)).astype(bf16)
    norm2_o[...] = norm2
    flush(5)
    slots[...] = mm(dispatch_of(get(6)[...]), norm2).astype(bf16)
    flush(0)
    lane = lax.broadcasted_iota(i32, (ROWS, 128), 1)
    logits = jnp.where(lane < E, mm(norm2, get(5)[...]), 0.0)
    raised = jnp.where(lane < E, jnp.exp(logits), 0.0)
    router_o[...] = raised / jnp.sum(raised, axis=1, keepdims=True)
    flush(7)


class Staged:
    def __init__(self, far, near, sems, base):
        self.near = near
        self.copies = [
            pltpu.make_async_copy(f, v, sems.at[base + k])
            for k, (f, v) in enumerate(zip(far, near))
        ]
        self.waited = set()

    def start(self, k):
        self.copies[k].start()

    def get(self, k):
        if k not in self.waited:
            self.copies[k].wait()
            self.waited.add(k)
        return self.near[k]


def call(kernel, ins, outs, name, limit):
    n_in, n_out = len(ins), len(outs)

    def body(*refs):
        far_in, far_out = refs[:n_in], refs[n_in : n_in + n_out]
        near = refs[n_in + n_out : -1]
        sems = refs[-1]
        source = Staged(far_in, near[:n_in], sems, 0)
        for k in range(n_in):
            source.start(k)
        sink = Staged(near[n_in:], far_out, sems, n_in)
        kernel(source.get, near[n_in:], sink.start)
        for k in range(n_in):
            source.get(k)
        for k in range(n_out):
            sink.get(k)

    return pl.pallas_call(
        body,
        in_specs=[pl.BlockSpec(memory_space=pl.ANY)] * n_in,
        out_specs=[pl.BlockSpec(memory_space=pltpu.HBM)] * n_out,
        out_shape=[pltpu.HBM(shape, dtype) for shape, dtype in outs],
        scratch_shapes=[pltpu.VMEM(a.shape, a.dtype) for a in ins]
        + [pltpu.VMEM(shape, dtype) for shape, dtype in outs]
        + [pltpu.SemaphoreType.DMA((n_in + n_out,))],
        compiler_params=pltpu.CompilerParams(vmem_limit_bytes=limit << 20),
        name=name,
    )(*ins)


def attend_forward(x, placed, par):
    names = ("slots", "residual", "prob", "acts", "norm1", "norm2", "context", "router")
    outs = call(
        forward_kernel,
        (x, par["vec"], par["qkv_a"], par["qkv_b"], par["out_t"], par["small"], placed),
        [
            ((SLOTS, D), bf16), ((ROWS, D), f32), ((HEADS, ROWS, ROWS), bf16),
            ((ROWS, 3 * D), bf16), ((ROWS, D), bf16), ((ROWS, D), bf16), ((ROWS, D), bf16),
            ((ROWS, 128), f32),
        ],
        "attend_forward",
        16,
    )
    return dict(zip(names, outs))


def backward_kernel(get, outs, flush):
    input_grad, ph, res_half_o, logit_o, gate_o, sums = outs
    rec, placed, small, cot, vec = get(0), get(1), get(2), get(3), get(4)
    row = lambda k: vec[k : k + 1, :]
    disp = dispatch_of(placed[...])
    lane = lax.broadcasted_iota(i32, (SLOTS, 128), 1)
    slot_expert = lax.broadcasted_iota(i32, (SLOTS, 128), 0) // CAP
    moe = 0.0
    pg = 0.0
    for o in range(rec.shape[1]):
        rows = rec[:, o, :, :].reshape(SLOTS, D + 128)
        moe = moe + mm(disp, rows[:, :D], 0, 0)
        gg = jnp.where((lane & 63) == slot_expert, rows[:, D:], jnp.zeros((SLOTS, 128), bf16))
        pg = pg + mm(disp, gg, 0, 0)
    pg = pg + pltpu.roll(pg, 64, 1)
    hot = mm(disp, (lane == slot_expert).astype(f32).astype(bf16), 0, 0)
    pg = (pg + pltpu.roll(mm(cot[...], small[...]), 128 - E, 1)) * hot
    prob_r = get(5)[...]
    gate_o[...] = prob_r * hot
    flush(4)
    logit = prob_r * (pg - jnp.sum(pg * prob_r, axis=1, keepdims=True))
    real = lax.broadcasted_iota(i32, (ROWS, 1), 0) < SEQ
    logit = jnp.where(real, logit, 0.0).astype(bf16)
    logit_o[...] = logit
    flush(3)
    second = moe + mm(logit, small[...], 1, 1)
    hat2, rstd2 = normalize(get(6)[...])
    sums[GAIN2 : GAIN2 + 1, :] = jnp.sum(second * hat2, axis=0, keepdims=True)
    sums[SHIFT2 : SHIFT2 + 1, :] = jnp.sum(second, axis=0, keepdims=True)
    res_grad = cot[...].astype(f32) + norm_back(second * row(GAIN2), hat2, rstd2)
    input_grad[...] = res_grad
    sums[BO : BO + 1, :] = jnp.sum(res_grad, axis=0, keepdims=True)
    res_half = res_grad.astype(bf16)
    res_half_o[...] = res_half
    flush(2)
    cg = mm(res_half, get(7)[...]).astype(bf16)
    prob, acts = get(8), get(9)
    for j in range(PAIRS):
        q = acts[:, j * 128 : (j + 1) * 128]
        k = acts[:, D + j * 128 : D + (j + 1) * 128]
        v = acts[:, 2 * D + j * 128 : 2 * D + (j + 1) * 128]
        c = cg[:, j * 128 : (j + 1) * 128]
        qs, ks, vs = [], [], []
        for h in range(2):
            p = prob[2 * j + h, :, :]
            pf = p.astype(f32)
            t = pf * mm(half_of(v, h), c, 1, 1)
            sg = ((t - pf * jnp.sum(t, axis=0, keepdims=True)) * SCALE).astype(bf16)
            vs.append(mm(p, c))
            qs.append(mm(sg, k, 0, 0))
            ks.append(mm(sg, q))
        qg, kg, vg = join(*qs), join(*ks), join(*vs)
        cols = slice(j * 128, (j + 1) * 128)
        sums[BQ : BQ + 1, cols] = jnp.sum(qg, axis=0, keepdims=True)
        sums[BV : BV + 1, cols] = jnp.sum(vg, axis=0, keepdims=True)
        ph[:, j * 128 : (j + 1) * 128] = qg.astype(bf16)
        ph[:, D + j * 128 : D + (j + 1) * 128] = kg.astype(bf16)
        ph[:, 2 * D + j * 128 : 2 * D + (j + 1) * 128] = vg.astype(bf16)
    flush(1)
    first = mm(ph[:, :CUT], get(10)[...], 1, 1) + mm(ph[:, CUT:], get(11)[...], 1, 1)
    hat1, rstd1 = normalize(get(12)[...].astype(f32))
    sums[GAIN1 : GAIN1 + 1, :] = jnp.sum(first * hat1, axis=0, keepdims=True)
    sums[SHIFT1 : SHIFT1 + 1, :] = jnp.sum(first, axis=0, keepdims=True)
    sums[7:8, :] = jnp.zeros((1, D), f32)
    flush(5)
    input_grad[...] += norm_back(first * row(GAIN1), hat1, rstd1)
    flush(0)


def token_backward(rec, x, cot, placed, s, par):
    return call(
        backward_kernel,
        (
            rec, placed, par["small"], cot, par["vec"], s["router"], s["residual"],
            par["out_t"], s["prob"], s["acts"], par["qkv_a"], par["qkv_b"], x,
        ),
        [
            ((ROWS, D), f32), ((ROWS, 3 * D), bf16), ((ROWS, D), bf16), ((ROWS, 128), bf16),
            ((ROWS, 128), f32), ((8, D), f32),
        ],
        "token_backward",
        24,
    )


def expert_kernel(
    idx, x, c, w_in, hidden, bias, router, act, back, d_rows, gated, gate, grad_bias, acc, gg
):
    r, f = pl.program_id(0), pl.program_id(1)
    rows, width = act.shape

    @pl.when(f == 0)
    def _():
        logits = mm(x[...], router[...])
        lane = lax.broadcasted_iota(i32, logits.shape, 1)
        raised = jnp.where(lane < E, jnp.exp(jnp.where(lane < E, logits, 0.0)), 0.0)
        picked = lane == idx[0]
        g = jnp.sum(jnp.where(picked, raised, 0.0), axis=1, keepdims=True)
        g = g / jnp.sum(raised, axis=1, keepdims=True)
        gate[...] = jnp.broadcast_to(g, gate.shape)
        rows_c = c[...].reshape(rows, D).astype(f32)
        gated[...] = (rows_c * g).astype(bf16)
        gg[...] = jnp.zeros_like(gg)
        acc[...] = jnp.zeros_like(acc)

    value, slope = gelu_terms(mm(x[...], w_in[...], 1, 1) + bias[...])
    hid = hidden[...].astype(f32)
    act[...] = value.astype(bf16)
    both = value * hid
    part = both[:, :128]
    for j in range(1, width // 128):
        part = part + both[:, j * 128 : (j + 1) * 128]
    gg[...] += part
    before = hid * slope * gate[:, :1]
    total = jnp.sum(before, axis=0, keepdims=True)
    half = before.astype(bf16)
    back[...] = half
    acc[...] += mm(half, w_in[...])
    cols = pl.ds(pl.multiple_of(f * width, width), width)

    @pl.when(r == 0)
    def _():
        grad_bias[:, cols] = total

    @pl.when(r > 0)
    def _():
        grad_bias[:, cols] += total

    @pl.when(f == pl.num_programs(1) - 1)
    def _():
        d_rows[:, :D] = acc[...].astype(bf16)
        g = jnp.sum(gg[...], axis=1, keepdims=True)
        high = g.astype(bf16)
        low = (g - high.astype(f32)).astype(bf16)
        lane = lax.broadcasted_iota(i32, (rows, 128), 1)
        d_rows[:, D:] = jnp.where(
            lane < 64, jnp.broadcast_to(high, lane.shape), jnp.broadcast_to(low, lane.shape)
        )


def expert_main(i, x, c, w_in, hidden, bias, router, expert):
    total, width = x.shape[0], w_in.shape[0]
    rb, fb = min(512, total), min(768, width)
    row = lambda r, f, *_: (r, 0)
    tile = lambda r, f, *_: (r, f)
    fixed = lambda r, f, *_: (0, 0)
    return pl.pallas_call(
        expert_kernel,
        grid_spec=pltpu.PrefetchScalarGridSpec(
            num_scalar_prefetch=1,
            grid=(total // rb, width // fb),
            in_specs=[
                pl.BlockSpec((rb, D), row),
                pl.BlockSpec((rb // CAP, None, CAP, D), lambda r, f, *_: (r, i, 0, 0)),
                pl.BlockSpec((fb, D), lambda r, f, *_: (f, 0)),
                pl.BlockSpec((None, rb, fb), lambda r, f, *_: (i, r, f)),
                pl.BlockSpec((1, fb), lambda r, f, *_: (0, f)),
                pl.BlockSpec((D, 128), fixed),
            ],
            out_specs=[
                pl.BlockSpec((rb, fb), tile),
                pl.BlockSpec((rb, fb), tile),
                pl.BlockSpec((rb, D + 128), row),
                pl.BlockSpec((rb, D), row),
                pl.BlockSpec((rb, 128), row),
                pl.BlockSpec((1, width), fixed),
            ],
            scratch_shapes=[
                pltpu.VMEM((rb, D), f32),
                pltpu.VMEM((rb, 128), f32),
            ],
        ),
        out_shape=[
            pltpu.HBM((total, width), bf16),
            pltpu.HBM((total, width), bf16),
            pltpu.HBM((total, D + 128), bf16),
            pltpu.HBM((total, D), bf16),
            pltpu.HBM((total, 128), f32),
            pltpu.HBM((1, width), f32),
        ],
        compiler_params=pltpu.CompilerParams(
            dimension_semantics=("arbitrary", "arbitrary"), vmem_limit_bytes=24 << 20
        ),
        name="expert_main",
    )(expert.reshape(1), x, c, w_in, hidden, bias.reshape(1, width), router)


def hidden_kernel(c, w_out, out):
    out[...] = mm(c[...].reshape(out.shape[0], D), w_out[...], 1, 1).astype(bf16)


def expert_hidden(cot_in, w_out):
    n, images = cot_in.shape[:2]
    total, width = n * CAP, w_out.shape[0]
    fb = min(768, width)
    return pl.pallas_call(
        hidden_kernel,
        grid=(width // fb, images),
        in_specs=[
            pl.BlockSpec((n, None, CAP, D), lambda f, i: (0, i, 0, 0)),
            pl.BlockSpec((fb, D), lambda f, i: (f, 0)),
        ],
        out_specs=pl.BlockSpec((None, total, fb), lambda f, i: (i, 0, f)),
        out_shape=pltpu.HBM((images, total, width), bf16),
        compiler_params=pltpu.CompilerParams(
            dimension_semantics=("arbitrary", "arbitrary"), vmem_limit_bytes=36 << 20
        ),
        name="expert_hidden",
    )(cot_in, w_out)


def parts_kernel(act0, act1, gate0, gate1, w_out, out, acc):
    f = pl.program_id(0)

    @pl.when(f == 0)
    def _():
        acc[...] = jnp.zeros_like(acc)

    for i, act in enumerate((act0, act1)):
        acc[i] += mm(act[...], w_out[...])

    @pl.when(f == pl.num_programs(0) - 1)
    def _():
        for i, gate in enumerate((gate0, gate1)):
            rows = (acc[i] * gate[:, :1]).astype(bf16)
            out[:, i, :, :] = rows.reshape(out.shape[0], CAP, D)


def expert_parts(acts, gates, w_out):
    total, width = acts[0].shape
    fb = min(768, width)
    n = total // CAP
    cols = pl.BlockSpec((total, fb), lambda f: (0, f))
    full = pl.BlockSpec((total, 128), lambda f: (0, 0))
    return pl.pallas_call(
        parts_kernel,
        grid=(width // fb,),
        in_specs=[cols, cols, full, full, pl.BlockSpec((fb, D), lambda f: (f, 0))],
        out_specs=pl.BlockSpec((n, 2, CAP, D), lambda f: (0, 0, 0, 0)),
        out_shape=pltpu.HBM((n, 2, CAP, D), bf16),
        scratch_shapes=[pltpu.VMEM((2, total, D), f32)],
        compiler_params=pltpu.CompilerParams(
            dimension_semantics=("arbitrary",), vmem_limit_bytes=48 << 20
        ),
        name="expert_parts",
    )(*acts, *gates, w_out)


def moved_kernel(get, outs, flush):
    perm_a, perm_b = get(0)[...], get(1)[...]
    for k in range(3):
        for i in range(2):
            value = get(2 + 2 * k + i)[...]
            outs[k][i] = mm(value, perm_b).astype(bf16)
            if k == 0:
                outs[3][i] = mm(value, perm_a).astype(bf16)
        flush(k)
    flush(3)


def grads_kernel(get, outs, flush):
    sent_a, kept_a, sent_b, kept_b = outs
    half = D // 2

    def lay(value, sent, kept, start):
        kept[:, start : start + value.shape[1]] = value[:half]
        sent[:, start : start + value.shape[1]] = value[half:].astype(bf16)

    norm1a, norm1b, ph = get(0), get(1), (get(2), get(3))
    lay(sum(mm(norm1a[i], ph[i][:, :CUT], 0, 0) for i in range(2)), sent_a, kept_a, 0)
    flush(0)
    flush(1)
    lay(sum(mm(norm1b[i], ph[i][:, CUT:], 0, 0) for i in range(2)), sent_b, kept_b, 0)
    start = 3 * D - CUT
    perm = get(4)[...]
    out = 0.0
    for i in range(2):
        out = out + mm(mm(get(5 + i)[...], perm).astype(bf16), get(7 + i)[...], 0, 0)
    lay(out, sent_b, kept_b, start)
    sums = get(9)[...] + get(10)[...]
    moved = sum(mm(p, perm) for p in pieces(sums, 3))
    zeros = jnp.zeros((56, D), f32)
    tail = jnp.concatenate([jnp.zeros((2 * E, D), f32), moved, zeros], axis=0).T
    for i in range(2):
        tail = tail + mm(get(11)[i], get(13 + i)[...], 0, 0)
        for p in pieces(pltpu.roll(get(15 + i)[...], E, 1), 2):
            tail = tail + mm(get(12)[i], p, 0, 0)
    lay(tail, sent_b, kept_b, start + D)
    flush(2)
    flush(3)


def output_kernel(get, outs, flush):
    block_out, input_grad = outs
    small, parts = get(0), get(1)
    for i in range(2):
        placed, residual, gate, grad = (get(2 + 4 * i + k) for k in range(4))
        input_grad[i * SEQ : (i + 1) * SEQ, :] = grad[:SEQ, :]
        disp = dispatch_of(placed[...])
        out = residual[...]
        for o in range(parts.shape[1]):
            out = out + mm(disp, parts[:, o, i, :, :].reshape(SLOTS, D), 0, 0)
        for p in pieces(pltpu.roll(gate[...], E, 1), 2):
            out = out + mm(p, small[...], 1, 1)
        block_out[i * SEQ : (i + 1) * SEQ, :] = out[:SEQ]
    flush(0)
    flush(1)


def weights_kernel(act0, act1, back0, back1, g0, g1, x0, x1, out_w, in_w):
    out_w[...] = mm(act0[...], g0[...], 0, 0) + mm(act1[...], g1[...], 0, 0)
    in_w[...] = mm(back0[...], x0[...], 0, 0) + mm(back1[...], x1[...], 0, 0)


def expert_weights(acts, backs, gated, xs):
    total, width = acts[0].shape
    fb = min(512, width)
    cols = pl.BlockSpec((total, fb), lambda f: (0, f))
    full = pl.BlockSpec((total, D), lambda f: (0, 0))
    rows = pl.BlockSpec((fb, D), lambda f: (f, 0))
    return pl.pallas_call(
        weights_kernel,
        grid=(width // fb,),
        in_specs=[cols] * 4 + [full] * 4,
        out_specs=[rows, rows],
        out_shape=[pltpu.HBM((width, D), f32)] * 2,
        compiler_params=pltpu.CompilerParams(
            dimension_semantics=("arbitrary",), vmem_limit_bytes=40 << 20
        ),
        name="expert_weights",
    )(*acts, *backs, *gated, *xs)


def on_device(
    block_in, out_cotangent, expert_routes, ln1_gain, ln1_shift, w_qkv, bias_query, bias_value,
    w_out, bias_out, ln2_gain, ln2_shift, w_router, expert_bias, w_expert_in, bias_hidden,
    w_expert_out,
):
    images = block_in.shape[0] // SEQ
    n = lax.axis_size(AXIS)
    owners = n // E
    expert = lax.axis_index(AXIS) // owners
    order_a, order_b = bit_orders()
    vectors = jnp.stack(
        [ln1_gain, ln1_shift, bias_query, bias_value, bias_out, ln2_gain, ln2_shift], axis=1
    )
    pad = jnp.zeros((vectors.shape[0], 128 - 2 * E - VECTORS), bf16)
    part_a = w_qkv[:, :CUT]
    part_b = jnp.concatenate(
        [w_qkv[:, CUT:], w_out.T, w_router, expert_bias.T, vectors, pad], axis=1
    )
    pad_rows = ((0, ROWS - SEQ), (0, 0))
    xs, cots, placed, states, outgoing = [], [], [], [], []
    for i in range(images):
        xs.append(jnp.pad(block_in[i * SEQ : (i + 1) * SEQ], pad_rows))
        cots.append(jnp.pad(out_cotangent[i * SEQ : (i + 1) * SEQ], pad_rows))
        placed.append(place(expert_routes[i * SEQ : (i + 1) * SEQ]))
        slots = mm(dispatch_of(placed[i]), cots[i]).astype(bf16)
        outgoing.append(to_owners(slots, owners))
    (full_a, full_b), outgoing = gather_rows(
        [part_a, part_b], 2, jnp.stack(outgoing, axis=1)
    )
    start = 3 * D - CUT
    small = full_b[:, start + D :]
    par = {
        "qkv_a": full_a,
        "qkv_b": full_b[:, :start],
        "out_t": full_b[:, start : start + D],
        "small": small,
        "vec": small[:, 2 * E : 2 * E + 8].T.astype(f32),
    }

    barrier = lax.optimization_barrier
    cot_in = exchange(outgoing)
    for i in range(images):
        states.append(attend_forward(xs[i], placed[i], par))
    hidden = expert_hidden(cot_in, w_expert_out)
    first = exchange(to_owners(states[0]["slots"], owners))
    slots, hidden = barrier((states[1]["slots"], hidden))
    second = exchange(to_owners(slots, owners))
    arrived = [first.reshape(-1, D), second.reshape(-1, D)]
    done = []
    grad_hidden = 0.0
    received = []
    for i in range(images):
        act, back, d_rows, gated, gate, gb = expert_main(
            i, arrived[i], cot_in, w_expert_in, hidden, bias_hidden, small, expert
        )
        done.append((act, back, gated, gate))
        grad_hidden = grad_hidden + gb[0]
        rows = exchange(d_rows.reshape(n, CAP, D + 128))
        received.append(rows.reshape(E, owners, CAP, D + 128))
    sent = expert_parts([d[0] for d in done], [d[3] for d in done], w_expert_out)
    sent, received[1] = barrier((sent, received[1]))
    parts = exchange(sent).reshape(E, owners, images, CAP, D)
    grad_expert_out, grad_expert_in = expert_weights(
        [d[0] for d in done], [d[1] for d in done], [d[2] for d in done], arrived
    )

    perm_b = permutation(order_b)
    both = lambda key: tuple(s[key] for s in states)
    norm1b, norm2b, cotb, norm1a = call(
        moved_kernel,
        (permutation(order_a), perm_b) + both("norm1") + both("norm2") + tuple(cots),
        [((2, ROWS, D), bf16)] * 4,
        "move_columns",
        24,
    )
    back = [
        token_backward(received[i], xs[i], cots[i], placed[i], states[i], par)
        for i in range(images)
    ]
    pair = lambda index: tuple(b[index] for b in back)
    sent_a, kept_a, sent_b, kept_b = call(
        grads_kernel,
        (norm1a, norm1b) + pair(1) + (perm_b,) + pair(2) + both("context") + pair(5)
        + (norm2b, cotb) + pair(3) + pair(4),
        [
            ((D // 2, CUT), bf16), ((D // 2, CUT), f32),
            ((D // 2, PACK - CUT), bf16), ((D // 2, PACK - CUT), f32),
        ],
        "pack_grads",
        40,
    )
    mine_a = scatter_rows(sent_a, kept_a, order_a)
    mine_b = scatter_rows(sent_b, kept_b, order_b)
    ins = ()
    for i in range(images):
        ins += (placed[i], states[i]["residual"], back[i][4], back[i][0])
    block_out, input_grad = call(
        output_kernel, (small, parts) + ins, [((images * SEQ, D), f32)] * 2, "outputs", 24
    )
    tail = mine_b[:, start + D :]
    vec = [tail[:, 2 * E + i] for i in range(VECTORS)]
    return (
        block_out, input_grad, vec[GAIN1], vec[SHIFT1],
        jnp.concatenate([mine_a, mine_b[:, :start]], axis=1), vec[BQ], vec[BV],
        mine_b[:, start : start + D].T, vec[BO], vec[GAIN2], vec[SHIFT2],
        tail[:, :E], tail[:, E : 2 * E].T, grad_expert_in, grad_hidden, grad_expert_out,
    )


def solution(mesh):
    rows, line, cols = P(AXIS, None), P(AXIS), P(None, AXIS)
    in_specs = (
        rows, rows, rows, line, line, rows, line, line, cols, line, line, line, rows, cols,
        rows, line, rows,
    )
    out_specs = (
        rows, rows, line, line, rows, line, line, cols, line, line, line, rows, cols, rows,
        line, rows,
    )
    return jax.shard_map(
        on_device, mesh=mesh, in_specs=in_specs, out_specs=out_specs, check_vma=False
    )
```

```python
import math

import jax
import jax.numpy as jnp
from jax import lax
from jax.experimental import pallas as pl
from jax.experimental.pallas import tpu as pltpu
from jax.sharding import PartitionSpec as P

D = 768
HEADS = 12
HEAD_DIM = 64
PAIRS = HEADS // 2
E = 32
SEQ = 197
ROWS = 208
CAP = 16
SLOTS = E * CAP
AXIS = "fsdp"
PACK = 3200
CUT = 1664
GAIN1, SHIFT1, BQ, BV, BO, GAIN2, SHIFT2, VECTORS = range(8)
SCALE = 1.0 / math.sqrt(HEAD_DIM)

epsilon = 1e-06
f32 = jnp.float32
bf16 = jnp.bfloat16
i32 = jnp.int32


def mm(a, b, ca=1, cb=0):
    return lax.dot_general(a, b, (((ca,), (cb,)), ((), ())), preferred_element_type=f32)


def pieces(v, n):
    out = []
    for _ in range(n):
        p = v.astype(bf16)
        out.append(p)
        v = v - p.astype(f32)
    return out


def normalize(values):
    centered = values - jnp.mean(values, axis=-1, keepdims=True)
    inverse = lax.rsqrt(jnp.mean(centered * centered, axis=-1, keepdims=True) + epsilon)
    return (centered * inverse, inverse)


def norm_back(upstream, normed, inverse):
    return inverse * (
        upstream
        - jnp.mean(upstream, axis=-1, keepdims=True)
        - normed * jnp.mean(upstream * normed, axis=-1, keepdims=True)
    )


def swap(values, bit):
    n = lax.axis_size(AXIS)
    return lax.ppermute(values, AXIS, [(d, d ^ (1 << bit)) for d in range(n)])


def bit_of(bit):
    return (lax.axis_index(AXIS) >> bit) & 1


def bit_orders():
    bits = lax.axis_size(AXIS).bit_length() - 1
    inner = (bits - 1) // 3 if bits != 5 else 1
    x = list(range(1, 1 + inner))
    y = list(range(1 + inner, 1 + 2 * inner))
    z = list(range(1 + 2 * inner, bits))
    return [0] + x + y + z, [0] + y + x + z


def gather_rows(shards, early, wait_for):
    orders = bit_orders()
    held = [(shard, []) for shard in shards]
    for step in range(len(orders[0])):
        moved = []
        for (values, done), order in zip(held, orders):
            bit = order[-1 - step]
            theirs = swap(values, bit)
            at = sum(1 for b in done if b > bit)
            lead = values.shape[0]
            high = 1 << at
            mine = values.reshape((high, lead // high) + values.shape[1:])
            theirs = theirs.reshape(mine.shape)
            which = lax.broadcasted_iota(i32, (1, 2, 1, 1, 1), 1) == bit_of(bit)
            both = jnp.where(which, mine[:, None], theirs[:, None])
            moved.append((both.reshape((2 * lead,) + values.shape[1:]), done + [bit]))
        held = moved
        if step + 1 == early:
            tied = lax.optimization_barrier([values for values, _ in held] + [wait_for])
            held = [(t, done) for t, (_, done) in zip(tied, held)]
            wait_for = tied[-1]
    return [values.reshape((-1, values.shape[-1])) for values, _ in held], wait_for


def owner_order(order):
    n = lax.axis_size(AXIS)
    own = D // n
    position = jnp.arange(D, dtype=i32)
    chunk = position // own
    owner = jnp.zeros_like(chunk)
    for step, bit in enumerate(order):
        owner = owner | (((chunk >> (len(order) - 1 - step)) & 1) << bit)
    return (owner ^ lax.axis_index(AXIS)) * own + position % own


def permutation(order):
    return (jnp.arange(D, dtype=i32)[:, None] == owner_order(order)[None]).astype(bf16)


def scatter_rows(sent, kept, order):
    for step, bit in enumerate(order):
        got = swap(sent, bit)
        if step + 1 == len(order):
            return kept, got
        held = kept + got.astype(f32)
        half = held.shape[0] // 2
        kept, sent = held[:half], held[half:].astype(bf16)


def exchange(blocks):
    return lax.all_to_all(blocks, AXIS, split_axis=0, concat_axis=0, tiled=True)


def to_owners(slot_rows, owners):
    rows = slot_rows.reshape((E, 1, CAP) + slot_rows.shape[1:])
    rows = jnp.broadcast_to(rows, (E, owners) + rows.shape[2:])
    return rows.reshape((E * owners, CAP) + slot_rows.shape[1:])


def place(routes):
    choice = jnp.pad(routes.T, ((0, 0), (0, ROWS - SEQ)), constant_values=-1)
    ids = jnp.arange(E, dtype=i32)[:, None]
    first = (choice[:1] == ids).astype(bf16)
    second = (choice[1:] == ids).astype(bf16)
    t = jnp.arange(ROWS, dtype=i32)
    earlier = (t[:, None] < t[None, :]).astype(bf16)
    before = mm(jnp.concatenate([first, second], axis=0), earlier)
    rank0 = jnp.sum(before[:E] * first, axis=0)
    seen = before[E:] + jnp.sum(first.astype(f32), axis=1, keepdims=True)
    rank1 = jnp.sum(seen * second, axis=0)
    return choice * CAP + jnp.stack([rank0, rank1]).astype(i32)


def gelu_terms(v):
    cumulative = 0.5 * (1.0 + lax.erf(v * (1.0 / math.sqrt(2.0))))
    density = jnp.exp(-0.5 * v * v) * (1.0 / math.sqrt(2.0 * math.pi))
    return v * cumulative, cumulative + v * density


def dispatch_of(placed):
    slot = lax.broadcasted_iota(i32, (SLOTS, ROWS), 0)
    hit = (slot == placed[0:1, :]) | (slot == placed[1:2, :])
    return hit.astype(f32).astype(bf16)


def half_of(pair, second):
    lane = lax.broadcasted_iota(i32, pair.shape, 1)
    keep = (lane >= HEAD_DIM) if second else (lane < HEAD_DIM)
    return jnp.where(keep, pair, jnp.zeros_like(pair))


def join(first, second):
    lane = lax.broadcasted_iota(i32, first.shape, 1)
    return jnp.where(lane < HEAD_DIM, first, second)


def forward_kernel(get, outs, flush):
    slots, residual, prob, acts, norm1_o, norm2_o, context_o, router_o = outs
    inputs = get(0)[...].astype(f32)
    hat1, _ = normalize(inputs)
    vec = vectors_of(get(4))
    row = lambda k: vec[k : k + 1, :]
    norm1 = (hat1 * row(GAIN1) + row(SHIFT1)).astype(bf16)
    norm1_o[...] = norm1
    flush(4)
    proj = jnp.concatenate([mm(norm1, get(1)[...]), mm(norm1, get(2)[...])], axis=1)
    acts[:, :D] = (proj[:, :D] + row(BQ)).astype(bf16)
    acts[:, D : 2 * D] = proj[:, D : 2 * D].astype(bf16)
    acts[:, 2 * D :] = (proj[:, 2 * D :] + row(BV)).astype(bf16)
    flush(3)
    token = lax.broadcasted_iota(i32, (ROWS, ROWS), 0) < SEQ
    for j in range(PAIRS):
        q = acts[:, j * 128 : (j + 1) * 128] * jnp.asarray(SCALE, bf16)
        k = acts[:, D + j * 128 : D + (j + 1) * 128]
        v = acts[:, 2 * D + j * 128 : 2 * D + (j + 1) * 128]
        both = []
        for h in range(2):
            raised = jnp.exp(mm(half_of(k, h), q, 1, 1))
            raised = jnp.where(token, raised, 0.0)
            p = (raised * (1.0 / jnp.sum(raised, axis=0, keepdims=True))).astype(bf16)
            prob[2 * j + h, :, :] = p
            both.append(mm(p, v, 0, 0))
        context_o[:, j * 128 : (j + 1) * 128] = join(both[0], both[1]).astype(bf16)
    flush(2)
    flush(6)
    res = inputs + mm(context_o[...], get(3)[...], 1, 1) + row(BO)
    residual[...] = res
    flush(1)
    hat2, _ = normalize(res)
    norm2 = (hat2 * row(GAIN2) + row(SHIFT2)).astype(bf16)
    norm2_o[...] = norm2
    flush(5)
    slots[...] = mm(dispatch_of(get(5)[...]), norm2).astype(bf16)
    flush(0)
    lane = lax.broadcasted_iota(i32, (ROWS, 128), 1)
    logits = jnp.where(lane < E, mm(norm2, get(4)[...]), 0.0)
    raised = jnp.where(lane < E, jnp.exp(logits), 0.0)
    router_o[...] = raised / jnp.sum(raised, axis=1, keepdims=True)
    flush(7)


class Staged:
    def __init__(self, far, near, sems, base):
        self.near = near
        self.copies = [
            pltpu.make_async_copy(f, v, sems.at[base + k])
            for k, (f, v) in enumerate(zip(far, near))
        ]
        self.waited = set()

    def start(self, k):
        self.copies[k].start()

    def get(self, k):
        if k not in self.waited:
            self.copies[k].wait()
            self.waited.add(k)
        return self.near[k]


def call(kernel, ins, outs, limit, temps=()):
    ins = [item if isinstance(item, tuple) else (item, None) for item in ins]
    n_in, n_out = len(ins), len(outs)
    shapes = []
    for array, cols in ins:
        shape = array.shape if cols is None else (array.shape[0], cols[1] - cols[0])
        shapes.append((shape, array.dtype))

    def body(*refs):
        far_in, far_out = refs[:n_in], refs[n_in : n_in + n_out]
        near = refs[n_in + n_out : -1]
        sems = refs[-1]
        far_in = [
            ref if cols is None else ref.at[:, cols[0] : cols[1]]
            for ref, (_, cols) in zip(far_in, ins)
        ]
        source = Staged(far_in, near[:n_in], sems, 0)
        for k in range(n_in):
            source.start(k)
        sink = Staged(near[n_in : n_in + n_out], far_out, sems, n_in)
        kernel(source.get, near[n_in:], sink.start)
        for k in range(n_in):
            source.get(k)
        for k in range(n_out):
            sink.get(k)

    return pl.pallas_call(
        body,
        in_specs=[pl.BlockSpec(memory_space=pltpu.HBM)] * n_in,
        out_specs=[pl.BlockSpec(memory_space=pltpu.HBM)] * n_out,
        out_shape=[pltpu.HBM(shape, dtype) for shape, dtype in outs],
        scratch_shapes=[pltpu.VMEM(shape, dtype) for shape, dtype in shapes]
        + [pltpu.VMEM(shape, dtype) for shape, dtype in list(outs) + list(temps)]
        + [pltpu.SemaphoreType.DMA((n_in + n_out,))],
        compiler_params=pltpu.CompilerParams(vmem_limit_bytes=limit << 20),
    )(*[array for array, _ in ins])


def in_hbm(*arrays):
    return [pltpu.with_memory_space_constraint(a, pltpu.HBM) for a in arrays]


def vectors_of(small):
    lane = lax.broadcasted_iota(i32, (8, 128), 1)
    pick = lane == lax.broadcasted_iota(i32, (8, 128), 0) + 2 * E
    return mm(pick.astype(f32).astype(bf16), small[...], 1, 1)


QKV_B = (0, 3 * D - CUT)
OUT_T = (3 * D - CUT, 4 * D - CUT)
SMALL = (4 * D - CUT, PACK - CUT)


def attend_forward(x, placed, full_a, full_b):
    names = ("slots", "residual", "prob", "acts", "norm1", "norm2", "context", "router")
    outs = call(
        forward_kernel,
        (x, full_a, (full_b, QKV_B), (full_b, OUT_T), (full_b, SMALL), placed),
        [
            ((SLOTS, D), bf16), ((ROWS, D), f32), ((HEADS, ROWS, ROWS), bf16),
            ((ROWS, 3 * D), bf16), ((ROWS, D), bf16), ((ROWS, D), bf16), ((ROWS, D), bf16),
            ((ROWS, 128), f32),
        ],
        16,
    )
    return dict(zip(names, outs))


def backward_kernel(get, outs, flush):
    input_grad, gate_o, ph, res_half_o, logit_o, sums = outs
    rec, placed, small, cot = get(0), get(1), get(2), get(3)
    vec = vectors_of(small)
    row = lambda k: vec[k : k + 1, :]
    disp = dispatch_of(placed[...])
    lane = lax.broadcasted_iota(i32, (SLOTS, 128), 1)
    slot_expert = lax.broadcasted_iota(i32, (SLOTS, 128), 0) // CAP
    moe = 0.0
    pg = 0.0
    for o in range(rec.shape[1]):
        rows = rec[:, o, :, :].reshape(SLOTS, D + 128)
        moe = moe + mm(disp, rows[:, :D], 0, 0)
        gg = jnp.where((lane & 63) == slot_expert, rows[:, D:], jnp.zeros((SLOTS, 128), bf16))
        pg = pg + mm(disp, gg, 0, 0)
    pg = pg + pltpu.roll(pg, 64, 1)
    hot = mm(disp, (lane == slot_expert).astype(f32).astype(bf16), 0, 0)
    pg = (pg + pltpu.roll(mm(cot[...], small[...]), 128 - E, 1)) * hot
    prob_r = get(4)[...]
    gate_o[...] = prob_r * hot
    flush(1)
    logit = prob_r * (pg - jnp.sum(pg * prob_r, axis=1, keepdims=True))
    real = lax.broadcasted_iota(i32, (ROWS, 1), 0) < SEQ
    logit = jnp.where(real, logit, 0.0).astype(bf16)
    logit_o[...] = logit
    flush(4)
    second = moe + mm(logit, small[...], 1, 1)
    hat2, rstd2 = normalize(get(5)[...])
    sums[GAIN2 : GAIN2 + 1, :] = jnp.sum(second * hat2, axis=0, keepdims=True)
    sums[SHIFT2 : SHIFT2 + 1, :] = jnp.sum(second, axis=0, keepdims=True)
    res_grad = cot[...].astype(f32) + norm_back(second * row(GAIN2), hat2, rstd2)
    input_grad[...] = res_grad
    sums[BO : BO + 1, :] = jnp.sum(res_grad, axis=0, keepdims=True)
    res_half = res_grad.astype(bf16)
    res_half_o[...] = res_half
    flush(3)
    cg = mm(res_half, get(6)[...]).astype(bf16)
    prob, acts = get(7), get(8)
    for j in range(PAIRS):
        q = acts[:, j * 128 : (j + 1) * 128]
        k = acts[:, D + j * 128 : D + (j + 1) * 128]
        v = acts[:, 2 * D + j * 128 : 2 * D + (j + 1) * 128]
        c = cg[:, j * 128 : (j + 1) * 128]
        qs, ks, vs = [], [], []
        for h in range(2):
            p = prob[2 * j + h, :, :]
            pf = p.astype(f32)
            t = pf * mm(half_of(v, h), c, 1, 1)
            sg = ((t - pf * jnp.sum(t, axis=0, keepdims=True)) * SCALE).astype(bf16)
            vs.append(mm(p, c))
            qs.append(mm(sg, k, 0, 0))
            ks.append(mm(sg, q))
        qg, kg, vg = join(*qs), join(*ks), join(*vs)
        cols = slice(j * 128, (j + 1) * 128)
        sums[BQ : BQ + 1, cols] = jnp.sum(qg, axis=0, keepdims=True)
        sums[BV : BV + 1, cols] = jnp.sum(vg, axis=0, keepdims=True)
        ph[:, j * 128 : (j + 1) * 128] = qg.astype(bf16)
        ph[:, D + j * 128 : D + (j + 1) * 128] = kg.astype(bf16)
        ph[:, 2 * D + j * 128 : 2 * D + (j + 1) * 128] = vg.astype(bf16)
    flush(2)
    first = mm(ph[:, :CUT], get(9)[...], 1, 1) + mm(ph[:, CUT:], get(10)[...], 1, 1)
    hat1, rstd1 = normalize(get(11)[...].astype(f32))
    sums[GAIN1 : GAIN1 + 1, :] = jnp.sum(first * hat1, axis=0, keepdims=True)
    sums[SHIFT1 : SHIFT1 + 1, :] = jnp.sum(first, axis=0, keepdims=True)
    sums[7:8, :] = jnp.zeros((1, D), f32)
    flush(5)
    input_grad[...] += norm_back(first * row(GAIN1), hat1, rstd1)
    flush(0)


BACKWARD_TEMPS = [
    ((ROWS, 3 * D), bf16), ((ROWS, D), bf16), ((ROWS, 128), bf16), ((8, D), f32),
]


def backward_operands(rec, x, cot, placed, s, full_a, full_b):
    return (
        rec, placed, (full_b, SMALL), cot, s["router"], s["residual"], (full_b, OUT_T),
        s["prob"], s["acts"], full_a, (full_b, QKV_B), x,
    )


def token_backward(*args):
    return call(
        backward_kernel,
        backward_operands(*args),
        [((ROWS, D), f32), ((ROWS, 128), f32)] + BACKWARD_TEMPS,
        24,
    )


def expert_kernel(
    idx, x, c, w_in, hidden, bias, router, act, back, d_rows, gated, gate, grad_bias, acc, gg
):
    r, f = pl.program_id(0), pl.program_id(1)
    rows, width = act.shape

    @pl.when(f == 0)
    def _():
        logits = mm(x[...], router[...])
        lane = lax.broadcasted_iota(i32, logits.shape, 1)
        raised = jnp.where(lane < E, jnp.exp(jnp.where(lane < E, logits, 0.0)), 0.0)
        picked = lane == idx[0]
        g = jnp.sum(jnp.where(picked, raised, 0.0), axis=1, keepdims=True)
        g = g / jnp.sum(raised, axis=1, keepdims=True)
        gate[...] = jnp.broadcast_to(g, gate.shape)
        rows_c = c[...].reshape(rows, D).astype(f32)
        gated[...] = (rows_c * g).astype(bf16)
        gg[...] = jnp.zeros_like(gg)
        acc[...] = jnp.zeros_like(acc)

    value, slope = gelu_terms(mm(x[...], w_in[...], 1, 1) + bias[...])
    hid = hidden[...].astype(f32)
    act[...] = value.astype(bf16)
    both = value * hid
    part = both[:, :128]
    for j in range(1, width // 128):
        part = part + both[:, j * 128 : (j + 1) * 128]
    gg[...] += part
    before = hid * slope * gate[:, :1]
    total = jnp.sum(before, axis=0, keepdims=True)
    half = before.astype(bf16)
    back[...] = half
    acc[...] += mm(half, w_in[...])
    cols = pl.ds(pl.multiple_of(f * width, width), width)

    @pl.when(r == 0)
    def _():
        grad_bias[:, cols] = total

    @pl.when(r > 0)
    def _():
        grad_bias[:, cols] += total

    @pl.when(f == pl.num_programs(1) - 1)
    def _():
        d_rows[:, :D] = acc[...].astype(bf16)
        g = jnp.sum(gg[...], axis=1, keepdims=True)
        high = g.astype(bf16)
        low = (g - high.astype(f32)).astype(bf16)
        lane = lax.broadcasted_iota(i32, (rows, 128), 1)
        d_rows[:, D:] = jnp.where(
            lane < 64, jnp.broadcast_to(high, lane.shape), jnp.broadcast_to(low, lane.shape)
        )


def expert_main(i, x, c, w_in, hidden, bias, router, expert):
    total, width = x.shape[0], w_in.shape[0]
    rb, fb = min(512, total), min(768, width)
    row = lambda r, f, *_: (r, 0)
    tile = lambda r, f, *_: (r, f)
    fixed = lambda r, f, *_: (0, 0)
    return pl.pallas_call(
        expert_kernel,
        grid_spec=pltpu.PrefetchScalarGridSpec(
            num_scalar_prefetch=1,
            grid=(total // rb, width // fb),
            in_specs=[
                pl.BlockSpec((rb, D), row),
                pl.BlockSpec((rb // CAP, None, CAP, D), lambda r, f, *_: (r, i, 0, 0)),
                pl.BlockSpec((fb, D), lambda r, f, *_: (f, 0)),
                pl.BlockSpec((None, rb, fb), lambda r, f, *_: (i, r, f)),
                pl.BlockSpec((1, fb), lambda r, f, *_: (0, f)),
                pl.BlockSpec((D, 128), lambda r, f, *_: (0, SMALL[0] // 128)),
            ],
            out_specs=[
                pl.BlockSpec((rb, fb), tile),
                pl.BlockSpec((rb, fb), tile),
                pl.BlockSpec((rb, D + 128), row),
                pl.BlockSpec((rb, D), row),
                pl.BlockSpec((rb, 128), row),
                pl.BlockSpec((1, width), fixed),
            ],
            scratch_shapes=[
                pltpu.VMEM((rb, D), f32),
                pltpu.VMEM((rb, 128), f32),
            ],
        ),
        out_shape=[
            pltpu.HBM((total, width), bf16),
            pltpu.HBM((total, width), bf16),
            pltpu.HBM((total, D + 128), bf16),
            pltpu.HBM((total, D), bf16),
            pltpu.HBM((total, 128), f32),
            pltpu.HBM((1, width), f32),
        ],
        compiler_params=pltpu.CompilerParams(
            dimension_semantics=("arbitrary", "arbitrary"), vmem_limit_bytes=24 << 20
        ),
        name="expert_main",
    )(expert.reshape(1), *in_hbm(x, c, w_in, hidden, bias.reshape(1, width), router))


def hidden_kernel(c, w_out, out):
    out[...] = mm(c[...].reshape(out.shape[0], D), w_out[...], 1, 1).astype(bf16)


def expert_hidden(cot_in, w_out):
    n, images = cot_in.shape[:2]
    total, width = n * CAP, w_out.shape[0]
    fb = min(768, width)
    return pl.pallas_call(
        hidden_kernel,
        grid=(width // fb, images),
        in_specs=[
            pl.BlockSpec((n, None, CAP, D), lambda f, i: (0, i, 0, 0)),
            pl.BlockSpec((fb, D), lambda f, i: (f, 0)),
        ],
        out_specs=pl.BlockSpec((None, total, fb), lambda f, i: (i, 0, f)),
        out_shape=pltpu.HBM((images, total, width), bf16),
        compiler_params=pltpu.CompilerParams(
            dimension_semantics=("arbitrary", "arbitrary"), vmem_limit_bytes=36 << 20
        ),
        name="expert_hidden",
    )(*in_hbm(cot_in, w_out))


def parts_kernel(act0, act1, gate0, gate1, w_out, out, acc):
    f = pl.program_id(0)

    @pl.when(f == 0)
    def _():
        acc[...] = jnp.zeros_like(acc)

    for i, act in enumerate((act0, act1)):
        acc[i] += mm(act[...], w_out[...])

    @pl.when(f == pl.num_programs(0) - 1)
    def _():
        for i, gate in enumerate((gate0, gate1)):
            rows = (acc[i] * gate[:, :1]).astype(bf16)
            out[:, i, :, :] = rows.reshape(out.shape[0], CAP, D)


def expert_parts(acts, gates, w_out):
    total, width = acts[0].shape
    fb = min(768, width)
    n = total // CAP
    cols = pl.BlockSpec((total, fb), lambda f: (0, f))
    full = pl.BlockSpec((total, 128), lambda f: (0, 0))
    return pl.pallas_call(
        parts_kernel,
        grid=(width // fb,),
        in_specs=[cols, cols, full, full, pl.BlockSpec((fb, D), lambda f: (f, 0))],
        out_specs=pl.BlockSpec((n, 2, CAP, D), lambda f: (0, 0, 0, 0)),
        out_shape=pltpu.HBM((n, 2, CAP, D), bf16),
        scratch_shapes=[pltpu.VMEM((2, total, D), f32)],
        compiler_params=pltpu.CompilerParams(
            dimension_semantics=("arbitrary",), vmem_limit_bytes=48 << 20
        ),
        name="expert_parts",
    )(*in_hbm(*acts, *gates, w_out))


def moved_kernel(get, outs, flush):
    perm_a, perm_b = get(0)[...], get(1)[...]
    for k in range(3):
        for i in range(2):
            value = get(2 + 2 * k + i)[...]
            outs[k][i] = mm(value, perm_b).astype(bf16)
            if k == 0:
                outs[3][i] = mm(value, perm_a).astype(bf16)
        flush(k)
    flush(3)


def last_kernel(get, outs, flush):
    input_grad, gate1, sent_a, kept_a, sent_b, kept_b, ph1, rh1, lg1, sums1 = outs
    backward_kernel(
        get,
        (input_grad, gate1, ph1, rh1, lg1, sums1),
        lambda k: flush(k) if k < 2 else None,
    )
    base = 12
    half = D // 2

    def lay(value, sent, kept, start):
        kept[:, start : start + value.shape[1]] = value[:half]
        sent[:, start : start + value.shape[1]] = value[half:].astype(bf16)

    norm1a, norm1b, ph = get(base), get(base + 1), (get(base + 2), ph1)
    lay(sum(mm(norm1a[i], ph[i][:, :CUT], 0, 0) for i in range(2)), sent_a, kept_a, 0)
    flush(2)
    flush(3)
    lay(sum(mm(norm1b[i], ph[i][:, CUT:], 0, 0) for i in range(2)), sent_b, kept_b, 0)
    start = 3 * D - CUT
    perm = get(base + 3)[...]
    out = 0.0
    for i, rh in enumerate((get(base + 4), rh1)):
        out = out + mm(mm(rh[...], perm).astype(bf16), get(base + 5 + i)[...], 0, 0)
    lay(out, sent_b, kept_b, start)
    sums = get(base + 7)[...] + sums1[...]
    moved = sum(mm(p, perm) for p in pieces(sums, 3))
    zeros = jnp.zeros((56, D), f32)
    tail = jnp.concatenate([jnp.zeros((2 * E, D), f32), moved, zeros], axis=0).T
    for i, lg in enumerate((get(base + 10), lg1)):
        tail = tail + mm(get(base + 8)[i], lg[...], 0, 0)
    for i, gt in enumerate((get(base + 11), gate1)):
        for p in pieces(pltpu.roll(gt[...], E, 1), 2):
            tail = tail + mm(get(base + 9)[i], p, 0, 0)
    lay(tail, sent_b, kept_b, start + D)
    flush(4)
    flush(5)


def eye(size, width=None, shift=0):
    shape = (size, width or size)
    hit = lax.broadcasted_iota(i32, shape, 1) == lax.broadcasted_iota(i32, shape, 0) + shift
    return hit.astype(f32).astype(bf16)


def pack_kernel(w_qkv, w_out, router, bias, vectors, part_a, part_b):
    own = w_qkv.shape[0]
    part_a[0] = w_qkv[:, :CUT]
    part_b[0, :, QKV_B[0] : QKV_B[1]] = w_qkv[:, CUT:]
    part_b[0, :, OUT_T[0] : OUT_T[1]] = mm(eye(own), w_out[...], 1, 1).astype(bf16)
    tail = mm(router[...], eye(E, 128))
    tail = tail + mm(mm(eye(own), bias[...], 1, 1).astype(bf16), eye(E, 128, E))
    columns = mm(eye(own), vectors[...], 1, 1).astype(bf16)
    tail = tail + mm(columns, eye(VECTORS, 128, 2 * E))
    part_b[0, :, SMALL[0] :] = tail.astype(bf16)


def unpack_kernel(kept_a, got_a, kept_b, got_b, w_qkv, w_out, router, bias, vectors):
    own = w_qkv.shape[0]
    w_qkv[:, :CUT] = kept_a[...] + got_a[...].astype(f32)
    mine = kept_b[...] + got_b[...].astype(f32)
    w_qkv[:, CUT:] = mine[:, QKV_B[0] : QKV_B[1]]
    w_out[...] = sum(mm(p, eye(own), 0, 0) for p in pieces(mine[:, OUT_T[0] : OUT_T[1]], 3))
    tail = mine[:, SMALL[0] :]
    router[...] = tail[:, :E]
    bias[...] = sum(mm(eye(E, 128, E), p, 1, 1) for p in pieces(tail, 3))
    vectors[...] = sum(mm(eye(8, 128, 2 * E), p, 1, 1) for p in pieces(tail, 3))


def output_kernel(get, outs, flush):
    block_out, input_grad = outs
    small, parts = get(0), get(1)
    for i in range(2):
        placed, residual, gate, grad = (get(2 + 4 * i + k) for k in range(4))
        input_grad[i * SEQ : (i + 1) * SEQ, :] = grad[:SEQ, :]
        disp = dispatch_of(placed[...])
        out = residual[...]
        for o in range(parts.shape[1]):
            out = out + mm(disp, parts[:, o, i, :, :].reshape(SLOTS, D), 0, 0)
        for p in pieces(pltpu.roll(gate[...], E, 1), 2):
            out = out + mm(p, small[...], 1, 1)
        block_out[i * SEQ : (i + 1) * SEQ, :] = out[:SEQ]
    flush(0)
    flush(1)


def weights_kernel(act0, act1, back0, back1, g0, g1, x0, x1, out_w, in_w):
    out_w[...] = mm(act0[...], g0[...], 0, 0) + mm(act1[...], g1[...], 0, 0)
    in_w[...] = mm(back0[...], x0[...], 0, 0) + mm(back1[...], x1[...], 0, 0)


def expert_weights(acts, backs, gated, xs):
    total, width = acts[0].shape
    fb = min(512, width)
    cols = pl.BlockSpec((total, fb), lambda f: (0, f))
    full = pl.BlockSpec((total, D), lambda f: (0, 0))
    rows = pl.BlockSpec((fb, D), lambda f: (f, 0))
    return pl.pallas_call(
        weights_kernel,
        grid=(width // fb,),
        in_specs=[cols] * 4 + [full] * 4,
        out_specs=[rows, rows],
        out_shape=[pltpu.HBM((width, D), f32)] * 2,
        compiler_params=pltpu.CompilerParams(
            dimension_semantics=("arbitrary",), vmem_limit_bytes=40 << 20
        ),
        name="expert_weights",
    )(*in_hbm(*acts, *backs, *gated, *xs))


def on_device(
    block_in, out_cotangent, expert_routes, ln1_gain, ln1_shift, w_qkv, bias_query, bias_value,
    w_out, bias_out, ln2_gain, ln2_shift, w_router, expert_bias, w_expert_in, bias_hidden,
    w_expert_out,
):
    images = block_in.shape[0] // SEQ
    n = lax.axis_size(AXIS)
    owners = n // E
    own = ln1_gain.shape[0]
    expert = lax.axis_index(AXIS) // owners
    order_a, order_b = bit_orders()
    barrier = lax.optimization_barrier
    vectors = jnp.concatenate(
        [ln1_gain, ln1_shift, bias_query, bias_value, bias_out, ln2_gain, ln2_shift]
    )
    shards = pl.pallas_call(
        pack_kernel,
        out_shape=[
            jax.ShapeDtypeStruct((1, own, CUT), bf16),
            jax.ShapeDtypeStruct((1, own, PACK - CUT), bf16),
        ],
        compiler_params=pltpu.CompilerParams(vmem_limit_bytes=8 << 20),
        name="pack_params",
    )(w_qkv, w_out, w_router, expert_bias, vectors.reshape(VECTORS, own))

    pad_rows = ((0, ROWS - SEQ), (0, 0))
    xs, cots, placed, states, outgoing = [], [], [], [], []
    for i in range(images):
        xs.append(jnp.pad(block_in[i * SEQ : (i + 1) * SEQ], pad_rows))
        cots.append(jnp.pad(out_cotangent[i * SEQ : (i + 1) * SEQ], pad_rows))
        placed.append(place(expert_routes[i * SEQ : (i + 1) * SEQ]))
        slots = mm(dispatch_of(placed[i]), cots[i]).astype(bf16)
        outgoing.append(to_owners(slots, owners))
    (full_a, full_b), outgoing = gather_rows(shards, 2, jnp.stack(outgoing, axis=1))
    cot_in = exchange(outgoing)
    for i in range(images):
        states.append(attend_forward(xs[i], placed[i], full_a, full_b))
    hidden = expert_hidden(cot_in, w_expert_out)
    first = exchange(to_owners(states[0]["slots"], owners))
    slots, hidden = barrier((states[1]["slots"], hidden))
    second = exchange(to_owners(slots, owners))
    arrived = [first.reshape(-1, D), second.reshape(-1, D)]
    done = []
    grad_hidden = 0.0
    received = []
    for i in range(images):
        act, back, d_rows, gated, gate, gb = expert_main(
            i, arrived[i], cot_in, w_expert_in, hidden, bias_hidden, full_b, expert
        )
        done.append((act, back, gated, gate))
        grad_hidden = grad_hidden + gb[0]
        rows = exchange(d_rows.reshape(n, CAP, D + 128))
        received.append(rows.reshape(E, owners, CAP, D + 128))
    sent = expert_parts([d[0] for d in done], [d[3] for d in done], w_expert_out)
    parts = exchange(sent).reshape(E, owners, images, CAP, D)
    grad_expert_out, grad_expert_in = expert_weights(
        [d[0] for d in done], [d[1] for d in done], [d[2] for d in done], arrived
    )

    perm_b = permutation(order_b)
    both = lambda key: tuple(s[key] for s in states)
    norm1b, norm2b, cotb, norm1a = call(
        moved_kernel,
        (permutation(order_a), perm_b) + both("norm1") + both("norm2") + tuple(cots),
        [((2, ROWS, D), bf16)] * 4,
        24,
    )
    grad0, gate0, ph0, rh0, lg0, sums0 = token_backward(
        received[0], xs[0], cots[0], placed[0], states[0], full_a, full_b
    )
    grad1, gate1, sent_a, kept_a, sent_b, kept_b = call(
        last_kernel,
        backward_operands(
            received[1], xs[1], cots[1], placed[1], states[1], full_a, full_b
        )
        + (norm1a, norm1b, ph0, perm_b, rh0) + both("context")
        + (sums0, norm2b, cotb, lg0, gate0),
        [
            ((ROWS, D), f32), ((ROWS, 128), f32),
            ((D // 2, CUT), bf16), ((D // 2, CUT), f32),
            ((D // 2, PACK - CUT), bf16), ((D // 2, PACK - CUT), f32),
        ],
        44,
        BACKWARD_TEMPS,
    )
    ends = scatter_rows(sent_a, kept_a, order_a)
    ends += scatter_rows(sent_b, kept_b, order_b)
    block_out, input_grad = call(
        output_kernel,
        ((full_b, SMALL), parts, placed[0], states[0]["residual"], gate0, grad0)
        + (placed[1], states[1]["residual"], gate1, grad1),
        [((images * SEQ, D), f32)] * 2,
        24,
    )
    grad_qkv, grad_out, grad_router, grad_bias, vec = pl.pallas_call(
        unpack_kernel,
        out_shape=[
            jax.ShapeDtypeStruct(shape, f32)
            for shape in ((own, 3 * D), (D, own), (own, E), (E, own), (8, own))
        ],
        compiler_params=pltpu.CompilerParams(vmem_limit_bytes=8 << 20),
        name="unpack_grads",
    )(*ends)
    return (
        block_out, input_grad, vec[GAIN1], vec[SHIFT1], grad_qkv, vec[BQ], vec[BV],
        grad_out, vec[BO], vec[GAIN2], vec[SHIFT2], grad_router, grad_bias,
        grad_expert_in, grad_hidden, grad_expert_out,
    )


def solution(mesh):
    rows, line, cols = P(AXIS, None), P(AXIS), P(None, AXIS)
    in_specs = (
        rows, rows, rows, line, line, rows, line, line, cols, line, line, line, rows, cols,
        rows, line, rows,
    )
    out_specs = (
        rows, rows, line, line, rows, line, line, cols, line, line, line, rows, cols, rows,
        line, rows,
    )

    return jax.shard_map(
        on_device, mesh=mesh, in_specs=in_specs, out_specs=out_specs, check_vma=False
    )
```

```python
import math

import jax
import jax.numpy as jnp
from jax import lax
from jax.experimental import pallas as pl
from jax.experimental.pallas import tpu as pltpu
from jax.sharding import PartitionSpec as P

D = 768
HEADS = 12
HEAD_DIM = 64
PAIRS = HEADS // 2
E = 32
SEQ = 197
ROWS = 208
CAP = 16
SLOTS = E * CAP
AXIS = "fsdp"
PACK = 3200
CUT = 1664
GAIN1, SHIFT1, BQ, BV, BO, GAIN2, SHIFT2, VECTORS = range(8)
SCALE = 1.0 / math.sqrt(HEAD_DIM)

epsilon = 1e-06
f32 = jnp.float32
bf16 = jnp.bfloat16
i32 = jnp.int32


def mm(a, b, ca=1, cb=0):
    return lax.dot_general(a, b, (((ca,), (cb,)), ((), ())), preferred_element_type=f32)


def pieces(v, n):
    out = []
    for _ in range(n):
        p = v.astype(bf16)
        out.append(p)
        v = v - p.astype(f32)
    return out


def normalize(values):
    centered = values - jnp.mean(values, axis=-1, keepdims=True)
    inverse = lax.rsqrt(jnp.mean(centered * centered, axis=-1, keepdims=True) + epsilon)
    return (centered * inverse, inverse)


def norm_back(upstream, normed, inverse):
    return inverse * (
        upstream
        - jnp.mean(upstream, axis=-1, keepdims=True)
        - normed * jnp.mean(upstream * normed, axis=-1, keepdims=True)
    )


def swap(values, bit):
    n = lax.axis_size(AXIS)
    return lax.ppermute(values, AXIS, [(d, d ^ (1 << bit)) for d in range(n)])


def bit_of(bit):
    return (lax.axis_index(AXIS) >> bit) & 1


def bit_orders():
    bits = lax.axis_size(AXIS).bit_length() - 1
    inner = (bits - 1) // 3 if bits != 5 else 1
    x = list(range(1, 1 + inner))
    y = list(range(1 + inner, 1 + 2 * inner))
    z = list(range(1 + 2 * inner, bits))
    return [0] + x + y + z, [0] + y + x + z


def gather_rows(shards, early, wait_for):
    orders = bit_orders()
    held = [(shard, []) for shard in shards]
    for step in range(len(orders[0])):
        bits = [order[-1 - step] for order in orders]
        theirs = [swap(values, bit) for (values, _), bit in zip(held, bits)]
        moved = []
        for (values, done), other, bit in zip(held, theirs, bits):
            at = sum(1 for b in done if b > bit)
            lead = values.shape[0]
            high = 1 << at
            mine = values.reshape((high, lead // high) + values.shape[1:])
            other = other.reshape(mine.shape)
            which = lax.broadcasted_iota(i32, (1, 2, 1, 1, 1), 1) == bit_of(bit)
            both = jnp.where(which, mine[:, None], other[:, None])
            moved.append((both.reshape((2 * lead,) + values.shape[1:]), done + [bit]))
        held = moved
        if step + 1 < len(orders[0]):
            tied = [values for values, _ in held]
            if step + 1 == early:
                tied.append(wait_for)
            tied = lax.optimization_barrier(tied)
            held = [(t, done) for t, (_, done) in zip(tied, held)]
            if step + 1 == early:
                wait_for = tied[-1]
    return [values.reshape((-1, values.shape[-1])) for values, _ in held], wait_for


def owner_order(order):
    n = lax.axis_size(AXIS)
    own = D // n
    position = jnp.arange(D, dtype=i32)
    chunk = position // own
    owner = jnp.zeros_like(chunk)
    for step, bit in enumerate(order):
        owner = owner | (((chunk >> (len(order) - 1 - step)) & 1) << bit)
    return (owner ^ lax.axis_index(AXIS)) * own + position % own


def permutation(order):
    return (jnp.arange(D, dtype=i32)[:, None] == owner_order(order)[None]).astype(bf16)


def scatter_rows(parts):
    steps = len(parts[0][2])
    for step in range(steps):
        got = [swap(sent, order[step]) for sent, _, order in parts]
        if step + 1 == steps:
            return [x for (_, kept, _), g in zip(parts, got) for x in (kept, g)]
        ready = []
        for (_, kept, _), g in zip(parts, got):
            held = kept + g.astype(f32)
            half = held.shape[0] // 2
            ready += [held[half:].astype(bf16), held[:half]]
        ready = lax.optimization_barrier(ready)
        parts = [(ready[2 * k], ready[2 * k + 1], p[2]) for k, p in enumerate(parts)]


def exchange(blocks):
    return lax.all_to_all(blocks, AXIS, split_axis=0, concat_axis=0, tiled=True)


def to_owners(slot_rows, owners):
    rows = slot_rows.reshape((E, 1, CAP) + slot_rows.shape[1:])
    rows = jnp.broadcast_to(rows, (E, owners) + rows.shape[2:])
    return rows.reshape((E * owners, CAP) + slot_rows.shape[1:])


def place(routes):
    choice = jnp.pad(routes.T, ((0, 0), (0, ROWS - SEQ)), constant_values=-1)
    ids = jnp.arange(E, dtype=i32)[:, None]
    first = (choice[:1] == ids).astype(bf16)
    second = (choice[1:] == ids).astype(bf16)
    t = jnp.arange(ROWS, dtype=i32)
    earlier = (t[:, None] < t[None, :]).astype(bf16)
    before = mm(jnp.concatenate([first, second], axis=0), earlier)
    rank0 = jnp.sum(before[:E] * first, axis=0)
    seen = before[E:] + jnp.sum(first.astype(f32), axis=1, keepdims=True)
    rank1 = jnp.sum(seen * second, axis=0)
    return choice * CAP + jnp.stack([rank0, rank1]).astype(i32)


def gelu_terms(v):
    cumulative = 0.5 * (1.0 + lax.erf(v * (1.0 / math.sqrt(2.0))))
    density = jnp.exp(-0.5 * v * v) * (1.0 / math.sqrt(2.0 * math.pi))
    return v * cumulative, cumulative + v * density


def dispatch_of(placed):
    slot = lax.broadcasted_iota(i32, (SLOTS, ROWS), 0)
    hit = (slot == placed[0:1, :]) | (slot == placed[1:2, :])
    return hit.astype(f32).astype(bf16)


def half_of(pair, second):
    lane = lax.broadcasted_iota(i32, pair.shape, 1)
    keep = (lane >= HEAD_DIM) if second else (lane < HEAD_DIM)
    return jnp.where(keep, pair, jnp.zeros_like(pair))


def join(first, second):
    lane = lax.broadcasted_iota(i32, first.shape, 1)
    return jnp.where(lane < HEAD_DIM, first, second)


def forward_kernel(get, outs, flush):
    slots, residual, prob, acts, norm1_o, norm2_o, context_o, router_o = outs
    inputs = get(0)[...].astype(f32)
    hat1, _ = normalize(inputs)
    vec = vectors_of(get(4))
    row = lambda k: vec[k : k + 1, :]
    norm1 = (hat1 * row(GAIN1) + row(SHIFT1)).astype(bf16)
    norm1_o[...] = norm1
    flush(4)
    proj = jnp.concatenate([mm(norm1, get(1)[...]), mm(norm1, get(2)[...])], axis=1)
    acts[:, :D] = (proj[:, :D] + row(BQ)).astype(bf16)
    acts[:, D : 2 * D] = proj[:, D : 2 * D].astype(bf16)
    acts[:, 2 * D :] = (proj[:, 2 * D :] + row(BV)).astype(bf16)
    flush(3)
    token = lax.broadcasted_iota(i32, (ROWS, ROWS), 0) < SEQ
    for j in range(PAIRS):
        q = acts[:, j * 128 : (j + 1) * 128] * jnp.asarray(SCALE, bf16)
        k = acts[:, D + j * 128 : D + (j + 1) * 128]
        v = acts[:, 2 * D + j * 128 : 2 * D + (j + 1) * 128]
        both = []
        for h in range(2):
            raised = jnp.exp(mm(half_of(k, h), q, 1, 1))
            raised = jnp.where(token, raised, 0.0)
            p = (raised * (1.0 / jnp.sum(raised, axis=0, keepdims=True))).astype(bf16)
            prob[2 * j + h, :, :] = p
            both.append(mm(p, v, 0, 0))
        context_o[:, j * 128 : (j + 1) * 128] = join(both[0], both[1]).astype(bf16)
    flush(2)
    flush(6)
    res = inputs + mm(context_o[...], get(3)[...], 1, 1) + row(BO)
    residual[...] = res
    flush(1)
    hat2, _ = normalize(res)
    norm2 = (hat2 * row(GAIN2) + row(SHIFT2)).astype(bf16)
    norm2_o[...] = norm2
    flush(5)
    slots[...] = mm(dispatch_of(get(5)[...]), norm2).astype(bf16)
    flush(0)
    lane = lax.broadcasted_iota(i32, (ROWS, 128), 1)
    logits = jnp.where(lane < E, mm(norm2, get(4)[...]), 0.0)
    raised = jnp.where(lane < E, jnp.exp(logits), 0.0)
    router_o[...] = raised / jnp.sum(raised, axis=1, keepdims=True)
    flush(7)


class Staged:
    def __init__(self, far, near, sems, base):
        self.near = near
        self.copies = [
            pltpu.make_async_copy(f, v, sems.at[base + k])
            for k, (f, v) in enumerate(zip(far, near))
        ]
        self.waited = set()

    def start(self, k):
        self.copies[k].start()

    def get(self, k):
        if k not in self.waited:
            self.copies[k].wait()
            self.waited.add(k)
        return self.near[k]


def call(kernel, ins, outs, limit, temps=()):
    ins = [item if isinstance(item, tuple) else (item, None) for item in ins]
    n_in, n_out = len(ins), len(outs)
    shapes = []
    for array, cols in ins:
        shape = array.shape if cols is None else (array.shape[0], cols[1] - cols[0])
        shapes.append((shape, array.dtype))

    def body(*refs):
        far_in, far_out = refs[:n_in], refs[n_in : n_in + n_out]
        near = refs[n_in + n_out : -1]
        sems = refs[-1]
        far_in = [
            ref if cols is None else ref.at[:, cols[0] : cols[1]]
            for ref, (_, cols) in zip(far_in, ins)
        ]
        source = Staged(far_in, near[:n_in], sems, 0)
        for k in range(n_in):
            source.start(k)
        sink = Staged(near[n_in : n_in + n_out], far_out, sems, n_in)
        kernel(source.get, near[n_in:], sink.start)
        for k in range(n_in):
            source.get(k)
        for k in range(n_out):
            sink.get(k)

    return pl.pallas_call(
        body,
        in_specs=[pl.BlockSpec(memory_space=pltpu.HBM)] * n_in,
        out_specs=[pl.BlockSpec(memory_space=pltpu.HBM)] * n_out,
        out_shape=[pltpu.HBM(shape, dtype) for shape, dtype in outs],
        scratch_shapes=[pltpu.VMEM(shape, dtype) for shape, dtype in shapes]
        + [pltpu.VMEM(shape, dtype) for shape, dtype in list(outs) + list(temps)]
        + [pltpu.SemaphoreType.DMA((n_in + n_out,))],
        compiler_params=pltpu.CompilerParams(vmem_limit_bytes=limit << 20),
    )(*in_hbm(*[array for array, _ in ins]))


def in_hbm(*arrays):
    return [pltpu.with_memory_space_constraint(a, pltpu.HBM) for a in arrays]


def vectors_of(small):
    lane = lax.broadcasted_iota(i32, (8, 128), 1)
    pick = lane == lax.broadcasted_iota(i32, (8, 128), 0) + 2 * E
    return mm(pick.astype(f32).astype(bf16), small[...], 1, 1)


QKV_B = (0, 3 * D - CUT)
OUT_T = (3 * D - CUT, 4 * D - CUT)
SMALL = (4 * D - CUT, PACK - CUT)


def attend_forward(x, placed, full_a, full_b):
    names = ("slots", "residual", "prob", "acts", "norm1", "norm2", "context", "router")
    outs = call(
        forward_kernel,
        (x, full_a, (full_b, QKV_B), (full_b, OUT_T), (full_b, SMALL), placed),
        [
            ((SLOTS, D), bf16), ((ROWS, D), f32), ((HEADS, ROWS, ROWS), bf16),
            ((ROWS, 3 * D), bf16), ((ROWS, D), bf16), ((ROWS, D), bf16), ((ROWS, D), bf16),
            ((ROWS, 128), f32),
        ],
        16,
    )
    return dict(zip(names, outs))


def backward_kernel(get, outs, flush):
    input_grad, gate_o, ph, res_half_o, logit_o, sums = outs
    rec, placed, small, cot = get(0), get(1), get(2), get(3)
    vec = vectors_of(small)
    row = lambda k: vec[k : k + 1, :]
    disp = dispatch_of(placed[...])
    lane = lax.broadcasted_iota(i32, (SLOTS, 128), 1)
    slot_expert = lax.broadcasted_iota(i32, (SLOTS, 128), 0) // CAP
    moe = 0.0
    pg = 0.0
    for o in range(rec.shape[1]):
        rows = rec[:, o, :, :].reshape(SLOTS, D + 128)
        moe = moe + mm(disp, rows[:, :D], 0, 0)
        gg = jnp.where((lane & 63) == slot_expert, rows[:, D:], jnp.zeros((SLOTS, 128), bf16))
        pg = pg + mm(disp, gg, 0, 0)
    pg = pg + pltpu.roll(pg, 64, 1)
    hot = mm(disp, (lane == slot_expert).astype(f32).astype(bf16), 0, 0)
    pg = (pg + pltpu.roll(mm(cot[...], small[...]), 128 - E, 1)) * hot
    prob_r = get(4)[...]
    gate_o[...] = prob_r * hot
    flush(1)
    logit = prob_r * (pg - jnp.sum(pg * prob_r, axis=1, keepdims=True))
    real = lax.broadcasted_iota(i32, (ROWS, 1), 0) < SEQ
    logit = jnp.where(real, logit, 0.0).astype(bf16)
    logit_o[...] = logit
    flush(4)
    second = moe + mm(logit, small[...], 1, 1)
    hat2, rstd2 = normalize(get(5)[...])
    sums[GAIN2 : GAIN2 + 1, :] = jnp.sum(second * hat2, axis=0, keepdims=True)
    sums[SHIFT2 : SHIFT2 + 1, :] = jnp.sum(second, axis=0, keepdims=True)
    res_grad = cot[...].astype(f32) + norm_back(second * row(GAIN2), hat2, rstd2)
    input_grad[...] = res_grad
    sums[BO : BO + 1, :] = jnp.sum(res_grad, axis=0, keepdims=True)
    res_half = res_grad.astype(bf16)
    res_half_o[...] = res_half
    flush(3)
    cg = mm(res_half, get(6)[...]).astype(bf16)
    prob, acts = get(7), get(8)
    for j in range(PAIRS):
        q = acts[:, j * 128 : (j + 1) * 128]
        k = acts[:, D + j * 128 : D + (j + 1) * 128]
        v = acts[:, 2 * D + j * 128 : 2 * D + (j + 1) * 128]
        c = cg[:, j * 128 : (j + 1) * 128]
        qs, ks, vs = [], [], []
        for h in range(2):
            p = prob[2 * j + h, :, :]
            pf = p.astype(f32)
            t = pf * mm(half_of(v, h), c, 1, 1)
            sg = ((t - pf * jnp.sum(t, axis=0, keepdims=True)) * SCALE).astype(bf16)
            vs.append(mm(p, c))
            qs.append(mm(sg, k, 0, 0))
            ks.append(mm(sg, q))
        qg, kg, vg = join(*qs), join(*ks), join(*vs)
        cols = slice(j * 128, (j + 1) * 128)
        sums[BQ : BQ + 1, cols] = jnp.sum(qg, axis=0, keepdims=True)
        sums[BV : BV + 1, cols] = jnp.sum(vg, axis=0, keepdims=True)
        ph[:, j * 128 : (j + 1) * 128] = qg.astype(bf16)
        ph[:, D + j * 128 : D + (j + 1) * 128] = kg.astype(bf16)
        ph[:, 2 * D + j * 128 : 2 * D + (j + 1) * 128] = vg.astype(bf16)
    flush(2)
    first = mm(ph[:, :CUT], get(9)[...], 1, 1) + mm(ph[:, CUT:], get(10)[...], 1, 1)
    hat1, rstd1 = normalize(get(11)[...].astype(f32))
    sums[GAIN1 : GAIN1 + 1, :] = jnp.sum(first * hat1, axis=0, keepdims=True)
    sums[SHIFT1 : SHIFT1 + 1, :] = jnp.sum(first, axis=0, keepdims=True)
    sums[7:8, :] = jnp.zeros((1, D), f32)
    flush(5)
    input_grad[...] += norm_back(first * row(GAIN1), hat1, rstd1)
    flush(0)


BACKWARD_TEMPS = [
    ((ROWS, 3 * D), bf16), ((ROWS, D), bf16), ((ROWS, 128), bf16), ((8, D), f32),
]


def backward_operands(rec, x, cot, placed, s, full_a, full_b):
    return (
        rec, placed, (full_b, SMALL), cot, s["router"], s["residual"], (full_b, OUT_T),
        s["prob"], s["acts"], full_a, (full_b, QKV_B), x,
    )


def token_backward(*args):
    return call(
        backward_kernel,
        backward_operands(*args),
        [((ROWS, D), f32), ((ROWS, 128), f32)] + BACKWARD_TEMPS,
        24,
    )


def expert_kernel(
    idx, x, c, w_in, hidden, bias, router, act, back, d_rows, gated, gate, grad_bias, acc, gg
):
    r, f = pl.program_id(0), pl.program_id(1)
    rows, width = act.shape

    @pl.when(f == 0)
    def _():
        logits = mm(x[...], router[...])
        lane = lax.broadcasted_iota(i32, logits.shape, 1)
        raised = jnp.where(lane < E, jnp.exp(jnp.where(lane < E, logits, 0.0)), 0.0)
        picked = lane == idx[0]
        g = jnp.sum(jnp.where(picked, raised, 0.0), axis=1, keepdims=True)
        g = g / jnp.sum(raised, axis=1, keepdims=True)
        gate[...] = jnp.broadcast_to(g, gate.shape)
        rows_c = c[...].reshape(rows, D).astype(f32)
        gated[...] = (rows_c * g).astype(bf16)
        gg[...] = jnp.zeros_like(gg)
        acc[...] = jnp.zeros_like(acc)

    value, slope = gelu_terms(mm(x[...], w_in[...], 1, 1) + bias[...])
    hid = hidden[...].astype(f32)
    act[...] = value.astype(bf16)
    both = value * hid
    part = both[:, :128]
    for j in range(1, width // 128):
        part = part + both[:, j * 128 : (j + 1) * 128]
    gg[...] += part
    before = hid * slope * gate[:, :1]
    total = jnp.sum(before, axis=0, keepdims=True)
    half = before.astype(bf16)
    back[...] = half
    acc[...] += mm(half, w_in[...])
    cols = pl.ds(pl.multiple_of(f * width, width), width)

    @pl.when(r == 0)
    def _():
        grad_bias[:, cols] = total

    @pl.when(r > 0)
    def _():
        grad_bias[:, cols] += total

    @pl.when(f == pl.num_programs(1) - 1)
    def _():
        d_rows[:, :D] = acc[...].astype(bf16)
        g = jnp.sum(gg[...], axis=1, keepdims=True)
        high = g.astype(bf16)
        low = (g - high.astype(f32)).astype(bf16)
        lane = lax.broadcasted_iota(i32, (rows, 128), 1)
        d_rows[:, D:] = jnp.where(
            lane < 64, jnp.broadcast_to(high, lane.shape), jnp.broadcast_to(low, lane.shape)
        )


def expert_main(i, x, c, w_in, hidden, bias, router, expert):
    total, width = x.shape[0], w_in.shape[0]
    rb, fb = min(512, total), min(768, width)
    row = lambda r, f, *_: (r, 0)
    tile = lambda r, f, *_: (r, f)
    fixed = lambda r, f, *_: (0, 0)
    return pl.pallas_call(
        expert_kernel,
        grid_spec=pltpu.PrefetchScalarGridSpec(
            num_scalar_prefetch=1,
            grid=(total // rb, width // fb),
            in_specs=[
                pl.BlockSpec((rb, D), row),
                pl.BlockSpec((rb // CAP, None, CAP, D), lambda r, f, *_: (r, i, 0, 0)),
                pl.BlockSpec((fb, D), lambda r, f, *_: (f, 0)),
                pl.BlockSpec((None, rb, fb), lambda r, f, *_: (i, r, f)),
                pl.BlockSpec((1, fb), lambda r, f, *_: (0, f)),
                pl.BlockSpec((D, 128), lambda r, f, *_: (0, SMALL[0] // 128)),
            ],
            out_specs=[
                pl.BlockSpec((rb, fb), tile),
                pl.BlockSpec((rb, fb), tile),
                pl.BlockSpec((rb, D + 128), row),
                pl.BlockSpec((rb, D), row),
                pl.BlockSpec((rb, 128), row),
                pl.BlockSpec((1, width), fixed),
            ],
            scratch_shapes=[
                pltpu.VMEM((rb, D), f32),
                pltpu.VMEM((rb, 128), f32),
            ],
        ),
        out_shape=[
            pltpu.HBM((total, width), bf16),
            pltpu.HBM((total, width), bf16),
            pltpu.HBM((total, D + 128), bf16),
            pltpu.HBM((total, D), bf16),
            pltpu.HBM((total, 128), f32),
            pltpu.HBM((1, width), f32),
        ],
        compiler_params=pltpu.CompilerParams(
            dimension_semantics=("arbitrary", "arbitrary"), vmem_limit_bytes=24 << 20
        ),
        name="expert_main",
    )(expert.reshape(1), *in_hbm(x, c, w_in, hidden, bias.reshape(1, width), router))


def hidden_kernel(c, w_out, out):
    out[...] = mm(c[...].reshape(out.shape[0], D), w_out[...], 1, 1).astype(bf16)


def expert_hidden(cot_in, w_out):
    n, images = cot_in.shape[:2]
    total, width = n * CAP, w_out.shape[0]
    fb = min(768, width)
    return pl.pallas_call(
        hidden_kernel,
        grid=(width // fb, images),
        in_specs=[
            pl.BlockSpec((n, None, CAP, D), lambda f, i: (0, i, 0, 0)),
            pl.BlockSpec((fb, D), lambda f, i: (f, 0)),
        ],
        out_specs=pl.BlockSpec((None, total, fb), lambda f, i: (i, 0, f)),
        out_shape=pltpu.HBM((images, total, width), bf16),
        compiler_params=pltpu.CompilerParams(
            dimension_semantics=("arbitrary", "arbitrary"), vmem_limit_bytes=36 << 20
        ),
        name="expert_hidden",
    )(*in_hbm(cot_in, w_out))


def parts_kernel(act0, act1, gate0, gate1, w_out, out, acc):
    f = pl.program_id(0)

    @pl.when(f == 0)
    def _():
        acc[...] = jnp.zeros_like(acc)

    for i, act in enumerate((act0, act1)):
        acc[i] += mm(act[...], w_out[...])

    @pl.when(f == pl.num_programs(0) - 1)
    def _():
        for i, gate in enumerate((gate0, gate1)):
            rows = (acc[i] * gate[:, :1]).astype(bf16)
            out[:, i, :, :] = rows.reshape(out.shape[0], CAP, D)


def expert_parts(acts, gates, w_out):
    total, width = acts[0].shape
    fb = min(768, width)
    n = total // CAP
    cols = pl.BlockSpec((total, fb), lambda f: (0, f))
    full = pl.BlockSpec((total, 128), lambda f: (0, 0))
    return pl.pallas_call(
        parts_kernel,
        grid=(width // fb,),
        in_specs=[cols, cols, full, full, pl.BlockSpec((fb, D), lambda f: (f, 0))],
        out_specs=pl.BlockSpec((n, 2, CAP, D), lambda f: (0, 0, 0, 0)),
        out_shape=pltpu.HBM((n, 2, CAP, D), bf16),
        scratch_shapes=[pltpu.VMEM((2, total, D), f32)],
        compiler_params=pltpu.CompilerParams(
            dimension_semantics=("arbitrary",), vmem_limit_bytes=48 << 20
        ),
        name="expert_parts",
    )(*in_hbm(*acts, *gates, w_out))


def moved_kernel(get, outs, flush):
    perm_a, perm_b = get(0)[...], get(1)[...]
    for k in range(3):
        for i in range(2):
            value = get(2 + 2 * k + i)[...]
            outs[k][i] = mm(value, perm_b).astype(bf16)
            if k == 0:
                outs[3][i] = mm(value, perm_a).astype(bf16)
        flush(k)
    flush(3)


def last_kernel(get, outs, flush):
    input_grad, gate1, sent_a, kept_a, sent_b, kept_b, ph1, rh1, lg1, sums1 = outs
    backward_kernel(
        get,
        (input_grad, gate1, ph1, rh1, lg1, sums1),
        lambda k: flush(k) if k < 2 else None,
    )
    base = 12
    half = D // 2

    def lay(value, sent, kept, start):
        kept[:, start : start + value.shape[1]] = value[:half]
        sent[:, start : start + value.shape[1]] = value[half:].astype(bf16)

    norm1a, norm1b, ph = get(base), get(base + 1), (get(base + 2), ph1)
    lay(sum(mm(norm1a[i], ph[i][:, :CUT], 0, 0) for i in range(2)), sent_a, kept_a, 0)
    flush(2)
    flush(3)
    lay(sum(mm(norm1b[i], ph[i][:, CUT:], 0, 0) for i in range(2)), sent_b, kept_b, 0)
    start = 3 * D - CUT
    perm = get(base + 3)[...]
    out = 0.0
    for i, rh in enumerate((get(base + 4), rh1)):
        out = out + mm(mm(rh[...], perm).astype(bf16), get(base + 5 + i)[...], 0, 0)
    lay(out, sent_b, kept_b, start)
    sums = get(base + 7)[...] + sums1[...]
    moved = sum(mm(p, perm) for p in pieces(sums, 3))
    zeros = jnp.zeros((56, D), f32)
    tail = jnp.concatenate([jnp.zeros((2 * E, D), f32), moved, zeros], axis=0).T
    for i, lg in enumerate((get(base + 10), lg1)):
        tail = tail + mm(get(base + 8)[i], lg[...], 0, 0)
    for i, gt in enumerate((get(base + 11), gate1)):
        for p in pieces(pltpu.roll(gt[...], E, 1), 2):
            tail = tail + mm(get(base + 9)[i], p, 0, 0)
    lay(tail, sent_b, kept_b, start + D)
    flush(4)
    flush(5)


def eye(size, width=None, shift=0):
    shape = (size, width or size)
    hit = lax.broadcasted_iota(i32, shape, 1) == lax.broadcasted_iota(i32, shape, 0) + shift
    return hit.astype(f32).astype(bf16)


def pack_kernel(w_qkv, w_out, router, bias, vectors, part_a, part_b):
    own = w_qkv.shape[0]
    part_a[0] = w_qkv[:, :CUT]
    part_b[0, :, QKV_B[0] : QKV_B[1]] = w_qkv[:, CUT:]
    part_b[0, :, OUT_T[0] : OUT_T[1]] = w_out[...]
    tail = mm(router[...], eye(E, 128))
    tail = tail + mm(bias[...], eye(E, 128, E))
    columns = mm(eye(own), vectors[...], 1, 1).astype(bf16)
    tail = tail + mm(columns, eye(VECTORS, 128, 2 * E))
    part_b[0, :, SMALL[0] :] = tail.astype(bf16)


def unpack_kernel(kept_a, got_a, kept_b, got_b, w_qkv, w_out, router, bias, vectors):
    w_qkv[:, :CUT] = kept_a[...] + got_a[...].astype(f32)
    mine = kept_b[...] + got_b[...].astype(f32)
    w_qkv[:, CUT:] = mine[:, QKV_B[0] : QKV_B[1]]
    w_out[...] = mine[:, OUT_T[0] : OUT_T[1]]
    tail = mine[:, SMALL[0] :]
    router[...] = tail[:, :E]
    bias[...] = tail[:, E : 2 * E]
    vectors[...] = sum(mm(eye(8, 128, 2 * E), p, 1, 1) for p in pieces(tail, 3))


def output_kernel(get, outs, flush):
    block_out, input_grad = outs
    small, parts = get(0), get(1)
    for i in range(2):
        placed, residual, gate, grad = (get(2 + 4 * i + k) for k in range(4))
        input_grad[i * SEQ : (i + 1) * SEQ, :] = grad[:SEQ, :]
        disp = dispatch_of(placed[...])
        out = residual[...]
        for o in range(parts.shape[1]):
            out = out + mm(disp, parts[:, o, i, :, :].reshape(SLOTS, D), 0, 0)
        for p in pieces(pltpu.roll(gate[...], E, 1), 2):
            out = out + mm(p, small[...], 1, 1)
        block_out[i * SEQ : (i + 1) * SEQ, :] = out[:SEQ]
    flush(0)
    flush(1)


def weights_kernel(act0, act1, back0, back1, g0, g1, x0, x1, out_w, in_w):
    out_w[...] = mm(act0[...], g0[...], 0, 0) + mm(act1[...], g1[...], 0, 0)
    in_w[...] = mm(back0[...], x0[...], 0, 0) + mm(back1[...], x1[...], 0, 0)


def expert_weights(acts, backs, gated, xs):
    total, width = acts[0].shape
    fb = min(512, width)
    cols = pl.BlockSpec((total, fb), lambda f: (0, f))
    full = pl.BlockSpec((total, D), lambda f: (0, 0))
    rows = pl.BlockSpec((fb, D), lambda f: (f, 0))
    return pl.pallas_call(
        weights_kernel,
        grid=(width // fb,),
        in_specs=[cols] * 4 + [full] * 4,
        out_specs=[rows, rows],
        out_shape=[pltpu.HBM((width, D), f32)] * 2,
        compiler_params=pltpu.CompilerParams(
            dimension_semantics=("arbitrary",), vmem_limit_bytes=40 << 20
        ),
        name="expert_weights",
    )(*in_hbm(*acts, *backs, *gated, *xs))


def on_device(
    block_in, out_cotangent, expert_routes, ln1_gain, ln1_shift, w_qkv, bias_query, bias_value,
    w_out, bias_out, ln2_gain, ln2_shift, w_router, expert_bias, w_expert_in, bias_hidden,
    w_expert_out,
):
    images = block_in.shape[0] // SEQ
    n = lax.axis_size(AXIS)
    owners = n // E
    own = ln1_gain.shape[0]
    expert = lax.axis_index(AXIS) // owners
    order_a, order_b = bit_orders()
    barrier = lax.optimization_barrier
    vectors = jnp.concatenate(
        [ln1_gain, ln1_shift, bias_query, bias_value, bias_out, ln2_gain, ln2_shift]
    )
    shards = pl.pallas_call(
        pack_kernel,
        out_shape=[
            jax.ShapeDtypeStruct((1, own, CUT), bf16),
            jax.ShapeDtypeStruct((1, own, PACK - CUT), bf16),
        ],
        compiler_params=pltpu.CompilerParams(vmem_limit_bytes=8 << 20),
        name="pack_params",
    )(w_qkv, w_out.T, w_router, expert_bias.T, vectors.reshape(VECTORS, own))

    pad_rows = ((0, ROWS - SEQ), (0, 0))
    xs, cots, placed, states, outgoing = [], [], [], [], []
    for i in range(images):
        xs.append(jnp.pad(block_in[i * SEQ : (i + 1) * SEQ], pad_rows))
        cots.append(jnp.pad(out_cotangent[i * SEQ : (i + 1) * SEQ], pad_rows))
        placed.append(place(expert_routes[i * SEQ : (i + 1) * SEQ]))
        slots = mm(dispatch_of(placed[i]), cots[i]).astype(bf16)
        outgoing.append(to_owners(slots, owners))
    (full_a, full_b), outgoing = gather_rows(shards, 2, jnp.stack(outgoing, axis=1))
    cot_in = exchange(outgoing)
    for i in range(images):
        states.append(attend_forward(xs[i], placed[i], full_a, full_b))
    hidden = expert_hidden(cot_in, w_expert_out)
    first = exchange(to_owners(states[0]["slots"], owners))
    slots, hidden = barrier((states[1]["slots"], hidden))
    second = exchange(to_owners(slots, owners))
    arrived = [first.reshape(-1, D), second.reshape(-1, D)]
    done = []
    grad_hidden = 0.0
    received = []
    for i in range(images):
        act, back, d_rows, gated, gate, gb = expert_main(
            i, arrived[i], cot_in, w_expert_in, hidden, bias_hidden, full_b, expert
        )
        done.append((act, back, gated, gate))
        grad_hidden = grad_hidden + gb[0]
        rows = exchange(d_rows.reshape(n, CAP, D + 128))
        received.append(rows.reshape(E, owners, CAP, D + 128))
    sent = expert_parts([d[0] for d in done], [d[3] for d in done], w_expert_out)
    parts = exchange(sent).reshape(E, owners, images, CAP, D)
    grad_expert_out, grad_expert_in = expert_weights(
        [d[0] for d in done], [d[1] for d in done], [d[2] for d in done], arrived
    )

    perm_b = permutation(order_b)
    both = lambda key: tuple(s[key] for s in states)
    norm1b, norm2b, cotb, norm1a = call(
        moved_kernel,
        (permutation(order_a), perm_b) + both("norm1") + both("norm2") + tuple(cots),
        [((2, ROWS, D), bf16)] * 4,
        24,
    )
    grad0, gate0, ph0, rh0, lg0, sums0 = token_backward(
        received[0], xs[0], cots[0], placed[0], states[0], full_a, full_b
    )
    grad1, gate1, sent_a, kept_a, sent_b, kept_b = call(
        last_kernel,
        backward_operands(
            received[1], xs[1], cots[1], placed[1], states[1], full_a, full_b
        )
        + (norm1a, norm1b, ph0, perm_b, rh0) + both("context")
        + (sums0, norm2b, cotb, lg0, gate0),
        [
            ((ROWS, D), f32), ((ROWS, 128), f32),
            ((D // 2, CUT), bf16), ((D // 2, CUT), f32),
            ((D // 2, PACK - CUT), bf16), ((D // 2, PACK - CUT), f32),
        ],
        44,
        BACKWARD_TEMPS,
    )
    ends = scatter_rows([(sent_a, kept_a, order_a), (sent_b, kept_b, order_b)])
    block_out, input_grad = call(
        output_kernel,
        ((full_b, SMALL), parts, placed[0], states[0]["residual"], gate0, grad0)
        + (placed[1], states[1]["residual"], gate1, grad1),
        [((images * SEQ, D), f32)] * 2,
        24,
    )
    grad_qkv, grad_out, grad_router, grad_bias, vec = pl.pallas_call(
        unpack_kernel,
        out_shape=[
            jax.ShapeDtypeStruct(shape, f32)
            for shape in ((own, 3 * D), (own, D), (own, E), (own, E), (8, own))
        ],
        compiler_params=pltpu.CompilerParams(vmem_limit_bytes=8 << 20),
        name="unpack_grads",
    )(*ends)
    return (
        block_out, input_grad, vec[GAIN1], vec[SHIFT1], grad_qkv, vec[BQ], vec[BV],
        grad_out.T, vec[BO], vec[GAIN2], vec[SHIFT2], grad_router, grad_bias.T,
        grad_expert_in, grad_hidden, grad_expert_out,
    )


def solution(mesh):
    rows, line, cols = P(AXIS, None), P(AXIS), P(None, AXIS)
    in_specs = (
        rows, rows, rows, line, line, rows, line, line, cols, line, line, line, rows, cols,
        rows, line, rows,
    )
    out_specs = (
        rows, rows, line, line, rows, line, line, cols, line, line, line, rows, cols, rows,
        line, rows,
    )

    return jax.shard_map(
        on_device, mesh=mesh, in_specs=in_specs, out_specs=out_specs, check_vma=False
    )
```

```python
import math

import jax
import jax.numpy as jnp
from jax import lax
from jax.experimental import pallas as pl
from jax.experimental.pallas import tpu as pltpu
from jax.sharding import PartitionSpec as P

D = 768
HEADS = 12
HEAD_DIM = 64
PAIRS = HEADS // 2
E = 32
SEQ = 197
ROWS = 208
CAP = 16
SLOTS = E * CAP
AXIS = "fsdp"
PACK = 3200
CUT = 1664
GAIN1, SHIFT1, BQ, BV, BO, GAIN2, SHIFT2, VECTORS = range(8)
SCALE = 1.0 / math.sqrt(HEAD_DIM)
UNROLL = 2

epsilon = 1e-06
f32 = jnp.float32
bf16 = jnp.bfloat16
i32 = jnp.int32


def mm(a, b, ca=1, cb=0):
    return lax.dot_general(a, b, (((ca,), (cb,)), ((), ())), preferred_element_type=f32)


def pieces(v, n):
    out = []
    for _ in range(n):
        p = v.astype(bf16)
        out.append(p)
        v = v - p.astype(f32)
    return out


def normalize(values):
    centered = values - jnp.mean(values, axis=-1, keepdims=True)
    inverse = lax.rsqrt(jnp.mean(centered * centered, axis=-1, keepdims=True) + epsilon)
    return (centered * inverse, inverse)


def norm_back(upstream, normed, inverse):
    return inverse * (
        upstream
        - jnp.mean(upstream, axis=-1, keepdims=True)
        - normed * jnp.mean(upstream * normed, axis=-1, keepdims=True)
    )


def swap(values, bit):
    n = lax.axis_size(AXIS)
    return lax.ppermute(values, AXIS, [(d, d ^ (1 << bit)) for d in range(n)])


def bit_of(bit):
    return (lax.axis_index(AXIS) >> bit) & 1


def bit_orders():
    bits = lax.axis_size(AXIS).bit_length() - 1
    inner = (bits - 1) // 3 if bits != 5 else 1
    x = list(range(1, 1 + inner))
    y = list(range(1 + inner, 1 + 2 * inner))
    z = list(range(1 + 2 * inner, bits))
    return [0] + x + y + z, [0] + y + x + z


def merged(values, other, bit, done):
    at = sum(1 for b in done if b > bit)
    lead = values.shape[0]
    high = 1 << at
    mine = values.reshape((high, lead // high) + values.shape[1:])
    other = other.reshape(mine.shape)
    which = lax.broadcasted_iota(i32, (1, 2, 1, 1, 1), 1) == bit_of(bit)
    both = jnp.where(which, mine[:, None], other[:, None])
    return both.reshape((2 * lead,) + values.shape[1:])


def gather_rows(shards, early, wait_for):
    orders = bit_orders()
    held = [(shard, []) for shard in shards]
    steps = len(orders[0])
    for step in range(steps):
        bits = [order[-1 - step] for order in orders]
        theirs = [swap(values, bit) for (values, _), bit in zip(held, bits)]
        if step + 1 == steps:
            return [(values, other) for (values, _), other in zip(held, theirs)], wait_for
        tied = [
            merged(values, other, bit, done)
            for (values, done), other, bit in zip(held, theirs, bits)
        ]
        if step + 1 == early:
            tied.append(wait_for)
        tied = lax.optimization_barrier(tied)
        if step + 1 == early:
            wait_for = tied[-1]
        held = [(t, done + [bit]) for t, (_, done), bit in zip(tied, held, bits)]


def owner_order(order):
    n = lax.axis_size(AXIS)
    own = D // n
    position = jnp.arange(D, dtype=i32)
    chunk = position // own
    owner = jnp.zeros_like(chunk)
    for step, bit in enumerate(order):
        owner = owner | (((chunk >> (len(order) - 1 - step)) & 1) << bit)
    return (owner ^ lax.axis_index(AXIS)) * own + position % own


def pair_order():
    own = D // lax.axis_size(AXIS)
    position = jnp.arange(D, dtype=i32)
    inside = position % (D // 2)
    lowest = bit_of(0) ^ (position // (D // 2))
    return (2 * (inside // own) + lowest) * own + inside % own


def permutation(order):
    return (jnp.arange(D, dtype=i32)[:, None] == order[None]).astype(bf16)


def scatter_rows(parts):
    steps = len(parts[0][2])
    for step in range(steps):
        got = []
        for sent, _, order in parts:
            got.append(swap(sent, order[step]))
        if step + 1 == steps:
            return [x for (_, kept, _), g in zip(parts, got) for x in (kept, g)]
        ready = []
        for (_, kept, _), g in zip(parts, got):
            half = kept.shape[0] // 2
            for part in (slice(half, None), slice(0, half)):
                ready.append((kept[part].astype(f32) + g[part].astype(f32)).astype(bf16))
        ready = lax.optimization_barrier(ready)
        parts = [(ready[2 * k], ready[2 * k + 1], p[2]) for k, p in enumerate(parts)]


def exchange(blocks):
    return lax.all_to_all(blocks, AXIS, split_axis=0, concat_axis=0, tiled=True)


def to_owners(slot_rows, owners):
    rows = slot_rows.reshape((E, 1, CAP) + slot_rows.shape[1:])
    rows = jnp.broadcast_to(rows, (E, owners) + rows.shape[2:])
    return rows.reshape((E * owners, CAP) + slot_rows.shape[1:])


def place(routes):
    choice = jnp.pad(routes.T, ((0, 0), (0, ROWS - SEQ)), constant_values=-1)
    ids = jnp.arange(E, dtype=i32)[:, None]
    first = (choice[:1] == ids).astype(bf16)
    second = (choice[1:] == ids).astype(bf16)
    t = jnp.arange(ROWS, dtype=i32)
    earlier = (t[:, None] < t[None, :]).astype(bf16)
    before = mm(jnp.concatenate([first, second], axis=0), earlier)
    rank0 = jnp.sum(before[:E] * first, axis=0)
    seen = before[E:] + jnp.sum(first.astype(f32), axis=1, keepdims=True)
    rank1 = jnp.sum(seen * second, axis=0)
    return choice * CAP + jnp.stack([rank0, rank1]).astype(i32)


def gelu_terms(v):
    cumulative = 0.5 * (1.0 + lax.erf(v * (1.0 / math.sqrt(2.0))))
    density = jnp.exp(-0.5 * v * v) * (1.0 / math.sqrt(2.0 * math.pi))
    return v * cumulative, cumulative + v * density


def dispatch_of(placed):
    slot = lax.broadcasted_iota(i32, (SLOTS, ROWS), 0)
    hit = (slot == placed[0:1, :]) | (slot == placed[1:2, :])
    return hit.astype(f32).astype(bf16)


def half_of(pair, second):
    lane = lax.broadcasted_iota(i32, pair.shape, 1)
    keep = (lane >= HEAD_DIM) if second else (lane < HEAD_DIM)
    return jnp.where(keep, pair, jnp.zeros_like(pair))


def join(first, second):
    lane = lax.broadcasted_iota(i32, first.shape, 1)
    return jnp.where(lane < HEAD_DIM, first, second)


def forward_kernel(get, outs, flush):
    slots, residual, prob, acts, norm1_o, norm2_o, context_o, router_o, out_t, small = outs
    half = D // 2
    sel = get(2)
    rest = mm(sel[:, :half], get(0)[...]) + mm(sel[:, half:], get(1)[...])
    out_t[...] = rest[:, :D].astype(bf16)
    flush(8)
    small[...] = rest[:, D:].astype(bf16)
    flush(9)
    vec = vectors_of(small)
    row = lambda k: vec[k : k + 1, :]
    inputs = get(3)[...].astype(f32)
    hat1, _ = normalize(inputs)
    norm1 = (hat1 * row(GAIN1) + row(SHIFT1)).astype(bf16)
    norm1_o[...] = norm1
    flush(4)
    moved = mm(norm1, sel[...]).astype(bf16)
    left, right = moved[:, :half], moved[:, half:]
    proj_a = mm(left, get(4)[...]) + mm(right, get(5)[...])
    proj_b = mm(left, get(6)[...]) + mm(right, get(7)[...])
    proj = jnp.concatenate([proj_a, proj_b], axis=1)
    acts[:, :D] = (proj[:, :D] + row(BQ)).astype(bf16)
    acts[:, D : 2 * D] = proj[:, D : 2 * D].astype(bf16)
    acts[:, 2 * D :] = (proj[:, 2 * D :] + row(BV)).astype(bf16)
    flush(3)
    token = lax.broadcasted_iota(i32, (ROWS, ROWS), 0) < SEQ

    def pair(j, _):
        at = lambda part: pl.ds(pl.multiple_of(part * D + j * 128, 128), 128)
        q = acts[:, at(0)] * jnp.asarray(SCALE, bf16)
        k, v = acts[:, at(1)], acts[:, at(2)]
        both = []
        for h in range(2):
            raised = jnp.exp(mm(half_of(k, h), q, 1, 1))
            raised = jnp.where(token, raised, 0.0)
            p = (raised * (1.0 / jnp.sum(raised, axis=0, keepdims=True))).astype(bf16)
            prob[2 * j + h, :, :] = p
            both.append(mm(p, v, 0, 0))
        context_o[:, at(0)] = join(both[0], both[1]).astype(bf16)
        return 0

    lax.fori_loop(0, PAIRS, pair, 0, unroll=UNROLL)
    flush(2)
    flush(6)
    res = inputs + mm(context_o[...], out_t[...], 1, 1) + row(BO)
    residual[...] = res
    flush(1)
    hat2, _ = normalize(res)
    norm2 = (hat2 * row(GAIN2) + row(SHIFT2)).astype(bf16)
    norm2_o[...] = norm2
    flush(5)
    slots[...] = mm(dispatch_of(get(8)[...]), norm2).astype(bf16)
    flush(0)
    lane = lax.broadcasted_iota(i32, (ROWS, 128), 1)
    logits = jnp.where(lane < E, mm(norm2, small[...]), 0.0)
    raised = jnp.where(lane < E, jnp.exp(logits), 0.0)
    router_o[...] = raised / jnp.sum(raised, axis=1, keepdims=True)
    flush(7)


class Staged:
    def __init__(self, far, near, sems, base):
        self.near = near
        self.copies = [
            pltpu.make_async_copy(f, v, sems.at[base + k])
            for k, (f, v) in enumerate(zip(far, near))
        ]
        self.waited = set()

    def start(self, k):
        self.copies[k].start()

    def get(self, k):
        if k not in self.waited:
            self.copies[k].wait()
            self.waited.add(k)
        return self.near[k]


def call(kernel, ins, outs, limit, temps=()):
    ins = [item if isinstance(item, tuple) else (item, None) for item in ins]
    n_in, n_out = len(ins), len(outs)
    shapes = []
    for array, cols in ins:
        shape = array.shape if cols is None else (array.shape[0], cols[1] - cols[0])
        shapes.append((shape, array.dtype))

    def body(*refs):
        far_in, far_out = refs[:n_in], refs[n_in : n_in + n_out]
        near = refs[n_in + n_out : -1]
        sems = refs[-1]
        far_in = [
            ref if cols is None else ref.at[:, cols[0] : cols[1]]
            for ref, (_, cols) in zip(far_in, ins)
        ]
        source = Staged(far_in, near[:n_in], sems, 0)
        for k in range(n_in):
            source.start(k)
        sink = Staged(near[n_in : n_in + n_out], far_out, sems, n_in)
        kernel(source.get, near[n_in:], sink.start)
        for k in range(n_in):
            source.get(k)
        for k in range(n_out):
            sink.get(k)

    return pl.pallas_call(
        body,
        in_specs=[pl.BlockSpec(memory_space=pltpu.HBM)] * n_in,
        out_specs=[pl.BlockSpec(memory_space=pltpu.HBM)] * n_out,
        out_shape=[pltpu.HBM(shape, dtype) for shape, dtype in outs],
        scratch_shapes=[pltpu.VMEM(shape, dtype) for shape, dtype in shapes]
        + [pltpu.VMEM(shape, dtype) for shape, dtype in list(outs) + list(temps)]
        + [pltpu.SemaphoreType.DMA((n_in + n_out,))],
        compiler_params=pltpu.CompilerParams(vmem_limit_bytes=limit << 20),
    )(*in_hbm(*[array for array, _ in ins]))


def in_hbm(*arrays):
    return [pltpu.with_memory_space_constraint(a, pltpu.HBM) for a in arrays]


def vectors_of(small):
    lane = lax.broadcasted_iota(i32, (8, 128), 1)
    pick = lane == lax.broadcasted_iota(i32, (8, 128), 0) + 2 * E
    return mm(pick.astype(f32).astype(bf16), small[...], 1, 1)


QKV_B = (0, 3 * D - CUT)
OUT_T = (3 * D - CUT, 4 * D - CUT)
SMALL = (4 * D - CUT, PACK - CUT)


def attend_forward(x, placed, halves_a, halves_b, sel):
    names = ("slots", "residual", "prob", "acts", "norm1", "norm2", "context", "router")
    names += ("out_t", "small")
    outs = call(
        forward_kernel,
        tuple((b, (QKV_B[1], PACK - CUT)) for b in halves_b) + (sel, x) + halves_a
        + tuple((b, QKV_B) for b in halves_b) + (placed,),
        [
            ((SLOTS, D), bf16), ((ROWS, D), f32), ((HEADS, ROWS, ROWS), bf16),
            ((ROWS, 3 * D), bf16), ((ROWS, D), bf16), ((ROWS, D), bf16), ((ROWS, D), bf16),
            ((ROWS, 128), f32), ((D, D), bf16), ((D, 128), bf16),
        ],
        24,
    )
    return dict(zip(names, outs))


def backward_kernel(get, outs, flush):
    input_grad, gate_o, ph, res_half_o, logit_o, sums, cgs = outs
    rec, placed, small, cot = get(0), get(1), get(2), get(3)
    vec = vectors_of(small)
    row = lambda k: vec[k : k + 1, :]
    disp = dispatch_of(placed[...])
    lane = lax.broadcasted_iota(i32, (SLOTS, 128), 1)
    slot_expert = lax.broadcasted_iota(i32, (SLOTS, 128), 0) // CAP
    moe = 0.0
    pg = 0.0
    for o in range(rec.shape[1]):
        rows = rec[:, o, :, :].reshape(SLOTS, D + 128)
        moe = moe + mm(disp, rows[:, :D], 0, 0)
        gg = jnp.where((lane & 63) == slot_expert, rows[:, D:], jnp.zeros((SLOTS, 128), bf16))
        pg = pg + mm(disp, gg, 0, 0)
    pg = pg + pltpu.roll(pg, 64, 1)
    hot = mm(disp, (lane == slot_expert).astype(f32).astype(bf16), 0, 0)
    pg = (pg + pltpu.roll(mm(cot[...], small[...]), 128 - E, 1)) * hot
    prob_r = get(4)[...]
    gate_o[...] = prob_r * hot
    flush(1)
    logit = prob_r * (pg - jnp.sum(pg * prob_r, axis=1, keepdims=True))
    real = lax.broadcasted_iota(i32, (ROWS, 1), 0) < SEQ
    logit = jnp.where(real, logit, 0.0).astype(bf16)
    logit_o[...] = logit
    flush(4)
    second = moe + mm(logit, small[...], 1, 1)
    hat2, rstd2 = normalize(get(5)[...])
    sums[GAIN2 : GAIN2 + 1, :] = jnp.sum(second * hat2, axis=0, keepdims=True)
    sums[SHIFT2 : SHIFT2 + 1, :] = jnp.sum(second, axis=0, keepdims=True)
    res_grad = cot[...].astype(f32) + norm_back(second * row(GAIN2), hat2, rstd2)
    input_grad[...] = res_grad
    sums[BO : BO + 1, :] = jnp.sum(res_grad, axis=0, keepdims=True)
    res_half = res_grad.astype(bf16)
    res_half_o[...] = res_half
    flush(3)
    cgs[...] = mm(res_half, get(6)[...]).astype(bf16)
    prob, acts = get(7), get(8)

    def pair(j, _):
        at = lambda part: pl.ds(pl.multiple_of(part * D + j * 128, 128), 128)
        q, k, v = acts[:, at(0)], acts[:, at(1)], acts[:, at(2)]
        c = cgs[:, at(0)]
        qs, ks, vs = [], [], []
        for h in range(2):
            p = prob[2 * j + h, :, :]
            pf = p.astype(f32)
            t = pf * mm(half_of(v, h), c, 1, 1)
            sg = ((t - pf * jnp.sum(t, axis=0, keepdims=True)) * SCALE).astype(bf16)
            vs.append(mm(p, c))
            qs.append(mm(sg, k, 0, 0))
            ks.append(mm(sg, q))
        qg, kg, vg = join(*qs), join(*ks), join(*vs)
        sums[BQ : BQ + 1, at(0)] = jnp.sum(qg, axis=0, keepdims=True)
        sums[BV : BV + 1, at(0)] = jnp.sum(vg, axis=0, keepdims=True)
        ph[:, at(0)] = qg.astype(bf16)
        ph[:, at(1)] = kg.astype(bf16)
        ph[:, at(2)] = vg.astype(bf16)
        return 0

    lax.fori_loop(0, PAIRS, pair, 0, unroll=UNROLL)
    flush(2)
    first = mm(ph[:, :CUT], get(9)[...], 1, 1) + mm(ph[:, CUT:], get(10)[...], 1, 1)
    hat1, rstd1 = normalize(get(11)[...].astype(f32))
    sums[GAIN1 : GAIN1 + 1, :] = jnp.sum(first * hat1, axis=0, keepdims=True)
    sums[SHIFT1 : SHIFT1 + 1, :] = jnp.sum(first, axis=0, keepdims=True)
    sums[7:8, :] = jnp.zeros((1, D), f32)
    flush(5)
    input_grad[...] += norm_back(first * row(GAIN1), hat1, rstd1)
    flush(0)


BACKWARD_TEMPS = [
    ((ROWS, 3 * D), bf16), ((ROWS, D), bf16), ((ROWS, 128), bf16), ((8, D), f32),
]


def backward_operands(rec, x, cot, placed, s, qkv_a, qkv_b, out_t, small):
    return (
        rec, placed, small, cot, s["router"], s["residual"], out_t, s["prob"], s["acts"],
        qkv_a, qkv_b, x,
    )


def token_backward(*args):
    return call(
        backward_kernel,
        backward_operands(*args),
        [((ROWS, D), f32), ((ROWS, 128), f32)] + BACKWARD_TEMPS,
        24,
        [((ROWS, D), bf16)],
    )


def expert_kernel(
    idx, x, c, w_in, hidden, bias, router, act, back, d_rows, gated, gate, grad_bias, acc, gg
):
    r, f = pl.program_id(0), pl.program_id(1)
    rows, width = act.shape

    @pl.when(f == 0)
    def _():
        logits = mm(x[...], router[...])
        lane = lax.broadcasted_iota(i32, logits.shape, 1)
        raised = jnp.where(lane < E, jnp.exp(jnp.where(lane < E, logits, 0.0)), 0.0)
        picked = lane == idx[0]
        g = jnp.sum(jnp.where(picked, raised, 0.0), axis=1, keepdims=True)
        g = g / jnp.sum(raised, axis=1, keepdims=True)
        gate[...] = jnp.broadcast_to(g, gate.shape)
        rows_c = c[...].reshape(rows, D).astype(f32)
        gated[...] = (rows_c * g).astype(bf16)
        gg[...] = jnp.zeros_like(gg)
        acc[...] = jnp.zeros_like(acc)

    value, slope = gelu_terms(mm(x[...], w_in[...], 1, 1) + bias[...])
    hid = hidden[...].astype(f32)
    act[...] = value.astype(bf16)
    both = value * hid
    part = both[:, :128]
    for j in range(1, width // 128):
        part = part + both[:, j * 128 : (j + 1) * 128]
    gg[...] += part
    before = hid * slope * gate[:, :1]
    total = jnp.sum(before, axis=0, keepdims=True)
    half = before.astype(bf16)
    back[...] = half
    acc[...] += mm(half, w_in[...])
    cols = pl.ds(pl.multiple_of(f * width, width), width)

    @pl.when(r == 0)
    def _():
        grad_bias[:, cols] = total

    @pl.when(r > 0)
    def _():
        grad_bias[:, cols] += total

    @pl.when(f == pl.num_programs(1) - 1)
    def _():
        d_rows[:, :D] = acc[...].astype(bf16)
        g = jnp.sum(gg[...], axis=1, keepdims=True)
        high = g.astype(bf16)
        low = (g - high.astype(f32)).astype(bf16)
        lane = lax.broadcasted_iota(i32, (rows, 128), 1)
        d_rows[:, D:] = jnp.where(
            lane < 64, jnp.broadcast_to(high, lane.shape), jnp.broadcast_to(low, lane.shape)
        )


def expert_main(i, x, c, w_in, hidden, bias, router, expert):
    total, width = x.shape[0], w_in.shape[0]
    rb, fb = min(512, total), min(768, width)
    row = lambda r, f, *_: (r, 0)
    tile = lambda r, f, *_: (r, f)
    fixed = lambda r, f, *_: (0, 0)
    return pl.pallas_call(
        expert_kernel,
        grid_spec=pltpu.PrefetchScalarGridSpec(
            num_scalar_prefetch=1,
            grid=(total // rb, width // fb),
            in_specs=[
                pl.BlockSpec((rb, D), row),
                pl.BlockSpec((rb // CAP, None, CAP, D), lambda r, f, *_: (r, i, 0, 0)),
                pl.BlockSpec((fb, D), lambda r, f, *_: (f, 0)),
                pl.BlockSpec((None, rb, fb), lambda r, f, *_: (i, r, f)),
                pl.BlockSpec((1, fb), lambda r, f, *_: (0, f)),
                pl.BlockSpec((D, 128), fixed),
            ],
            out_specs=[
                pl.BlockSpec((rb, fb), tile),
                pl.BlockSpec((rb, fb), tile),
                pl.BlockSpec((rb, D + 128), row),
                pl.BlockSpec((rb, D), row),
                pl.BlockSpec((rb, 128), row),
                pl.BlockSpec((1, width), fixed),
            ],
            scratch_shapes=[
                pltpu.VMEM((rb, D), f32),
                pltpu.VMEM((rb, 128), f32),
            ],
        ),
        out_shape=[
            pltpu.HBM((total, width), bf16),
            pltpu.HBM((total, width), bf16),
            pltpu.HBM((total, D + 128), bf16),
            pltpu.HBM((total, D), bf16),
            pltpu.HBM((total, 128), f32),
            pltpu.HBM((1, width), f32),
        ],
        compiler_params=pltpu.CompilerParams(
            dimension_semantics=("arbitrary", "arbitrary"), vmem_limit_bytes=24 << 20
        ),
        name="expert_main",
    )(expert.reshape(1), *in_hbm(x, c, w_in, hidden, bias.reshape(1, width), router))


def hidden_kernel(c, w_out, out):
    out[...] = mm(c[...].reshape(out.shape[0], D), w_out[...], 1, 1).astype(bf16)


def expert_hidden(cot_in, w_out):
    n, images = cot_in.shape[:2]
    total, width = n * CAP, w_out.shape[0]
    fb = min(768, width)
    return pl.pallas_call(
        hidden_kernel,
        grid=(width // fb, images),
        in_specs=[
            pl.BlockSpec((n, None, CAP, D), lambda f, i: (0, i, 0, 0)),
            pl.BlockSpec((fb, D), lambda f, i: (f, 0)),
        ],
        out_specs=pl.BlockSpec((None, total, fb), lambda f, i: (i, 0, f)),
        out_shape=pltpu.HBM((images, total, width), bf16),
        compiler_params=pltpu.CompilerParams(
            dimension_semantics=("arbitrary", "arbitrary"), vmem_limit_bytes=36 << 20
        ),
        name="expert_hidden",
    )(*in_hbm(cot_in, w_out))


def parts_kernel(act0, act1, gate0, gate1, w_out, out, acc):
    f = pl.program_id(0)

    @pl.when(f == 0)
    def _():
        acc[...] = jnp.zeros_like(acc)

    for i, act in enumerate((act0, act1)):
        acc[i] += mm(act[...], w_out[...])

    @pl.when(f == pl.num_programs(0) - 1)
    def _():
        for i, gate in enumerate((gate0, gate1)):
            rows = (acc[i] * gate[:, :1]).astype(bf16)
            out[:, i, :, :] = rows.reshape(out.shape[0], CAP, D)


def expert_parts(acts, gates, w_out):
    total, width = acts[0].shape
    fb = min(768, width)
    n = total // CAP
    cols = pl.BlockSpec((total, fb), lambda f: (0, f))
    full = pl.BlockSpec((total, 128), lambda f: (0, 0))
    return pl.pallas_call(
        parts_kernel,
        grid=(width // fb,),
        in_specs=[cols, cols, full, full, pl.BlockSpec((fb, D), lambda f: (f, 0))],
        out_specs=pl.BlockSpec((n, 2, CAP, D), lambda f: (0, 0, 0, 0)),
        out_shape=pltpu.HBM((n, 2, CAP, D), bf16),
        scratch_shapes=[pltpu.VMEM((2, total, D), f32)],
        compiler_params=pltpu.CompilerParams(
            dimension_semantics=("arbitrary",), vmem_limit_bytes=48 << 20
        ),
        name="expert_parts",
    )(*in_hbm(*acts, *gates, w_out))


def moved_kernel(get, outs, flush):
    perm_a, perm_b = get(0)[...], get(1)[...]
    for k in range(3):
        for i in range(2):
            value = get(2 + 2 * k + i)[...]
            outs[k][i] = mm(perm_b, value, 0, 1).astype(bf16)
            if k == 0:
                outs[3][i] = mm(perm_a, value, 0, 1).astype(bf16)
        flush(k)
    flush(3)


def last_kernel(get, outs, flush):
    input_grad, gate1, sent_a, kept_a, sent_b, kept_b, ph1, rh1, lg1, sums1, cgs = outs
    backward_kernel(
        get,
        (input_grad, gate1, ph1, rh1, lg1, sums1, cgs),
        lambda k: flush(k) if k < 2 else None,
    )
    base = 12
    half = D // 2

    def lay(value, sent, kept, start):
        kept[:, start : start + value.shape[1]] = value[:half].astype(bf16)
        sent[:, start : start + value.shape[1]] = value[half:].astype(bf16)

    norm1a, norm1b, ph = get(base), get(base + 1), (get(base + 2), ph1)
    lay(sum(mm(norm1a[i], ph[i][:, :CUT]) for i in range(2)), sent_a, kept_a, 0)
    flush(2)
    flush(3)
    lay(sum(mm(norm1b[i], ph[i][:, CUT:]) for i in range(2)), sent_b, kept_b, 0)
    start = 3 * D - CUT
    perm = get(base + 3)[...]
    out = 0.0
    for i, rh in enumerate((get(base + 4), rh1)):
        out = out + mm(mm(perm, rh[...], 0, 1).astype(bf16), get(base + 5 + i)[...])
    lay(out, sent_b, kept_b, start)
    sums = get(base + 7)[...] + sums1[...]
    rows = lax.broadcasted_iota(i32, (128, 8), 0) == lax.broadcasted_iota(i32, (128, 8), 1) + 2 * E
    tail = 0.0
    for p in pieces(sums, 3):
        spread = mm(rows.astype(f32).astype(bf16), p).astype(bf16)
        tail = tail + mm(perm, spread, 0, 1)
    for i, lg in enumerate((get(base + 10), lg1)):
        tail = tail + mm(get(base + 8)[i], lg[...])
    for i, gt in enumerate((get(base + 11), gate1)):
        for p in pieces(pltpu.roll(gt[...], E, 1), 2):
            tail = tail + mm(get(base + 9)[i], p)
    lay(tail, sent_b, kept_b, start + D)
    flush(4)
    flush(5)


def eye(size, width=None, shift=0):
    shape = (size, width or size)
    hit = lax.broadcasted_iota(i32, shape, 1) == lax.broadcasted_iota(i32, shape, 0) + shift
    return hit.astype(f32).astype(bf16)


def pack_kernel(get, outs, flush):
    part_a, part_b = outs
    w_qkv, w_out, router, bias = (get(k) for k in range(4))
    own = w_qkv.shape[0]
    part_a[0] = w_qkv[:, :CUT]
    flush(0)
    part_b[0, :, QKV_B[0] : QKV_B[1]] = w_qkv[:, CUT:]
    part_b[0, :, OUT_T[0] : OUT_T[1]] = w_out[...]
    rows = [get(4 + k)[...].astype(f32).reshape(1, own) for k in range(VECTORS)]
    rows = jnp.concatenate(rows + [jnp.zeros((1, own), f32)], axis=0).astype(bf16)
    columns = mm(eye(own), rows, 1, 1).astype(bf16)
    tail = mm(router[...], eye(E, 128)) + mm(bias[...], eye(E, 128, E))
    tail = tail + mm(columns, eye(8, 128, 2 * E))
    part_b[0, :, SMALL[0] :] = tail.astype(bf16)
    flush(1)


def unpack_kernel(get, outs, flush):
    w_qkv, w_out, router, bias = outs[:4]
    add = lambda k: get(k)[...].astype(f32) + get(k + 1)[...].astype(f32)
    w_qkv[:, :CUT] = add(0)
    mine = add(2)
    w_qkv[:, CUT:] = mine[:, QKV_B[0] : QKV_B[1]]
    flush(0)
    w_out[...] = mine[:, OUT_T[0] : OUT_T[1]]
    flush(1)
    tail = mine[:, SMALL[0] :]
    router[...] = tail[:, :E]
    flush(2)
    bias[...] = tail[:, E : 2 * E]
    flush(3)
    rows = sum(mm(eye(8, 128, 2 * E), p, 1, 1) for p in pieces(tail, 3))
    for k in range(VECTORS):
        outs[4 + k][...] = rows[k]
        flush(4 + k)


def output_kernel(get, outs, flush):
    block_out, input_grad = outs
    small, parts = get(0), get(1)
    for i in range(2):
        placed, residual, gate, grad = (get(2 + 4 * i + k) for k in range(4))
        input_grad[i * SEQ : (i + 1) * SEQ, :] = grad[:SEQ, :]
        disp = dispatch_of(placed[...])
        out = residual[...]
        for o in range(parts.shape[1]):
            out = out + mm(disp, parts[:, o, i, :, :].reshape(SLOTS, D), 0, 0)
        for p in pieces(pltpu.roll(gate[...], E, 1), 2):
            out = out + mm(p, small[...], 1, 1)
        block_out[i * SEQ : (i + 1) * SEQ, :] = out[:SEQ]
    flush(0)
    flush(1)


def weights_kernel(left0, left1, right0, right1, out):
    out[...] = mm(left0[...], right0[...], 0, 0) + mm(left1[...], right1[...], 0, 0)


def expert_weights(left, right):
    total, width = left[0].shape
    fb = min(512, width)
    cols = pl.BlockSpec((total, fb), lambda f: (0, f))
    full = pl.BlockSpec((total, D), lambda f: (0, 0))
    return pl.pallas_call(
        weights_kernel,
        grid=(width // fb,),
        in_specs=[cols] * 2 + [full] * 2,
        out_specs=pl.BlockSpec((fb, D), lambda f: (f, 0)),
        out_shape=pltpu.HBM((width, D), f32),
        compiler_params=pltpu.CompilerParams(
            dimension_semantics=("arbitrary",), vmem_limit_bytes=32 << 20
        ),
    )(*in_hbm(*left, *right))


def on_device(
    block_in, out_cotangent, expert_routes, ln1_gain, ln1_shift, w_qkv, bias_query, bias_value,
    w_out, bias_out, ln2_gain, ln2_shift, w_router, expert_bias, w_expert_in, bias_hidden,
    w_expert_out,
):
    images = block_in.shape[0] // SEQ
    n = lax.axis_size(AXIS)
    owners = n // E
    own = ln1_gain.shape[0]
    expert = lax.axis_index(AXIS) // owners
    order_a, order_b = bit_orders()
    barrier = lax.optimization_barrier
    shards = call(
        pack_kernel,
        (w_qkv, w_out.T, w_router, expert_bias.T)
        + (ln1_gain, ln1_shift, bias_query, bias_value, bias_out, ln2_gain, ln2_shift),
        [((1, own, CUT), bf16), ((1, own, PACK - CUT), bf16)],
        8,
    )

    pad_rows = ((0, ROWS - SEQ), (0, 0))
    xs, cots, placed, states, outgoing = [], [], [], [], []
    for i in range(images):
        xs.append(jnp.pad(block_in[i * SEQ : (i + 1) * SEQ], pad_rows))
        cots.append(jnp.pad(out_cotangent[i * SEQ : (i + 1) * SEQ], pad_rows))
        placed.append(place(expert_routes[i * SEQ : (i + 1) * SEQ]))
        slots = mm(dispatch_of(placed[i]), cots[i]).astype(bf16)
        outgoing.append(to_owners(slots, owners))
    halves, outgoing = gather_rows(shards, 3, jnp.stack(outgoing, axis=1))
    flat = [tuple(h.reshape(D // 2, h.shape[-1]) for h in pair) for pair in halves]
    sel = permutation(pair_order())
    cot_in = exchange(outgoing)
    for i in range(images):
        states.append(attend_forward(xs[i], placed[i], flat[0], flat[1], sel))
    hidden = expert_hidden(cot_in, w_expert_out)
    first = exchange(to_owners(states[0]["slots"], owners))
    slots, hidden = barrier((states[1]["slots"], hidden))
    second = exchange(to_owners(slots, owners))
    arrived = [first.reshape(-1, D), second.reshape(-1, D)]
    small, out_t = states[0]["small"], states[0]["out_t"]
    rest = list(range(lax.axis_size(AXIS).bit_length() - 1))[1:]
    natural = [
        merged(mine, theirs, 0, rest)
        for mine, theirs in (halves[0], tuple(h[..., : QKV_B[1]] for h in halves[1]))
    ]
    qkv_a, qkv_b = [v.reshape(D, v.shape[-1]) for v in natural]
    done = []
    grad_hidden = 0.0
    received = []
    for i in range(images):
        act, back, d_rows, gated, gate, gb = expert_main(
            i, arrived[i], cot_in, w_expert_in, hidden, bias_hidden, small, expert
        )
        done.append((act, back, gated, gate))
        grad_hidden = grad_hidden + gb[0]
        if i == 0:
            d_rows, qkv_a, qkv_b = barrier((d_rows, qkv_a, qkv_b))
        rows = exchange(d_rows.reshape(n, CAP, D + 128))
        received.append(rows.reshape(E, owners, CAP, D + 128))
    sent = expert_parts([d[0] for d in done], [d[3] for d in done], w_expert_out)
    parts = exchange(sent).reshape(E, owners, images, CAP, D)
    column = lambda k: [d[k] for d in done]
    grad_expert_out = expert_weights(column(0), column(2))
    grad_expert_in = expert_weights(column(1), arrived)

    perm_b = permutation(owner_order(order_b))
    both = lambda key: tuple(s[key] for s in states)
    norm1b, norm2b, cotb, norm1a = call(
        moved_kernel,
        (permutation(owner_order(order_a)), perm_b) + both("norm1") + both("norm2") + tuple(cots),
        [((2, D, ROWS), bf16)] * 4,
        24,
    )
    grad0, gate0, ph0, rh0, lg0, sums0 = token_backward(
        received[0], xs[0], cots[0], placed[0], states[0], qkv_a, qkv_b, out_t, small
    )
    grad1, gate1, sent_a, kept_a, sent_b, kept_b = call(
        last_kernel,
        backward_operands(
            received[1], xs[1], cots[1], placed[1], states[1], qkv_a, qkv_b, out_t, small
        )
        + (norm1a, norm1b, ph0, perm_b, rh0) + both("context")
        + (sums0, norm2b, cotb, lg0, gate0),
        [
            ((ROWS, D), f32), ((ROWS, 128), f32),
            ((D // 2, CUT), bf16), ((D // 2, CUT), bf16),
            ((D // 2, PACK - CUT), bf16), ((D // 2, PACK - CUT), bf16),
        ],
        44,
        BACKWARD_TEMPS + [((ROWS, D), bf16)],
    )
    ends = scatter_rows([(sent_a, kept_a, order_a), (sent_b, kept_b, order_b)])
    block_out, input_grad = call(
        output_kernel,
        (small, parts, placed[0], states[0]["residual"], gate0, grad0)
        + (placed[1], states[1]["residual"], gate1, grad1),
        [((images * SEQ, D), f32)] * 2,
        24,
    )
    grad_qkv, grad_out, grad_router, grad_bias, *vec = call(
        unpack_kernel,
        tuple(ends),
        [(shape, f32) for shape in ((own, 3 * D), (own, D), (own, E), (own, E))]
        + [((own,), f32)] * VECTORS,
        8,
    )
    return (
        block_out, input_grad, vec[GAIN1], vec[SHIFT1], grad_qkv, vec[BQ], vec[BV],
        grad_out.T, vec[BO], vec[GAIN2], vec[SHIFT2], grad_router, grad_bias.T,
        grad_expert_in, grad_hidden, grad_expert_out,
    )


def solution(mesh):
    rows, line, cols = P(AXIS, None), P(AXIS), P(None, AXIS)
    in_specs = (
        rows, rows, rows, line, line, rows, line, line, cols, line, line, line, rows, cols,
        rows, line, rows,
    )
    out_specs = (
        rows, rows, line, line, rows, line, line, cols, line, line, line, rows, cols, rows,
        line, rows,
    )

    return jax.shard_map(
        on_device, mesh=mesh, in_specs=in_specs, out_specs=out_specs, check_vma=False
    )
```

```python
import math

import jax
import jax.numpy as jnp
from jax import lax
from jax.experimental import pallas as pl
from jax.experimental.pallas import tpu as pltpu
from jax.sharding import PartitionSpec as P

D = 768
HEADS = 12
HEAD_DIM = 64
PAIRS = HEADS // 2
E = 32
SEQ = 197
ROWS = 208
CAP = 16
SLOTS = E * CAP
AXIS = "fsdp"
PACK = 3200
CUT = 1664
GAIN1, SHIFT1, BQ, BV, BO, GAIN2, SHIFT2, VECTORS = range(8)
SCALE = 1.0 / math.sqrt(HEAD_DIM)
UNROLL = PAIRS

epsilon = 1e-06
f32 = jnp.float32
bf16 = jnp.bfloat16
i32 = jnp.int32


def mm(a, b, ca=1, cb=0):
    return lax.dot_general(a, b, (((ca,), (cb,)), ((), ())), preferred_element_type=f32)


def pieces(v, n):
    out = []
    for _ in range(n):
        p = v.astype(bf16)
        out.append(p)
        v = v - p.astype(f32)
    return out


def normalize(values):
    centered = values - jnp.mean(values, axis=-1, keepdims=True)
    inverse = lax.rsqrt(jnp.mean(centered * centered, axis=-1, keepdims=True) + epsilon)
    return (centered * inverse, inverse)


def norm_back(upstream, normed, inverse):
    return inverse * (
        upstream
        - jnp.mean(upstream, axis=-1, keepdims=True)
        - normed * jnp.mean(upstream * normed, axis=-1, keepdims=True)
    )


def swap(values, bit):
    n = lax.axis_size(AXIS)
    return lax.ppermute(values, AXIS, [(d, d ^ (1 << bit)) for d in range(n)])


def bit_of(bit):
    return (lax.axis_index(AXIS) >> bit) & 1


def bit_orders():
    bits = lax.axis_size(AXIS).bit_length() - 1
    inner = (bits - 1) // 3 if bits != 5 else 1
    x = list(range(1, 1 + inner))
    y = list(range(1 + inner, 1 + 2 * inner))
    z = list(range(1 + 2 * inner, bits))
    return [0] + x + y + z, [0] + y + x + z


def merged(values, other, bit, done):
    at = sum(1 for b in done if b > bit)
    lead = values.shape[0]
    high = 1 << at
    mine = values.reshape((high, lead // high) + values.shape[1:])
    other = other.reshape(mine.shape)
    which = lax.broadcasted_iota(i32, (1, 2, 1, 1, 1), 1) == bit_of(bit)
    both = jnp.where(which, mine[:, None], other[:, None])
    return both.reshape((2 * lead,) + values.shape[1:])


def gather_rows(shards, early, wait_for):
    orders = bit_orders()
    held = [(shard, []) for shard in shards]
    steps = len(orders[0])
    for step in range(steps):
        bits = [order[-1 - step] for order in orders]
        theirs = [swap(values, bit) for (values, _), bit in zip(held, bits)]
        if step + 1 == steps:
            return [(values, other) for (values, _), other in zip(held, theirs)], wait_for
        tied = [
            merged(values, other, bit, done)
            for (values, done), other, bit in zip(held, theirs, bits)
        ]
        if step + 1 == early:
            tied.append(wait_for)
        tied = lax.optimization_barrier(tied)
        if step + 1 == early:
            wait_for = tied[-1]
        held = [(t, done + [bit]) for t, (_, done), bit in zip(tied, held, bits)]


def owner_order(order):
    n = lax.axis_size(AXIS)
    own = D // n
    position = jnp.arange(D, dtype=i32)
    chunk = position // own
    owner = jnp.zeros_like(chunk)
    for step, bit in enumerate(order):
        owner = owner | (((chunk >> (len(order) - 1 - step)) & 1) << bit)
    return (owner ^ lax.axis_index(AXIS)) * own + position % own


def pair_order():
    own = D // lax.axis_size(AXIS)
    position = jnp.arange(D, dtype=i32)
    inside = position % (D // 2)
    lowest = bit_of(0) ^ (position // (D // 2))
    return (2 * (inside // own) + lowest) * own + inside % own


def permutation(order):
    return (jnp.arange(D, dtype=i32)[:, None] == order[None]).astype(bf16)


def scatter_rows(parts):
    steps = len(parts[0][2])
    for step in range(steps):
        got = []
        for sent, _, order in parts:
            got.append(swap(sent, order[step]))
        if step + 1 == steps:
            return [x for (_, kept, _), g in zip(parts, got) for x in (kept, g)]
        ready = []
        for (_, kept, _), g in zip(parts, got):
            half = kept.shape[0] // 2
            for part in (slice(half, None), slice(0, half)):
                ready.append((kept[part].astype(f32) + g[part].astype(f32)).astype(bf16))
        ready = lax.optimization_barrier(ready)
        parts = [(ready[2 * k], ready[2 * k + 1], p[2]) for k, p in enumerate(parts)]


def exchange(blocks):
    return lax.all_to_all(blocks, AXIS, split_axis=0, concat_axis=0, tiled=True)


def to_owners(slot_rows, owners):
    rows = slot_rows.reshape((E, 1, CAP) + slot_rows.shape[1:])
    rows = jnp.broadcast_to(rows, (E, owners) + rows.shape[2:])
    return rows.reshape((E * owners, CAP) + slot_rows.shape[1:])


def place(routes):
    choice = jnp.pad(routes.T, ((0, 0), (0, ROWS - SEQ)), constant_values=-1)
    ids = jnp.arange(E, dtype=i32)[:, None]
    first = (choice[:1] == ids).astype(bf16)
    second = (choice[1:] == ids).astype(bf16)
    t = jnp.arange(ROWS, dtype=i32)
    earlier = (t[:, None] < t[None, :]).astype(bf16)
    before = mm(jnp.concatenate([first, second], axis=0), earlier)
    rank0 = jnp.sum(before[:E] * first, axis=0)
    seen = before[E:] + jnp.sum(first.astype(f32), axis=1, keepdims=True)
    rank1 = jnp.sum(seen * second, axis=0)
    return choice * CAP + jnp.stack([rank0, rank1]).astype(i32)


def gelu_terms(v):
    cumulative = 0.5 * (1.0 + lax.erf(v * (1.0 / math.sqrt(2.0))))
    density = jnp.exp(-0.5 * v * v) * (1.0 / math.sqrt(2.0 * math.pi))
    return v * cumulative, cumulative + v * density


def dispatch_of(placed):
    slot = lax.broadcasted_iota(i32, (SLOTS, ROWS), 0)
    hit = (slot == placed[0:1, :]) | (slot == placed[1:2, :])
    return hit.astype(f32).astype(bf16)


def half_of(pair, second):
    lane = lax.broadcasted_iota(i32, pair.shape, 1)
    keep = (lane >= HEAD_DIM) if second else (lane < HEAD_DIM)
    return jnp.where(keep, pair, jnp.zeros_like(pair))


def join(first, second):
    lane = lax.broadcasted_iota(i32, first.shape, 1)
    return jnp.where(lane < HEAD_DIM, first, second)


def forward_kernel(get, outs, flush):
    slots, residual, prob, acts, norm1_o, norm2_o, context_o, router_o, out_t, small = outs
    half = D // 2
    sel = get(2)
    first, second = get(0), get(1)
    rest = mm(sel[:, :half], first[:, QKV_B[1] :]) + mm(sel[:, half:], second[:, QKV_B[1] :])
    out_t[...] = rest[:, :D].astype(bf16)
    flush(8)
    small[...] = rest[:, D:].astype(bf16)
    flush(9)
    vec = vectors_of(small)
    row = lambda k: vec[k : k + 1, :]
    inputs = get(3)[...].astype(f32)
    hat1, _ = normalize(inputs)
    norm1 = (hat1 * row(GAIN1) + row(SHIFT1)).astype(bf16)
    norm1_o[...] = norm1
    flush(4)
    moved = mm(norm1, sel[...]).astype(bf16)
    left, right = moved[:, :half], moved[:, half:]
    proj_a = mm(left, get(4)[...]) + mm(right, get(5)[...])
    proj_b = mm(left, first[:, : QKV_B[1]]) + mm(right, second[:, : QKV_B[1]])
    proj = jnp.concatenate([proj_a, proj_b], axis=1)
    acts[:, :D] = (proj[:, :D] + row(BQ)).astype(bf16)
    acts[:, D : 2 * D] = proj[:, D : 2 * D].astype(bf16)
    acts[:, 2 * D :] = (proj[:, 2 * D :] + row(BV)).astype(bf16)
    flush(3)
    token = lax.broadcasted_iota(i32, (ROWS, ROWS), 0) < SEQ

    def pair(j, _):
        at = lambda part: pl.ds(pl.multiple_of(part * D + j * 128, 128), 128)
        q = acts[:, at(0)] * jnp.asarray(SCALE, bf16)
        k, v = acts[:, at(1)], acts[:, at(2)]
        both = []
        for h in range(2):
            raised = jnp.exp(mm(half_of(k, h), q, 1, 1))
            raised = jnp.where(token, raised, 0.0)
            p = (raised * (1.0 / jnp.sum(raised, axis=0, keepdims=True))).astype(bf16)
            prob[2 * j + h, :, :] = p
            both.append(mm(p, v, 0, 0))
        context_o[:, at(0)] = join(both[0], both[1]).astype(bf16)
        return 0

    lax.fori_loop(0, PAIRS, pair, 0, unroll=UNROLL)
    flush(2)
    flush(6)
    res = inputs + mm(context_o[...], out_t[...], 1, 1) + row(BO)
    residual[...] = res
    flush(1)
    hat2, _ = normalize(res)
    norm2 = (hat2 * row(GAIN2) + row(SHIFT2)).astype(bf16)
    norm2_o[...] = norm2
    flush(5)
    slots[...] = mm(dispatch_of(get(6)[...]), norm2).astype(bf16)
    flush(0)
    lane = lax.broadcasted_iota(i32, (ROWS, 128), 1)
    logits = jnp.where(lane < E, mm(norm2, small[...]), 0.0)
    raised = jnp.where(lane < E, jnp.exp(logits), 0.0)
    router_o[...] = raised / jnp.sum(raised, axis=1, keepdims=True)
    flush(7)


class Near:
    def __init__(self, array):
        self.array = array


class Stack:
    def __init__(self, arrays, rows):
        self.arrays, self.rows = arrays, rows


class Columns:
    def __init__(self, array, start, stop):
        self.array, self.start, self.stop = array, start, stop


class Fetch:
    def __init__(self, copies, groups, refs):
        self.copies, self.groups, self.refs = copies, groups, refs
        self.begun = 0
        self.waited = set()
        self.begin(2)

    def begin(self, count):
        while self.begun < min(count, len(self.groups)):
            for k in self.groups[self.begun]:
                for copy in self.copies[k]:
                    copy.start()
            self.begun += 1

    def get(self, k):
        if k in self.copies and k not in self.waited:
            at = next(g for g, group in enumerate(self.groups) if k in group)
            self.begin(at + 1)
            for copy in self.copies[k]:
                copy.wait()
            self.waited.add(k)
            if all(m in self.waited for m in self.groups[at]):
                self.begin(at + 3)
        return self.refs[k]


def call(kernel, ins, outs, limit, temps=(), groups=None):
    arrays, specs, scratch, plan = [], [], [], []
    for item in ins:
        if isinstance(item, Near):
            plan.append(("near", len(arrays), None))
            arrays.append(item.array)
            specs.append(pl.BlockSpec(memory_space=pltpu.VMEM))
            continue
        if isinstance(item, Stack):
            group, shape = item.arrays, (item.rows, item.arrays[0].shape[1])
            cut = None
        elif isinstance(item, Columns):
            group, shape = [item.array], (item.array.shape[0], item.stop - item.start)
            cut = (item.start, item.stop)
        else:
            group, shape, cut = [item], item.shape, None
        plan.append(("far", list(range(len(arrays), len(arrays) + len(group))), cut))
        scratch.append(pltpu.VMEM(shape, group[0].dtype))
        for array in group:
            arrays += in_hbm(array)
            specs.append(pl.BlockSpec(memory_space=pltpu.HBM))
    n_in, n_out, n_far = len(arrays), len(outs), len(scratch)

    def body(*refs):
        far_in, far_out = refs[:n_in], refs[n_in : n_in + n_out]
        near = refs[n_in + n_out : -1]
        sems = refs[-1]
        copies, views, used, sem = {}, [], 0, 0
        for k, (kind, index, cut) in enumerate(plan):
            if kind == "near":
                views.append(far_in[index])
                continue
            target = near[used]
            used += 1
            views.append(target)
            copies[k], row = [], 0
            for at in index:
                source = far_in[at]
                if cut is not None:
                    source = source.at[:, cut[0] : cut[1]]
                if len(target.shape) > 1 and source.shape[0] != target.shape[0]:
                    place_at = target.at[row : row + source.shape[0], :]
                else:
                    place_at = target
                row += source.shape[0]
                copies[k].append(pltpu.make_async_copy(source, place_at, sems.at[sem]))
                sem += 1
        order = groups if groups is not None else [list(range(len(plan)))]
        order = [[k for k in group if k in copies] for group in order]
        source = Fetch(copies, order, views)
        results = near[n_far : n_far + n_out]
        sinks = [
            pltpu.make_async_copy(v, f, sems.at[sem + k])
            for k, (v, f) in enumerate(zip(results, far_out))
        ]
        kernel(source.get, near[n_far:], lambda k: sinks[k].start())
        for k in copies:
            source.get(k)
        for sink in sinks:
            sink.wait()

    n_sems = sum(len(index) for kind, index, _ in plan if kind == "far") + n_out
    return pl.pallas_call(
        body,
        in_specs=specs,
        out_specs=[pl.BlockSpec(memory_space=pltpu.HBM)] * n_out,
        out_shape=[pltpu.HBM(shape, dtype) for shape, dtype in outs],
        scratch_shapes=scratch
        + [pltpu.VMEM(shape, dtype) for shape, dtype in list(outs) + list(temps)]
        + [pltpu.SemaphoreType.DMA((n_sems,))],
        compiler_params=pltpu.CompilerParams(vmem_limit_bytes=limit << 20),
    )(*arrays)


def in_hbm(*arrays):
    return [pltpu.with_memory_space_constraint(a, pltpu.HBM) for a in arrays]


def vectors_of(small):
    lane = lax.broadcasted_iota(i32, (8, 128), 1)
    pick = lane == lax.broadcasted_iota(i32, (8, 128), 0) + 2 * E
    return mm(pick.astype(f32).astype(bf16), small[...], 1, 1)


QKV_B = (0, 3 * D - CUT)
OUT_T = (3 * D - CUT, 4 * D - CUT)
SMALL = (4 * D - CUT, PACK - CUT)


def attend_forward(x, placed, halves_a, halves_b, sel):
    names = ("slots", "residual", "prob", "acts", "norm1", "norm2", "context", "router")
    names += ("out_t", "small")
    outs = call(
        forward_kernel,
        tuple(Near(half) for half in halves_b) + (sel, x)
        + tuple(Near(half) for half in halves_a) + (placed,),
        [
            ((SLOTS, D), bf16), ((ROWS, D), f32), ((HEADS, ROWS, ROWS), bf16),
            ((ROWS, 3 * D), bf16), ((ROWS, D), bf16), ((ROWS, D), bf16), ((ROWS, D), bf16),
            ((ROWS, 128), f32), ((D, D), bf16), ((D, 128), bf16),
        ],
        24,
    )
    return dict(zip(names, outs))


def backward_kernel(get, outs, flush):
    input_grad, gate_o, ph, res_half_o, logit_o, sums, cgs = outs
    rec, placed, small, cot = get(0), get(1), get(2), get(3)
    vec = vectors_of(small)
    row = lambda k: vec[k : k + 1, :]
    disp = dispatch_of(placed[...])
    lane = lax.broadcasted_iota(i32, (SLOTS, 128), 1)
    slot_expert = lax.broadcasted_iota(i32, (SLOTS, 128), 0) // CAP
    moe = 0.0
    pg = 0.0
    for o in range(rec.shape[1]):
        rows = rec[:, o, :, :].reshape(SLOTS, D + 128)
        moe = moe + mm(disp, rows[:, :D], 0, 0)
        gg = jnp.where((lane & 63) == slot_expert, rows[:, D:], jnp.zeros((SLOTS, 128), bf16))
        pg = pg + mm(disp, gg, 0, 0)
    pg = pg + pltpu.roll(pg, 64, 1)
    hot = mm(disp, (lane == slot_expert).astype(f32).astype(bf16), 0, 0)
    pg = (pg + pltpu.roll(mm(cot[...], small[...]), 128 - E, 1)) * hot
    prob_r = get(4)[...]
    gate_o[...] = prob_r * hot
    flush(1)
    logit = prob_r * (pg - jnp.sum(pg * prob_r, axis=1, keepdims=True))
    real = lax.broadcasted_iota(i32, (ROWS, 1), 0) < SEQ
    logit = jnp.where(real, logit, 0.0).astype(bf16)
    logit_o[...] = logit
    flush(4)
    second = moe + mm(logit, small[...], 1, 1)
    hat2, rstd2 = normalize(get(5)[...])
    sums[GAIN2 : GAIN2 + 1, :] = jnp.sum(second * hat2, axis=0, keepdims=True)
    sums[SHIFT2 : SHIFT2 + 1, :] = jnp.sum(second, axis=0, keepdims=True)
    res_grad = cot[...].astype(f32) + norm_back(second * row(GAIN2), hat2, rstd2)
    input_grad[...] = res_grad
    sums[BO : BO + 1, :] = jnp.sum(res_grad, axis=0, keepdims=True)
    res_half = res_grad.astype(bf16)
    res_half_o[...] = res_half
    flush(3)
    cgs[...] = mm(res_half, get(6)[...]).astype(bf16)
    prob, acts = get(7), get(8)

    def pair(j, _):
        at = lambda part: pl.ds(pl.multiple_of(part * D + j * 128, 128), 128)
        q, k, v = acts[:, at(0)], acts[:, at(1)], acts[:, at(2)]
        c = cgs[:, at(0)]
        qs, ks, vs = [], [], []
        for h in range(2):
            p = prob[2 * j + h, :, :]
            pf = p.astype(f32)
            t = pf * mm(half_of(v, h), c, 1, 1)
            sg = ((t - pf * jnp.sum(t, axis=0, keepdims=True)) * SCALE).astype(bf16)
            vs.append(mm(p, c))
            qs.append(mm(sg, k, 0, 0))
            ks.append(mm(sg, q))
        qg, kg, vg = join(*qs), join(*ks), join(*vs)
        sums[BQ : BQ + 1, at(0)] = jnp.sum(qg, axis=0, keepdims=True)
        sums[BV : BV + 1, at(0)] = jnp.sum(vg, axis=0, keepdims=True)
        ph[:, at(0)] = qg.astype(bf16)
        ph[:, at(1)] = kg.astype(bf16)
        ph[:, at(2)] = vg.astype(bf16)
        return 0

    lax.fori_loop(0, PAIRS, pair, 0, unroll=UNROLL)
    flush(2)
    first = mm(ph[:, :CUT], get(9)[...], 1, 1) + mm(ph[:, CUT:], get(10)[...], 1, 1)
    hat1, rstd1 = normalize(get(11)[...].astype(f32))
    sums[GAIN1 : GAIN1 + 1, :] = jnp.sum(first * hat1, axis=0, keepdims=True)
    sums[SHIFT1 : SHIFT1 + 1, :] = jnp.sum(first, axis=0, keepdims=True)
    sums[7:8, :] = jnp.zeros((1, D), f32)
    flush(5)
    input_grad[...] += norm_back(first * row(GAIN1), hat1, rstd1)
    flush(0)


BACKWARD_TEMPS = [
    ((ROWS, 3 * D), bf16), ((ROWS, D), bf16), ((ROWS, 128), bf16), ((8, D), f32),
]


def backward_operands(rec, x, cot, placed, s, qkv_a, qkv_b, out_t, small):
    return (
        Near(rec), placed, small, cot, s["router"], s["residual"], out_t, s["prob"],
        s["acts"], qkv_a, qkv_b, x,
    )


BACKWARD_GROUPS = [[1, 2, 3, 4, 5], [6, 7, 8], [9, 10, 11]]


def token_backward(*args):
    return call(
        backward_kernel,
        backward_operands(*args),
        [((ROWS, D), f32), ((ROWS, 128), f32)] + BACKWARD_TEMPS,
        24,
        [((ROWS, D), bf16)],
        BACKWARD_GROUPS,
    )


def expert_kernel(
    idx, x, c, w_in, w_out, bias, router, act, back, d_rows, gated, gate, grad_bias, acc, gg
):
    r, f = pl.program_id(0), pl.program_id(1)
    rows, width = act.shape

    @pl.when(f == 0)
    def _():
        logits = mm(x[...], router[...])
        lane = lax.broadcasted_iota(i32, logits.shape, 1)
        raised = jnp.where(lane < E, jnp.exp(jnp.where(lane < E, logits, 0.0)), 0.0)
        picked = lane == idx[0]
        g = jnp.sum(jnp.where(picked, raised, 0.0), axis=1, keepdims=True)
        g = g / jnp.sum(raised, axis=1, keepdims=True)
        gate[...] = jnp.broadcast_to(g, gate.shape)
        rows_c = c[...].reshape(rows, D).astype(f32)
        gated[...] = (rows_c * g).astype(bf16)
        gg[...] = jnp.zeros_like(gg)
        acc[...] = jnp.zeros_like(acc)

    value, slope = gelu_terms(mm(x[...], w_in[...], 1, 1) + bias[...])
    hid = mm(c[...].reshape(rows, D), w_out[...], 1, 1)
    act[...] = value.astype(bf16)
    both = value * hid
    part = both[:, :128]
    for j in range(1, width // 128):
        part = part + both[:, j * 128 : (j + 1) * 128]
    gg[...] += part
    before = hid * slope * gate[:, :1]
    total = jnp.sum(before, axis=0, keepdims=True)
    half = before.astype(bf16)
    back[...] = half
    acc[...] += mm(half, w_in[...])
    cols = pl.ds(pl.multiple_of(f * width, width), width)

    @pl.when(r == 0)
    def _():
        grad_bias[:, cols] = total

    @pl.when(r > 0)
    def _():
        grad_bias[:, cols] += total

    @pl.when(f == pl.num_programs(1) - 1)
    def _():
        d_rows[:, :D] = acc[...].astype(bf16)
        g = jnp.sum(gg[...], axis=1, keepdims=True)
        high = g.astype(bf16)
        low = (g - high.astype(f32)).astype(bf16)
        lane = lax.broadcasted_iota(i32, (rows, 128), 1)
        d_rows[:, D:] = jnp.where(
            lane < 64, jnp.broadcast_to(high, lane.shape), jnp.broadcast_to(low, lane.shape)
        )


def expert_main(i, x, c, w_in, w_out, bias, router, expert):
    total, width = x.shape[0], w_in.shape[0]
    rb, fb = min(512, total), min(768, width)
    row = lambda r, f, *_: (r, 0)
    tile = lambda r, f, *_: (r, f)
    fixed = lambda r, f, *_: (0, 0)
    return pl.pallas_call(
        expert_kernel,
        grid_spec=pltpu.PrefetchScalarGridSpec(
            num_scalar_prefetch=1,
            grid=(total // rb, width // fb),
            in_specs=[
                pl.BlockSpec((rb, D), row),
                pl.BlockSpec((rb // CAP, None, CAP, D), lambda r, f, idx: (r, idx[1], 0, 0)),
                pl.BlockSpec((fb, D), lambda r, f, *_: (f, 0)),
                pl.BlockSpec((fb, D), lambda r, f, *_: (f, 0)),
                pl.BlockSpec((1, fb), lambda r, f, *_: (0, f)),
                pl.BlockSpec((D, 128), fixed),
            ],
            out_specs=[
                pl.BlockSpec((rb, fb), tile),
                pl.BlockSpec((rb, fb), tile),
                pl.BlockSpec((rb, D + 128), row),
                pl.BlockSpec((rb, D), row),
                pl.BlockSpec((rb, 128), row),
                pl.BlockSpec((1, width), fixed),
            ],
            scratch_shapes=[
                pltpu.VMEM((rb, D), f32),
                pltpu.VMEM((rb, 128), f32),
            ],
        ),
        out_shape=[
            pltpu.HBM((total, width), bf16),
            pltpu.HBM((total, width), bf16),
            pltpu.HBM((total, D + 128), bf16),
            pltpu.HBM((total, D), bf16),
            pltpu.HBM((total, 128), f32),
            pltpu.HBM((1, width), f32),
        ],
        compiler_params=pltpu.CompilerParams(
            dimension_semantics=("arbitrary", "arbitrary"), vmem_limit_bytes=24 << 20
        ),
        name="expert_main",
    )(jnp.stack([expert, jnp.int32(i)]), x, *in_hbm(c, w_in, w_out, bias.reshape(1, width), router))


def parts_kernel(act0, act1, gate0, gate1, w_out, out, acc):
    f = pl.program_id(0)

    @pl.when(f == 0)
    def _():
        acc[...] = jnp.zeros_like(acc)

    for i, act in enumerate((act0, act1)):
        acc[i] += mm(act[...], w_out[...])

    @pl.when(f == pl.num_programs(0) - 1)
    def _():
        for i, gate in enumerate((gate0, gate1)):
            rows = (acc[i] * gate[:, :1]).astype(bf16)
            out[:, i, :, :] = rows.reshape(out.shape[0], CAP, D)


def expert_parts(acts, gates, w_out):
    total, width = acts[0].shape
    fb = min(768, width)
    n = total // CAP
    cols = pl.BlockSpec((total, fb), lambda f: (0, f))
    full = pl.BlockSpec((total, 128), lambda f: (0, 0))
    return pl.pallas_call(
        parts_kernel,
        grid=(width // fb,),
        in_specs=[cols, cols, full, full, pl.BlockSpec((fb, D), lambda f: (f, 0))],
        out_specs=pl.BlockSpec((n, 2, CAP, D), lambda f: (0, 0, 0, 0)),
        out_shape=pltpu.HBM((n, 2, CAP, D), bf16),
        scratch_shapes=[pltpu.VMEM((2, total, D), f32)],
        compiler_params=pltpu.CompilerParams(
            dimension_semantics=("arbitrary",), vmem_limit_bytes=48 << 20
        ),
        name="expert_parts",
    )(*in_hbm(*acts, *gates, w_out))


def moved_kernel(get, outs, flush):
    for k, (value, perm) in enumerate(((0, 3), (0, 4), (1, 4), (2, 4))):
        outs[k][...] = mm(get(perm)[...], get(value)[...], 0, 1).astype(bf16)
        flush(k)


def last_kernel(get, outs, flush):
    input_grad, gate1, sent_a, kept_a, sent_b, kept_b, lg1, sums1, cgs = outs
    base = 12
    ph, rh = get(base + 2), get(base + 4)
    backward_kernel(
        get,
        (input_grad, gate1, ph.at[ROWS:, :], rh.at[ROWS:, :], lg1, sums1, cgs),
        lambda k: flush(k) if k < 2 else None,
    )
    half = D // 2

    def lay(value, sent, kept, start):
        kept[:, start : start + value.shape[1]] = value[:half].astype(bf16)
        sent[:, start : start + value.shape[1]] = value[half:].astype(bf16)

    lay(mm(get(base)[...], ph[:, :CUT]), sent_a, kept_a, 0)
    flush(2)
    flush(3)
    lay(mm(get(base + 1)[...], ph[:, CUT:]), sent_b, kept_b, 0)
    start = 3 * D - CUT
    perm = get(base + 3)[...]
    out = mm(mm(perm, rh[...], 0, 1).astype(bf16), get(base + 5)[...])
    lay(out, sent_b, kept_b, start)
    sums = get(base + 6)[...] + sums1[...]
    rows = lax.broadcasted_iota(i32, (128, 8), 0) == lax.broadcasted_iota(i32, (128, 8), 1) + 2 * E
    tail = 0.0
    for p in pieces(sums, 3):
        spread = mm(rows.astype(f32).astype(bf16), p).astype(bf16)
        tail = tail + mm(perm, spread, 0, 1)
    norm2 = get(base + 7)
    tail = tail + mm(norm2[...], jnp.concatenate([get(base + 9)[...], lg1[...]], axis=0))
    gates = jnp.concatenate([get(base + 10)[...], gate1[...]], axis=0)
    for p in pieces(pltpu.roll(gates, E, 1), 2):
        tail = tail + mm(get(base + 8)[...], p)
    lay(tail, sent_b, kept_b, start + D)
    flush(4)
    flush(5)


def eye(size, width=None, shift=0):
    shape = (size, width or size)
    hit = lax.broadcasted_iota(i32, shape, 1) == lax.broadcasted_iota(i32, shape, 0) + shift
    return hit.astype(f32).astype(bf16)


def pack_kernel(get, outs, flush):
    part_a, part_b = outs
    w_qkv, w_out, router, bias = (get(k) for k in range(4))
    own = w_qkv.shape[0]
    part_a[0] = w_qkv[:, :CUT]
    flush(0)
    part_b[0, :, QKV_B[0] : QKV_B[1]] = w_qkv[:, CUT:]
    part_b[0, :, OUT_T[0] : OUT_T[1]] = w_out[...]
    rows = [get(4 + k)[...].astype(f32).reshape(1, own) for k in range(VECTORS)]
    rows = jnp.concatenate(rows + [jnp.zeros((1, own), f32)], axis=0).astype(bf16)
    columns = mm(eye(own), rows, 1, 1).astype(bf16)
    tail = mm(router[...], eye(E, 128)) + mm(bias[...], eye(E, 128, E))
    tail = tail + mm(columns, eye(8, 128, 2 * E))
    part_b[0, :, SMALL[0] :] = tail.astype(bf16)
    flush(1)


def unpack_kernel(get, outs, flush):
    w_qkv, w_out, router, bias = outs[:4]
    add = lambda k: get(k)[...].astype(f32) + get(k + 1)[...].astype(f32)
    w_qkv[:, :CUT] = add(0)
    mine = add(2)
    w_qkv[:, CUT:] = mine[:, QKV_B[0] : QKV_B[1]]
    flush(0)
    w_out[...] = mine[:, OUT_T[0] : OUT_T[1]]
    flush(1)
    tail = mine[:, SMALL[0] :]
    router[...] = tail[:, :E]
    flush(2)
    bias[...] = tail[:, E : 2 * E]
    flush(3)
    rows = sum(mm(eye(8, 128, 2 * E), p, 1, 1) for p in pieces(tail, 3))
    for k in range(VECTORS):
        outs[4 + k][...] = rows[k]
        flush(4 + k)


def output_kernel(get, outs, flush):
    block_out, input_grad = outs
    small, parts = get(0), get(1)
    for i in range(2):
        placed, residual, gate, grad = (get(2 + 4 * i + k) for k in range(4))
        input_grad[i * SEQ : (i + 1) * SEQ, :] = grad[:SEQ, :]
        disp = dispatch_of(placed[...])
        out = residual[...]
        for o in range(parts.shape[1]):
            out = out + mm(disp, parts[:, o, i, :, :].reshape(SLOTS, D), 0, 0)
        for p in pieces(pltpu.roll(gate[...], E, 1), 2):
            out = out + mm(p, small[...], 1, 1)
        block_out[i * SEQ : (i + 1) * SEQ, :] = out[:SEQ]
    flush(0)
    flush(1)


def weights_kernel(act0, act1, back0, back1, g0, g1, x0, x1, out_w, in_w):
    out_w[...] = mm(act0[...], g0[...], 0, 0) + mm(act1[...], g1[...], 0, 0)
    in_w[...] = mm(back0[...], x0[...], 0, 0) + mm(back1[...], x1[...], 0, 0)


def expert_weights(acts, backs, gated, xs):
    total, width = acts[0].shape
    fb = min(512, width)
    cols = pl.BlockSpec((total, fb), lambda f: (0, f))
    full = pl.BlockSpec((total, D), lambda f: (0, 0))
    rows = pl.BlockSpec((fb, D), lambda f: (f, 0))
    return pl.pallas_call(
        weights_kernel,
        grid=(width // fb,),
        in_specs=[cols] * 4 + [full] * 4,
        out_specs=[rows, rows],
        out_shape=[pltpu.HBM((width, D), f32)] * 2,
        compiler_params=pltpu.CompilerParams(
            dimension_semantics=("arbitrary",), vmem_limit_bytes=40 << 20
        ),
        name="expert_weights",
    )(*in_hbm(*acts, *backs, *gated, *xs))


def on_device(
    block_in, out_cotangent, expert_routes, ln1_gain, ln1_shift, w_qkv, bias_query, bias_value,
    w_out, bias_out, ln2_gain, ln2_shift, w_router, expert_bias, w_expert_in, bias_hidden,
    w_expert_out,
):
    images = block_in.shape[0] // SEQ
    n = lax.axis_size(AXIS)
    owners = n // E
    own = ln1_gain.shape[0]
    expert = lax.axis_index(AXIS) // owners
    order_a, order_b = bit_orders()
    barrier = lax.optimization_barrier
    shards = call(
        pack_kernel,
        (w_qkv, w_out.T, w_router, expert_bias.T)
        + (ln1_gain, ln1_shift, bias_query, bias_value, bias_out, ln2_gain, ln2_shift),
        [((1, own, CUT), bf16), ((1, own, PACK - CUT), bf16)],
        8,
    )

    pad_rows = ((0, ROWS - SEQ), (0, 0))
    xs, cots, placed, states, outgoing = [], [], [], [], []
    for i in range(images):
        xs.append(jnp.pad(block_in[i * SEQ : (i + 1) * SEQ], pad_rows))
        cots.append(jnp.pad(out_cotangent[i * SEQ : (i + 1) * SEQ], pad_rows))
        placed.append(place(expert_routes[i * SEQ : (i + 1) * SEQ]))
        slots = mm(dispatch_of(placed[i]), cots[i]).astype(bf16)
        outgoing.append(to_owners(slots, owners))
    halves, outgoing = gather_rows(shards, 3, jnp.stack(outgoing, axis=1))
    flat = [tuple(h.reshape(D // 2, h.shape[-1]) for h in pair) for pair in halves]
    sel = permutation(pair_order())
    cot_in = exchange(outgoing)
    for i in range(images):
        states.append(attend_forward(xs[i], placed[i], flat[0], flat[1], sel))
    perm_b = permutation(owner_order(order_b))
    both = lambda key: [s[key] for s in states]
    norm1a, norm1b, norm2b, cotb = call(
        moved_kernel,
        (Stack(both("norm1"), 2 * ROWS), Stack(both("norm2"), 2 * ROWS))
        + (Stack(cots, 2 * ROWS), permutation(owner_order(order_a)), perm_b),
        [((D, 2 * ROWS), bf16)] * 4,
        24,
    )
    first = exchange(to_owners(states[0]["slots"], owners))
    second = exchange(to_owners(states[1]["slots"], owners))
    arrived = [first.reshape(-1, D), second.reshape(-1, D)]
    small, out_t = states[0]["small"], states[0]["out_t"]
    rest = list(range(lax.axis_size(AXIS).bit_length() - 1))[1:]
    natural = [
        merged(mine, theirs, 0, rest)
        for mine, theirs in (halves[0], tuple(h[..., : QKV_B[1]] for h in halves[1]))
    ]
    qkv_a, qkv_b = [v.reshape(D, v.shape[-1]) for v in natural]
    done = []
    grad_hidden = 0.0
    received = []
    for i in range(images):
        act, back, d_rows, gated, gate, gb = expert_main(
            i, arrived[i], cot_in, w_expert_in, w_expert_out, bias_hidden, small, expert
        )
        done.append((act, back, gated, gate))
        grad_hidden = grad_hidden + gb[0]
        if i == 0:
            d_rows, qkv_a, qkv_b = barrier((d_rows, qkv_a, qkv_b))
        rows = exchange(d_rows.reshape(n, CAP, D + 128))
        received.append(rows.reshape(E, owners, CAP, D + 128))
    sent = expert_parts([d[0] for d in done], [d[3] for d in done], w_expert_out)
    parts = exchange(sent).reshape(E, owners, images, CAP, D)
    column = lambda k: [d[k] for d in done]
    grad_expert_out, grad_expert_in = expert_weights(
        column(0), column(1), column(2), arrived
    )
    grad0, gate0, ph0, rh0, lg0, sums0 = token_backward(
        received[0], xs[0], cots[0], placed[0], states[0], qkv_a, qkv_b, out_t, small
    )
    grad1, gate1, sent_a, kept_a, sent_b, kept_b = call(
        last_kernel,
        backward_operands(
            received[1], xs[1], cots[1], placed[1], states[1], qkv_a, qkv_b, out_t, small
        )
        + (norm1a, norm1b, Stack([ph0], 2 * ROWS), perm_b, Stack([rh0], 2 * ROWS))
        + (Stack(both("context"), 2 * ROWS), sums0, norm2b, cotb, lg0, gate0),
        [
            ((ROWS, D), f32), ((ROWS, 128), f32),
            ((D // 2, CUT), bf16), ((D // 2, CUT), bf16),
            ((D // 2, PACK - CUT), bf16), ((D // 2, PACK - CUT), bf16),
        ],
        44,
        BACKWARD_TEMPS[2:] + [((ROWS, D), bf16)],
        BACKWARD_GROUPS + [[12, 13, 14, 15, 16], [17, 18, 19, 20, 21, 22]],
    )
    ends = scatter_rows([(sent_a, kept_a, order_a), (sent_b, kept_b, order_b)])
    block_out, input_grad = call(
        output_kernel,
        (small, parts, placed[0], states[0]["residual"], gate0, grad0)
        + (placed[1], states[1]["residual"], gate1, grad1),
        [((images * SEQ, D), f32)] * 2,
        24,
    )
    grad_qkv, grad_out, grad_router, grad_bias, *vec = call(
        unpack_kernel,
        tuple(ends),
        [(shape, f32) for shape in ((own, 3 * D), (own, D), (own, E), (own, E))]
        + [((own,), f32)] * VECTORS,
        8,
    )
    return (
        block_out, input_grad, vec[GAIN1], vec[SHIFT1], grad_qkv, vec[BQ], vec[BV],
        grad_out.T, vec[BO], vec[GAIN2], vec[SHIFT2], grad_router, grad_bias.T,
        grad_expert_in, grad_hidden, grad_expert_out,
    )


def solution(mesh):
    rows, line, cols = P(AXIS, None), P(AXIS), P(None, AXIS)
    in_specs = (
        rows, rows, rows, line, line, rows, line, line, cols, line, line, line, rows, cols,
        rows, line, rows,
    )
    out_specs = (
        rows, rows, line, line, rows, line, line, cols, line, line, line, rows, cols, rows,
        line, rows,
    )

    return jax.shard_map(
        on_device, mesh=mesh, in_specs=in_specs, out_specs=out_specs, check_vma=False
    )
```

```python
import math

import jax
import jax.numpy as jnp
from jax import lax
from jax.experimental import pallas as pl
from jax.experimental.pallas import tpu as pltpu
from jax.sharding import PartitionSpec as P

D = 768
HEADS = 12
HEAD_DIM = 64
PAIRS = HEADS // 2
E = 32
SEQ = 197
ROWS = 208
CAP = 16
SLOTS = E * CAP
AXIS = "fsdp"
PACK = 3200
CUT = 1664
GAIN1, SHIFT1, BQ, BV, BO, GAIN2, SHIFT2, VECTORS = range(8)
SCALE = 1.0 / math.sqrt(HEAD_DIM)
UNROLL = PAIRS

epsilon = 1e-06
f32 = jnp.float32
bf16 = jnp.bfloat16
i32 = jnp.int32


def mm(a, b, ca=1, cb=0):
    return lax.dot_general(a, b, (((ca,), (cb,)), ((), ())), preferred_element_type=f32)


def pieces(v, n):
    out = []
    for _ in range(n):
        p = v.astype(bf16)
        out.append(p)
        v = v - p.astype(f32)
    return out


def normalize(values):
    centered = values - jnp.mean(values, axis=-1, keepdims=True)
    inverse = lax.rsqrt(jnp.mean(centered * centered, axis=-1, keepdims=True) + epsilon)
    return (centered * inverse, inverse)


def norm_back(upstream, normed, inverse):
    return inverse * (
        upstream
        - jnp.mean(upstream, axis=-1, keepdims=True)
        - normed * jnp.mean(upstream * normed, axis=-1, keepdims=True)
    )


def swap(values, bit):
    n = lax.axis_size(AXIS)
    return lax.ppermute(values, AXIS, [(d, d ^ (1 << bit)) for d in range(n)])


def bit_of(bit):
    return (lax.axis_index(AXIS) >> bit) & 1


def bit_orders():
    bits = lax.axis_size(AXIS).bit_length() - 1
    inner = (bits - 1) // 3 if bits != 5 else 1
    x = list(range(1, 1 + inner))
    y = list(range(1 + inner, 1 + 2 * inner))
    z = list(range(1 + 2 * inner, bits))
    return [0] + x + y + z, [0] + y + x + z


def merged(values, other, bit, done):
    at = sum(1 for b in done if b > bit)
    lead = values.shape[0]
    high = 1 << at
    mine = values.reshape((high, lead // high) + values.shape[1:])
    other = other.reshape(mine.shape)
    which = lax.broadcasted_iota(i32, (1, 2, 1, 1, 1), 1) == bit_of(bit)
    both = jnp.where(which, mine[:, None], other[:, None])
    return both.reshape((2 * lead,) + values.shape[1:])


def gather_rows(shards, early, wait_for, late):
    orders = bit_orders()
    held = [(shard, []) for shard in shards]
    steps = len(orders[0])
    for step in range(steps):
        bits = [order[-1 - step] for order in orders]
        theirs = [swap(values, bit) for (values, _), bit in zip(held, bits)]
        if step + 1 == steps:
            pairs = [(values, other) for (values, _), other in zip(held, theirs)]
            return pairs, wait_for, late
        tied = [
            merged(values, other, bit, done)
            for (values, done), other, bit in zip(held, theirs, bits)
        ]
        if step + 1 == early:
            tied.append(wait_for)
        if step + 2 == steps:
            tied, late = lax.optimization_barrier((tied, late))
        else:
            tied = lax.optimization_barrier(tied)
        if step + 1 == early:
            wait_for = tied[-1]
        held = [(t, done + [bit]) for t, (_, done), bit in zip(tied, held, bits)]


def owner_order(order):
    n = lax.axis_size(AXIS)
    own = D // n
    position = jnp.arange(D, dtype=i32)
    chunk = position // own
    owner = jnp.zeros_like(chunk)
    for step, bit in enumerate(order):
        owner = owner | (((chunk >> (len(order) - 1 - step)) & 1) << bit)
    return (owner ^ lax.axis_index(AXIS)) * own + position % own


def pair_order():
    own = D // lax.axis_size(AXIS)
    position = jnp.arange(D, dtype=i32)
    inside = position % (D // 2)
    lowest = bit_of(0) ^ (position // (D // 2))
    return (2 * (inside // own) + lowest) * own + inside % own


def permutation(order):
    return (jnp.arange(D, dtype=i32)[:, None] == order[None]).astype(bf16)


def row_permutation(order):
    return (order[:, None] == jnp.arange(D, dtype=i32)[None]).astype(bf16)


def scatter_rows(parts):
    steps = len(parts[0][2])
    for step in range(steps):
        got = []
        for sent, _, order in parts:
            got.append(swap(sent, order[step]))
        if step + 1 == steps:
            return [x for (_, kept, _), g in zip(parts, got) for x in (kept, g)]
        ready = []
        for (_, kept, _), g in zip(parts, got):
            half = kept.shape[0] // 2
            for part in (slice(half, None), slice(0, half)):
                ready.append((kept[part].astype(f32) + g[part].astype(f32)).astype(bf16))
        ready = lax.optimization_barrier(ready)
        parts = [(ready[2 * k], ready[2 * k + 1], p[2]) for k, p in enumerate(parts)]


def exchange(blocks):
    return lax.all_to_all(blocks, AXIS, split_axis=0, concat_axis=0, tiled=True)


def to_owners(slot_rows, owners):
    rows = slot_rows.reshape((E, 1, CAP) + slot_rows.shape[1:])
    rows = jnp.broadcast_to(rows, (E, owners) + rows.shape[2:])
    return rows.reshape((E * owners, CAP) + slot_rows.shape[1:])


def place(routes):
    choice = jnp.pad(routes.T, ((0, 0), (0, ROWS - SEQ)), constant_values=-1)
    ids = jnp.arange(E, dtype=i32)[:, None]
    first = (choice[:1] == ids).astype(bf16)
    second = (choice[1:] == ids).astype(bf16)
    t = jnp.arange(ROWS, dtype=i32)
    earlier = (t[:, None] < t[None, :]).astype(bf16)
    before = mm(jnp.concatenate([first, second], axis=0), earlier)
    rank0 = jnp.sum(before[:E] * first, axis=0)
    seen = before[E:] + jnp.sum(first.astype(f32), axis=1, keepdims=True)
    rank1 = jnp.sum(seen * second, axis=0)
    return choice * CAP + jnp.stack([rank0, rank1]).astype(i32)


def gelu_terms(v):
    cumulative = 0.5 * (1.0 + lax.erf(v * (1.0 / math.sqrt(2.0))))
    density = jnp.exp(-0.5 * v * v) * (1.0 / math.sqrt(2.0 * math.pi))
    return v * cumulative, cumulative + v * density


def dispatch_of(placed):
    slot = lax.broadcasted_iota(i32, (SLOTS, ROWS), 0)
    hit = (slot == placed[0:1, :]) | (slot == placed[1:2, :])
    return hit.astype(f32).astype(bf16)


def dispatch_rows(placed):
    slot = lax.broadcasted_iota(i32, (ROWS, SLOTS), 1)
    hit = (slot == placed[:, 0:1]) | (slot == placed[:, 1:2])
    return hit.astype(f32).astype(bf16)


def half_of(pair, second):
    lane = lax.broadcasted_iota(i32, pair.shape, 1)
    keep = (lane >= HEAD_DIM) if second else (lane < HEAD_DIM)
    return jnp.where(keep, pair, jnp.zeros_like(pair))


def join(first, second):
    lane = lax.broadcasted_iota(i32, first.shape, 1)
    return jnp.where(lane < HEAD_DIM, first, second)


def forward_kernel(get, outs, flush):
    slots, residual, prob, acts, norm1_o, norm2_o, context_o, router_o, out_t, small = outs
    half = D // 2
    sel = get(2)
    first, second = get(0), get(1)
    rest = mm(sel[:, :half], first[:, QKV_B[1] :]) + mm(sel[:, half:], second[:, QKV_B[1] :])
    out_t[...] = rest[:, :D].astype(bf16)
    flush(8)
    small[...] = rest[:, D:].astype(bf16)
    flush(9)
    vec = vectors_of(small)
    row = lambda k: vec[k : k + 1, :]
    inputs = get(3)[...].astype(f32)
    hat1, _ = normalize(inputs)
    norm1 = (hat1 * row(GAIN1) + row(SHIFT1)).astype(bf16)
    norm1_o[...] = norm1
    flush(4)
    moved = mm(norm1, sel[...]).astype(bf16)
    left, right = moved[:, :half], moved[:, half:]
    proj_a = mm(left, get(4)[...]) + mm(right, get(5)[...])
    proj_b = mm(left, first[:, : QKV_B[1]]) + mm(right, second[:, : QKV_B[1]])
    proj = jnp.concatenate([proj_a, proj_b], axis=1)
    acts[:, :D] = (proj[:, :D] + row(BQ)).astype(bf16)
    acts[:, D : 2 * D] = proj[:, D : 2 * D].astype(bf16)
    acts[:, 2 * D :] = (proj[:, 2 * D :] + row(BV)).astype(bf16)
    flush(3)
    token = lax.broadcasted_iota(i32, (ROWS, ROWS), 0) < SEQ

    def pair(j, _):
        at = lambda part: pl.ds(pl.multiple_of(part * D + j * 128, 128), 128)
        q = acts[:, at(0)] * jnp.asarray(SCALE, bf16)
        k, v = acts[:, at(1)], acts[:, at(2)]
        both = []
        for h in range(2):
            raised = jnp.exp(mm(half_of(k, h), q, 1, 1))
            raised = jnp.where(token, raised, 0.0)
            p = (raised * (1.0 / jnp.sum(raised, axis=0, keepdims=True))).astype(bf16)
            prob[2 * j + h, :, :] = p
            both.append(mm(p, v, 0, 0))
        context_o[:, at(0)] = join(both[0], both[1]).astype(bf16)
        return 0

    lax.fori_loop(0, PAIRS, pair, 0, unroll=UNROLL)
    flush(2)
    flush(6)
    res = inputs + mm(context_o[...], out_t[...], 1, 1) + row(BO)
    residual[...] = res
    flush(1)
    hat2, _ = normalize(res)
    norm2 = (hat2 * row(GAIN2) + row(SHIFT2)).astype(bf16)
    norm2_o[...] = norm2
    flush(5)
    slots[...] = mm(dispatch_of(get(6)[...]), norm2).astype(bf16)
    flush(0)
    lane = lax.broadcasted_iota(i32, (ROWS, 128), 1)
    logits = jnp.where(lane < E, mm(norm2, small[...]), 0.0)
    raised = jnp.where(lane < E, jnp.exp(logits), 0.0)
    router_o[...] = raised / jnp.sum(raised, axis=1, keepdims=True)
    flush(7)


class Near:
    def __init__(self, array):
        self.array = array


class Stack:
    def __init__(self, arrays, rows):
        self.arrays, self.rows = arrays, rows


class Columns:
    def __init__(self, array, start, stop):
        self.array, self.start, self.stop = array, start, stop


class Fetch:
    def __init__(self, copies, groups, refs):
        self.copies, self.groups, self.refs = copies, groups, refs
        self.begun = 0
        self.waited = set()
        self.begin(2)

    def begin(self, count):
        while self.begun < min(count, len(self.groups)):
            for k in self.groups[self.begun]:
                for copy in self.copies[k]:
                    copy.start()
            self.begun += 1

    def get(self, k):
        if k in self.copies and k not in self.waited:
            at = next(g for g, group in enumerate(self.groups) if k in group)
            self.begin(at + 1)
            for copy in self.copies[k]:
                copy.wait()
            self.waited.add(k)
            if all(m in self.waited for m in self.groups[at]):
                self.begin(at + 3)
        return self.refs[k]


def call(kernel, ins, outs, limit, temps=(), groups=None):
    arrays, specs, scratch, plan = [], [], [], []
    for item in ins:
        if isinstance(item, Near):
            plan.append(("near", len(arrays), None))
            arrays.append(item.array)
            specs.append(pl.BlockSpec(memory_space=pltpu.VMEM))
            continue
        if isinstance(item, Stack):
            group, shape = item.arrays, (item.rows, item.arrays[0].shape[1])
            cut = None
        elif isinstance(item, Columns):
            group, shape = [item.array], (item.array.shape[0], item.stop - item.start)
            cut = (item.start, item.stop)
        else:
            group, shape, cut = [item], item.shape, None
        plan.append(("far", list(range(len(arrays), len(arrays) + len(group))), cut))
        scratch.append(pltpu.VMEM(shape, group[0].dtype))
        for array in group:
            arrays += in_hbm(array)
            specs.append(pl.BlockSpec(memory_space=pltpu.HBM))
    n_in, n_out, n_far = len(arrays), len(outs), len(scratch)

    def body(*refs):
        far_in, far_out = refs[:n_in], refs[n_in : n_in + n_out]
        near = refs[n_in + n_out : -1]
        sems = refs[-1]
        copies, views, used, sem = {}, [], 0, 0
        for k, (kind, index, cut) in enumerate(plan):
            if kind == "near":
                views.append(far_in[index])
                continue
            target = near[used]
            used += 1
            views.append(target)
            copies[k], row = [], 0
            for at in index:
                source = far_in[at]
                if cut is not None:
                    source = source.at[:, cut[0] : cut[1]]
                if len(target.shape) > 1 and source.shape[0] != target.shape[0]:
                    place_at = target.at[row : row + source.shape[0], :]
                else:
                    place_at = target
                row += source.shape[0]
                copies[k].append(pltpu.make_async_copy(source, place_at, sems.at[sem]))
                sem += 1
        order = groups if groups is not None else [list(range(len(plan)))]
        order = [[k for k in group if k in copies] for group in order]
        source = Fetch(copies, order, views)
        results = near[n_far : n_far + n_out]
        sinks = [
            pltpu.make_async_copy(v, f, sems.at[sem + k])
            for k, (v, f) in enumerate(zip(results, far_out))
        ]
        kernel(source.get, near[n_far:], lambda k: sinks[k].start())
        for k in copies:
            source.get(k)
        for sink in sinks:
            sink.wait()

    n_sems = sum(len(index) for kind, index, _ in plan if kind == "far") + n_out
    return pl.pallas_call(
        body,
        in_specs=specs,
        out_specs=[pl.BlockSpec(memory_space=pltpu.HBM)] * n_out,
        out_shape=[pltpu.HBM(shape, dtype) for shape, dtype in outs],
        scratch_shapes=scratch
        + [pltpu.VMEM(shape, dtype) for shape, dtype in list(outs) + list(temps)]
        + [pltpu.SemaphoreType.DMA((n_sems,))],
        compiler_params=pltpu.CompilerParams(vmem_limit_bytes=limit << 20),
    )(*arrays)


def in_hbm(*arrays):
    return [pltpu.with_memory_space_constraint(a, pltpu.HBM) for a in arrays]


def vectors_of(small):
    lane = lax.broadcasted_iota(i32, (8, 128), 1)
    pick = lane == lax.broadcasted_iota(i32, (8, 128), 0) + 2 * E
    return mm(pick.astype(f32).astype(bf16), small[...], 1, 1)


QKV_B = (0, 3 * D - CUT)
OUT_T = (3 * D - CUT, 4 * D - CUT)
SMALL = (4 * D - CUT, PACK - CUT)


def attend_forward(x, placed, halves_a, halves_b, sel):
    names = ("slots", "residual", "prob", "acts", "norm1", "norm2", "context", "router")
    names += ("out_t", "small")
    outs = call(
        forward_kernel,
        tuple(Near(half) for half in halves_b) + (sel, x)
        + tuple(Near(half) for half in halves_a) + (placed,),
        [
            ((SLOTS, D), bf16), ((ROWS, D), f32), ((HEADS, ROWS, ROWS), bf16),
            ((ROWS, 3 * D), bf16), ((ROWS, D), bf16), ((ROWS, D), bf16), ((ROWS, D), bf16),
            ((ROWS, 128), f32), ((D, D), bf16), ((D, 128), bf16),
        ],
        12,
    )
    return dict(zip(names, outs))


def backward_kernel(get, outs, flush):
    input_grad, gate_o, ph, res_half_o, logit_o, sums, cgs = outs
    rec, placed, small, cot = get(0), get(1), get(2), get(3)
    vec = vectors_of(small)
    row = lambda k: vec[k : k + 1, :]
    disp = dispatch_rows(placed[...])
    lane = lax.broadcasted_iota(i32, (SLOTS, 128), 1)
    slot_expert = lax.broadcasted_iota(i32, (SLOTS, 128), 0) // CAP
    moe = 0.0
    pg = 0.0
    for o in range(rec.shape[1]):
        rows = rec[:, o, :, :].reshape(SLOTS, D + 128)
        moe = moe + mm(disp, rows[:, :D])
        gg = jnp.where((lane & 63) == slot_expert, rows[:, D:], jnp.zeros((SLOTS, 128), bf16))
        pg = pg + mm(disp, gg)
    pg = pg + pltpu.roll(pg, 64, 1)
    hot = mm(disp, (lane == slot_expert).astype(f32).astype(bf16))
    pg = (pg + pltpu.roll(mm(cot[...], small[...]), 128 - E, 1)) * hot
    prob_r = get(4)[...]
    gate_o[...] = prob_r * hot
    flush(1)
    logit = prob_r * (pg - jnp.sum(pg * prob_r, axis=1, keepdims=True))
    real = lax.broadcasted_iota(i32, (ROWS, 1), 0) < SEQ
    logit = jnp.where(real, logit, 0.0).astype(bf16)
    logit_o[...] = logit
    flush(4)
    second = moe + mm(logit, small[...], 1, 1)
    hat2, rstd2 = normalize(get(5)[...])
    sums[GAIN2 : GAIN2 + 1, :] = jnp.sum(second * hat2, axis=0, keepdims=True)
    sums[SHIFT2 : SHIFT2 + 1, :] = jnp.sum(second, axis=0, keepdims=True)
    res_grad = cot[...].astype(f32) + norm_back(second * row(GAIN2), hat2, rstd2)
    input_grad[...] = res_grad
    sums[BO : BO + 1, :] = jnp.sum(res_grad, axis=0, keepdims=True)
    res_half = res_grad.astype(bf16)
    res_half_o[...] = res_half
    flush(3)
    cgs[...] = mm(res_half, get(6)[...]).astype(bf16)
    prob, acts = get(7), get(8)

    def pair(j, _):
        at = lambda part: pl.ds(pl.multiple_of(part * D + j * 128, 128), 128)
        q, k, v = acts[:, at(0)], acts[:, at(1)], acts[:, at(2)]
        c = cgs[:, at(0)]
        qs, ks, vs = [], [], []
        for h in range(2):
            p = prob[2 * j + h, :, :]
            pf = p.astype(f32)
            t = pf * mm(half_of(v, h), c, 1, 1)
            sg = ((t - pf * jnp.sum(t, axis=0, keepdims=True)) * SCALE).astype(bf16)
            vs.append(mm(p, c))
            qs.append(mm(sg, k, 0, 0))
            ks.append(mm(sg, q))
        qg, kg, vg = join(*qs), join(*ks), join(*vs)
        sums[BQ : BQ + 1, at(0)] = jnp.sum(qg, axis=0, keepdims=True)
        sums[BV : BV + 1, at(0)] = jnp.sum(vg, axis=0, keepdims=True)
        ph[:, at(0)] = qg.astype(bf16)
        ph[:, at(1)] = kg.astype(bf16)
        ph[:, at(2)] = vg.astype(bf16)
        return 0

    lax.fori_loop(0, PAIRS, pair, 0, unroll=UNROLL)
    flush(2)
    first = mm(ph[:, :CUT], get(9)[...], 1, 1) + mm(ph[:, CUT:], get(10)[...], 1, 1)
    hat1, rstd1 = normalize(get(11)[...].astype(f32))
    sums[GAIN1 : GAIN1 + 1, :] = jnp.sum(first * hat1, axis=0, keepdims=True)
    sums[SHIFT1 : SHIFT1 + 1, :] = jnp.sum(first, axis=0, keepdims=True)
    sums[7:8, :] = jnp.zeros((1, D), f32)
    flush(5)
    input_grad[...] += norm_back(first * row(GAIN1), hat1, rstd1)
    flush(0)


BACKWARD_TEMPS = [
    ((ROWS, 3 * D), bf16), ((ROWS, D), bf16), ((ROWS, 128), bf16), ((8, D), f32),
]


def backward_operands(rec, x, cot, placed, s, qkv_a, qkv_b, out_t, small):
    return (
        Near(rec), placed, small, cot, s["router"], s["residual"], out_t, s["prob"],
        s["acts"], qkv_a, qkv_b, x,
    )


BACKWARD_GROUPS = [[1, 2, 3, 4, 5], [6, 7, 8], [9, 10, 11]]


def token_backward(*args):
    return call(
        backward_kernel,
        backward_operands(*args),
        [((ROWS, D), f32), ((ROWS, 128), f32)] + BACKWARD_TEMPS,
        12 + 4 * args[0].shape[1],
        [((ROWS, D), bf16)],
        BACKWARD_GROUPS,
    )


def expert_kernel(
    idx, x, c, w_in, w_out, bias, router, act, back, d_rows, gated, gate, grad_bias, acc, gg
):
    r, f = pl.program_id(0), pl.program_id(1)
    rows, width = act.shape

    @pl.when(f == 0)
    def _():
        logits = mm(x[...], router[...])
        lane = lax.broadcasted_iota(i32, logits.shape, 1)
        raised = jnp.where(lane < E, jnp.exp(jnp.where(lane < E, logits, 0.0)), 0.0)
        picked = lane == idx[0]
        g = jnp.sum(jnp.where(picked, raised, 0.0), axis=1, keepdims=True)
        g = g / jnp.sum(raised, axis=1, keepdims=True)
        gate[...] = jnp.broadcast_to(g, gate.shape)
        rows_c = c[...].reshape(rows, D).astype(f32)
        gated[...] = (rows_c * g).astype(bf16)
        gg[...] = jnp.zeros_like(gg)
        acc[...] = jnp.zeros_like(acc)

    value, slope = gelu_terms(mm(x[...], w_in[...], 1, 1) + bias[...])
    hid = mm(c[...].reshape(rows, D), w_out[...], 1, 1)
    act[...] = value.astype(bf16)
    both = value * hid
    part = both[:, :128]
    for j in range(1, width // 128):
        part = part + both[:, j * 128 : (j + 1) * 128]
    gg[...] += part
    before = hid * slope * gate[:, :1]
    total = jnp.sum(before, axis=0, keepdims=True)
    half = before.astype(bf16)
    back[...] = half
    acc[...] += mm(half, w_in[...])
    cols = pl.ds(pl.multiple_of(f * width, width), width)

    @pl.when(r == 0)
    def _():
        grad_bias[:, cols] = total

    @pl.when(r > 0)
    def _():
        grad_bias[:, cols] += total

    @pl.when(f == pl.num_programs(1) - 1)
    def _():
        d_rows[:, :D] = acc[...].astype(bf16)
        g = jnp.sum(gg[...], axis=1, keepdims=True)
        high = g.astype(bf16)
        low = (g - high.astype(f32)).astype(bf16)
        lane = lax.broadcasted_iota(i32, (rows, 128), 1)
        d_rows[:, D:] = jnp.where(
            lane < 64, jnp.broadcast_to(high, lane.shape), jnp.broadcast_to(low, lane.shape)
        )


def expert_main(i, x, c, w_in, w_out, bias, router, expert):
    total, width = x.shape[0], w_in.shape[0]
    rb, fb = min(512, total), min(768, width)
    row = lambda r, f, *_: (r, 0)
    tile = lambda r, f, *_: (r, f)
    fixed = lambda r, f, *_: (0, 0)
    return pl.pallas_call(
        expert_kernel,
        grid_spec=pltpu.PrefetchScalarGridSpec(
            num_scalar_prefetch=1,
            grid=(total // rb, width // fb),
            in_specs=[
                pl.BlockSpec((rb, D), row),
                pl.BlockSpec((rb // CAP, None, CAP, D), lambda r, f, idx: (r, idx[1], 0, 0)),
                pl.BlockSpec((fb, D), lambda r, f, *_: (f, 0)),
                pl.BlockSpec((fb, D), lambda r, f, *_: (f, 0)),
                pl.BlockSpec((1, fb), lambda r, f, *_: (0, f)),
                pl.BlockSpec((D, 128), fixed),
            ],
            out_specs=[
                pl.BlockSpec((rb, fb), tile),
                pl.BlockSpec((rb, fb), tile),
                pl.BlockSpec((rb, D + 128), row),
                pl.BlockSpec((rb, D), row),
                pl.BlockSpec((rb, 128), row),
                pl.BlockSpec((1, width), fixed),
            ],
            scratch_shapes=[
                pltpu.VMEM((rb, D), f32),
                pltpu.VMEM((rb, 128), f32),
            ],
        ),
        out_shape=[
            pltpu.HBM((total, width), bf16),
            pltpu.HBM((total, width), bf16),
            pltpu.HBM((total, D + 128), bf16),
            pltpu.HBM((total, D), bf16),
            pltpu.HBM((total, 128), f32),
            pltpu.HBM((1, width), f32),
        ],
        compiler_params=pltpu.CompilerParams(
            dimension_semantics=("arbitrary", "arbitrary"), vmem_limit_bytes=22 << 20
        ),
        name="expert_main",
    )(jnp.stack([expert, jnp.int32(i)]), *in_hbm(x, c, w_in, w_out, bias.reshape(1, width), router))


def parts_kernel(act0, act1, gate0, gate1, w_out, out, acc):
    f = pl.program_id(0)

    @pl.when(f == 0)
    def _():
        acc[...] = jnp.zeros_like(acc)

    for i, act in enumerate((act0, act1)):
        acc[i] += mm(act[...], w_out[...])

    @pl.when(f == pl.num_programs(0) - 1)
    def _():
        for i, gate in enumerate((gate0, gate1)):
            rows = (acc[i] * gate[:, :1]).astype(bf16)
            out[:, i, :, :] = rows.reshape(out.shape[0], CAP, D)


def expert_parts(acts, gates, w_out):
    total, width = acts[0].shape
    fb = min(768, width)
    n = total // CAP
    cols = pl.BlockSpec((total, fb), lambda f: (0, f))
    full = pl.BlockSpec((total, 128), lambda f: (0, 0))
    return pl.pallas_call(
        parts_kernel,
        grid=(width // fb,),
        in_specs=[cols, cols, full, full, pl.BlockSpec((fb, D), lambda f: (f, 0))],
        out_specs=pl.BlockSpec((n, 2, CAP, D), lambda f: (0, 0, 0, 0)),
        out_shape=pltpu.HBM((n, 2, CAP, D), bf16),
        scratch_shapes=[pltpu.VMEM((2, total, D), f32)],
        compiler_params=pltpu.CompilerParams(
            dimension_semantics=("arbitrary",),
            vmem_limit_bytes=(18 if total <= 512 else 48) << 20,
        ),
        name="expert_parts",
    )(*in_hbm(*acts, *gates, w_out))


def moved_kernel(get, outs, flush):
    for k, (value, perm) in enumerate(((0, 3), (0, 4), (1, 4), (2, 4))):
        outs[k][...] = mm(get(perm)[...], get(value)[...], 1, 1).astype(bf16)
        flush(k)


def last_kernel(get, outs, flush):
    input_grad, gate1, sent_a, kept_a, sent_b, kept_b, lg1, sums1, cgs = outs
    base = 12
    ph, rh = get(base + 2), get(base + 4)
    backward_kernel(
        get,
        (input_grad, gate1, ph.at[ROWS:, :], rh.at[ROWS:, :], lg1, sums1, cgs),
        lambda k: flush(k) if k < 2 else None,
    )
    half = D // 2

    def lay(value, sent, kept, start):
        kept[:, start : start + value.shape[1]] = value[:half].astype(bf16)
        sent[:, start : start + value.shape[1]] = value[half:].astype(bf16)

    lay(mm(get(base)[...], ph[:, :CUT]), sent_a, kept_a, 0)
    flush(2)
    flush(3)
    lay(mm(get(base + 1)[...], ph[:, CUT:]), sent_b, kept_b, 0)
    start = 3 * D - CUT
    perm = get(base + 3)[...]
    out = mm(mm(perm, rh[...], 1, 1).astype(bf16), get(base + 5)[...])
    lay(out, sent_b, kept_b, start)
    sums = get(base + 6)[...] + sums1[...]
    zeros = lambda n: jnp.zeros((n, D), f32)
    spread = jnp.concatenate([zeros(2 * E), sums, zeros(128 - 2 * E - 8)], axis=0)
    tail = sum(mm(perm, p, 1, 1) for p in pieces(spread, 3))
    norm2 = get(base + 7)
    tail = tail + mm(norm2[...], jnp.concatenate([get(base + 9)[...], lg1[...]], axis=0))
    gates = jnp.concatenate([get(base + 10)[...], gate1[...]], axis=0)
    for p in pieces(pltpu.roll(gates, E, 1), 2):
        tail = tail + mm(get(base + 8)[...], p)
    lay(tail, sent_b, kept_b, start + D)
    flush(4)
    flush(5)


def eye(size, width=None, shift=0):
    shape = (size, width or size)
    hit = lax.broadcasted_iota(i32, shape, 1) == lax.broadcasted_iota(i32, shape, 0) + shift
    return hit.astype(f32).astype(bf16)


def pack_kernel(get, outs, flush):
    part_a, part_b = outs
    w_qkv, w_out, router, bias = (get(k) for k in range(4))
    own = w_qkv.shape[0]
    part_a[0] = w_qkv[:, :CUT]
    flush(0)
    part_b[0, :, QKV_B[0] : QKV_B[1]] = w_qkv[:, CUT:]
    part_b[0, :, OUT_T[0] : OUT_T[1]] = w_out[...]
    rows = [get(4 + k)[...].astype(f32).reshape(1, own) for k in range(VECTORS)]
    rows = jnp.concatenate(rows + [jnp.zeros((1, own), f32)], axis=0).astype(bf16)
    columns = mm(eye(own), rows, 1, 1).astype(bf16)
    tail = mm(router[...], eye(E, 128)) + mm(bias[...], eye(E, 128, E))
    tail = tail + mm(columns, eye(8, 128, 2 * E))
    part_b[0, :, SMALL[0] :] = tail.astype(bf16)
    flush(1)


def unpack_kernel(get, outs, flush):
    w_qkv, w_out, router, bias = outs[:4]
    add = lambda k: get(k)[...].astype(f32) + get(k + 1)[...].astype(f32)
    w_qkv[:, :CUT] = add(0)
    mine = add(2)
    w_qkv[:, CUT:] = mine[:, QKV_B[0] : QKV_B[1]]
    flush(0)
    w_out[...] = mine[:, OUT_T[0] : OUT_T[1]]
    flush(1)
    tail = mine[:, SMALL[0] :]
    router[...] = tail[:, :E]
    flush(2)
    bias[...] = tail[:, E : 2 * E]
    flush(3)
    rows = sum(mm(eye(8, 128, 2 * E), p, 1, 1) for p in pieces(tail, 3))
    for k in range(VECTORS):
        outs[4 + k][...] = rows[k]
        flush(4 + k)


def output_kernel(get, outs, flush):
    block_out, input_grad = outs
    small, parts = get(0), get(1)
    for i in range(2):
        placed, residual, gate, grad = (get(2 + 4 * i + k) for k in range(4))
        input_grad[i * SEQ : (i + 1) * SEQ, :] = grad[:SEQ, :]
        disp = dispatch_rows(placed[...])
        out = residual[...]
        for o in range(parts.shape[1]):
            out = out + mm(disp, parts[:, o, i, :, :].reshape(SLOTS, D))
        for p in pieces(pltpu.roll(gate[...], E, 1), 2):
            out = out + mm(p, small[...], 1, 1)
        block_out[i * SEQ : (i + 1) * SEQ, :] = out[:SEQ]
    flush(0)
    flush(1)


def weights_kernel(act0, act1, back0, back1, g0, g1, x0, x1, out_w, in_w):
    out_w[...] = mm(act0[...], g0[...], 0, 0) + mm(act1[...], g1[...], 0, 0)
    in_w[...] = mm(back0[...], x0[...], 0, 0) + mm(back1[...], x1[...], 0, 0)


def expert_weights(acts, backs, gated, xs):
    total, width = acts[0].shape
    fb = min(512, width)
    cols = pl.BlockSpec((total, fb), lambda f: (0, f))
    full = pl.BlockSpec((total, D), lambda f: (0, 0))
    rows = pl.BlockSpec((fb, D), lambda f: (f, 0))
    return pl.pallas_call(
        weights_kernel,
        grid=(width // fb,),
        in_specs=[cols] * 4 + [full] * 4,
        out_specs=[rows, rows],
        out_shape=[pltpu.HBM((width, D), f32)] * 2,
        compiler_params=pltpu.CompilerParams(
            dimension_semantics=("arbitrary",),
            vmem_limit_bytes=(22 if total <= 512 else 40) << 20,
        ),
        name="expert_weights",
    )(*in_hbm(*acts, *backs, *gated, *xs))


def on_device(
    block_in, out_cotangent, expert_routes, ln1_gain, ln1_shift, w_qkv, bias_query, bias_value,
    w_out, bias_out, ln2_gain, ln2_shift, w_router, expert_bias, w_expert_in, bias_hidden,
    w_expert_out,
):
    images = block_in.shape[0] // SEQ
    n = lax.axis_size(AXIS)
    owners = n // E
    own = ln1_gain.shape[0]
    expert = lax.axis_index(AXIS) // owners
    order_a, order_b = bit_orders()
    barrier = lax.optimization_barrier
    shards = call(
        pack_kernel,
        (w_qkv, w_out.T, w_router, expert_bias.T)
        + (ln1_gain, ln1_shift, bias_query, bias_value, bias_out, ln2_gain, ln2_shift),
        [((1, own, CUT), bf16), ((1, own, PACK - CUT), bf16)],
        8,
    )

    pad_rows = ((0, ROWS - SEQ), (0, 0))
    xs, cots, placed, states, outgoing = [], [], [], [], []
    for i in range(images):
        xs.append(jnp.pad(block_in[i * SEQ : (i + 1) * SEQ], pad_rows))
        cots.append(jnp.pad(out_cotangent[i * SEQ : (i + 1) * SEQ], pad_rows))
        placed.append(place(expert_routes[i * SEQ : (i + 1) * SEQ]))
        slots = mm(dispatch_of(placed[i]), cots[i]).astype(bf16)
        outgoing.append(to_owners(slots, owners))
    late = (
        xs, cots, [p.T for p in placed], permutation(pair_order()),
        row_permutation(owner_order(order_a)), row_permutation(owner_order(order_b)),
    )
    halves, outgoing, late = gather_rows(shards, 3, jnp.stack(outgoing, axis=1), late)
    xs, cots, columns, sel, perm_a, perm_b = late
    flat = [tuple(h.reshape(D // 2, h.shape[-1]) for h in pair) for pair in halves]
    cot_in = exchange(outgoing)
    for i in range(images):
        states.append(attend_forward(xs[i], placed[i], flat[0], flat[1], sel))
    both = lambda key: [s[key] for s in states]
    norm1a, norm1b, norm2b, cotb = call(
        moved_kernel,
        (Stack(both("norm1"), 2 * ROWS), Stack(both("norm2"), 2 * ROWS))
        + (Stack(cots, 2 * ROWS), perm_a, perm_b),
        [((D, 2 * ROWS), bf16)] * 4,
        12,
    )
    first = exchange(to_owners(states[0]["slots"], owners))
    second = exchange(to_owners(states[1]["slots"], owners))
    arrived = [first.reshape(-1, D), second.reshape(-1, D)]
    small, out_t = states[0]["small"], states[0]["out_t"]
    rest = list(range(lax.axis_size(AXIS).bit_length() - 1))[1:]
    natural = [
        merged(mine, theirs, 0, rest)
        for mine, theirs in (halves[0], tuple(h[..., : QKV_B[1]] for h in halves[1]))
    ]
    qkv_a, qkv_b = [v.reshape(D, v.shape[-1]) for v in natural]
    done = []
    grad_hidden = 0.0
    received = []
    for i in range(images):
        act, back, d_rows, gated, gate, gb = expert_main(
            i, arrived[i], cot_in, w_expert_in, w_expert_out, bias_hidden, small, expert
        )
        done.append((act, back, gated, gate))
        grad_hidden = grad_hidden + gb[0]
        if i == 1:
            d_rows, qkv_a, qkv_b = barrier((d_rows, qkv_a, qkv_b))
        rows = exchange(d_rows.reshape(n, CAP, D + 128))
        received.append(rows.reshape(E, owners, CAP, D + 128))
    sent = expert_parts([d[0] for d in done], [d[3] for d in done], w_expert_out)
    parts = exchange(sent).reshape(E, owners, images, CAP, D)
    column = lambda k: [d[k] for d in done]
    grad_expert_out, grad_expert_in = expert_weights(
        column(0), column(1), column(2), arrived
    )
    grad0, gate0, ph0, rh0, lg0, sums0 = token_backward(
        received[0], xs[0], cots[0], columns[0], states[0], qkv_a, qkv_b, out_t, small
    )
    grad1, gate1, sent_a, kept_a, sent_b, kept_b = call(
        last_kernel,
        backward_operands(
            received[1], xs[1], cots[1], columns[1], states[1], qkv_a, qkv_b, out_t, small
        )
        + (norm1a, norm1b, Stack([ph0], 2 * ROWS), perm_b, Stack([rh0], 2 * ROWS))
        + (Stack(both("context"), 2 * ROWS), sums0, norm2b, cotb, lg0, gate0),
        [
            ((ROWS, D), f32), ((ROWS, 128), f32),
            ((D // 2, CUT), bf16), ((D // 2, CUT), bf16),
            ((D // 2, PACK - CUT), bf16), ((D // 2, PACK - CUT), bf16),
        ],
        26 + 4 * owners,
        BACKWARD_TEMPS[2:] + [((ROWS, D), bf16)],
        BACKWARD_GROUPS + [[12, 13, 14, 15, 16], [17, 18, 19, 20, 21, 22]],
    )
    ends = scatter_rows([(sent_a, kept_a, order_a), (sent_b, kept_b, order_b)])
    block_out, input_grad = call(
        output_kernel,
        (small, Near(parts), columns[0], states[0]["residual"], gate0, grad0)
        + (columns[1], states[1]["residual"], gate1, grad1),
        [((images * SEQ, D), f32)] * 2,
        6 + 6 * owners,
    )
    grad_qkv, grad_out, grad_router, grad_bias, *vec = call(
        unpack_kernel,
        tuple(Near(end) for end in ends),
        [(shape, f32) for shape in ((own, 3 * D), (own, D), (own, E), (own, E))]
        + [((own,), f32)] * VECTORS,
        8,
    )
    return (
        block_out, input_grad, vec[GAIN1], vec[SHIFT1], grad_qkv, vec[BQ], vec[BV],
        grad_out.T, vec[BO], vec[GAIN2], vec[SHIFT2], grad_router, grad_bias.T,
        grad_expert_in, grad_hidden, grad_expert_out,
    )


def solution(mesh):
    rows, line, cols = P(AXIS, None), P(AXIS), P(None, AXIS)
    in_specs = (
        rows, rows, rows, line, line, rows, line, line, cols, line, line, line, rows, cols,
        rows, line, rows,
    )
    out_specs = (
        rows, rows, line, line, rows, line, line, cols, line, line, line, rows, cols, rows,
        line, rows,
    )

    return jax.shard_map(
        on_device, mesh=mesh, in_specs=in_specs, out_specs=out_specs, check_vma=False
    )
```

```python
import math

import jax
import jax.numpy as jnp
from jax import lax
from jax.experimental import pallas as pl
from jax.experimental.pallas import tpu as pltpu
from jax.sharding import PartitionSpec as P

D = 768
HEADS = 12
HEAD_DIM = 64
PAIRS = HEADS // 2
E = 32
SEQ = 197
ROWS = 208
CAP = 16
SLOTS = E * CAP
AXIS = "fsdp"
PACK = 3200
CUT = 1664
GAIN1, SHIFT1, BQ, BV, BO, GAIN2, SHIFT2, VECTORS = range(8)
SCALE = 1.0 / math.sqrt(HEAD_DIM)
UNROLL = PAIRS

epsilon = 1e-06
f32 = jnp.float32
bf16 = jnp.bfloat16
i32 = jnp.int32


def mm(a, b, ca=1, cb=0):
    return lax.dot_general(a, b, (((ca,), (cb,)), ((), ())), preferred_element_type=f32)


def pieces(v, n):
    out = []
    for _ in range(n):
        p = v.astype(bf16)
        out.append(p)
        v = v - p.astype(f32)
    return out


def normalize(values):
    centered = values - jnp.mean(values, axis=-1, keepdims=True)
    inverse = lax.rsqrt(jnp.mean(centered * centered, axis=-1, keepdims=True) + epsilon)
    return (centered * inverse, inverse)


def norm_back(upstream, normed, inverse):
    return inverse * (
        upstream
        - jnp.mean(upstream, axis=-1, keepdims=True)
        - normed * jnp.mean(upstream * normed, axis=-1, keepdims=True)
    )


def swap(values, bit):
    n = lax.axis_size(AXIS)
    return lax.ppermute(values, AXIS, [(d, d ^ (1 << bit)) for d in range(n)])


def bit_of(bit):
    return (lax.axis_index(AXIS) >> bit) & 1


def bit_orders():
    bits = lax.axis_size(AXIS).bit_length() - 1
    inner = (bits - 1) // 3 if bits != 5 else 1
    x = list(range(1, 1 + inner))
    y = list(range(1 + inner, 1 + 2 * inner))
    z = list(range(1 + 2 * inner, bits))
    return [0] + x + y + z, [0] + y + x + z


def merged(values, other, bit, done):
    at = sum(1 for b in done if b > bit)
    lead = values.shape[0]
    high = 1 << at
    mine = values.reshape((high, lead // high) + values.shape[1:])
    other = other.reshape(mine.shape)
    which = lax.broadcasted_iota(i32, (1, 2, 1, 1, 1), 1) == bit_of(bit)
    both = jnp.where(which, mine[:, None], other[:, None])
    return both.reshape((2 * lead,) + values.shape[1:])


def gather_rows(shard, early, wait_for, late):
    orders = bit_orders()
    steps = len(orders[0])
    common = 0
    while orders[0][-1 - common] == orders[1][-1 - common]:
        common += 1
    held, done = shard, []
    for step in range(common):
        bit = orders[0][-1 - step]
        held = lax.optimization_barrier(merged(held, swap(held, bit), bit, done))
        done.append(bit)
    held = [(held[..., :CUT], list(done)), (held[..., CUT:], list(done))]
    for step in range(common, steps):
        bits = [order[-1 - step] for order in orders]
        theirs = []
        for (values, _), bit in zip(held, bits):
            theirs.append(swap(values, bit))
        if step + 1 == steps:
            pairs = [(values, other) for (values, _), other in zip(held, theirs)]
            return pairs, wait_for, late
        tied = [
            merged(values, other, bit, seen)
            for (values, seen), other, bit in zip(held, theirs, bits)
        ]
        if step + 1 == early:
            tied.append(wait_for)
        if step + 2 == steps:
            tied, late = lax.optimization_barrier((tied, late))
        else:
            tied = lax.optimization_barrier(tied)
        if step + 1 == early:
            wait_for = tied[-1]
        held = [(t, seen + [bit]) for t, (_, seen), bit in zip(tied, held, bits)]


def owner_order(order):
    n = lax.axis_size(AXIS)
    own = D // n
    position = jnp.arange(D, dtype=i32)
    chunk = position // own
    owner = jnp.zeros_like(chunk)
    for step, bit in enumerate(order):
        owner = owner | (((chunk >> (len(order) - 1 - step)) & 1) << bit)
    return (owner ^ lax.axis_index(AXIS)) * own + position % own


def pair_order():
    own = D // lax.axis_size(AXIS)
    position = jnp.arange(D, dtype=i32)
    inside = position % (D // 2)
    lowest = bit_of(0) ^ (position // (D // 2))
    return (2 * (inside // own) + lowest) * own + inside % own


def permutation(order):
    return (jnp.arange(D, dtype=i32)[:, None] == order[None]).astype(bf16)


def row_permutation(order):
    return (order[:, None] == jnp.arange(D, dtype=i32)[None]).astype(bf16)


def scatter_rows(parts):
    ends = []
    for sent, kept, order in parts:
        for step, bit in enumerate(order):
            got = swap(sent, bit)
            if step + 1 == len(order):
                ends += [kept, got]
                break
            half = kept.shape[0] // 2
            sent, kept = lax.optimization_barrier(
                tuple(
                    (kept[part].astype(f32) + got[part].astype(f32)).astype(bf16)
                    for part in (slice(half, None), slice(0, half))
                )
            )
    return ends


def exchange(blocks):
    return lax.all_to_all(blocks, AXIS, split_axis=0, concat_axis=0, tiled=True)


def to_owners(slot_rows, owners):
    rows = slot_rows.reshape((E, 1, CAP) + slot_rows.shape[1:])
    rows = jnp.broadcast_to(rows, (E, owners) + rows.shape[2:])
    return rows.reshape((E * owners, CAP) + slot_rows.shape[1:])


def place(routes):
    choice = jnp.pad(routes.T, ((0, 0), (0, ROWS - SEQ)), constant_values=-1)
    ids = jnp.arange(E, dtype=i32)[:, None]
    first = (choice[:1] == ids).astype(bf16)
    second = (choice[1:] == ids).astype(bf16)
    t = jnp.arange(ROWS, dtype=i32)
    earlier = (t[:, None] < t[None, :]).astype(bf16)
    before = mm(jnp.concatenate([first, second], axis=0), earlier)
    rank0 = jnp.sum(before[:E] * first, axis=0)
    seen = before[E:] + jnp.sum(first.astype(f32), axis=1, keepdims=True)
    rank1 = jnp.sum(seen * second, axis=0)
    return choice * CAP + jnp.stack([rank0, rank1]).astype(i32)


def gelu_terms(v):
    cumulative = 0.5 * (1.0 + lax.erf(v * (1.0 / math.sqrt(2.0))))
    density = jnp.exp(-0.5 * v * v) * (1.0 / math.sqrt(2.0 * math.pi))
    return v * cumulative, cumulative + v * density


def dispatch_of(placed):
    slot = lax.broadcasted_iota(i32, (SLOTS, ROWS), 0)
    hit = (slot == placed[0:1, :]) | (slot == placed[1:2, :])
    return hit.astype(f32).astype(bf16)


def dispatch_rows(placed):
    slot = lax.broadcasted_iota(i32, (ROWS, SLOTS), 1)
    hit = (slot == placed[:, 0:1]) | (slot == placed[:, 1:2])
    return hit.astype(f32).astype(bf16)


def half_of(pair, second):
    lane = lax.broadcasted_iota(i32, pair.shape, 1)
    keep = (lane >= HEAD_DIM) if second else (lane < HEAD_DIM)
    return jnp.where(keep, pair, jnp.zeros_like(pair))


def join(first, second):
    lane = lax.broadcasted_iota(i32, first.shape, 1)
    return jnp.where(lane < HEAD_DIM, first, second)


def forward_kernel(get, outs, flush):
    slots, residual, prob, acts, norm1_o, norm2_o, context_o, router_o, out_t, small = outs
    sel = get(2)
    first, second = get(0), get(1)
    joined = lambda a, b: jnp.concatenate([a, b], axis=0)
    rest = mm(sel[...], joined(first[:, QKV_B[1] :], second[:, QKV_B[1] :]))
    out_t[...] = rest[:, :D].astype(bf16)
    flush(8)
    small[...] = rest[:, D:].astype(bf16)
    flush(9)
    vec = vectors_of(small)
    row = lambda k: vec[k : k + 1, :]
    inputs = get(3)[...].astype(f32)
    hat1, _ = normalize(inputs)
    norm1 = (hat1 * row(GAIN1) + row(SHIFT1)).astype(bf16)
    norm1_o[...] = norm1
    flush(4)
    moved = mm(norm1, sel[...]).astype(bf16)
    proj_a = mm(moved, joined(get(4)[...], get(5)[...]))
    proj_b = mm(moved, joined(first[:, : QKV_B[1]], second[:, : QKV_B[1]]))
    proj = jnp.concatenate([proj_a, proj_b], axis=1)
    acts[:, :D] = (proj[:, :D] + row(BQ)).astype(bf16)
    acts[:, D : 2 * D] = proj[:, D : 2 * D].astype(bf16)
    acts[:, 2 * D :] = (proj[:, 2 * D :] + row(BV)).astype(bf16)
    flush(3)
    token = lax.broadcasted_iota(i32, (ROWS, ROWS), 0) < SEQ

    def pair(j, _):
        at = lambda part: pl.ds(pl.multiple_of(part * D + j * 128, 128), 128)
        q = acts[:, at(0)] * jnp.asarray(SCALE, bf16)
        k, v = acts[:, at(1)], acts[:, at(2)]
        both = []
        for h in range(2):
            raised = jnp.exp(mm(half_of(k, h), q, 1, 1))
            raised = jnp.where(token, raised, 0.0)
            p = (raised * (1.0 / jnp.sum(raised, axis=0, keepdims=True))).astype(bf16)
            prob[2 * j + h, :, :] = p
            both.append(mm(p, v, 0, 0))
        context_o[:, at(0)] = join(both[0], both[1]).astype(bf16)
        return 0

    lax.fori_loop(0, PAIRS, pair, 0, unroll=UNROLL)
    flush(2)
    flush(6)
    res = inputs + mm(context_o[...], out_t[...], 1, 1) + row(BO)
    residual[...] = res
    flush(1)
    hat2, _ = normalize(res)
    norm2 = (hat2 * row(GAIN2) + row(SHIFT2)).astype(bf16)
    norm2_o[...] = norm2
    flush(5)
    slots[...] = mm(dispatch_of(get(6)[...]), norm2).astype(bf16)
    flush(0)
    lane = lax.broadcasted_iota(i32, (ROWS, 128), 1)
    logits = jnp.where(lane < E, mm(norm2, small[...]), 0.0)
    raised = jnp.where(lane < E, jnp.exp(logits), 0.0)
    router_o[...] = raised / jnp.sum(raised, axis=1, keepdims=True)
    flush(7)


class Near:
    def __init__(self, array):
        self.array = array


class Stack:
    def __init__(self, arrays, rows):
        self.arrays, self.rows = arrays, rows


class Columns:
    def __init__(self, array, start, stop):
        self.array, self.start, self.stop = array, start, stop


class Fetch:
    def __init__(self, copies, groups, refs):
        self.copies, self.groups, self.refs = copies, groups, refs
        self.begun = 0
        self.waited = set()
        self.begin(2)

    def begin(self, count):
        while self.begun < min(count, len(self.groups)):
            for k in self.groups[self.begun]:
                for copy in self.copies[k]:
                    copy.start()
            self.begun += 1

    def get(self, k):
        if k in self.copies and k not in self.waited:
            at = next(g for g, group in enumerate(self.groups) if k in group)
            self.begin(at + 1)
            for copy in self.copies[k]:
                copy.wait()
            self.waited.add(k)
            if all(m in self.waited for m in self.groups[at]):
                self.begin(at + 3)
        return self.refs[k]


def call(kernel, ins, outs, limit, temps=(), groups=None, shared=None, part=0, blank=()):
    arrays, specs, scratch, plan = [], [], [], []
    for item in ins:
        if isinstance(item, Near):
            plan.append(("near", len(arrays), None))
            arrays.append(item.array)
            specs.append(pl.BlockSpec(memory_space=pltpu.VMEM))
            continue
        if isinstance(item, Stack):
            group, shape = item.arrays, (item.rows, item.arrays[0].shape[1])
            cut = None
        elif isinstance(item, Columns):
            group, shape = [item.array], (item.array.shape[0], item.stop - item.start)
            cut = (item.start, item.stop)
        else:
            group, shape, cut = [item], item.shape, None
        plan.append(("far", list(range(len(arrays), len(arrays) + len(group))), cut))
        scratch.append(pltpu.VMEM(shape, group[0].dtype))
        for array in group:
            arrays += in_hbm(array)
            specs.append(pl.BlockSpec(memory_space=pltpu.HBM))
    n_in, n_out, n_far = len(arrays), len(outs), len(scratch)
    results_in = [pltpu.VMEM(shape, dtype) for shape, dtype in outs]
    aliases = {}
    outs = list(outs)
    if shared is not None:
        slot, buffer = shared
        aliases = {n_in: slot}
        arrays += in_hbm(buffer) + [jnp.full((1,), part, i32)]
        specs += [
            pl.BlockSpec(memory_space=pltpu.HBM), pl.BlockSpec(memory_space=pltpu.SMEM),
        ]
        outs[slot] = (buffer.shape, buffer.dtype)

    def body(*refs):
        if shared is not None:
            which = refs[n_in + 1]
            refs = refs[:n_in] + refs[n_in + 2 :]
        far_in, far_out = refs[:n_in], refs[n_in : n_in + n_out]
        near = refs[n_in + n_out + len(blank) : -1]
        sems = refs[-1]
        copies, views, used, sem = {}, [], 0, 0
        for k, (kind, index, cut) in enumerate(plan):
            if kind == "near":
                views.append(far_in[index])
                continue
            target = near[used]
            used += 1
            views.append(target)
            copies[k], row = [], 0
            for at in index:
                source = far_in[at]
                if cut is not None:
                    source = source.at[:, cut[0] : cut[1]]
                if len(target.shape) > 1 and source.shape[0] != target.shape[0]:
                    place_at = target.at[row : row + source.shape[0], :]
                else:
                    place_at = target
                row += source.shape[0]
                copies[k].append(pltpu.make_async_copy(source, place_at, sems.at[sem]))
                sem += 1
        order = groups if groups is not None else [list(range(len(plan)))]
        order = [[k for k in group if k in copies] for group in order]
        source = Fetch(copies, order, views)
        results = near[n_far : n_far + n_out]
        far_out = list(far_out)
        if shared is not None:
            rows = results[slot].shape[0]
            at = pl.multiple_of(which[0] * rows, 16)
            far_out[slot] = far_out[slot].at[pl.ds(at, rows), :]
        sinks = [
            pltpu.make_async_copy(v, f, sems.at[sem + k])
            for k, (v, f) in enumerate(zip(results, far_out))
        ]
        kernel(source.get, near[n_far:], lambda k: sinks[k].start())
        for k in copies:
            source.get(k)
        for sink in sinks:
            sink.wait()

    n_sems = sum(len(index) for kind, index, _ in plan if kind == "far") + n_out
    return pl.pallas_call(
        body,
        in_specs=specs,
        out_specs=[pl.BlockSpec(memory_space=pltpu.HBM)] * (n_out + len(blank)),
        out_shape=[pltpu.HBM(shape, dtype) for shape, dtype in outs + list(blank)],
        scratch_shapes=scratch
        + results_in
        + [pltpu.VMEM(shape, dtype) for shape, dtype in temps]
        + [pltpu.SemaphoreType.DMA((n_sems,))],
        input_output_aliases=aliases,
        compiler_params=pltpu.CompilerParams(vmem_limit_bytes=limit << 20),
    )(*arrays)


def in_hbm(*arrays):
    return [pltpu.with_memory_space_constraint(a, pltpu.HBM) for a in arrays]


def vectors_of(small):
    lane = lax.broadcasted_iota(i32, (8, 128), 1)
    pick = lane == lax.broadcasted_iota(i32, (8, 128), 0) + 2 * E
    return mm(pick.astype(f32).astype(bf16), small[...], 1, 1)


QKV_B = (0, 3 * D - CUT)
OUT_T = (3 * D - CUT, 4 * D - CUT)
SMALL = (4 * D - CUT, PACK - CUT)


def attend_forward(x, placed, halves_a, halves_b, sel):
    names = ("slots", "residual", "prob", "acts", "norm1", "norm2", "context", "router")
    names += ("out_t", "small")
    outs = call(
        forward_kernel,
        tuple(Near(half) for half in halves_b) + (sel, x)
        + tuple(Near(half) for half in halves_a) + (placed,),
        [
            ((SLOTS, D), bf16), ((ROWS, D), f32), ((HEADS, ROWS, ROWS), bf16),
            ((ROWS, 3 * D), bf16), ((ROWS, D), bf16), ((ROWS, D), bf16), ((ROWS, D), bf16),
            ((ROWS, 128), f32), ((D, D), bf16), ((D, 128), bf16),
        ],
        12,
    )
    return dict(zip(names, outs))


def backward_kernel(get, outs, flush):
    input_grad, gate_o, ph, res_half_o, logit_o, sums, cgs = outs
    rec, placed, small, cot = get(0), get(1), get(2), get(3)
    vec = vectors_of(small)
    row = lambda k: vec[k : k + 1, :]
    disp = dispatch_rows(placed[...])
    lane = lax.broadcasted_iota(i32, (SLOTS, 128), 1)
    slot_expert = lax.broadcasted_iota(i32, (SLOTS, 128), 0) // CAP
    moe = 0.0
    pg = 0.0
    for o in range(rec.shape[1]):
        rows = rec[:, o, :, :].reshape(SLOTS, D + 128)
        moe = moe + mm(disp, rows[:, :D])
        gg = jnp.where((lane & 63) == slot_expert, rows[:, D:], jnp.zeros((SLOTS, 128), bf16))
        pg = pg + mm(disp, gg)
    pg = pg + pltpu.roll(pg, 64, 1)
    hot = mm(disp, (lane == slot_expert).astype(f32).astype(bf16))
    pg = (pg + pltpu.roll(mm(cot[...], small[...]), 128 - E, 1)) * hot
    prob_r = get(4)[...]
    gate_o[...] = prob_r * hot
    flush(1)
    logit = prob_r * (pg - jnp.sum(pg * prob_r, axis=1, keepdims=True))
    real = lax.broadcasted_iota(i32, (ROWS, 1), 0) < SEQ
    logit = jnp.where(real, logit, 0.0).astype(bf16)
    logit_o[...] = logit
    flush(4)
    second = moe + mm(logit, small[...], 1, 1)
    hat2, rstd2 = normalize(get(5)[...])
    sums[GAIN2 : GAIN2 + 1, :] = jnp.sum(second * hat2, axis=0, keepdims=True)
    sums[SHIFT2 : SHIFT2 + 1, :] = jnp.sum(second, axis=0, keepdims=True)
    res_grad = cot[...].astype(f32) + norm_back(second * row(GAIN2), hat2, rstd2)
    input_grad[...] = res_grad
    sums[BO : BO + 1, :] = jnp.sum(res_grad, axis=0, keepdims=True)
    res_half = res_grad.astype(bf16)
    res_half_o[...] = res_half
    flush(3)
    cgs[...] = mm(res_half, get(6)[...]).astype(bf16)
    prob, acts = get(7), get(8)

    def pair(j, _):
        at = lambda part: pl.ds(pl.multiple_of(part * D + j * 128, 128), 128)
        q, k, v = acts[:, at(0)], acts[:, at(1)], acts[:, at(2)]
        c = cgs[:, at(0)]
        qs, ks, vs = [], [], []
        for h in range(2):
            p = prob[2 * j + h, :, :]
            pf = p.astype(f32)
            t = pf * mm(half_of(v, h), c, 1, 1)
            sg = ((t - pf * jnp.sum(t, axis=0, keepdims=True)) * SCALE).astype(bf16)
            vs.append(mm(p, c))
            qs.append(mm(sg, k, 0, 0))
            ks.append(mm(sg, q))
        qg, kg, vg = join(*qs), join(*ks), join(*vs)
        sums[BQ : BQ + 1, at(0)] = jnp.sum(qg, axis=0, keepdims=True)
        sums[BV : BV + 1, at(0)] = jnp.sum(vg, axis=0, keepdims=True)
        ph[:, at(0)] = qg.astype(bf16)
        ph[:, at(1)] = kg.astype(bf16)
        ph[:, at(2)] = vg.astype(bf16)
        return 0

    lax.fori_loop(0, PAIRS, pair, 0, unroll=UNROLL)
    flush(2)
    first = mm(ph[:, :CUT], get(9)[...], 1, 1) + mm(ph[:, CUT:], get(10)[...], 1, 1)
    hat1, rstd1 = normalize(get(11)[...].astype(f32))
    sums[GAIN1 : GAIN1 + 1, :] = jnp.sum(first * hat1, axis=0, keepdims=True)
    sums[SHIFT1 : SHIFT1 + 1, :] = jnp.sum(first, axis=0, keepdims=True)
    sums[7:8, :] = jnp.zeros((1, D), f32)
    flush(5)
    input_grad[...] += norm_back(first * row(GAIN1), hat1, rstd1)
    flush(0)


BACKWARD_TEMPS = [
    ((ROWS, 3 * D), bf16), ((ROWS, D), bf16), ((ROWS, 128), bf16), ((8, D), f32),
]


def backward_operands(rec, x, cot, placed, s, qkv_a, qkv_b, out_t, small):
    return (
        rec, placed, small, cot, s["router"], s["residual"], out_t, s["prob"],
        s["acts"], qkv_a, qkv_b, x,
    )


BACKWARD_GROUPS = [[0, 1, 2, 3, 4, 5], [6, 7, 8], [9, 10, 11]]


def token_backward(part, buffer, *args):
    return call(
        backward_kernel,
        backward_operands(*args),
        [((ROWS, D), f32), ((ROWS, 128), f32)] + BACKWARD_TEMPS,
        14 + 4 * args[0].shape[1],
        [((ROWS, D), bf16)],
        BACKWARD_GROUPS,
        (2, buffer),
        part,
    )


def expert_kernel(
    idx, x, c, w_in, w_out, bias, router, act, back, d_rows, gated, gate, grad_bias, acc, gg
):
    r, f = pl.program_id(0), pl.program_id(1)
    rows, width = act.shape

    @pl.when(f == 0)
    def _():
        logits = mm(x[...], router[...])
        lane = lax.broadcasted_iota(i32, logits.shape, 1)
        raised = jnp.where(lane < E, jnp.exp(jnp.where(lane < E, logits, 0.0)), 0.0)
        picked = lane == idx[0]
        g = jnp.sum(jnp.where(picked, raised, 0.0), axis=1, keepdims=True)
        g = g / jnp.sum(raised, axis=1, keepdims=True)
        gate[...] = jnp.broadcast_to(g, gate.shape)
        rows_c = c[...].reshape(rows, D).astype(f32)
        gated[...] = (rows_c * g).astype(bf16)
        gg[...] = jnp.zeros_like(gg)
        acc[...] = jnp.zeros_like(acc)

    value, slope = gelu_terms(mm(x[...], w_in[...], 1, 1) + bias[...])
    hid = mm(c[...].reshape(rows, D), w_out[...], 1, 1)
    act[...] = value.astype(bf16)
    both = value * hid
    part = both[:, :128]
    for j in range(1, width // 128):
        part = part + both[:, j * 128 : (j + 1) * 128]
    gg[...] += part
    before = hid * slope * gate[:, :1]
    total = jnp.sum(before, axis=0, keepdims=True)
    half = before.astype(bf16)
    back[...] = half
    acc[...] += mm(half, w_in[...])
    cols = pl.ds(pl.multiple_of(f * width, width), width)

    @pl.when(r == 0)
    def _():
        grad_bias[:, cols] = total

    @pl.when(r > 0)
    def _():
        grad_bias[:, cols] += total

    @pl.when(f == pl.num_programs(1) - 1)
    def _():
        d_rows[:, :D] = acc[...].astype(bf16)
        g = jnp.sum(gg[...], axis=1, keepdims=True)
        high = g.astype(bf16)
        low = (g - high.astype(f32)).astype(bf16)
        lane = lax.broadcasted_iota(i32, (rows, 128), 1)
        d_rows[:, D:] = jnp.where(
            lane < 64, jnp.broadcast_to(high, lane.shape), jnp.broadcast_to(low, lane.shape)
        )


def expert_main(i, x, c, w_in, w_out, bias, router, expert):
    total, width = x.shape[0], w_in.shape[0]
    rb, fb = min(512, total), min(768, width)
    row = lambda r, f, *_: (r, 0)
    tile = lambda r, f, *_: (r, f)
    fixed = lambda r, f, *_: (0, 0)
    return pl.pallas_call(
        expert_kernel,
        grid_spec=pltpu.PrefetchScalarGridSpec(
            num_scalar_prefetch=1,
            grid=(total // rb, width // fb),
            in_specs=[
                pl.BlockSpec((rb, D), row),
                pl.BlockSpec((rb // CAP, None, CAP, D), lambda r, f, idx: (r, idx[1], 0, 0)),
                pl.BlockSpec((fb, D), lambda r, f, *_: (f, 0)),
                pl.BlockSpec((fb, D), lambda r, f, *_: (f, 0)),
                pl.BlockSpec((1, fb), lambda r, f, *_: (0, f)),
                pl.BlockSpec((D, 128), fixed),
            ],
            out_specs=[
                pl.BlockSpec((rb, fb), tile),
                pl.BlockSpec((rb, fb), tile),
                pl.BlockSpec((rb, D + 128), row),
                pl.BlockSpec((rb, D), row),
                pl.BlockSpec((rb, 128), row),
                pl.BlockSpec((1, width), fixed),
            ],
            scratch_shapes=[
                pltpu.VMEM((rb, D), f32),
                pltpu.VMEM((rb, 128), f32),
            ],
        ),
        out_shape=[
            pltpu.HBM((total, width), bf16),
            pltpu.HBM((total, width), bf16),
            pltpu.HBM((total, D + 128), bf16),
            pltpu.HBM((total, D), bf16),
            pltpu.HBM((total, 128), f32),
            pltpu.HBM((1, width), f32),
        ],
        compiler_params=pltpu.CompilerParams(
            dimension_semantics=("arbitrary", "arbitrary"), vmem_limit_bytes=22 << 20
        ),
        name="expert_main",
    )(jnp.stack([expert, jnp.int32(i)]), *in_hbm(x, c, w_in, w_out, bias.reshape(1, width), router))


def parts_kernel(act0, act1, gate0, gate1, w_out, out, acc):
    f = pl.program_id(0)

    @pl.when(f == 0)
    def _():
        acc[...] = jnp.zeros_like(acc)

    for i, act in enumerate((act0, act1)):
        acc[i] += mm(act[...], w_out[...])

    @pl.when(f == pl.num_programs(0) - 1)
    def _():
        for i, gate in enumerate((gate0, gate1)):
            rows = (acc[i] * gate[:, :1]).astype(bf16)
            out[:, i, :, :] = rows.reshape(out.shape[0], CAP, D)


def expert_parts(acts, gates, w_out):
    total, width = acts[0].shape
    fb = min(768, width)
    n = total // CAP
    cols = pl.BlockSpec((total, fb), lambda f: (0, f))
    full = pl.BlockSpec((total, 128), lambda f: (0, 0))
    return pl.pallas_call(
        parts_kernel,
        grid=(width // fb,),
        in_specs=[cols, cols, full, full, pl.BlockSpec((fb, D), lambda f: (f, 0))],
        out_specs=pl.BlockSpec((n, 2, CAP, D), lambda f: (0, 0, 0, 0)),
        out_shape=pltpu.HBM((n, 2, CAP, D), bf16),
        scratch_shapes=[pltpu.VMEM((2, total, D), f32)],
        compiler_params=pltpu.CompilerParams(
            dimension_semantics=("arbitrary",),
            vmem_limit_bytes=(18 if total <= 512 else 48) << 20,
        ),
        name="expert_parts",
    )(*in_hbm(*acts, *gates, w_out))


def moved_kernel(get, outs, flush):
    for k, (value, perm) in enumerate(((0, 3), (0, 4), (1, 4), (2, 4))):
        outs[k][...] = mm(get(perm)[...], get(value)[...], 1, 1).astype(bf16)
        flush(k)


def rest_kernel(get, outs, flush):
    sent_b, kept_b = outs
    half = D // 2

    def lay(value, start):
        kept_b[:, start : start + value.shape[1]] = value[:half].astype(bf16)
        sent_b[:, start : start + value.shape[1]] = value[half:].astype(bf16)

    lay(mm(get(0)[...], get(1)[...]), 0)
    perm = get(2)[...]
    out = mm(mm(perm, get(3)[...], 1, 1).astype(bf16), get(4)[...])
    lay(out, OUT_T[0])
    sums = get(5)[...] + get(6)[...]
    zeros = lambda n: jnp.zeros((n, D), f32)
    spread = jnp.concatenate([zeros(2 * E), sums, zeros(128 - 2 * E - 8)], axis=0)
    tail = mm(perm, spread.astype(bf16), 1, 1) + mm(get(7)[...], get(9)[...])
    tail = tail + mm(get(8)[...], pltpu.roll(get(10)[...], E, 1).astype(bf16))
    lay(tail, SMALL[0])
    flush(0)
    flush(1)


def eye(size, width=None, shift=0):
    shape = (size, width or size)
    hit = lax.broadcasted_iota(i32, shape, 1) == lax.broadcasted_iota(i32, shape, 0) + shift
    return hit.astype(f32).astype(bf16)


def pack_kernel(get, outs, flush):
    packed = outs[0]
    w_qkv, w_out, router, bias = (get(k) for k in range(4))
    own = w_qkv.shape[0]
    packed[0, :, : 3 * D] = w_qkv[...]
    packed[0, :, 3 * D : 4 * D] = w_out[...]
    rows = [get(4 + k)[...].astype(f32).reshape(1, own) for k in range(VECTORS)]
    rows = jnp.concatenate(rows + [jnp.zeros((1, own), f32)], axis=0).astype(bf16)
    columns = mm(eye(own), rows, 1, 1).astype(bf16)
    tail = mm(router[...], eye(E, 128)) + mm(bias[...], eye(E, 128, E))
    tail = tail + mm(columns, eye(8, 128, 2 * E))
    packed[0, :, 4 * D :] = tail.astype(bf16)
    flush(0)


def unpack_kernel(get, outs, flush):
    w_qkv, w_out, router, bias = outs[:4]
    add = lambda k: get(k)[...].astype(f32) + get(k + 1)[...].astype(f32)
    w_qkv[:, :CUT] = add(0)
    mine = add(2)
    w_qkv[:, CUT:] = mine[:, QKV_B[0] : QKV_B[1]]
    flush(0)
    w_out[...] = mine[:, OUT_T[0] : OUT_T[1]]
    flush(1)
    tail = mine[:, SMALL[0] :]
    router[...] = tail[:, :E]
    flush(2)
    bias[...] = tail[:, E : 2 * E]
    flush(3)
    rows = sum(mm(eye(8, 128, 2 * E), p, 1, 1) for p in pieces(tail, 3))
    for k in range(VECTORS):
        outs[4 + k][...] = rows[k]
        flush(4 + k)


def output_kernel(get, outs, flush):
    block_out, input_grad = outs
    small, parts = get(0), get(1)
    for i in range(2):
        placed, residual, gate, grad = (get(2 + 4 * i + k) for k in range(4))
        input_grad[i * SEQ : (i + 1) * SEQ, :] = grad[:SEQ, :]
        disp = dispatch_rows(placed[...])
        out = residual[...]
        for o in range(parts.shape[1]):
            out = out + mm(disp, parts[:, o, i, :, :].reshape(SLOTS, D))
        for p in pieces(pltpu.roll(gate[...], E, 1), 2):
            out = out + mm(p, small[...], 1, 1)
        block_out[i * SEQ : (i + 1) * SEQ, :] = out[:SEQ]
    flush(0)
    flush(1)


def weights_kernel(act0, act1, back0, back1, g0, g1, x0, x1, out_w, in_w):
    out_w[...] = mm(act0[...], g0[...], 0, 0) + mm(act1[...], g1[...], 0, 0)
    in_w[...] = mm(back0[...], x0[...], 0, 0) + mm(back1[...], x1[...], 0, 0)


def expert_weights(acts, backs, gated, xs):
    total, width = acts[0].shape
    fb = min(512, width)
    cols = pl.BlockSpec((total, fb), lambda f: (0, f))
    full = pl.BlockSpec((total, D), lambda f: (0, 0))
    rows = pl.BlockSpec((fb, D), lambda f: (f, 0))
    return pl.pallas_call(
        weights_kernel,
        grid=(width // fb,),
        in_specs=[cols] * 4 + [full] * 4,
        out_specs=[rows, rows],
        out_shape=[pltpu.HBM((width, D), f32)] * 2,
        compiler_params=pltpu.CompilerParams(
            dimension_semantics=("arbitrary",),
            vmem_limit_bytes=(22 if total <= 512 else 40) << 20,
        ),
        name="expert_weights",
    )(*in_hbm(*acts, *backs, *gated, *xs))


def on_device(
    block_in, out_cotangent, expert_routes, ln1_gain, ln1_shift, w_qkv, bias_query, bias_value,
    w_out, bias_out, ln2_gain, ln2_shift, w_router, expert_bias, w_expert_in, bias_hidden,
    w_expert_out,
):
    images = block_in.shape[0] // SEQ
    n = lax.axis_size(AXIS)
    owners = n // E
    own = ln1_gain.shape[0]
    expert = lax.axis_index(AXIS) // owners
    order_a, order_b = bit_orders()
    barrier = lax.optimization_barrier
    (shard,) = call(
        pack_kernel,
        (w_qkv, w_out.T, w_router, expert_bias.T)
        + (ln1_gain, ln1_shift, bias_query, bias_value, bias_out, ln2_gain, ln2_shift),
        [((1, own, PACK), bf16)],
        8,
    )

    pad_rows = ((0, ROWS - SEQ), (0, 0))
    xs, cots, placed, states, outgoing = [], [], [], [], []
    for i in range(images):
        xs.append(jnp.pad(block_in[i * SEQ : (i + 1) * SEQ], pad_rows))
        cots.append(jnp.pad(out_cotangent[i * SEQ : (i + 1) * SEQ], pad_rows))
        placed.append(place(expert_routes[i * SEQ : (i + 1) * SEQ]))
        slots = mm(dispatch_of(placed[i]), cots[i]).astype(bf16)
        outgoing.append(to_owners(slots, owners))
    late = (
        xs, cots, [p.T for p in placed], permutation(pair_order()),
        row_permutation(owner_order(order_a)), row_permutation(owner_order(order_b)),
    )
    halves, outgoing, late = gather_rows(shard, 3, jnp.stack(outgoing, axis=1), late)
    xs, cots, columns, sel, perm_a, perm_b = late
    flat = [tuple(h.reshape(D // 2, h.shape[-1]) for h in pair) for pair in halves]
    cot_in = exchange(outgoing)
    for i in range(images):
        states.append(attend_forward(xs[i], placed[i], flat[0], flat[1], sel))
    both = lambda key: [s[key] for s in states]
    norm1a, norm1b, norm2b, cotb, ph = call(
        moved_kernel,
        (Stack(both("norm1"), 2 * ROWS), Stack(both("norm2"), 2 * ROWS))
        + (Stack(cots, 2 * ROWS), perm_a, perm_b),
        [((D, 2 * ROWS), bf16)] * 4,
        12,
        blank=[((images * ROWS, 3 * D), bf16)],
    )
    first = exchange(to_owners(states[0]["slots"], owners))
    second = exchange(to_owners(states[1]["slots"], owners))
    arrived = [first.reshape(-1, D), second.reshape(-1, D)]
    small, out_t = states[0]["small"], states[0]["out_t"]
    rest = list(range(lax.axis_size(AXIS).bit_length() - 1))[1:]
    natural = [
        merged(mine, theirs, 0, rest)
        for mine, theirs in (halves[0], tuple(h[..., : QKV_B[1]] for h in halves[1]))
    ]
    qkv_a, qkv_b = [v.reshape(D, v.shape[-1]) for v in natural]
    done = []
    grad_hidden = 0.0
    received = []
    for i in range(images):
        act, back, d_rows, gated, gate, gb = expert_main(
            i, arrived[i], cot_in, w_expert_in, w_expert_out, bias_hidden, small, expert
        )
        done.append((act, back, gated, gate))
        grad_hidden = grad_hidden + gb[0]
        if i == 1:
            d_rows, qkv_a, qkv_b = barrier((d_rows, qkv_a, qkv_b))
        rows = exchange(d_rows.reshape(n, CAP, D + 128))
        received.append(rows.reshape(E, owners, CAP, D + 128))
    sent = expert_parts([d[0] for d in done], [d[3] for d in done], w_expert_out)
    parts = exchange(sent).reshape(E, owners, images, CAP, D)
    column = lambda k: [d[k] for d in done]
    grad_expert_out, grad_expert_in = expert_weights(
        column(0), column(1), column(2), arrived
    )
    back = []
    for i in range(images):
        results = token_backward(
            i, ph, received[i], xs[i], cots[i], columns[i], states[i],
            qkv_a, qkv_b, out_t, small,
        )
        ph = results[2]
        back.append(results)
    pair = lambda k: [b[k] for b in back]
    sent_a = mm(norm1a[D // 2 :], ph[:, :CUT]).astype(bf16)
    kept_a = mm(norm1a[: D // 2], ph[:, :CUT]).astype(bf16)
    sent_b, kept_b = call(
        rest_kernel,
        (norm1b, Columns(ph, CUT, 3 * D), perm_b, Stack(pair(3), 2 * ROWS))
        + (Stack(both("context"), 2 * ROWS),) + tuple(pair(5))
        + (norm2b, cotb, Stack(pair(4), 2 * ROWS), Stack(pair(1), 2 * ROWS)),
        [((D // 2, PACK - CUT), bf16)] * 2,
        24,
        (),
        [[0, 1], [2, 3, 4], [5, 6, 7, 8, 9, 10]],
    )
    ends = scatter_rows([(sent_a, kept_a, order_a), (sent_b, kept_b, order_b)])
    block_out, input_grad = call(
        output_kernel,
        (small, Near(parts), columns[0], states[0]["residual"], back[0][1], back[0][0])
        + (columns[1], states[1]["residual"], back[1][1], back[1][0]),
        [((images * SEQ, D), f32)] * 2,
        6 + 6 * owners,
    )
    grad_qkv, grad_out, grad_router, grad_bias, *vec = call(
        unpack_kernel,
        tuple(Near(end) for end in ends),
        [(shape, f32) for shape in ((own, 3 * D), (own, D), (own, E), (own, E))]
        + [((own,), f32)] * VECTORS,
        8,
    )
    return (
        block_out, input_grad, vec[GAIN1], vec[SHIFT1], grad_qkv, vec[BQ], vec[BV],
        grad_out.T, vec[BO], vec[GAIN2], vec[SHIFT2], grad_router, grad_bias.T,
        grad_expert_in, grad_hidden, grad_expert_out,
    )


def solution(mesh):
    rows, line, cols = P(AXIS, None), P(AXIS), P(None, AXIS)
    in_specs = (
        rows, rows, rows, line, line, rows, line, line, cols, line, line, line, rows, cols,
        rows, line, rows,
    )
    out_specs = (
        rows, rows, line, line, rows, line, line, cols, line, line, line, rows, cols, rows,
        line, rows,
    )

    return jax.shard_map(
        on_device, mesh=mesh, in_specs=in_specs, out_specs=out_specs, check_vma=False
    )
```

```python
import math

import jax
import jax.numpy as jnp
from jax import lax
from jax.experimental import pallas as pl
from jax.experimental.pallas import tpu as pltpu
from jax.sharding import PartitionSpec as P

D = 768
HEADS = 12
HEAD_DIM = 64
PAIRS = HEADS // 2
E = 32
SEQ = 197
ROWS = 208
CAP = 16
SLOTS = E * CAP
AXIS = "fsdp"
PACK = 3200
CUT = 1664
GAIN1, SHIFT1, BQ, BV, BO, GAIN2, SHIFT2, VECTORS = range(8)
SCALE = 1.0 / math.sqrt(HEAD_DIM)
UNROLL = PAIRS

epsilon = 1e-06
f32 = jnp.float32
bf16 = jnp.bfloat16
i32 = jnp.int32


def mm(a, b, ca=1, cb=0):
    return lax.dot_general(a, b, (((ca,), (cb,)), ((), ())), preferred_element_type=f32)


def pieces(v, n):
    out = []
    for _ in range(n):
        p = v.astype(bf16)
        out.append(p)
        v = v - p.astype(f32)
    return out


def normalize(values):
    centered = values - jnp.mean(values, axis=-1, keepdims=True)
    inverse = lax.rsqrt(jnp.mean(centered * centered, axis=-1, keepdims=True) + epsilon)
    return (centered * inverse, inverse)


def norm_back(upstream, normed, inverse):
    return inverse * (
        upstream
        - jnp.mean(upstream, axis=-1, keepdims=True)
        - normed * jnp.mean(upstream * normed, axis=-1, keepdims=True)
    )


def swap(values, bit):
    n = lax.axis_size(AXIS)
    return lax.ppermute(values, AXIS, [(d, d ^ (1 << bit)) for d in range(n)])


def bit_of(bit):
    return (lax.axis_index(AXIS) >> bit) & 1


def bit_orders():
    bits = lax.axis_size(AXIS).bit_length() - 1
    inner = (bits - 1) // 3 if bits != 5 else 1
    x = list(range(1, 1 + inner))
    y = list(range(1 + inner, 1 + 2 * inner))
    z = list(range(1 + 2 * inner, bits))
    return [0] + x + y + z, [0] + y + x + z


def merged(values, other, bit, done):
    at = sum(1 for b in done if b > bit)
    lead = values.shape[0]
    high = 1 << at
    mine = values.reshape((high, lead // high) + values.shape[1:])
    other = other.reshape(mine.shape)
    which = lax.broadcasted_iota(i32, (1, 2, 1, 1, 1), 1) == bit_of(bit)
    both = jnp.where(which, mine[:, None], other[:, None])
    return both.reshape((2 * lead,) + values.shape[1:])


def gather_rows(shard, early, wait_for, late):
    orders = bit_orders()
    steps = len(orders[0])
    common = 0
    while orders[0][-1 - common] == orders[1][-1 - common]:
        common += 1
    held, done = shard, []
    for step in range(common):
        bit = orders[0][-1 - step]
        held = lax.optimization_barrier(merged(held, swap(held, bit), bit, done))
        done.append(bit)
    held = [(held[..., :CUT], list(done)), (held[..., CUT:], list(done))]
    for step in range(common, steps):
        bits = [order[-1 - step] for order in orders]
        theirs = []
        for (values, _), bit in zip(held, bits):
            theirs.append(swap(values, bit))
        if step + 1 == steps:
            pairs = [(values, other) for (values, _), other in zip(held, theirs)]
            return pairs, wait_for, late
        tied = [
            merged(values, other, bit, seen)
            for (values, seen), other, bit in zip(held, theirs, bits)
        ]
        if step + 1 == early:
            tied.append(wait_for)
        if step + 2 == steps:
            tied, late = lax.optimization_barrier((tied, late))
        else:
            tied = lax.optimization_barrier(tied)
        if step + 1 == early:
            wait_for = tied[-1]
        held = [(t, seen + [bit]) for t, (_, seen), bit in zip(tied, held, bits)]


def owner_order(order):
    n = lax.axis_size(AXIS)
    own = D // n
    position = jnp.arange(D, dtype=i32)
    chunk = position // own
    owner = jnp.zeros_like(chunk)
    for step, bit in enumerate(order):
        owner = owner | (((chunk >> (len(order) - 1 - step)) & 1) << bit)
    return (owner ^ lax.axis_index(AXIS)) * own + position % own


def pair_order():
    own = D // lax.axis_size(AXIS)
    position = jnp.arange(D, dtype=i32)
    inside = position % (D // 2)
    lowest = bit_of(0) ^ (position // (D // 2))
    return (2 * (inside // own) + lowest) * own + inside % own


def permutation(order):
    return (jnp.arange(D, dtype=i32)[:, None] == order[None]).astype(bf16)


def row_permutation(order):
    return (order[:, None] == jnp.arange(D, dtype=i32)[None]).astype(bf16)


def scatter_rows(parts):
    ends = []
    for sent, kept, order in parts:
        for step, bit in enumerate(order):
            got = swap(sent, bit)
            if step + 1 == len(order):
                ends += [kept, got]
                break
            half = kept.shape[0] // 2
            sent, kept = lax.optimization_barrier(
                tuple(
                    (kept[part].astype(f32) + got[part].astype(f32)).astype(bf16)
                    for part in (slice(half, None), slice(0, half))
                )
            )
    return ends


def exchange(blocks):
    return lax.all_to_all(blocks, AXIS, split_axis=0, concat_axis=0, tiled=True)


def to_owners(slot_rows, owners):
    rows = slot_rows.reshape((E, 1, CAP) + slot_rows.shape[1:])
    rows = jnp.broadcast_to(rows, (E, owners) + rows.shape[2:])
    return rows.reshape((E * owners, CAP) + slot_rows.shape[1:])


def place(routes):
    choice = jnp.pad(routes.T, ((0, 0), (0, ROWS - SEQ)), constant_values=-1)
    ids = jnp.arange(E, dtype=i32)[:, None]
    first = (choice[:1] == ids).astype(bf16)
    second = (choice[1:] == ids).astype(bf16)
    t = jnp.arange(ROWS, dtype=i32)
    earlier = (t[:, None] < t[None, :]).astype(bf16)
    before = mm(jnp.concatenate([first, second], axis=0), earlier)
    rank0 = jnp.sum(before[:E] * first, axis=0)
    seen = before[E:] + jnp.sum(first.astype(f32), axis=1, keepdims=True)
    rank1 = jnp.sum(seen * second, axis=0)
    return choice * CAP + jnp.stack([rank0, rank1]).astype(i32)


def gelu_terms(v):
    cumulative = 0.5 * (1.0 + lax.erf(v * (1.0 / math.sqrt(2.0))))
    density = jnp.exp(-0.5 * v * v) * (1.0 / math.sqrt(2.0 * math.pi))
    return v * cumulative, cumulative + v * density


def dispatch_of(placed):
    slot = lax.broadcasted_iota(i32, (SLOTS, ROWS), 0)
    hit = (slot == placed[0:1, :]) | (slot == placed[1:2, :])
    return hit.astype(f32).astype(bf16)


def dispatch_rows(placed):
    slot = lax.broadcasted_iota(i32, (ROWS, SLOTS), 1)
    hit = (slot == placed[:, 0:1]) | (slot == placed[:, 1:2])
    return hit.astype(f32).astype(bf16)


def half_of(pair, second):
    lane = lax.broadcasted_iota(i32, pair.shape, 1)
    keep = (lane >= HEAD_DIM) if second else (lane < HEAD_DIM)
    return jnp.where(keep, pair, jnp.zeros_like(pair))


def join(first, second):
    lane = lax.broadcasted_iota(i32, first.shape, 1)
    return jnp.where(lane < HEAD_DIM, first, second)


def forward_kernel(get, outs, flush):
    slots, residual, prob, acts, norm1_o, context_o, router_o, out_t, small, norm2_o = outs
    sel = get(2)
    first, second = get(0), get(1)
    joined = lambda a, b: jnp.concatenate([a, b], axis=0)
    rest = mm(sel[...], joined(first[:, QKV_B[1] :], second[:, QKV_B[1] :]))
    out_t[...] = rest[:, :D].astype(bf16)
    flush(7)
    small[...] = rest[:, D:].astype(bf16)
    flush(8)
    vec = vectors_of(small)
    row = lambda k: vec[k : k + 1, :]
    inputs = get(3)[...].astype(f32)
    hat1, _ = normalize(inputs)
    norm1 = (hat1 * row(GAIN1) + row(SHIFT1)).astype(bf16)
    norm1_o[...] = norm1
    flush(4)
    moved = mm(norm1, sel[...]).astype(bf16)
    proj_a = mm(moved, joined(get(4)[...], get(5)[...]))
    proj_b = mm(moved, joined(first[:, : QKV_B[1]], second[:, : QKV_B[1]]))
    proj = jnp.concatenate([proj_a, proj_b], axis=1)
    acts[:, :D] = (proj[:, :D] + row(BQ)).astype(bf16)
    acts[:, D : 2 * D] = proj[:, D : 2 * D].astype(bf16)
    acts[:, 2 * D :] = (proj[:, 2 * D :] + row(BV)).astype(bf16)
    flush(3)
    token = lax.broadcasted_iota(i32, (ROWS, ROWS), 0) < SEQ

    def pair(j, _):
        at = lambda part: pl.ds(pl.multiple_of(part * D + j * 128, 128), 128)
        q = acts[:, at(0)] * jnp.asarray(SCALE, bf16)
        k, v = acts[:, at(1)], acts[:, at(2)]
        both = []
        for h in range(2):
            raised = jnp.exp(mm(half_of(k, h), q, 1, 1))
            raised = jnp.where(token, raised, 0.0)
            p = (raised * (1.0 / jnp.sum(raised, axis=0, keepdims=True))).astype(bf16)
            prob[2 * j + h, :, :] = p
            both.append(mm(p, v, 0, 0))
        context_o[:, at(0)] = join(both[0], both[1]).astype(bf16)
        return 0

    lax.fori_loop(0, PAIRS, pair, 0, unroll=UNROLL)
    flush(2)
    flush(5)
    res = inputs + mm(context_o[...], out_t[...], 1, 1) + row(BO)
    residual[...] = res
    flush(1)
    hat2, _ = normalize(res)
    norm2 = (hat2 * row(GAIN2) + row(SHIFT2)).astype(bf16)
    norm2_o[...] = norm2
    slots[...] = mm(dispatch_of(get(6)[...]), norm2).astype(bf16)
    flush(0)
    lane = lax.broadcasted_iota(i32, (ROWS, 128), 1)
    logits = jnp.where(lane < E, mm(norm2, small[...]), 0.0)
    raised = jnp.where(lane < E, jnp.exp(logits), 0.0)
    router_o[...] = raised / jnp.sum(raised, axis=1, keepdims=True)
    flush(6)


class Near:
    def __init__(self, array):
        self.array = array


class Stack:
    def __init__(self, arrays, rows):
        self.arrays, self.rows = arrays, rows


class Columns:
    def __init__(self, array, start, stop):
        self.array, self.start, self.stop = array, start, stop


class Fetch:
    def __init__(self, copies, groups, refs):
        self.copies, self.groups, self.refs = copies, groups, refs
        self.begun = 0
        self.waited = set()
        self.begin(2)

    def begin(self, count):
        while self.begun < min(count, len(self.groups)):
            for k in self.groups[self.begun]:
                for copy in self.copies[k]:
                    copy.start()
            self.begun += 1

    def get(self, k):
        if k in self.copies and k not in self.waited:
            at = next(g for g, group in enumerate(self.groups) if k in group)
            self.begin(at + 1)
            for copy in self.copies[k]:
                copy.wait()
            self.waited.add(k)
            if all(m in self.waited for m in self.groups[at]):
                self.begin(at + 3)
        return self.refs[k]


def call(kernel, ins, outs, limit, temps=(), groups=None, shared=None, part=0, blank=()):
    arrays, specs, scratch, plan = [], [], [], []
    for item in ins:
        if isinstance(item, Near):
            plan.append(("near", len(arrays), None))
            arrays.append(item.array)
            specs.append(pl.BlockSpec(memory_space=pltpu.VMEM))
            continue
        if isinstance(item, Stack):
            group, shape = item.arrays, (item.rows, item.arrays[0].shape[1])
            cut = None
        elif isinstance(item, Columns):
            group, shape = [item.array], (item.array.shape[0], item.stop - item.start)
            cut = (item.start, item.stop)
        else:
            group, shape, cut = [item], item.shape, None
        plan.append(("far", list(range(len(arrays), len(arrays) + len(group))), cut))
        scratch.append(pltpu.VMEM(shape, group[0].dtype))
        for array in group:
            arrays += in_hbm(array)
            specs.append(pl.BlockSpec(memory_space=pltpu.HBM))
    n_in, n_out, n_far = len(arrays), len(outs), len(scratch)
    results_in = [pltpu.VMEM(shape, dtype) for shape, dtype in outs]
    aliases = {}
    outs = list(outs)
    if shared is not None:
        slot, buffer = shared
        aliases = {n_in: slot}
        arrays += in_hbm(buffer) + [jnp.full((1,), part, i32)]
        specs += [
            pl.BlockSpec(memory_space=pltpu.HBM), pl.BlockSpec(memory_space=pltpu.SMEM),
        ]
        outs[slot] = (buffer.shape, buffer.dtype)

    def body(*refs):
        if shared is not None:
            which = refs[n_in + 1]
            refs = refs[:n_in] + refs[n_in + 2 :]
        far_in, far_out = refs[:n_in], refs[n_in : n_in + n_out]
        near = refs[n_in + n_out + len(blank) : -1]
        sems = refs[-1]
        copies, views, used, sem = {}, [], 0, 0
        for k, (kind, index, cut) in enumerate(plan):
            if kind == "near":
                views.append(far_in[index])
                continue
            target = near[used]
            used += 1
            views.append(target)
            copies[k], row = [], 0
            for at in index:
                source = far_in[at]
                if cut is not None:
                    source = source.at[:, cut[0] : cut[1]]
                if len(target.shape) > 1 and source.shape[0] != target.shape[0]:
                    place_at = target.at[row : row + source.shape[0], :]
                else:
                    place_at = target
                row += source.shape[0]
                copies[k].append(pltpu.make_async_copy(source, place_at, sems.at[sem]))
                sem += 1
        order = groups if groups is not None else [list(range(len(plan)))]
        order = [[k for k in group if k in copies] for group in order]
        source = Fetch(copies, order, views)
        results = near[n_far : n_far + n_out]
        far_out = list(far_out)
        if shared is not None:
            rows = results[slot].shape[0]
            at = pl.multiple_of(which[0] * rows, 16)
            far_out[slot] = far_out[slot].at[pl.ds(at, rows), :]
        sinks = [
            pltpu.make_async_copy(v, f, sems.at[sem + k])
            for k, (v, f) in enumerate(zip(results, far_out))
        ]
        kernel(source.get, near[n_far:], lambda k: sinks[k].start())
        for k in copies:
            source.get(k)
        for sink in sinks:
            sink.wait()

    n_sems = sum(len(index) for kind, index, _ in plan if kind == "far") + n_out
    return pl.pallas_call(
        body,
        in_specs=specs,
        out_specs=[pl.BlockSpec(memory_space=pltpu.HBM)] * (n_out + len(blank)),
        out_shape=[pltpu.HBM(shape, dtype) for shape, dtype in outs + list(blank)],
        scratch_shapes=scratch
        + results_in
        + [pltpu.VMEM(shape, dtype) for shape, dtype in temps]
        + [pltpu.SemaphoreType.DMA((n_sems,))],
        input_output_aliases=aliases,
        compiler_params=pltpu.CompilerParams(vmem_limit_bytes=limit << 20),
    )(*arrays)


def in_hbm(*arrays):
    return [pltpu.with_memory_space_constraint(a, pltpu.HBM) for a in arrays]


def vectors_of(small):
    lane = lax.broadcasted_iota(i32, (8, 128), 1)
    pick = lane == lax.broadcasted_iota(i32, (8, 128), 0) + 2 * E
    return mm(pick.astype(f32).astype(bf16), small[...], 1, 1)


QKV_B = (0, 3 * D - CUT)
OUT_T = (3 * D - CUT, 4 * D - CUT)
SMALL = (4 * D - CUT, PACK - CUT)


def attend_forward(x, placed, halves_a, halves_b, sel):
    names = ("slots", "residual", "prob", "acts", "norm1", "context", "router")
    names += ("out_t", "small")
    outs = call(
        forward_kernel,
        tuple(Near(half) for half in halves_b) + (sel, x)
        + tuple(Near(half) for half in halves_a) + (placed,),
        [
            ((SLOTS, D), bf16), ((ROWS, D), f32), ((HEADS, ROWS, ROWS), bf16),
            ((ROWS, 3 * D), bf16), ((ROWS, D), bf16), ((ROWS, D), bf16),
            ((ROWS, 128), f32), ((D, D), bf16), ((D, 128), bf16),
        ],
        12,
        [((ROWS, D), bf16)],
    )
    return dict(zip(names, outs))


def backward_kernel(get, outs, flush):
    input_grad, gate_o, ph, res_half_o, sums, cgs = outs
    rec, placed, small, cot = get(0), get(1), get(2), get(3)
    vec = vectors_of(small)
    row = lambda k: vec[k : k + 1, :]
    disp = dispatch_rows(placed[...])
    lane = lax.broadcasted_iota(i32, (ROWS, 128), 1)
    chosen = (lane == placed[:, 0:1] // CAP) | (lane == placed[:, 1:2] // CAP)
    gate_o[...] = jnp.where(chosen, get(4)[...], 0.0)
    flush(1)
    second = 0.0
    for o in range(rec.shape[1]):
        second = second + mm(disp, rec[:, o, :, :].reshape(SLOTS, D))
    hat2, rstd2 = normalize(get(5)[...])
    sums[GAIN2 : GAIN2 + 1, :] = jnp.sum(second * hat2, axis=0, keepdims=True)
    sums[SHIFT2 : SHIFT2 + 1, :] = jnp.sum(second, axis=0, keepdims=True)
    res_grad = cot[...].astype(f32) + norm_back(second * row(GAIN2), hat2, rstd2)
    input_grad[...] = res_grad
    sums[BO : BO + 1, :] = jnp.sum(res_grad, axis=0, keepdims=True)
    res_half = res_grad.astype(bf16)
    res_half_o[...] = res_half
    flush(3)
    cgs[...] = mm(res_half, get(6)[...]).astype(bf16)
    prob, acts = get(7), get(8)

    def pair(j, _):
        at = lambda part: pl.ds(pl.multiple_of(part * D + j * 128, 128), 128)
        q, k, v = acts[:, at(0)], acts[:, at(1)], acts[:, at(2)]
        c = cgs[:, at(0)]
        qs, ks, vs = [], [], []
        for h in range(2):
            p = prob[2 * j + h, :, :]
            pf = p.astype(f32)
            t = pf * mm(half_of(v, h), c, 1, 1)
            sg = ((t - pf * jnp.sum(t, axis=0, keepdims=True)) * SCALE).astype(bf16)
            vs.append(mm(p, c))
            qs.append(mm(sg, k, 0, 0))
            ks.append(mm(sg, q))
        qg, kg, vg = join(*qs), join(*ks), join(*vs)
        sums[BQ : BQ + 1, at(0)] = jnp.sum(qg, axis=0, keepdims=True)
        sums[BV : BV + 1, at(0)] = jnp.sum(vg, axis=0, keepdims=True)
        ph[:, at(0)] = qg.astype(bf16)
        ph[:, at(1)] = kg.astype(bf16)
        ph[:, at(2)] = vg.astype(bf16)
        return 0

    lax.fori_loop(0, PAIRS, pair, 0, unroll=UNROLL)
    flush(2)
    first = mm(ph[:, :CUT], get(9)[...], 1, 1) + mm(ph[:, CUT:], get(10)[...], 1, 1)
    hat1, rstd1 = normalize(get(11)[...].astype(f32))
    sums[GAIN1 : GAIN1 + 1, :] = jnp.sum(first * hat1, axis=0, keepdims=True)
    sums[SHIFT1 : SHIFT1 + 1, :] = jnp.sum(first, axis=0, keepdims=True)
    sums[7:8, :] = jnp.zeros((1, D), f32)
    flush(4)
    input_grad[...] += norm_back(first * row(GAIN1), hat1, rstd1)
    flush(0)


BACKWARD_TEMPS = [
    ((ROWS, 3 * D), bf16), ((ROWS, D), bf16), ((8, D), f32),
]


def backward_operands(rec, x, cot, placed, s, qkv_a, qkv_b, out_t, small):
    return (
        rec, placed, small, cot, s["router"], s["residual"], out_t, s["prob"],
        s["acts"], qkv_a, qkv_b, x,
    )


BACKWARD_GROUPS = [[0, 1, 2, 3, 4, 5], [6, 7, 8], [9, 10, 11]]


def token_backward(part, buffer, *args):
    return call(
        backward_kernel,
        backward_operands(*args),
        [((ROWS, D), f32), ((ROWS, 128), f32)] + BACKWARD_TEMPS,
        14 + 4 * args[0].shape[1],
        [((ROWS, D), bf16)],
        BACKWARD_GROUPS,
        (2, buffer),
        part,
    )


def expert_kernel(
    idx, x, c, w_in, w_out, bias, small, act, back, d_rows, gated, gate, grad_bias, grad_router,
    acc, gg, prob,
):
    r, f = pl.program_id(0), pl.program_id(1)
    rows, width = act.shape
    slices = pl.num_programs(0) * rows // SLOTS

    @pl.when(f == 0)
    def _():
        logits = mm(x[...], small[...])
        lane = lax.broadcasted_iota(i32, logits.shape, 1)
        raised = jnp.where(lane < E, jnp.exp(jnp.where(lane < E, logits, 0.0)), 0.0)
        raised = raised / jnp.sum(raised, axis=1, keepdims=True)
        prob[...] = raised
        g = jnp.sum(jnp.where(lane == idx[0], raised, 0.0), axis=1, keepdims=True)
        gate[...] = jnp.broadcast_to(g, gate.shape)
        rows_c = c[...].reshape(rows, D)
        gated[...] = (rows_c.astype(f32) * g).astype(bf16)
        dots = jnp.where(lane == idx[0] + E, mm(rows_c, small[...]), 0.0)
        gg[...] = dots * (1.0 / slices)
        acc[...] = jnp.zeros_like(acc)

    value, slope = gelu_terms(mm(x[...], w_in[...], 1, 1) + bias[...])
    hid = mm(c[...].reshape(rows, D), w_out[...], 1, 1)
    act[...] = value.astype(bf16)
    both = value * hid
    part = both[:, :128]
    for j in range(1, width // 128):
        part = part + both[:, j * 128 : (j + 1) * 128]
    gg[...] += part
    before = hid * slope * gate[:, :1]
    total = jnp.sum(before, axis=0, keepdims=True)
    half = before.astype(bf16)
    back[...] = half
    acc[...] += mm(half, w_in[...])
    cols = pl.ds(pl.multiple_of(f * width, width), width)

    @pl.when(r == 0)
    def _():
        grad_bias[:, cols] = total

    @pl.when(r > 0)
    def _():
        grad_bias[:, cols] += total

    @pl.when(f == pl.num_programs(1) - 1)
    def _():
        g = jnp.sum(gg[...], axis=1, keepdims=True)
        lane = lax.broadcasted_iota(i32, (rows, 128), 1)
        picked = (lane == idx[0]).astype(f32)
        logit = (g * prob[...] * (picked - gate[...])).astype(bf16)
        d_rows[...] = (acc[...] + mm(logit, small[...], 1, 1)).astype(bf16)
        share = mm(x[...], logit, 0, 0)

        @pl.when(r == 0)
        def _():
            grad_router[...] = share

        @pl.when(r > 0)
        def _():
            grad_router[...] += share


def expert_main(i, x, c, w_in, w_out, bias, router, expert):
    total, width = x.shape[0], w_in.shape[0]
    rb, fb = min(512, total), min(768, width)
    row = lambda r, f, *_: (r, 0)
    tile = lambda r, f, *_: (r, f)
    fixed = lambda r, f, *_: (0, 0)
    return pl.pallas_call(
        expert_kernel,
        grid_spec=pltpu.PrefetchScalarGridSpec(
            num_scalar_prefetch=1,
            grid=(total // rb, width // fb),
            in_specs=[
                pl.BlockSpec((rb, D), row),
                pl.BlockSpec((rb // CAP, None, CAP, D), lambda r, f, idx: (r, idx[1], 0, 0)),
                pl.BlockSpec((fb, D), lambda r, f, *_: (f, 0)),
                pl.BlockSpec((fb, D), lambda r, f, *_: (f, 0)),
                pl.BlockSpec((1, fb), lambda r, f, *_: (0, f)),
                pl.BlockSpec((D, 128), fixed),
            ],
            out_specs=[
                pl.BlockSpec((rb, fb), tile),
                pl.BlockSpec((rb, fb), tile),
                pl.BlockSpec((rb, D), row),
                pl.BlockSpec((rb, D), row),
                pl.BlockSpec((rb, 128), row),
                pl.BlockSpec((1, width), fixed),
                pl.BlockSpec((D, 128), fixed),
            ],
            scratch_shapes=[
                pltpu.VMEM((rb, D), f32),
                pltpu.VMEM((rb, 128), f32),
                pltpu.VMEM((rb, 128), f32),
            ],
        ),
        out_shape=[
            pltpu.HBM((total, width), bf16),
            pltpu.HBM((total, width), bf16),
            pltpu.HBM((total, D), bf16),
            pltpu.HBM((total, D), bf16),
            pltpu.HBM((total, 128), f32),
            pltpu.HBM((1, width), f32),
            pltpu.HBM((D, 128), f32),
        ],
        compiler_params=pltpu.CompilerParams(
            dimension_semantics=("arbitrary", "arbitrary"), vmem_limit_bytes=22 << 20
        ),
        name="expert_main",
    )(jnp.stack([expert, jnp.int32(i)]), *in_hbm(x, c, w_in, w_out, bias.reshape(1, width), router))


def parts_kernel(act0, act1, gate0, gate1, w_out, out, acc):
    f = pl.program_id(0)

    @pl.when(f == 0)
    def _():
        acc[...] = jnp.zeros_like(acc)

    for i, act in enumerate((act0, act1)):
        acc[i] += mm(act[...], w_out[...])

    @pl.when(f == pl.num_programs(0) - 1)
    def _():
        for i, gate in enumerate((gate0, gate1)):
            rows = (acc[i] * gate[:, :1]).astype(bf16)
            out[:, i, :, :] = rows.reshape(out.shape[0], CAP, D)


def expert_parts(acts, gates, w_out):
    total, width = acts[0].shape
    fb = min(768, width)
    n = total // CAP
    cols = pl.BlockSpec((total, fb), lambda f: (0, f))
    full = pl.BlockSpec((total, 128), lambda f: (0, 0))
    return pl.pallas_call(
        parts_kernel,
        grid=(width // fb,),
        in_specs=[cols, cols, full, full, pl.BlockSpec((fb, D), lambda f: (f, 0))],
        out_specs=pl.BlockSpec((n, 2, CAP, D), lambda f: (0, 0, 0, 0)),
        out_shape=pltpu.HBM((n, 2, CAP, D), bf16),
        scratch_shapes=[pltpu.VMEM((2, total, D), f32)],
        compiler_params=pltpu.CompilerParams(
            dimension_semantics=("arbitrary",),
            vmem_limit_bytes=(18 if total <= 512 else 48) << 20,
        ),
        name="expert_parts",
    )(*in_hbm(*acts, *gates, w_out))


def moved_kernel(get, outs, flush):
    for k, (value, perm) in enumerate(((0, 2), (0, 3), (1, 3))):
        outs[k][...] = mm(get(perm)[...], get(value)[...], 1, 1).astype(bf16)
        flush(k)


def rest_kernel(get, outs, flush):
    sent_b, kept_b = outs
    half = D // 2

    def lay(value, start):
        kept_b[:, start : start + value.shape[1]] = value[:half].astype(bf16)
        sent_b[:, start : start + value.shape[1]] = value[half:].astype(bf16)

    lay(mm(get(0)[...], get(1)[...]), 0)
    perm = get(2)[...]
    out = mm(mm(perm, get(3)[...], 1, 1).astype(bf16), get(4)[...])
    lay(out, OUT_T[0])
    sums = get(5)[...] + get(6)[...]
    zeros = lambda n: jnp.zeros((n, D), f32)
    spread = jnp.concatenate([zeros(2 * E), sums, zeros(128 - 2 * E - 8)], axis=0)
    router = (get(7)[...] + get(8)[...]).astype(bf16)
    tail = mm(perm, spread.astype(bf16), 1, 1) + mm(perm, router)
    tail = tail + mm(get(9)[...], pltpu.roll(get(10)[...], E, 1).astype(bf16))
    lay(tail, SMALL[0])
    flush(0)
    flush(1)


def eye(size, width=None, shift=0):
    shape = (size, width or size)
    hit = lax.broadcasted_iota(i32, shape, 1) == lax.broadcasted_iota(i32, shape, 0) + shift
    return hit.astype(f32).astype(bf16)


def pack_kernel(get, outs, flush):
    packed = outs[0]
    w_qkv, w_out, router, bias = (get(k) for k in range(4))
    own = w_qkv.shape[0]
    packed[0, :, : 3 * D] = w_qkv[...]
    packed[0, :, 3 * D : 4 * D] = w_out[...]
    rows = [get(4 + k)[...].astype(f32).reshape(1, own) for k in range(VECTORS)]
    rows = jnp.concatenate(rows + [jnp.zeros((1, own), f32)], axis=0).astype(bf16)
    columns = mm(eye(own), rows, 1, 1).astype(bf16)
    tail = mm(router[...], eye(E, 128)) + mm(bias[...], eye(E, 128, E))
    tail = tail + mm(columns, eye(8, 128, 2 * E))
    packed[0, :, 4 * D :] = tail.astype(bf16)
    flush(0)


def unpack_kernel(get, outs, flush):
    w_qkv, w_out, router, bias = outs[:4]
    add = lambda k: get(k)[...].astype(f32) + get(k + 1)[...].astype(f32)
    w_qkv[:, :CUT] = add(0)
    mine = add(2)
    w_qkv[:, CUT:] = mine[:, QKV_B[0] : QKV_B[1]]
    flush(0)
    w_out[...] = mine[:, OUT_T[0] : OUT_T[1]]
    flush(1)
    tail = mine[:, SMALL[0] :]
    router[...] = tail[:, :E]
    flush(2)
    bias[...] = tail[:, E : 2 * E]
    flush(3)
    rows = sum(mm(eye(8, 128, 2 * E), p, 1, 1) for p in pieces(tail, 3))
    for k in range(VECTORS):
        outs[4 + k][...] = rows[k]
        flush(4 + k)


def output_kernel(get, outs, flush):
    block_out, input_grad = outs
    small, parts = get(0), get(1)
    for i in range(2):
        placed, residual, gate, grad = (get(2 + 4 * i + k) for k in range(4))
        input_grad[i * SEQ : (i + 1) * SEQ, :] = grad[:SEQ, :]
        disp = dispatch_rows(placed[...])
        out = residual[...]
        for o in range(parts.shape[1]):
            out = out + mm(disp, parts[:, o, i, :, :].reshape(SLOTS, D))
        for p in pieces(pltpu.roll(gate[...], E, 1), 2):
            out = out + mm(p, small[...], 1, 1)
        block_out[i * SEQ : (i + 1) * SEQ, :] = out[:SEQ]
    flush(0)
    flush(1)


def weights_kernel(act0, act1, back0, back1, g0, g1, x0, x1, out_w, in_w):
    out_w[...] = mm(act0[...], g0[...], 0, 0) + mm(act1[...], g1[...], 0, 0)
    in_w[...] = mm(back0[...], x0[...], 0, 0) + mm(back1[...], x1[...], 0, 0)


def expert_weights(acts, backs, gated, xs):
    total, width = acts[0].shape
    fb = 512 if width % 512 == 0 else 384
    cols = pl.BlockSpec((total, fb), lambda f: (0, f))
    full = pl.BlockSpec((total, D), lambda f: (0, 0))
    rows = pl.BlockSpec((fb, D), lambda f: (f, 0))
    return pl.pallas_call(
        weights_kernel,
        grid=(width // fb,),
        in_specs=[cols] * 4 + [full] * 4,
        out_specs=[rows, rows],
        out_shape=[pltpu.HBM((width, D), f32)] * 2,
        compiler_params=pltpu.CompilerParams(
            dimension_semantics=("arbitrary",),
            vmem_limit_bytes=(22 if total <= 512 else 40) << 20,
        ),
        name="expert_weights",
    )(*in_hbm(*acts, *backs, *gated, *xs))


def on_device(
    block_in, out_cotangent, expert_routes, ln1_gain, ln1_shift, w_qkv, bias_query, bias_value,
    w_out, bias_out, ln2_gain, ln2_shift, w_router, expert_bias, w_expert_in, bias_hidden,
    w_expert_out,
):
    images = block_in.shape[0] // SEQ
    n = lax.axis_size(AXIS)
    owners = n // E
    own = ln1_gain.shape[0]
    expert = lax.axis_index(AXIS) // owners
    order_a, order_b = bit_orders()
    barrier = lax.optimization_barrier
    (shard,) = call(
        pack_kernel,
        (w_qkv, w_out.T, w_router, expert_bias.T)
        + (ln1_gain, ln1_shift, bias_query, bias_value, bias_out, ln2_gain, ln2_shift),
        [((1, own, PACK), bf16)],
        8,
    )

    pad_rows = ((0, ROWS - SEQ), (0, 0))
    xs, cots, placed, states, outgoing = [], [], [], [], []
    for i in range(images):
        xs.append(jnp.pad(block_in[i * SEQ : (i + 1) * SEQ], pad_rows))
        cots.append(jnp.pad(out_cotangent[i * SEQ : (i + 1) * SEQ], pad_rows))
        placed.append(place(expert_routes[i * SEQ : (i + 1) * SEQ]))
        slots = mm(dispatch_of(placed[i]), cots[i]).astype(bf16)
        outgoing.append(to_owners(slots, owners))
    late = (
        xs, cots, [p.T for p in placed], permutation(pair_order()),
        row_permutation(owner_order(order_a)), row_permutation(owner_order(order_b)),
    )
    halves, outgoing, late = gather_rows(shard, 3, jnp.stack(outgoing, axis=1), late)
    xs, cots, columns, sel, perm_a, perm_b = late
    flat = [tuple(h.reshape(D // 2, h.shape[-1]) for h in pair) for pair in halves]
    cot_in = exchange(outgoing)
    for i in range(images):
        states.append(attend_forward(xs[i], placed[i], flat[0], flat[1], sel))
    both = lambda key: [s[key] for s in states]
    norm1a, norm1b, cotb, ph = call(
        moved_kernel,
        (Stack(both("norm1"), 2 * ROWS), Stack(cots, 2 * ROWS), perm_a, perm_b),
        [((D, 2 * ROWS), bf16)] * 3,
        12,
        blank=[((images * ROWS, 3 * D), bf16)],
    )
    first = exchange(to_owners(states[0]["slots"], owners))
    second = exchange(to_owners(states[1]["slots"], owners))
    arrived = [first.reshape(-1, D), second.reshape(-1, D)]
    small, out_t = states[0]["small"], states[0]["out_t"]
    rest = list(range(lax.axis_size(AXIS).bit_length() - 1))[1:]
    natural = [
        merged(mine, theirs, 0, rest)
        for mine, theirs in (halves[0], tuple(h[..., : QKV_B[1]] for h in halves[1]))
    ]
    qkv_a, qkv_b = [v.reshape(D, v.shape[-1]) for v in natural]
    done = []
    grad_hidden = 0.0
    received = []
    router_grads = []
    for i in range(images):
        act, back, d_rows, gated, gate, gb, gr = expert_main(
            i, arrived[i], cot_in, w_expert_in, w_expert_out, bias_hidden, small, expert
        )
        done.append((act, back, gated, gate))
        router_grads.append(gr)
        grad_hidden = grad_hidden + gb[0]
        if i == 0:
            d_rows, qkv_b = barrier((d_rows, qkv_b))
        else:
            d_rows, qkv_a = barrier((d_rows, qkv_a))
        rows = exchange(d_rows.reshape(n, CAP, D))
        received.append(rows.reshape(E, owners, CAP, D))
    sent = expert_parts([d[0] for d in done], [d[3] for d in done], w_expert_out)
    parts = exchange(sent).reshape(E, owners, images, CAP, D)
    column = lambda k: [d[k] for d in done]
    grad_expert_out, grad_expert_in = expert_weights(
        column(0), column(1), column(2), arrived
    )
    back = []
    for i in range(images):
        results = token_backward(
            i, ph, received[i], xs[i], cots[i], columns[i], states[i],
            qkv_a, qkv_b, out_t, small,
        )
        ph = results[2]
        back.append(results)
    pair = lambda k: [b[k] for b in back]
    sent_a = mm(norm1a[D // 2 :], ph[:, :CUT]).astype(bf16)
    kept_a = mm(norm1a[: D // 2], ph[:, :CUT]).astype(bf16)
    sent_b, kept_b = call(
        rest_kernel,
        (norm1b, Columns(ph, CUT, 3 * D), perm_b, Stack(pair(3), 2 * ROWS))
        + (Stack(both("context"), 2 * ROWS),) + tuple(pair(4)) + tuple(router_grads)
        + (cotb, Stack(pair(1), 2 * ROWS)),
        [((D // 2, PACK - CUT), bf16)] * 2,
        24,
        (),
        [[0, 1], [2, 3, 4], [5, 6, 7, 8, 9, 10]],
    )
    ends = scatter_rows([(sent_a, kept_a, order_a), (sent_b, kept_b, order_b)])
    block_out, input_grad = call(
        output_kernel,
        (small, Near(parts), columns[0], states[0]["residual"], back[0][1], back[0][0])
        + (columns[1], states[1]["residual"], back[1][1], back[1][0]),
        [((images * SEQ, D), f32)] * 2,
        6 + 6 * owners,
    )
    grad_qkv, grad_out, grad_router, grad_bias, *vec = call(
        unpack_kernel,
        tuple(Near(end) for end in ends),
        [(shape, f32) for shape in ((own, 3 * D), (own, D), (own, E), (own, E))]
        + [((own,), f32)] * VECTORS,
        8,
    )
    return (
        block_out, input_grad, vec[GAIN1], vec[SHIFT1], grad_qkv, vec[BQ], vec[BV],
        grad_out.T, vec[BO], vec[GAIN2], vec[SHIFT2], grad_router, grad_bias.T,
        grad_expert_in, grad_hidden, grad_expert_out,
    )


def solution(mesh):
    rows, line, cols = P(AXIS, None), P(AXIS), P(None, AXIS)
    in_specs = (
        rows, rows, rows, line, line, rows, line, line, cols, line, line, line, rows, cols,
        rows, line, rows,
    )
    out_specs = (
        rows, rows, line, line, rows, line, line, cols, line, line, line, rows, cols, rows,
        line, rows,
    )

    return jax.shard_map(
        on_device, mesh=mesh, in_specs=in_specs, out_specs=out_specs, check_vma=False
    )
```

```python
import math

import jax
import jax.numpy as jnp
from jax import lax
from jax.experimental import pallas as pl
from jax.experimental.pallas import tpu as pltpu
from jax.sharding import PartitionSpec as P

D = 768
HEADS = 12
HEAD_DIM = 64
PAIRS = HEADS // 2
E = 32
SEQ = 197
ROWS = 208
CAP = 16
SLOTS = E * CAP
AXIS = "fsdp"
PACK = 3200
CUT = 1664
GAIN1, SHIFT1, BQ, BV, BO, GAIN2, SHIFT2, VECTORS = range(8)
SCALE = 1.0 / math.sqrt(HEAD_DIM)
UNROLL = PAIRS

epsilon = 1e-06
f32 = jnp.float32
bf16 = jnp.bfloat16
i32 = jnp.int32


def mm(a, b, ca=1, cb=0):
    return lax.dot_general(a, b, (((ca,), (cb,)), ((), ())), preferred_element_type=f32)


def pieces(v, n):
    out = []
    for _ in range(n):
        p = v.astype(bf16)
        out.append(p)
        v = v - p.astype(f32)
    return out


def normalize(values):
    centered = values - jnp.mean(values, axis=-1, keepdims=True)
    inverse = lax.rsqrt(jnp.mean(centered * centered, axis=-1, keepdims=True) + epsilon)
    return (centered * inverse, inverse)


def norm_back(upstream, normed, inverse):
    return inverse * (
        upstream
        - jnp.mean(upstream, axis=-1, keepdims=True)
        - normed * jnp.mean(upstream * normed, axis=-1, keepdims=True)
    )


def swap(values, bit):
    n = lax.axis_size(AXIS)
    return lax.ppermute(values, AXIS, [(d, d ^ (1 << bit)) for d in range(n)])


def bit_of(bit):
    return (lax.axis_index(AXIS) >> bit) & 1


def bit_orders():
    bits = lax.axis_size(AXIS).bit_length() - 1
    inner = (bits - 1) // 3 if bits != 5 else 1
    x = list(range(1, 1 + inner))
    y = list(range(1 + inner, 1 + 2 * inner))
    z = list(range(1 + 2 * inner, bits))
    return [0] + x + y + z, [0] + y + x + z


def merged(values, other, bit, done):
    at = sum(1 for b in done if b > bit)
    lead = values.shape[0]
    high = 1 << at
    mine = values.reshape((high, lead // high) + values.shape[1:])
    other = other.reshape(mine.shape)
    which = lax.broadcasted_iota(i32, (1, 2, 1, 1, 1), 1) == bit_of(bit)
    both = jnp.where(which, mine[:, None], other[:, None])
    return both.reshape((2 * lead,) + values.shape[1:])


def gather_rows(shard, early, wait_for, late):
    orders = bit_orders()
    steps = len(orders[0])
    common = 0
    while orders[0][-1 - common] == orders[1][-1 - common]:
        common += 1
    held, done = shard, []
    for step in range(common):
        bit = orders[0][-1 - step]
        held = lax.optimization_barrier(merged(held, swap(held, bit), bit, done))
        done.append(bit)
    held = [(held[..., :CUT], list(done)), (held[..., CUT:], list(done))]
    for step in range(common, steps):
        bits = [order[-1 - step] for order in orders]
        theirs = []
        for (values, _), bit in zip(held, bits):
            theirs.append(swap(values, bit))
        if step + 1 == steps:
            pairs = [(values, other) for (values, _), other in zip(held, theirs)]
            return pairs, wait_for, late
        tied = [
            merged(values, other, bit, seen)
            for (values, seen), other, bit in zip(held, theirs, bits)
        ]
        if step + 1 == early:
            tied.append(wait_for)
        if step + 2 == steps:
            tied, late = lax.optimization_barrier((tied, late))
        else:
            tied = lax.optimization_barrier(tied)
        if step + 1 == early:
            wait_for = tied[-1]
        held = [(t, seen + [bit]) for t, (_, seen), bit in zip(tied, held, bits)]


def owner_order(order):
    n = lax.axis_size(AXIS)
    own = D // n
    position = jnp.arange(D, dtype=i32)
    chunk = position // own
    owner = jnp.zeros_like(chunk)
    for step, bit in enumerate(order):
        owner = owner | (((chunk >> (len(order) - 1 - step)) & 1) << bit)
    return (owner ^ lax.axis_index(AXIS)) * own + position % own


def pair_order():
    own = D // lax.axis_size(AXIS)
    position = jnp.arange(D, dtype=i32)
    inside = position % (D // 2)
    lowest = bit_of(0) ^ (position // (D // 2))
    return (2 * (inside // own) + lowest) * own + inside % own


def permutation(order):
    return (jnp.arange(D, dtype=i32)[:, None] == order[None]).astype(bf16)


def row_permutation(order):
    return (order[:, None] == jnp.arange(D, dtype=i32)[None]).astype(bf16)


def scatter_rows(parts):
    ends = []
    for sent, kept, order in parts:
        for step, bit in enumerate(order):
            got = swap(sent, bit)
            if step + 1 == len(order):
                ends += [kept, got]
                break
            half = kept.shape[0] // 2
            sent, kept = lax.optimization_barrier(
                tuple(
                    (kept[part].astype(f32) + got[part].astype(f32)).astype(bf16)
                    for part in (slice(half, None), slice(0, half))
                )
            )
    return ends


def exchange(blocks):
    return lax.all_to_all(blocks, AXIS, split_axis=0, concat_axis=0, tiled=True)


def to_owners(slot_rows, owners):
    rows = slot_rows.reshape((E, 1, CAP) + slot_rows.shape[1:])
    rows = jnp.broadcast_to(rows, (E, owners) + rows.shape[2:])
    return rows.reshape((E * owners, CAP) + slot_rows.shape[1:])


def place(routes):
    choice = jnp.pad(routes.T, ((0, 0), (0, ROWS - SEQ)), constant_values=-1)
    ids = jnp.arange(E, dtype=i32)[:, None]
    first = (choice[:1] == ids).astype(bf16)
    second = (choice[1:] == ids).astype(bf16)
    t = jnp.arange(ROWS, dtype=i32)
    earlier = (t[:, None] < t[None, :]).astype(bf16)
    before = mm(jnp.concatenate([first, second], axis=0), earlier)
    rank0 = jnp.sum(before[:E] * first, axis=0)
    seen = before[E:] + jnp.sum(first.astype(f32), axis=1, keepdims=True)
    rank1 = jnp.sum(seen * second, axis=0)
    return choice * CAP + jnp.stack([rank0, rank1]).astype(i32)


def gelu_terms(v):
    cumulative = 0.5 * (1.0 + lax.erf(v * (1.0 / math.sqrt(2.0))))
    density = jnp.exp(-0.5 * v * v) * (1.0 / math.sqrt(2.0 * math.pi))
    return v * cumulative, cumulative + v * density


def dispatch_of(placed):
    slot = lax.broadcasted_iota(i32, (SLOTS, ROWS), 0)
    hit = (slot == placed[0:1, :]) | (slot == placed[1:2, :])
    return hit.astype(f32).astype(bf16)


def dispatch_rows(placed):
    slot = lax.broadcasted_iota(i32, (ROWS, SLOTS), 1)
    hit = (slot == placed[:, 0:1]) | (slot == placed[:, 1:2])
    return hit.astype(f32).astype(bf16)


def half_of(pair, second):
    lane = lax.broadcasted_iota(i32, pair.shape, 1)
    keep = (lane >= HEAD_DIM) if second else (lane < HEAD_DIM)
    return jnp.where(keep, pair, jnp.zeros_like(pair))


def join(first, second):
    lane = lax.broadcasted_iota(i32, first.shape, 1)
    return jnp.where(lane < HEAD_DIM, first, second)


def forward_kernel(get, outs, flush):
    slots, residual, prob, acts, norm1_o, context_o, router_o, out_t, small, norm2_o = outs
    sel = get(2)
    first, second = get(0), get(1)
    joined = lambda a, b: jnp.concatenate([a, b], axis=0)
    rest = mm(sel[...], joined(first[:, QKV_B[1] :], second[:, QKV_B[1] :]))
    out_t[...] = rest[:, :D].astype(bf16)
    flush(7)
    small[...] = rest[:, D:].astype(bf16)
    flush(8)
    vec = vectors_of(small)
    row = lambda k: vec[k : k + 1, :]
    inputs = get(3)[...].astype(f32)
    hat1, _ = normalize(inputs)
    norm1 = (hat1 * row(GAIN1) + row(SHIFT1)).astype(bf16)
    norm1_o[...] = norm1
    flush(4)
    moved = mm(norm1, sel[...]).astype(bf16)
    proj_a = mm(moved, joined(get(4)[...], get(5)[...]))
    proj_b = mm(moved, joined(first[:, : QKV_B[1]], second[:, : QKV_B[1]]))
    proj = jnp.concatenate([proj_a, proj_b], axis=1)
    acts[:, :D] = (proj[:, :D] + row(BQ)).astype(bf16)
    acts[:, D : 2 * D] = proj[:, D : 2 * D].astype(bf16)
    acts[:, 2 * D :] = (proj[:, 2 * D :] + row(BV)).astype(bf16)
    flush(3)
    token = lax.broadcasted_iota(i32, (ROWS, ROWS), 0) < SEQ

    def pair(j, _):
        at = lambda part: pl.ds(pl.multiple_of(part * D + j * 128, 128), 128)
        q = acts[:, at(0)] * jnp.asarray(SCALE, bf16)
        k, v = acts[:, at(1)], acts[:, at(2)]
        both = []
        for h in range(2):
            raised = jnp.exp(mm(half_of(k, h), q, 1, 1))
            raised = jnp.where(token, raised, 0.0)
            p = (raised * (1.0 / jnp.sum(raised, axis=0, keepdims=True))).astype(bf16)
            prob[2 * j + h, :, :] = p
            both.append(mm(p, v, 0, 0))
        context_o[:, at(0)] = join(both[0], both[1]).astype(bf16)
        return 0

    lax.fori_loop(0, PAIRS, pair, 0, unroll=UNROLL)
    flush(2)
    flush(5)
    res = inputs + mm(context_o[...], out_t[...], 1, 1) + row(BO)
    residual[...] = res
    flush(1)
    hat2, _ = normalize(res)
    norm2 = (hat2 * row(GAIN2) + row(SHIFT2)).astype(bf16)
    norm2_o[...] = norm2
    slots[...] = mm(dispatch_of(get(6)[...]), norm2).astype(bf16)
    flush(0)
    lane = lax.broadcasted_iota(i32, (ROWS, 128), 1)
    logits = jnp.where(lane < E, mm(norm2, small[...]), 0.0)
    raised = jnp.where(lane < E, jnp.exp(logits), 0.0)
    router_o[...] = raised / jnp.sum(raised, axis=1, keepdims=True)
    flush(6)


class Near:
    def __init__(self, array):
        self.array = array


class Stack:
    def __init__(self, arrays, rows):
        self.arrays, self.rows = arrays, rows


class Columns:
    def __init__(self, array, start, stop):
        self.array, self.start, self.stop = array, start, stop


class Fetch:
    def __init__(self, copies, groups, refs):
        self.copies, self.groups, self.refs = copies, groups, refs
        self.begun = 0
        self.waited = set()
        self.begin(2)

    def begin(self, count):
        while self.begun < min(count, len(self.groups)):
            for k in self.groups[self.begun]:
                for copy in self.copies[k]:
                    copy.start()
            self.begun += 1

    def get(self, k):
        if k in self.copies and k not in self.waited:
            at = next(g for g, group in enumerate(self.groups) if k in group)
            self.begin(at + 1)
            for copy in self.copies[k]:
                copy.wait()
            self.waited.add(k)
            if all(m in self.waited for m in self.groups[at]):
                self.begin(at + 3)
        return self.refs[k]


def call(kernel, ins, outs, limit, temps=(), groups=None, shared=None, part=0, blank=()):
    arrays, specs, scratch, plan = [], [], [], []
    for item in ins:
        if isinstance(item, Near):
            plan.append(("near", len(arrays), None))
            arrays.append(item.array)
            specs.append(pl.BlockSpec(memory_space=pltpu.VMEM))
            continue
        if isinstance(item, Stack):
            group, shape = item.arrays, (item.rows, item.arrays[0].shape[1])
            cut = None
        elif isinstance(item, Columns):
            group, shape = [item.array], (item.array.shape[0], item.stop - item.start)
            cut = (item.start, item.stop)
        else:
            group, shape, cut = [item], item.shape, None
        plan.append(("far", list(range(len(arrays), len(arrays) + len(group))), cut))
        scratch.append(pltpu.VMEM(shape, group[0].dtype))
        for array in group:
            arrays += in_hbm(array)
            specs.append(pl.BlockSpec(memory_space=pltpu.HBM))
    n_in, n_out, n_far = len(arrays), len(outs), len(scratch)
    results_in = [pltpu.VMEM(shape, dtype) for shape, dtype in outs]
    aliases = {}
    outs = list(outs)
    if shared is not None:
        slot, buffer = shared
        aliases = {n_in: slot}
        arrays += in_hbm(buffer) + [jnp.full((1,), part, i32)]
        specs += [
            pl.BlockSpec(memory_space=pltpu.HBM), pl.BlockSpec(memory_space=pltpu.SMEM),
        ]
        outs[slot] = (buffer.shape, buffer.dtype)

    def body(*refs):
        if shared is not None:
            which = refs[n_in + 1]
            refs = refs[:n_in] + refs[n_in + 2 :]
        far_in, far_out = refs[:n_in], refs[n_in : n_in + n_out]
        near = refs[n_in + n_out + len(blank) : -1]
        sems = refs[-1]
        copies, views, used, sem = {}, [], 0, 0
        for k, (kind, index, cut) in enumerate(plan):
            if kind == "near":
                views.append(far_in[index])
                continue
            target = near[used]
            used += 1
            views.append(target)
            copies[k], row = [], 0
            for at in index:
                source = far_in[at]
                if cut is not None:
                    source = source.at[:, cut[0] : cut[1]]
                if len(target.shape) > 1 and source.shape[0] != target.shape[0]:
                    place_at = target.at[row : row + source.shape[0], :]
                else:
                    place_at = target
                row += source.shape[0]
                copies[k].append(pltpu.make_async_copy(source, place_at, sems.at[sem]))
                sem += 1
        order = groups if groups is not None else [list(range(len(plan)))]
        order = [[k for k in group if k in copies] for group in order]
        source = Fetch(copies, order, views)
        results = near[n_far : n_far + n_out]
        far_out = list(far_out)
        if shared is not None:
            rows = results[slot].shape[0]
            at = pl.multiple_of(which[0] * rows, 16)
            far_out[slot] = far_out[slot].at[pl.ds(at, rows), :]
        sinks = [
            pltpu.make_async_copy(v, f, sems.at[sem + k])
            for k, (v, f) in enumerate(zip(results, far_out))
        ]
        kernel(source.get, near[n_far:], lambda k: sinks[k].start())
        for k in copies:
            source.get(k)
        for sink in sinks:
            sink.wait()

    n_sems = sum(len(index) for kind, index, _ in plan if kind == "far") + n_out
    return pl.pallas_call(
        body,
        in_specs=specs,
        out_specs=[pl.BlockSpec(memory_space=pltpu.HBM)] * (n_out + len(blank)),
        out_shape=[pltpu.HBM(shape, dtype) for shape, dtype in outs + list(blank)],
        scratch_shapes=scratch
        + results_in
        + [pltpu.VMEM(shape, dtype) for shape, dtype in temps]
        + [pltpu.SemaphoreType.DMA((n_sems,))],
        input_output_aliases=aliases,
        compiler_params=pltpu.CompilerParams(vmem_limit_bytes=limit << 20),
    )(*arrays)


def in_hbm(*arrays):
    return [pltpu.with_memory_space_constraint(a, pltpu.HBM) for a in arrays]


def vectors_of(small):
    lane = lax.broadcasted_iota(i32, (8, 128), 1)
    pick = lane == lax.broadcasted_iota(i32, (8, 128), 0) + 2 * E
    return mm(pick.astype(f32).astype(bf16), small[...], 1, 1)


QKV_B = (0, 3 * D - CUT)
OUT_T = (3 * D - CUT, 4 * D - CUT)
SMALL = (4 * D - CUT, PACK - CUT)


def attend_forward(x, placed, halves_a, halves_b, sel):
    names = ("slots", "residual", "prob", "acts", "norm1", "context", "router")
    names += ("out_t", "small")
    outs = call(
        forward_kernel,
        tuple(Near(half) for half in halves_b) + (Near(sel), Near(x))
        + tuple(Near(half) for half in halves_a) + (placed,),
        [
            ((SLOTS, D), bf16), ((ROWS, D), f32), ((HEADS, ROWS, ROWS), bf16),
            ((ROWS, 3 * D), bf16), ((ROWS, D), bf16), ((ROWS, D), bf16),
            ((ROWS, 128), f32), ((D, D), bf16), ((D, 128), bf16),
        ],
        12,
        [((ROWS, D), bf16)],
    )
    return dict(zip(names, outs))


def backward_kernel(get, outs, flush):
    input_grad, gate_o, ph, res_half_o, sums, cgs = outs
    rec, placed, small, cot = get(0), get(1), get(2), get(3)
    vec = vectors_of(small)
    row = lambda k: vec[k : k + 1, :]
    disp = dispatch_rows(placed[...])
    lane = lax.broadcasted_iota(i32, (ROWS, 128), 1)
    chosen = (lane == placed[:, 0:1] // CAP) | (lane == placed[:, 1:2] // CAP)
    gate_o[...] = jnp.where(chosen, get(4)[...], 0.0)
    flush(1)
    second = 0.0
    for o in range(rec.shape[1]):
        second = second + mm(disp, rec[:, o, :, :].reshape(SLOTS, D))
    hat2, rstd2 = normalize(get(5)[...])
    sums[GAIN2 : GAIN2 + 1, :] = jnp.sum(second * hat2, axis=0, keepdims=True)
    sums[SHIFT2 : SHIFT2 + 1, :] = jnp.sum(second, axis=0, keepdims=True)
    res_grad = cot[...].astype(f32) + norm_back(second * row(GAIN2), hat2, rstd2)
    input_grad[...] = res_grad
    sums[BO : BO + 1, :] = jnp.sum(res_grad, axis=0, keepdims=True)
    res_half = res_grad.astype(bf16)
    res_half_o[...] = res_half
    flush(3)
    cgs[...] = mm(res_half, get(6)[...]).astype(bf16)
    prob, acts = get(7), get(8)

    def pair(j, _):
        at = lambda part: pl.ds(pl.multiple_of(part * D + j * 128, 128), 128)
        q, k, v = acts[:, at(0)], acts[:, at(1)], acts[:, at(2)]
        c = cgs[:, at(0)]
        qs, ks, vs = [], [], []
        for h in range(2):
            p = prob[2 * j + h, :, :]
            pf = p.astype(f32)
            t = pf * mm(half_of(v, h), c, 1, 1)
            sg = ((t - pf * jnp.sum(t, axis=0, keepdims=True)) * SCALE).astype(bf16)
            vs.append(mm(p, c))
            qs.append(mm(sg, k, 0, 0))
            ks.append(mm(sg, q))
        qg, kg, vg = join(*qs), join(*ks), join(*vs)
        sums[BQ : BQ + 1, at(0)] = jnp.sum(qg, axis=0, keepdims=True)
        sums[BV : BV + 1, at(0)] = jnp.sum(vg, axis=0, keepdims=True)
        ph[:, at(0)] = qg.astype(bf16)
        ph[:, at(1)] = kg.astype(bf16)
        ph[:, at(2)] = vg.astype(bf16)
        return 0

    lax.fori_loop(0, PAIRS, pair, 0, unroll=UNROLL)
    flush(2)
    first = mm(ph[:, :CUT], get(9)[...], 1, 1) + mm(ph[:, CUT:], get(10)[...], 1, 1)
    hat1, rstd1 = normalize(get(11)[...].astype(f32))
    sums[GAIN1 : GAIN1 + 1, :] = jnp.sum(first * hat1, axis=0, keepdims=True)
    sums[SHIFT1 : SHIFT1 + 1, :] = jnp.sum(first, axis=0, keepdims=True)
    sums[7:8, :] = jnp.zeros((1, D), f32)
    flush(4)
    input_grad[...] += norm_back(first * row(GAIN1), hat1, rstd1)
    flush(0)


BACKWARD_TEMPS = [
    ((ROWS, 3 * D), bf16), ((ROWS, D), bf16), ((8, D), f32),
]


def backward_operands(rec, x, cot, placed, s, qkv_a, qkv_b, out_t, small):
    return (
        rec, placed, small, cot, s["router"], s["residual"], Near(out_t), s["prob"],
        s["acts"], Near(qkv_a), Near(qkv_b), x,
    )


BACKWARD_GROUPS = [[0, 1, 2, 3, 4, 5], [7, 8], [11]]


def token_backward(part, buffer, *args):
    return call(
        backward_kernel,
        backward_operands(*args),
        [((ROWS, D), f32), ((ROWS, 128), f32)] + BACKWARD_TEMPS,
        14 + 4 * args[0].shape[1],
        [((ROWS, D), bf16)],
        BACKWARD_GROUPS,
        (2, buffer),
        part,
    )


def expert_kernel(
    idx, x, c, w_in, w_out, bias, small, act, back, d_rows, gated, gate, grad_bias, grad_router,
    acc, gg, prob,
):
    r, f = pl.program_id(0), pl.program_id(1)
    rows, width = act.shape
    slices = pl.num_programs(0) * rows // SLOTS

    @pl.when(f == 0)
    def _():
        logits = mm(x[...], small[...])
        lane = lax.broadcasted_iota(i32, logits.shape, 1)
        raised = jnp.where(lane < E, jnp.exp(jnp.where(lane < E, logits, 0.0)), 0.0)
        raised = raised / jnp.sum(raised, axis=1, keepdims=True)
        prob[...] = raised
        g = jnp.sum(jnp.where(lane == idx[0], raised, 0.0), axis=1, keepdims=True)
        gate[...] = jnp.broadcast_to(g, gate.shape)
        rows_c = c[...].reshape(rows, D)
        gated[...] = (rows_c.astype(f32) * g).astype(bf16)
        dots = jnp.where(lane == idx[0] + E, mm(rows_c, small[...]), 0.0)
        gg[...] = dots * (1.0 / slices)
        acc[...] = jnp.zeros_like(acc)

    value, slope = gelu_terms(mm(x[...], w_in[...], 1, 1) + bias[...])
    hid = mm(c[...].reshape(rows, D), w_out[...], 1, 1)
    act[...] = value.astype(bf16)
    both = value * hid
    part = both[:, :128]
    for j in range(1, width // 128):
        part = part + both[:, j * 128 : (j + 1) * 128]
    gg[...] += part
    before = hid * slope * gate[:, :1]
    total = jnp.sum(before, axis=0, keepdims=True)
    half = before.astype(bf16)
    back[...] = half
    acc[...] += mm(half, w_in[...])
    cols = pl.ds(pl.multiple_of(f * width, width), width)

    @pl.when(r == 0)
    def _():
        grad_bias[:, cols] = total

    @pl.when(r > 0)
    def _():
        grad_bias[:, cols] += total

    @pl.when(f == pl.num_programs(1) - 1)
    def _():
        g = jnp.sum(gg[...], axis=1, keepdims=True)
        lane = lax.broadcasted_iota(i32, (rows, 128), 1)
        picked = (lane == idx[0]).astype(f32)
        logit = (g * prob[...] * (picked - gate[...])).astype(bf16)
        d_rows[...] = (acc[...] + mm(logit, small[...], 1, 1)).astype(bf16)
        share = mm(x[...], logit, 0, 0)

        @pl.when(r == 0)
        def _():
            grad_router[...] = share

        @pl.when(r > 0)
        def _():
            grad_router[...] += share


def expert_main(i, x, c, w_in, w_out, bias, router, expert):
    total, width = x.shape[0], w_in.shape[0]
    rb, fb = min(512, total), min(768, width)
    row = lambda r, f, *_: (r, 0)
    tile = lambda r, f, *_: (r, f)
    fixed = lambda r, f, *_: (0, 0)
    return pl.pallas_call(
        expert_kernel,
        grid_spec=pltpu.PrefetchScalarGridSpec(
            num_scalar_prefetch=1,
            grid=(total // rb, width // fb),
            in_specs=[
                pl.BlockSpec((rb, D), row),
                pl.BlockSpec((rb // CAP, None, CAP, D), lambda r, f, idx: (r, idx[1], 0, 0)),
                pl.BlockSpec((fb, D), lambda r, f, *_: (f, 0)),
                pl.BlockSpec((fb, D), lambda r, f, *_: (f, 0)),
                pl.BlockSpec((1, fb), lambda r, f, *_: (0, f)),
                pl.BlockSpec((D, 128), fixed),
            ],
            out_specs=[
                pl.BlockSpec((rb, fb), tile),
                pl.BlockSpec((rb, fb), tile),
                pl.BlockSpec((rb, D), row),
                pl.BlockSpec((rb, D), row),
                pl.BlockSpec((rb, 128), row),
                pl.BlockSpec((1, width), fixed),
                pl.BlockSpec((D, 128), fixed),
            ],
            scratch_shapes=[
                pltpu.VMEM((rb, D), f32),
                pltpu.VMEM((rb, 128), f32),
                pltpu.VMEM((rb, 128), f32),
            ],
        ),
        out_shape=[
            pltpu.HBM((total, width), bf16),
            pltpu.HBM((total, width), bf16),
            pltpu.HBM((total, D), bf16),
            pltpu.HBM((total, D), bf16),
            pltpu.HBM((total, 128), f32),
            pltpu.HBM((1, width), f32),
            pltpu.HBM((D, 128), f32),
        ],
        compiler_params=pltpu.CompilerParams(
            dimension_semantics=("arbitrary", "arbitrary"), vmem_limit_bytes=22 << 20
        ),
        name="expert_main",
    )(jnp.stack([expert, jnp.int32(i)]), *in_hbm(x, c, w_in, w_out, bias.reshape(1, width), router))


def parts_kernel(act0, act1, gate0, gate1, w_out, out, acc):
    f = pl.program_id(0)

    @pl.when(f == 0)
    def _():
        acc[...] = jnp.zeros_like(acc)

    for i, act in enumerate((act0, act1)):
        acc[i] += mm(act[...], w_out[...])

    @pl.when(f == pl.num_programs(0) - 1)
    def _():
        for i, gate in enumerate((gate0, gate1)):
            rows = (acc[i] * gate[:, :1]).astype(bf16)
            out[:, i, :, :] = rows.reshape(out.shape[0], CAP, D)


def expert_parts(acts, gates, w_out):
    total, width = acts[0].shape
    fb = min(768, width)
    n = total // CAP
    cols = pl.BlockSpec((total, fb), lambda f: (0, f))
    full = pl.BlockSpec((total, 128), lambda f: (0, 0))
    return pl.pallas_call(
        parts_kernel,
        grid=(width // fb,),
        in_specs=[cols, cols, full, full, pl.BlockSpec((fb, D), lambda f: (f, 0))],
        out_specs=pl.BlockSpec((n, 2, CAP, D), lambda f: (0, 0, 0, 0)),
        out_shape=pltpu.HBM((n, 2, CAP, D), bf16),
        scratch_shapes=[pltpu.VMEM((2, total, D), f32)],
        compiler_params=pltpu.CompilerParams(
            dimension_semantics=("arbitrary",),
            vmem_limit_bytes=(18 if total <= 512 else 48) << 20,
        ),
        name="expert_parts",
    )(*in_hbm(*acts, *gates, w_out))


def moved_kernel(get, outs, flush):
    for k, (value, perm) in enumerate(((0, 2), (0, 3), (1, 3))):
        outs[k][...] = mm(get(perm)[...], get(value)[...], 1, 1).astype(bf16)
        flush(k)


def rest_kernel(get, outs, flush):
    sent_b, kept_b = outs
    half = D // 2

    def lay(value, start):
        kept_b[:, start : start + value.shape[1]] = value[:half].astype(bf16)
        sent_b[:, start : start + value.shape[1]] = value[half:].astype(bf16)

    lay(mm(get(0)[...], get(1)[...]), 0)
    perm = get(2)[...]
    out = mm(mm(perm, get(3)[...], 1, 1).astype(bf16), get(4)[...])
    lay(out, OUT_T[0])
    sums = get(5)[...] + get(6)[...]
    zeros = lambda n: jnp.zeros((n, D), f32)
    spread = jnp.concatenate([zeros(2 * E), sums, zeros(128 - 2 * E - 8)], axis=0)
    router = (get(7)[...] + get(8)[...]).astype(bf16)
    tail = mm(perm, spread.astype(bf16), 1, 1) + mm(perm, router)
    tail = tail + mm(get(9)[...], pltpu.roll(get(10)[...], E, 1).astype(bf16))
    lay(tail, SMALL[0])
    flush(0)
    flush(1)


def eye(size, width=None, shift=0):
    shape = (size, width or size)
    hit = lax.broadcasted_iota(i32, shape, 1) == lax.broadcasted_iota(i32, shape, 0) + shift
    return hit.astype(f32).astype(bf16)


def pack_kernel(get, outs, flush):
    packed = outs[0]
    w_qkv, w_out, router, bias = (get(k) for k in range(4))
    own = w_qkv.shape[0]
    packed[0, :, : 3 * D] = w_qkv[...]
    packed[0, :, 3 * D : 4 * D] = w_out[...]
    rows = [get(4 + k)[...].astype(f32).reshape(1, own) for k in range(VECTORS)]
    rows = jnp.concatenate(rows + [jnp.zeros((1, own), f32)], axis=0).astype(bf16)
    columns = mm(eye(own), rows, 1, 1).astype(bf16)
    tail = mm(router[...], eye(E, 128)) + mm(bias[...], eye(E, 128, E))
    tail = tail + mm(columns, eye(8, 128, 2 * E))
    packed[0, :, 4 * D :] = tail.astype(bf16)
    flush(0)


def unpack_kernel(get, outs, flush):
    w_qkv, w_out, router, bias = outs[:4]
    add = lambda k: get(k)[...].astype(f32) + get(k + 1)[...].astype(f32)
    w_qkv[:, :CUT] = add(0)
    mine = add(2)
    w_qkv[:, CUT:] = mine[:, QKV_B[0] : QKV_B[1]]
    flush(0)
    w_out[...] = mine[:, OUT_T[0] : OUT_T[1]]
    flush(1)
    tail = mine[:, SMALL[0] :]
    router[...] = tail[:, :E]
    flush(2)
    bias[...] = tail[:, E : 2 * E]
    flush(3)
    rows = sum(mm(eye(8, 128, 2 * E), p, 1, 1) for p in pieces(tail, 3))
    for k in range(VECTORS):
        outs[4 + k][...] = rows[k]
        flush(4 + k)


def output_kernel(get, outs, flush):
    block_out, input_grad = outs
    small, parts = get(0), get(1)
    for i in range(2):
        placed, residual, gate, grad = (get(2 + 4 * i + k) for k in range(4))
        input_grad[i * SEQ : (i + 1) * SEQ, :] = grad[:SEQ, :]
        disp = dispatch_rows(placed[...])
        out = residual[...]
        for o in range(parts.shape[1]):
            out = out + mm(disp, parts[:, o, i, :, :].reshape(SLOTS, D))
        for p in pieces(pltpu.roll(gate[...], E, 1), 2):
            out = out + mm(p, small[...], 1, 1)
        block_out[i * SEQ : (i + 1) * SEQ, :] = out[:SEQ]
    flush(0)
    flush(1)


def weights_kernel(act0, act1, back0, back1, g0, g1, x0, x1, out_w, in_w):
    out_w[...] = mm(act0[...], g0[...], 0, 0) + mm(act1[...], g1[...], 0, 0)
    in_w[...] = mm(back0[...], x0[...], 0, 0) + mm(back1[...], x1[...], 0, 0)


def expert_weights(acts, backs, gated, xs):
    total, width = acts[0].shape
    fb = 512 if width % 512 == 0 else 384
    cols = pl.BlockSpec((total, fb), lambda f: (0, f))
    full = pl.BlockSpec((total, D), lambda f: (0, 0))
    rows = pl.BlockSpec((fb, D), lambda f: (f, 0))
    return pl.pallas_call(
        weights_kernel,
        grid=(width // fb,),
        in_specs=[cols] * 4 + [full] * 4,
        out_specs=[rows, rows],
        out_shape=[pltpu.HBM((width, D), f32)] * 2,
        compiler_params=pltpu.CompilerParams(
            dimension_semantics=("arbitrary",),
            vmem_limit_bytes=(22 if total <= 512 else 40) << 20,
        ),
        name="expert_weights",
    )(*in_hbm(*acts, *backs, *gated, *xs))


def on_device(
    block_in, out_cotangent, expert_routes, ln1_gain, ln1_shift, w_qkv, bias_query, bias_value,
    w_out, bias_out, ln2_gain, ln2_shift, w_router, expert_bias, w_expert_in, bias_hidden,
    w_expert_out,
):
    images = block_in.shape[0] // SEQ
    n = lax.axis_size(AXIS)
    owners = n // E
    own = ln1_gain.shape[0]
    expert = lax.axis_index(AXIS) // owners
    order_a, order_b = bit_orders()
    barrier = lax.optimization_barrier
    (shard,) = call(
        pack_kernel,
        (w_qkv, w_out.T, w_router, expert_bias.T)
        + (ln1_gain, ln1_shift, bias_query, bias_value, bias_out, ln2_gain, ln2_shift),
        [((1, own, PACK), bf16)],
        8,
    )

    pad_rows = ((0, ROWS - SEQ), (0, 0))
    xs, cots, placed, states, outgoing = [], [], [], [], []
    for i in range(images):
        xs.append(jnp.pad(block_in[i * SEQ : (i + 1) * SEQ], pad_rows))
        cots.append(jnp.pad(out_cotangent[i * SEQ : (i + 1) * SEQ], pad_rows))
        placed.append(place(expert_routes[i * SEQ : (i + 1) * SEQ]))
        slots = mm(dispatch_of(placed[i]), cots[i]).astype(bf16)
        outgoing.append(to_owners(slots, owners))
    late = (
        xs, cots, [p.T for p in placed], permutation(pair_order()),
        row_permutation(owner_order(order_a)), row_permutation(owner_order(order_b)),
    )
    halves, outgoing, late = gather_rows(shard, 3, jnp.stack(outgoing, axis=1), late)
    xs, cots, columns, sel, perm_a, perm_b = late
    flat = [tuple(h.reshape(D // 2, h.shape[-1]) for h in pair) for pair in halves]
    cot_in = exchange(outgoing)
    for i in range(images):
        states.append(attend_forward(xs[i], placed[i], flat[0], flat[1], sel))
    both = lambda key: [s[key] for s in states]
    norm1a, norm1b, cotb, ph = call(
        moved_kernel,
        (Stack(both("norm1"), 2 * ROWS), Stack(cots, 2 * ROWS), perm_a, perm_b),
        [((D, 2 * ROWS), bf16)] * 3,
        12,
        blank=[((images * ROWS, 3 * D), bf16)],
    )
    first = exchange(to_owners(states[0]["slots"], owners))
    second = exchange(to_owners(states[1]["slots"], owners))
    arrived = [first.reshape(-1, D), second.reshape(-1, D)]
    small, out_t = states[0]["small"], states[0]["out_t"]
    rest = list(range(lax.axis_size(AXIS).bit_length() - 1))[1:]
    natural = [
        merged(mine, theirs, 0, rest)
        for mine, theirs in (halves[0], tuple(h[..., : QKV_B[1]] for h in halves[1]))
    ]
    qkv_a, qkv_b = [v.reshape(D, v.shape[-1]) for v in natural]
    done = []
    grad_hidden = 0.0
    received = []
    router_grads = []
    for i in range(images):
        act, back, d_rows, gated, gate, gb, gr = expert_main(
            i, arrived[i], cot_in, w_expert_in, w_expert_out, bias_hidden, small, expert
        )
        done.append((act, back, gated, gate))
        router_grads.append(gr)
        grad_hidden = grad_hidden + gb[0]
        if i == 0:
            d_rows, qkv_b = barrier((d_rows, qkv_b))
        else:
            d_rows, qkv_a = barrier((d_rows, qkv_a))
        rows = exchange(d_rows.reshape(n, CAP, D))
        received.append(rows.reshape(E, owners, CAP, D))
    sent = expert_parts([d[0] for d in done], [d[3] for d in done], w_expert_out)
    parts = exchange(sent).reshape(E, owners, images, CAP, D)
    column = lambda k: [d[k] for d in done]
    grad_expert_out, grad_expert_in = expert_weights(
        column(0), column(1), column(2), arrived
    )
    back = []
    for i in range(images):
        results = token_backward(
            i, ph, received[i], xs[i], cots[i], columns[i], states[i],
            qkv_a, qkv_b, out_t, small,
        )
        ph = results[2]
        back.append(results)
    pair = lambda k: [b[k] for b in back]
    sent_a = mm(norm1a[D // 2 :], ph[:, :CUT]).astype(bf16)
    kept_a = mm(norm1a[: D // 2], ph[:, :CUT]).astype(bf16)
    sent_b, kept_b = call(
        rest_kernel,
        (norm1b, Columns(ph, CUT, 3 * D), perm_b, Stack(pair(3), 2 * ROWS))
        + (Stack(both("context"), 2 * ROWS),) + tuple(pair(4)) + tuple(router_grads)
        + (cotb, Stack(pair(1), 2 * ROWS)),
        [((D // 2, PACK - CUT), bf16)] * 2,
        24,
        (),
        [[0, 1], [2, 3, 4], [5, 6, 7, 8, 9, 10]],
    )
    ends = scatter_rows([(sent_a, kept_a, order_a), (sent_b, kept_b, order_b)])
    block_out, input_grad = call(
        output_kernel,
        (small, Near(parts), columns[0], states[0]["residual"], back[0][1], back[0][0])
        + (columns[1], states[1]["residual"], back[1][1], back[1][0]),
        [((images * SEQ, D), f32)] * 2,
        6 + 6 * owners,
    )
    grad_qkv, grad_out, grad_router, grad_bias, *vec = call(
        unpack_kernel,
        tuple(Near(end) for end in ends),
        [(shape, f32) for shape in ((own, 3 * D), (own, D), (own, E), (own, E))]
        + [((own,), f32)] * VECTORS,
        8,
    )
    return (
        block_out, input_grad, vec[GAIN1], vec[SHIFT1], grad_qkv, vec[BQ], vec[BV],
        grad_out.T, vec[BO], vec[GAIN2], vec[SHIFT2], grad_router, grad_bias.T,
        grad_expert_in, grad_hidden, grad_expert_out,
    )


def solution(mesh):
    rows, line, cols = P(AXIS, None), P(AXIS), P(None, AXIS)
    in_specs = (
        rows, rows, rows, line, line, rows, line, line, cols, line, line, line, rows, cols,
        rows, line, rows,
    )
    out_specs = (
        rows, rows, line, line, rows, line, line, cols, line, line, line, rows, cols, rows,
        line, rows,
    )

    return jax.shard_map(
        on_device, mesh=mesh, in_specs=in_specs, out_specs=out_specs, check_vma=False
    )
```

```python
import math

import jax
import jax.numpy as jnp
from jax import lax
from jax.experimental import pallas as pl
from jax.experimental.pallas import tpu as pltpu
from jax.sharding import PartitionSpec as P

D = 768
HEADS = 12
HEAD_DIM = 64
PAIRS = HEADS // 2
E = 32
SEQ = 197
ROWS = 208
CAP = 16
SLOTS = E * CAP
AXIS = "fsdp"
PACK = 3200
CUT = 1664
GAIN1, SHIFT1, BQ, BV, BO, GAIN2, SHIFT2, VECTORS = range(8)
SCALE = 1.0 / math.sqrt(HEAD_DIM)
UNROLL = PAIRS

epsilon = 1e-06
f32 = jnp.float32
bf16 = jnp.bfloat16
i32 = jnp.int32


def mm(a, b, ca=1, cb=0):
    return lax.dot_general(a, b, (((ca,), (cb,)), ((), ())), preferred_element_type=f32)


def pieces(v, n):
    out = []
    for _ in range(n):
        p = v.astype(bf16)
        out.append(p)
        v = v - p.astype(f32)
    return out


def normalize(values):
    centered = values - jnp.mean(values, axis=-1, keepdims=True)
    inverse = lax.rsqrt(jnp.mean(centered * centered, axis=-1, keepdims=True) + epsilon)
    return (centered * inverse, inverse)


def norm_back(upstream, normed, inverse):
    return inverse * (
        upstream
        - jnp.mean(upstream, axis=-1, keepdims=True)
        - normed * jnp.mean(upstream * normed, axis=-1, keepdims=True)
    )


def swap(values, bit):
    n = lax.axis_size(AXIS)
    return lax.ppermute(values, AXIS, [(d, d ^ (1 << bit)) for d in range(n)])


def bit_of(bit):
    return (lax.axis_index(AXIS) >> bit) & 1


def bit_orders():
    bits = lax.axis_size(AXIS).bit_length() - 1
    inner = (bits - 1) // 3 if bits != 5 else 1
    x = list(range(1, 1 + inner))
    y = list(range(1 + inner, 1 + 2 * inner))
    z = list(range(1 + 2 * inner, bits))
    return [0] + x + y + z, [0] + y + x + z


def merged(values, other, bit, done):
    at = sum(1 for b in done if b > bit)
    lead = values.shape[0]
    high = 1 << at
    mine = values.reshape((high, lead // high) + values.shape[1:])
    other = other.reshape(mine.shape)
    which = lax.broadcasted_iota(i32, (1, 2, 1, 1, 1), 1) == bit_of(bit)
    both = jnp.where(which, mine[:, None], other[:, None])
    return both.reshape((2 * lead,) + values.shape[1:])


def gather_rows(shard, early, wait_for, late):
    orders = bit_orders()
    steps = len(orders[0])
    common = 0
    while orders[0][-1 - common] == orders[1][-1 - common]:
        common += 1
    held, done = shard, []
    for step in range(common):
        bit = orders[0][-1 - step]
        held = lax.optimization_barrier(merged(held, swap(held, bit), bit, done))
        done.append(bit)
    held = [(held[..., :CUT], list(done)), (held[..., CUT:], list(done))]
    for step in range(common, steps):
        bits = [order[-1 - step] for order in orders]
        theirs = []
        for (values, _), bit in zip(held, bits):
            theirs.append(swap(values, bit))
        if step + 1 == steps:
            pairs = [(values, other) for (values, _), other in zip(held, theirs)]
            return pairs, wait_for, late
        tied = [
            merged(values, other, bit, seen)
            for (values, seen), other, bit in zip(held, theirs, bits)
        ]
        if step + 1 == early:
            tied.append(wait_for)
        if step + 2 == steps:
            tied, late = lax.optimization_barrier((tied, late))
        else:
            tied = lax.optimization_barrier(tied)
        if step + 1 == early:
            wait_for = tied[-1]
        held = [(t, seen + [bit]) for t, (_, seen), bit in zip(tied, held, bits)]


def owner_order(order):
    n = lax.axis_size(AXIS)
    own = D // n
    position = jnp.arange(D, dtype=i32)
    chunk = position // own
    owner = jnp.zeros_like(chunk)
    for step, bit in enumerate(order):
        owner = owner | (((chunk >> (len(order) - 1 - step)) & 1) << bit)
    return (owner ^ lax.axis_index(AXIS)) * own + position % own


def pair_order():
    own = D // lax.axis_size(AXIS)
    position = jnp.arange(D, dtype=i32)
    inside = position % (D // 2)
    lowest = bit_of(0) ^ (position // (D // 2))
    return (2 * (inside // own) + lowest) * own + inside % own


def permutation(order):
    return (jnp.arange(D, dtype=i32)[:, None] == order[None]).astype(bf16)


def row_permutation(order):
    return (order[:, None] == jnp.arange(D, dtype=i32)[None]).astype(bf16)


def scatter_rows(parts):
    ends = []
    for sent, kept, order in parts:
        for step, bit in enumerate(order):
            got = swap(sent, bit)
            if step + 1 == len(order):
                ends += [kept, got]
                break
            half = kept.shape[0] // 2
            sent, kept = lax.optimization_barrier(
                tuple(
                    (kept[part].astype(f32) + got[part].astype(f32)).astype(bf16)
                    for part in (slice(half, None), slice(0, half))
                )
            )
    return ends


def exchange(blocks):
    return lax.all_to_all(blocks, AXIS, split_axis=0, concat_axis=0, tiled=True)


def to_owners(slot_rows, owners):
    rows = slot_rows.reshape((E, 1, CAP) + slot_rows.shape[1:])
    rows = jnp.broadcast_to(rows, (E, owners) + rows.shape[2:])
    return rows.reshape((E * owners, CAP) + slot_rows.shape[1:])


def place(routes):
    choice = jnp.pad(routes.T, ((0, 0), (0, ROWS - SEQ)), constant_values=-1)
    ids = jnp.arange(E, dtype=i32)[:, None]
    first = (choice[:1] == ids).astype(bf16)
    second = (choice[1:] == ids).astype(bf16)
    t = jnp.arange(ROWS, dtype=i32)
    earlier = (t[:, None] < t[None, :]).astype(bf16)
    before = mm(jnp.concatenate([first, second], axis=0), earlier)
    rank0 = jnp.sum(before[:E] * first, axis=0)
    seen = before[E:] + jnp.sum(first.astype(f32), axis=1, keepdims=True)
    rank1 = jnp.sum(seen * second, axis=0)
    return choice * CAP + jnp.stack([rank0, rank1]).astype(i32)


def gelu_terms(v):
    cumulative = 0.5 * (1.0 + lax.erf(v * (1.0 / math.sqrt(2.0))))
    density = jnp.exp(-0.5 * v * v) * (1.0 / math.sqrt(2.0 * math.pi))
    return v * cumulative, cumulative + v * density


def dispatch_of(placed):
    slot = lax.broadcasted_iota(i32, (SLOTS, ROWS), 0)
    hit = (slot == placed[0:1, :]) | (slot == placed[1:2, :])
    return hit.astype(f32).astype(bf16)


def dispatch_rows(placed):
    slot = lax.broadcasted_iota(i32, (ROWS, SLOTS), 1)
    hit = (slot == placed[:, 0:1]) | (slot == placed[:, 1:2])
    return hit.astype(f32).astype(bf16)


def half_of(pair, second):
    lane = lax.broadcasted_iota(i32, pair.shape, 1)
    keep = (lane >= HEAD_DIM) if second else (lane < HEAD_DIM)
    return jnp.where(keep, pair, jnp.zeros_like(pair))


def join(first, second):
    lane = lax.broadcasted_iota(i32, first.shape, 1)
    return jnp.where(lane < HEAD_DIM, first, second)


def forward_kernel(get, outs, flush):
    slots, residual, prob, acts, norm1_o, context_o, router_o, out_t, small, norm2_o = outs
    sel = get(2)
    first, second = get(0), get(1)
    joined = lambda a, b: jnp.concatenate([a, b], axis=0)
    rest = mm(sel[...], joined(first[:, QKV_B[1] :], second[:, QKV_B[1] :]))
    out_t[...] = rest[:, :D].astype(bf16)
    flush(7)
    small[...] = rest[:, D:].astype(bf16)
    flush(8)
    vec = vectors_of(small)
    row = lambda k: vec[k : k + 1, :]
    inputs = get(3)[...].astype(f32)
    hat1, _ = normalize(inputs)
    norm1 = (hat1 * row(GAIN1) + row(SHIFT1)).astype(bf16)
    norm1_o[...] = norm1
    flush(4)
    moved = mm(norm1, sel[...]).astype(bf16)
    proj_a = mm(moved, joined(get(4)[...], get(5)[...]))
    proj_b = mm(moved, joined(first[:, : QKV_B[1]], second[:, : QKV_B[1]]))
    proj = jnp.concatenate([proj_a, proj_b], axis=1)
    acts[:, :D] = (proj[:, :D] + row(BQ)).astype(bf16)
    acts[:, D : 2 * D] = proj[:, D : 2 * D].astype(bf16)
    acts[:, 2 * D :] = (proj[:, 2 * D :] + row(BV)).astype(bf16)
    flush(3)
    token = lax.broadcasted_iota(i32, (ROWS, ROWS), 0) < SEQ

    def pair(j, _):
        at = lambda part: pl.ds(pl.multiple_of(part * D + j * 128, 128), 128)
        q = acts[:, at(0)] * jnp.asarray(SCALE, bf16)
        k, v = acts[:, at(1)], acts[:, at(2)]
        both = []
        for h in range(2):
            raised = jnp.exp(mm(half_of(k, h), q, 1, 1))
            raised = jnp.where(token, raised, 0.0)
            p = (raised * (1.0 / jnp.sum(raised, axis=0, keepdims=True))).astype(bf16)
            prob[2 * j + h, :, :] = p
            both.append(mm(p, v, 0, 0))
        context_o[:, at(0)] = join(both[0], both[1]).astype(bf16)
        return 0

    lax.fori_loop(0, PAIRS, pair, 0, unroll=UNROLL)
    flush(2)
    flush(5)
    res = inputs + mm(context_o[...], out_t[...], 1, 1) + row(BO)
    residual[...] = res
    flush(1)
    hat2, _ = normalize(res)
    norm2 = (hat2 * row(GAIN2) + row(SHIFT2)).astype(bf16)
    norm2_o[...] = norm2
    slots[...] = mm(dispatch_of(get(6)[...]), norm2).astype(bf16)
    flush(0)
    lane = lax.broadcasted_iota(i32, (ROWS, 128), 1)
    logits = jnp.where(lane < E, mm(norm2, small[...]), 0.0)
    raised = jnp.where(lane < E, jnp.exp(logits), 0.0)
    router_o[...] = raised / jnp.sum(raised, axis=1, keepdims=True)
    flush(6)


class Near:
    def __init__(self, array):
        self.array = array


class Stack:
    def __init__(self, arrays, rows):
        self.arrays, self.rows = arrays, rows


class Columns:
    def __init__(self, array, start, stop):
        self.array, self.start, self.stop = array, start, stop


class Fetch:
    def __init__(self, copies, groups, refs):
        self.copies, self.groups, self.refs = copies, groups, refs
        self.begun = 0
        self.waited = set()
        self.begin(2)

    def begin(self, count):
        while self.begun < min(count, len(self.groups)):
            for k in self.groups[self.begun]:
                for copy in self.copies[k]:
                    copy.start()
            self.begun += 1

    def get(self, k):
        if k in self.copies and k not in self.waited:
            at = next(g for g, group in enumerate(self.groups) if k in group)
            self.begin(at + 1)
            for copy in self.copies[k]:
                copy.wait()
            self.waited.add(k)
            if all(m in self.waited for m in self.groups[at]):
                self.begin(at + 3)
        return self.refs[k]


def call(kernel, ins, outs, limit, temps=(), groups=None, shared=None, part=0, blank=()):
    arrays, specs, scratch, plan = [], [], [], []
    for item in ins:
        if isinstance(item, Near):
            plan.append(("near", len(arrays), None))
            arrays.append(item.array)
            specs.append(pl.BlockSpec(memory_space=pltpu.VMEM))
            continue
        if isinstance(item, Stack):
            group, shape = item.arrays, (item.rows, item.arrays[0].shape[1])
            cut = None
        elif isinstance(item, Columns):
            group, shape = [item.array], (item.array.shape[0], item.stop - item.start)
            cut = (item.start, item.stop)
        else:
            group, shape, cut = [item], item.shape, None
        plan.append(("far", list(range(len(arrays), len(arrays) + len(group))), cut))
        scratch.append(pltpu.VMEM(shape, group[0].dtype))
        for array in group:
            arrays += in_hbm(array)
            specs.append(pl.BlockSpec(memory_space=pltpu.HBM))
    n_in, n_out, n_far = len(arrays), len(outs), len(scratch)
    results_in = [pltpu.VMEM(shape, dtype) for shape, dtype in outs]
    aliases = {}
    outs = list(outs)
    if shared is not None:
        slot, buffer = shared
        aliases = {n_in: slot}
        arrays += in_hbm(buffer) + [jnp.full((1,), part, i32)]
        specs += [
            pl.BlockSpec(memory_space=pltpu.HBM), pl.BlockSpec(memory_space=pltpu.SMEM),
        ]
        outs[slot] = (buffer.shape, buffer.dtype)

    def body(*refs):
        if shared is not None:
            which = refs[n_in + 1]
            refs = refs[:n_in] + refs[n_in + 2 :]
        far_in, far_out = refs[:n_in], refs[n_in : n_in + n_out]
        near = refs[n_in + n_out + len(blank) : -1]
        sems = refs[-1]
        copies, views, used, sem = {}, [], 0, 0
        for k, (kind, index, cut) in enumerate(plan):
            if kind == "near":
                views.append(far_in[index])
                continue
            target = near[used]
            used += 1
            views.append(target)
            copies[k], row = [], 0
            for at in index:
                source = far_in[at]
                if cut is not None:
                    source = source.at[:, cut[0] : cut[1]]
                if len(target.shape) > 1 and source.shape[0] != target.shape[0]:
                    place_at = target.at[row : row + source.shape[0], :]
                else:
                    place_at = target
                row += source.shape[0]
                copies[k].append(pltpu.make_async_copy(source, place_at, sems.at[sem]))
                sem += 1
        order = groups if groups is not None else [list(range(len(plan)))]
        order = [[k for k in group if k in copies] for group in order]
        source = Fetch(copies, order, views)
        results = near[n_far : n_far + n_out]
        far_out = list(far_out)
        if shared is not None:
            rows = results[slot].shape[0]
            at = pl.multiple_of(which[0] * rows, 16)
            far_out[slot] = far_out[slot].at[pl.ds(at, rows), :]
        started = []

        def flush(k, cols=None):
            source_ref, target_ref = results[k], far_out[k]
            if cols is not None:
                source_ref, target_ref = source_ref.at[:, cols], target_ref.at[:, cols]
            at = sems.at[sem + len(started)]
            started.append(pltpu.make_async_copy(source_ref, target_ref, at))
            started[-1].start()

        kernel(source.get, near[n_far:], flush)
        for k in copies:
            source.get(k)
        for copy in started:
            copy.wait()

    n_sems = sum(len(index) for kind, index, _ in plan if kind == "far") + n_out + 2
    return pl.pallas_call(
        body,
        in_specs=specs,
        out_specs=[pl.BlockSpec(memory_space=pltpu.HBM)] * (n_out + len(blank)),
        out_shape=[pltpu.HBM(shape, dtype) for shape, dtype in outs + list(blank)],
        scratch_shapes=scratch
        + results_in
        + [pltpu.VMEM(shape, dtype) for shape, dtype in temps]
        + [pltpu.SemaphoreType.DMA((n_sems,))],
        input_output_aliases=aliases,
        compiler_params=pltpu.CompilerParams(vmem_limit_bytes=limit << 20),
    )(*arrays)


def in_hbm(*arrays):
    return [pltpu.with_memory_space_constraint(a, pltpu.HBM) for a in arrays]


def vectors_of(small):
    lane = lax.broadcasted_iota(i32, (8, 128), 1)
    pick = lane == lax.broadcasted_iota(i32, (8, 128), 0) + 2 * E
    return mm(pick.astype(f32).astype(bf16), small[...], 1, 1)


QKV_B = (0, 3 * D - CUT)
OUT_T = (3 * D - CUT, 4 * D - CUT)
SMALL = (4 * D - CUT, PACK - CUT)


def attend_forward(x, placed, halves_a, halves_b, sel):
    names = ("slots", "residual", "prob", "acts", "norm1", "context", "router")
    names += ("out_t", "small")
    outs = call(
        forward_kernel,
        tuple(Near(half) for half in halves_b) + (Near(sel), Near(x))
        + tuple(Near(half) for half in halves_a) + (placed,),
        [
            ((SLOTS, D), bf16), ((ROWS, D), f32), ((HEADS, ROWS, ROWS), bf16),
            ((ROWS, 3 * D), bf16), ((ROWS, D), bf16), ((ROWS, D), bf16),
            ((ROWS, 128), f32), ((D, D), bf16), ((D, 128), bf16),
        ],
        12,
        [((ROWS, D), bf16)],
    )
    return dict(zip(names, outs))


def backward_kernel(get, outs, flush):
    input_grad, gate_o, ph, res_half_o, sums, cgs = outs
    rec, placed, small, cot = get(0), get(1), get(2), get(3)
    vec = vectors_of(small)
    row = lambda k: vec[k : k + 1, :]
    disp = dispatch_rows(placed[...])
    lane = lax.broadcasted_iota(i32, (ROWS, 128), 1)
    chosen = (lane == placed[:, 0:1] // CAP) | (lane == placed[:, 1:2] // CAP)
    gate_o[...] = jnp.where(chosen, get(4)[...], 0.0)
    flush(1)
    second = 0.0
    for o in range(rec.shape[1]):
        second = second + mm(disp, rec[:, o, :, :].reshape(SLOTS, D))
    hat2, rstd2 = normalize(get(5)[...])
    sums[GAIN2 : GAIN2 + 1, :] = jnp.sum(second * hat2, axis=0, keepdims=True)
    sums[SHIFT2 : SHIFT2 + 1, :] = jnp.sum(second, axis=0, keepdims=True)
    res_grad = cot[...].astype(f32) + norm_back(second * row(GAIN2), hat2, rstd2)
    input_grad[...] = res_grad
    sums[BO : BO + 1, :] = jnp.sum(res_grad, axis=0, keepdims=True)
    res_half = res_grad.astype(bf16)
    res_half_o[...] = res_half
    flush(3)
    cgs[...] = mm(res_half, get(6)[...]).astype(bf16)
    prob, acts = get(7), get(8)

    def pair(j, _):
        at = lambda part: pl.ds(pl.multiple_of(part * D + j * 128, 128), 128)
        q, k, v = acts[:, at(0)], acts[:, at(1)], acts[:, at(2)]
        c = cgs[:, at(0)]
        qs, ks, vs = [], [], []
        for h in range(2):
            p = prob[2 * j + h, :, :]
            pf = p.astype(f32)
            t = pf * mm(half_of(v, h), c, 1, 1)
            sg = ((t - pf * jnp.sum(t, axis=0, keepdims=True)) * SCALE).astype(bf16)
            vs.append(mm(p, c))
            qs.append(mm(sg, k, 0, 0))
            ks.append(mm(sg, q))
        qg, kg, vg = join(*qs), join(*ks), join(*vs)
        sums[BQ : BQ + 1, at(0)] = jnp.sum(qg, axis=0, keepdims=True)
        sums[BV : BV + 1, at(0)] = jnp.sum(vg, axis=0, keepdims=True)
        ph[:, at(0)] = qg.astype(bf16)
        ph[:, at(1)] = kg.astype(bf16)
        ph[:, at(2)] = vg.astype(bf16)
        return 0

    lax.fori_loop(0, PAIRS, pair, 0, unroll=UNROLL)
    flush(2)
    first = mm(ph[:, :CUT], get(9)[...], 1, 1) + mm(ph[:, CUT:], get(10)[...], 1, 1)
    hat1, rstd1 = normalize(get(11)[...].astype(f32))
    sums[GAIN1 : GAIN1 + 1, :] = jnp.sum(first * hat1, axis=0, keepdims=True)
    sums[SHIFT1 : SHIFT1 + 1, :] = jnp.sum(first, axis=0, keepdims=True)
    sums[7:8, :] = jnp.zeros((1, D), f32)
    flush(4)
    input_grad[...] += norm_back(first * row(GAIN1), hat1, rstd1)
    flush(0)


BACKWARD_TEMPS = [
    ((ROWS, 3 * D), bf16), ((ROWS, D), bf16), ((8, D), f32),
]


def backward_operands(rec, x, cot, placed, s, qkv_a, qkv_b, out_t, small):
    return (
        rec, placed, small, cot, s["router"], s["residual"], Near(out_t), s["prob"],
        s["acts"], Near(qkv_a), Near(qkv_b), x,
    )


BACKWARD_GROUPS = [[0, 1, 2, 3, 4, 5], [7, 8], [11]]


def token_backward(part, buffer, *args):
    return call(
        backward_kernel,
        backward_operands(*args),
        [((ROWS, D), f32), ((ROWS, 128), f32)] + BACKWARD_TEMPS,
        14 + 4 * args[0].shape[1],
        [((ROWS, D), bf16)],
        BACKWARD_GROUPS,
        (2, buffer),
        part,
    )


def expert_kernel(
    idx, x, c, w_in, w_out, bias, small, act, back, d_rows, gated, gate, grad_bias, grad_router,
    acc, gg, prob,
):
    r, f = pl.program_id(0), pl.program_id(1)
    rows, width = act.shape
    slices = pl.num_programs(0) * rows // SLOTS

    @pl.when(f == 0)
    def _():
        logits = mm(x[...], small[...])
        lane = lax.broadcasted_iota(i32, logits.shape, 1)
        raised = jnp.where(lane < E, jnp.exp(jnp.where(lane < E, logits, 0.0)), 0.0)
        raised = raised / jnp.sum(raised, axis=1, keepdims=True)
        prob[...] = raised
        g = jnp.sum(jnp.where(lane == idx[0], raised, 0.0), axis=1, keepdims=True)
        gate[...] = jnp.broadcast_to(g, gate.shape)
        rows_c = c[...].reshape(rows, D)
        gated[...] = (rows_c.astype(f32) * g).astype(bf16)
        dots = jnp.where(lane == idx[0] + E, mm(rows_c, small[...]), 0.0)
        gg[...] = dots * (1.0 / slices)
        acc[...] = jnp.zeros_like(acc)

    value, slope = gelu_terms(mm(x[...], w_in[...], 1, 1) + bias[...])
    hid = mm(c[...].reshape(rows, D), w_out[...], 1, 1)
    act[...] = value.astype(bf16)
    both = value * hid
    part = both[:, :128]
    for j in range(1, width // 128):
        part = part + both[:, j * 128 : (j + 1) * 128]
    gg[...] += part
    before = hid * slope * gate[:, :1]
    total = jnp.sum(before, axis=0, keepdims=True)
    half = before.astype(bf16)
    back[...] = half
    acc[...] += mm(half, w_in[...])
    cols = pl.ds(pl.multiple_of(f * width, width), width)

    @pl.when(r == 0)
    def _():
        grad_bias[:, cols] = total

    @pl.when(r > 0)
    def _():
        grad_bias[:, cols] += total

    @pl.when(f == pl.num_programs(1) - 1)
    def _():
        g = jnp.sum(gg[...], axis=1, keepdims=True)
        lane = lax.broadcasted_iota(i32, (rows, 128), 1)
        picked = (lane == idx[0]).astype(f32)
        logit = (g * prob[...] * (picked - gate[...])).astype(bf16)
        d_rows[...] = (acc[...] + mm(logit, small[...], 1, 1)).astype(bf16)
        share = mm(x[...], logit, 0, 0)

        @pl.when(r == 0)
        def _():
            grad_router[...] = share

        @pl.when(r > 0)
        def _():
            grad_router[...] += share


def expert_main(i, x, c, w_in, w_out, bias, router, expert):
    total, width = x.shape[0], w_in.shape[0]
    rb, fb = min(512, total), min(768, width)
    row = lambda r, f, *_: (r, 0)
    tile = lambda r, f, *_: (r, f)
    fixed = lambda r, f, *_: (0, 0)
    return pl.pallas_call(
        expert_kernel,
        grid_spec=pltpu.PrefetchScalarGridSpec(
            num_scalar_prefetch=1,
            grid=(total // rb, width // fb),
            in_specs=[
                pl.BlockSpec((rb, D), row),
                pl.BlockSpec((rb // CAP, None, CAP, D), lambda r, f, idx: (r, idx[1], 0, 0)),
                pl.BlockSpec((fb, D), lambda r, f, *_: (f, 0)),
                pl.BlockSpec((fb, D), lambda r, f, *_: (f, 0)),
                pl.BlockSpec((1, fb), lambda r, f, *_: (0, f)),
                pl.BlockSpec((D, 128), fixed),
            ],
            out_specs=[
                pl.BlockSpec((rb, fb), tile),
                pl.BlockSpec((rb, fb), tile),
                pl.BlockSpec((rb, D), row),
                pl.BlockSpec((rb, D), row),
                pl.BlockSpec((rb, 128), row),
                pl.BlockSpec((1, width), fixed),
                pl.BlockSpec((D, 128), fixed),
            ],
            scratch_shapes=[
                pltpu.VMEM((rb, D), f32),
                pltpu.VMEM((rb, 128), f32),
                pltpu.VMEM((rb, 128), f32),
            ],
        ),
        out_shape=[
            pltpu.HBM((total, width), bf16),
            pltpu.HBM((total, width), bf16),
            pltpu.HBM((total, D), bf16),
            pltpu.HBM((total, D), bf16),
            pltpu.HBM((total, 128), f32),
            pltpu.HBM((1, width), f32),
            pltpu.HBM((D, 128), f32),
        ],
        compiler_params=pltpu.CompilerParams(
            dimension_semantics=("arbitrary", "arbitrary"), vmem_limit_bytes=22 << 20
        ),
        name="expert_main",
    )(jnp.stack([expert, jnp.int32(i)]), *in_hbm(x, c, w_in, w_out, bias.reshape(1, width), router))


def parts_kernel(act0, act1, gate0, gate1, w_out, out, acc):
    f = pl.program_id(0)

    @pl.when(f == 0)
    def _():
        acc[...] = jnp.zeros_like(acc)

    for i, act in enumerate((act0, act1)):
        acc[i] += mm(act[...], w_out[...])

    @pl.when(f == pl.num_programs(0) - 1)
    def _():
        for i, gate in enumerate((gate0, gate1)):
            rows = (acc[i] * gate[:, :1]).astype(bf16)
            out[:, i, :, :] = rows.reshape(out.shape[0], CAP, D)


def expert_parts(acts, gates, w_out):
    total, width = acts[0].shape
    fb = min(768, width)
    n = total // CAP
    cols = pl.BlockSpec((total, fb), lambda f: (0, f))
    full = pl.BlockSpec((total, 128), lambda f: (0, 0))
    return pl.pallas_call(
        parts_kernel,
        grid=(width // fb,),
        in_specs=[cols, cols, full, full, pl.BlockSpec((fb, D), lambda f: (f, 0))],
        out_specs=pl.BlockSpec((n, 2, CAP, D), lambda f: (0, 0, 0, 0)),
        out_shape=pltpu.HBM((n, 2, CAP, D), bf16),
        scratch_shapes=[pltpu.VMEM((2, total, D), f32)],
        compiler_params=pltpu.CompilerParams(
            dimension_semantics=("arbitrary",),
            vmem_limit_bytes=(18 if total <= 512 else 48) << 20,
        ),
        name="expert_parts",
    )(*in_hbm(*acts, *gates, w_out))


def moved_kernel(get, outs, flush):
    for k, (value, perm) in enumerate(((0, 2), (0, 3), (1, 3))):
        outs[k][...] = mm(get(perm)[...], get(value)[...], 1, 1).astype(bf16)
        flush(k)


def rest_kernel(get, outs, flush):
    sent_b, kept_b = outs
    half = D // 2

    def lay(value, start):
        kept_b[:, start : start + value.shape[1]] = value[:half].astype(bf16)
        sent_b[:, start : start + value.shape[1]] = value[half:].astype(bf16)

    lay(mm(get(0)[...], get(1)[...]), 0)
    perm = get(2)[...]
    out = mm(mm(perm, get(3)[...], 1, 1).astype(bf16), get(4)[...])
    lay(out, OUT_T[0])
    ready, last = slice(0, SMALL[0]), slice(SMALL[0], PACK - CUT)
    flush(0, ready)
    flush(1, ready)
    sums = get(5)[...] + get(6)[...]
    zeros = lambda n: jnp.zeros((n, D), f32)
    spread = jnp.concatenate([zeros(2 * E), sums, zeros(128 - 2 * E - 8)], axis=0)
    router = (get(7)[...] + get(8)[...]).astype(bf16)
    tail = mm(perm, spread.astype(bf16), 1, 1) + mm(perm, router)
    tail = tail + mm(get(9)[...], pltpu.roll(get(10)[...], E, 1).astype(bf16))
    lay(tail, SMALL[0])
    flush(0, last)
    flush(1, last)


def eye(size, width=None, shift=0):
    shape = (size, width or size)
    hit = lax.broadcasted_iota(i32, shape, 1) == lax.broadcasted_iota(i32, shape, 0) + shift
    return hit.astype(f32).astype(bf16)


def pack_kernel(get, outs, flush):
    packed = outs[0]
    w_qkv, w_out, router, bias = (get(k) for k in range(4))
    own = w_qkv.shape[0]
    packed[0, :, : 3 * D] = w_qkv[...]
    packed[0, :, 3 * D : 4 * D] = w_out[...]
    rows = [get(4 + k)[...].astype(f32).reshape(1, own) for k in range(VECTORS)]
    rows = jnp.concatenate(rows + [jnp.zeros((1, own), f32)], axis=0).astype(bf16)
    columns = mm(eye(own), rows, 1, 1).astype(bf16)
    tail = mm(router[...], eye(E, 128)) + mm(bias[...], eye(E, 128, E))
    tail = tail + mm(columns, eye(8, 128, 2 * E))
    packed[0, :, 4 * D :] = tail.astype(bf16)
    flush(0)


def unpack_kernel(get, outs, flush):
    w_qkv, w_out, router, bias = outs[:4]
    add = lambda k: get(k)[...].astype(f32) + get(k + 1)[...].astype(f32)
    w_qkv[:, :CUT] = add(0)
    mine = add(2)
    w_qkv[:, CUT:] = mine[:, QKV_B[0] : QKV_B[1]]
    flush(0)
    w_out[...] = mine[:, OUT_T[0] : OUT_T[1]]
    flush(1)
    tail = mine[:, SMALL[0] :]
    router[...] = tail[:, :E]
    flush(2)
    bias[...] = tail[:, E : 2 * E]
    flush(3)
    rows = sum(mm(eye(8, 128, 2 * E), p, 1, 1) for p in pieces(tail, 3))
    for k in range(VECTORS):
        outs[4 + k][...] = rows[k]
        flush(4 + k)


def output_kernel(get, outs, flush):
    block_out, input_grad = outs
    small, parts = get(0), get(1)
    for i in range(2):
        placed, residual, gate, grad = (get(2 + 4 * i + k) for k in range(4))
        input_grad[i * SEQ : (i + 1) * SEQ, :] = grad[:SEQ, :]
        disp = dispatch_rows(placed[...])
        out = residual[...]
        for o in range(parts.shape[1]):
            out = out + mm(disp, parts[:, o, i, :, :].reshape(SLOTS, D))
        for p in pieces(pltpu.roll(gate[...], E, 1), 2):
            out = out + mm(p, small[...], 1, 1)
        block_out[i * SEQ : (i + 1) * SEQ, :] = out[:SEQ]
    flush(0)
    flush(1)


def weights_kernel(act0, act1, back0, back1, g0, g1, x0, x1, out_w, in_w):
    out_w[...] = mm(act0[...], g0[...], 0, 0) + mm(act1[...], g1[...], 0, 0)
    in_w[...] = mm(back0[...], x0[...], 0, 0) + mm(back1[...], x1[...], 0, 0)


def expert_weights(acts, backs, gated, xs):
    total, width = acts[0].shape
    fb = 512 if width % 512 == 0 else 384
    cols = pl.BlockSpec((total, fb), lambda f: (0, f))
    full = pl.BlockSpec((total, D), lambda f: (0, 0))
    rows = pl.BlockSpec((fb, D), lambda f: (f, 0))
    return pl.pallas_call(
        weights_kernel,
        grid=(width // fb,),
        in_specs=[cols] * 4 + [full] * 4,
        out_specs=[rows, rows],
        out_shape=[pltpu.HBM((width, D), f32)] * 2,
        compiler_params=pltpu.CompilerParams(
            dimension_semantics=("arbitrary",),
            vmem_limit_bytes=(22 if total <= 512 else 40) << 20,
        ),
        name="expert_weights",
    )(*in_hbm(*acts, *backs, *gated, *xs))


def on_device(
    block_in, out_cotangent, expert_routes, ln1_gain, ln1_shift, w_qkv, bias_query, bias_value,
    w_out, bias_out, ln2_gain, ln2_shift, w_router, expert_bias, w_expert_in, bias_hidden,
    w_expert_out,
):
    images = block_in.shape[0] // SEQ
    n = lax.axis_size(AXIS)
    owners = n // E
    own = ln1_gain.shape[0]
    expert = lax.axis_index(AXIS) // owners
    order_a, order_b = bit_orders()
    barrier = lax.optimization_barrier
    (shard,) = call(
        pack_kernel,
        (w_qkv, w_out.T, w_router, expert_bias.T)
        + (ln1_gain, ln1_shift, bias_query, bias_value, bias_out, ln2_gain, ln2_shift),
        [((1, own, PACK), bf16)],
        8,
    )

    pad_rows = ((0, ROWS - SEQ), (0, 0))
    xs, cots, placed, states, outgoing = [], [], [], [], []
    for i in range(images):
        xs.append(jnp.pad(block_in[i * SEQ : (i + 1) * SEQ], pad_rows))
        cots.append(jnp.pad(out_cotangent[i * SEQ : (i + 1) * SEQ], pad_rows))
        placed.append(place(expert_routes[i * SEQ : (i + 1) * SEQ]))
        slots = mm(dispatch_of(placed[i]), cots[i]).astype(bf16)
        outgoing.append(to_owners(slots, owners))
    late = (
        xs, cots, [p.T for p in placed], permutation(pair_order()),
        row_permutation(owner_order(order_a)), row_permutation(owner_order(order_b)),
    )
    halves, outgoing, late = gather_rows(shard, 3, jnp.stack(outgoing, axis=1), late)
    xs, cots, columns, sel, perm_a, perm_b = late
    flat = [tuple(h.reshape(D // 2, h.shape[-1]) for h in pair) for pair in halves]
    cot_in = exchange(outgoing)
    for i in range(images):
        states.append(attend_forward(xs[i], placed[i], flat[0], flat[1], sel))
    both = lambda key: [s[key] for s in states]
    norm1a, norm1b, cotb, ph = call(
        moved_kernel,
        (Stack(both("norm1"), 2 * ROWS), Stack(cots, 2 * ROWS), perm_a, perm_b),
        [((D, 2 * ROWS), bf16)] * 3,
        12,
        blank=[((images * ROWS, 3 * D), bf16)],
    )
    first = exchange(to_owners(states[0]["slots"], owners))
    second = exchange(to_owners(states[1]["slots"], owners))
    arrived = [first.reshape(-1, D), second.reshape(-1, D)]
    small, out_t = states[0]["small"], states[0]["out_t"]
    rest = list(range(lax.axis_size(AXIS).bit_length() - 1))[1:]
    natural = [
        merged(mine, theirs, 0, rest)
        for mine, theirs in (halves[0], tuple(h[..., : QKV_B[1]] for h in halves[1]))
    ]
    qkv_a, qkv_b = [v.reshape(D, v.shape[-1]) for v in natural]
    done = []
    grad_hidden = 0.0
    received = []
    router_grads = []
    for i in range(images):
        act, back, d_rows, gated, gate, gb, gr = expert_main(
            i, arrived[i], cot_in, w_expert_in, w_expert_out, bias_hidden, small, expert
        )
        done.append((act, back, gated, gate))
        router_grads.append(gr)
        grad_hidden = grad_hidden + gb[0]
        if i == 0:
            d_rows, qkv_b = barrier((d_rows, qkv_b))
        else:
            d_rows, qkv_a = barrier((d_rows, qkv_a))
        rows = exchange(d_rows.reshape(n, CAP, D))
        received.append(rows.reshape(E, owners, CAP, D))
    sent = expert_parts([d[0] for d in done], [d[3] for d in done], w_expert_out)
    parts = exchange(sent).reshape(E, owners, images, CAP, D)
    column = lambda k: [d[k] for d in done]
    grad_expert_out, grad_expert_in = expert_weights(
        column(0), column(1), column(2), arrived
    )
    back = []
    for i in range(images):
        results = token_backward(
            i, ph, received[i], xs[i], cots[i], columns[i], states[i],
            qkv_a, qkv_b, out_t, small,
        )
        ph = results[2]
        back.append(results)
    pair = lambda k: [b[k] for b in back]
    sent_a = mm(norm1a[D // 2 :], ph[:, :CUT]).astype(bf16)
    kept_a = mm(norm1a[: D // 2], ph[:, :CUT]).astype(bf16)
    sent_b, kept_b = call(
        rest_kernel,
        (norm1b, Columns(ph, CUT, 3 * D), perm_b, Stack(pair(3), 2 * ROWS))
        + (Stack(both("context"), 2 * ROWS),) + tuple(pair(4)) + tuple(router_grads)
        + (cotb, Stack(pair(1), 2 * ROWS)),
        [((D // 2, PACK - CUT), bf16)] * 2,
        24,
        (),
        [[0, 1], [2, 3, 4], [5, 6, 7, 8, 9, 10]],
    )
    ends = scatter_rows([(sent_a, kept_a, order_a), (sent_b, kept_b, order_b)])
    block_out, input_grad = call(
        output_kernel,
        (small, Near(parts), columns[0], states[0]["residual"], back[0][1], back[0][0])
        + (columns[1], states[1]["residual"], back[1][1], back[1][0]),
        [((images * SEQ, D), f32)] * 2,
        6 + 6 * owners,
    )
    grad_qkv, grad_out, grad_router, grad_bias, *vec = call(
        unpack_kernel,
        tuple(Near(end) for end in ends),
        [(shape, f32) for shape in ((own, 3 * D), (own, D), (own, E), (own, E))]
        + [((own,), f32)] * VECTORS,
        8,
    )
    return (
        block_out, input_grad, vec[GAIN1], vec[SHIFT1], grad_qkv, vec[BQ], vec[BV],
        grad_out.T, vec[BO], vec[GAIN2], vec[SHIFT2], grad_router, grad_bias.T,
        grad_expert_in, grad_hidden, grad_expert_out,
    )


def solution(mesh):
    rows, line, cols = P(AXIS, None), P(AXIS), P(None, AXIS)
    in_specs = (
        rows, rows, rows, line, line, rows, line, line, cols, line, line, line, rows, cols,
        rows, line, rows,
    )
    out_specs = (
        rows, rows, line, line, rows, line, line, cols, line, line, line, rows, cols, rows,
        line, rows,
    )

    return jax.shard_map(
        on_device, mesh=mesh, in_specs=in_specs, out_specs=out_specs, check_vma=False
    )
```
